32 devices in a mesh: seq: 2 (over y), fsdp: 16 (over z, x, core).
Axes of the slice: x: 2, y: 2, z: 4, core: 2. Of those that a mesh axis runs over, the one named last changes fastest.
Arguments:
- tokens: bfloat16 [16, 1024, 768], P('fsdp', 'seq'), may hold values from -6 to 6
- doc_lengths: int32 [16, 16], P('fsdp'), may hold values from 1 to 256, 1024 in all within a row
- feature_ints: int32 [12, 64, 256], replicated, may hold values from -128 to 127
- w_query: bfloat16 [768, 768], P('fsdp'), may hold values from -0.21875 to 0.21875
- b_query: bfloat16 [768], P('fsdp'), may hold values from -1.75 to 1.75
- w_key: bfloat16 [768, 768], P('fsdp'), may hold values from -0.21875 to 0.21875
- b_key: bfloat16 [768], P('fsdp'), may hold values from -1.75 to 1.75
- w_value: bfloat16 [768, 768], P('fsdp'), may hold values from -0.21875 to 0.21875
- b_value: bfloat16 [768], P('fsdp'), may hold values from -3 to 3
- w_out: bfloat16 [768, 768], P('fsdp'), may hold values from -1.25 to 1.25
- b_out: bfloat16 [768], P('fsdp'), may hold values from -3 to 3
- norm1_gain: bfloat16 [768], P('fsdp'), may hold values from 0.25 to 1.75
- norm1_bias: bfloat16 [768], P('fsdp'), may hold values from -3 to 3
- w_in: bfloat16 [768, 3072], P('fsdp'), may hold values from -0.21875 to 0.21875
- b_in: bfloat16 [3072], P('fsdp'), may hold values from -3 to 3
- w_down: bfloat16 [3072, 768], P('fsdp'), may hold values from -0.109375 to 0.109375
- b_down: bfloat16 [768], P('fsdp'), may hold values from -3 to 3
- norm2_gain: bfloat16 [768], P('fsdp'), may hold values from 0.25 to 1.75
- norm2_bias: bfloat16 [768], P('fsdp'), may hold values from -3 to 3
- cotangent: bfloat16 [16, 1024, 768], P('fsdp', 'seq'), may hold values from -6 to 6
Outputs:
- layer_out: bfloat16 [16, 1024, 768], P('fsdp', 'seq')
- grad_tokens: float32 [16, 1024, 768], P('fsdp', 'seq')
- grad_w_query: float32 [768, 768], P('fsdp')
- grad_b_query: float32 [768], P('fsdp')
- grad_w_key: float32 [768, 768], P('fsdp')
- grad_b_key: float32 [768], P('fsdp')
- grad_w_value: float32 [768, 768], P('fsdp')
- grad_b_value: float32 [768], P('fsdp')
- grad_w_out: float32 [768, 768], P('fsdp')
- grad_b_out: float32 [768], P('fsdp')
- grad_norm1_gain: float32 [768], P('fsdp')
- grad_norm1_bias: float32 [768], P('fsdp')
- grad_w_in: float32 [768, 3072], P('fsdp')
- grad_b_in: float32 [3072], P('fsdp')
- grad_w_down: float32 [3072, 768], P('fsdp')
- grad_b_down: float32 [768], P('fsdp')
- grad_norm2_gain: float32 [768], P('fsdp')
- grad_norm2_bias: float32 [768], P('fsdp')
The draws below stay inside these ranges and needn't reach their ends.
Inputs may be any that keep to these rules, and one draw needn't show every extreme that they name: `doc_lengths`: each row lists the document lengths of one stream in order and sums to 1024; the longest document of every row has exactly 256 tokens.
All inputs are finite; a program needn't handle non-finite values.
Results may differ from the reference program's by a relative error of at most 0.03.
Values may be sent and summed in bfloat16 or wider, within the bound.
A program may use at most 128 MiB of HBM per device.

```python
import math
import jax
import jax.numpy as jnp
import numpy as np
from jax import lax

D = 768
H = 12
DH = 64
F = 256
FF = 3072
SLEN = 1024
NDOC = 16
STREAMS = 16


def plant(drawn, own_key, least, largest):
    longest = drawn.shape.index(max(drawn.shape))
    spots = []
    for shift in (0, 1):
        where = [jax.random.randint(jax.random.fold_in(own_key, axis), (), 0, length) for axis, length in enumerate(drawn.shape)]
        where[longest] = (where[longest] + shift) % drawn.shape[longest]
        spots.append(tuple(where))
    return drawn.at[spots[0]].set(least).at[spots[1]].set(largest)


def with_spikes(entries, rng, source, target, parts, factor):
    owner, partner = [(jnp.arange(entries.shape[axis_at]) // (entries.shape[axis_at] // parts)).reshape([-1 if axis == axis_at else 1 for axis in range(entries.ndim)]) for axis_at in (source, target)]
    chosen = jax.random.permutation(rng, parts)[partner]
    strong = (owner == chosen) | (owner == (partner + parts // 2) % parts)
    return jnp.where(strong, factor * entries, entries)


def block_levels(rng, dims, split, least, top_value):
    def one(dim, blocks):
        heights = jax.random.uniform(jax.random.fold_in(jax.random.fold_in(rng, 6), dim), (blocks,), jnp.float32, least / len(split), top_value / len(split))
        return jnp.repeat(jnp.exp(heights), dims[dim] // blocks).reshape((-1,) + (1,) * (len(dims) - dim - 1))

    loudness = one(*split[0])
    for cut in split[1:]:
        loudness = loudness * one(*cut)
    return loudness


def split_up(count, total, bound, lean):
    portions = [(1 << 20) // math.isqrt(standing ** lean) + 1 for standing in range(2, count + 1)]
    spare, given = total - bound - (count - 1), [1] * (count - 1)
    while spare > 0:
        free = [i for i in range(count - 1) if given[i] < bound]
        whole, left = sum([portions[i] for i in free]), spare
        for i in free:
            more = min(bound - given[i], max(1, left * portions[i] // whole), spare)
            given[i] = given[i] + more
            spare = spare - more
    return np.array([bound] + given)


def ragged(rng, count, total, limit, skew):
    if count == 2:
        one = jax.random.randint(rng, (), max(1, total - limit), min(limit, total - 1) + 1)
        return jnp.stack([one, total - one])
    lengths = jnp.asarray(split_up(count, total, limit, skew), jnp.int32)
    twos = (count - 1) // 2
    giver, sink = lengths[1:1 + 2 * twos:2], lengths[2:2 + 2 * twos:2]
    margin = jnp.minimum(giver - 1, limit - sink)
    moved = jax.random.randint(jax.random.fold_in(rng, 1), (twos,), 0, 1 << 20) % (margin + 1)
    lengths = lengths.at[1:1 + 2 * twos:2].set(giver - moved).at[2:2 + 2 * twos:2].set(sink + moved)
    return lengths[jax.random.permutation(jax.random.fold_in(rng, 2), count)]


def normal_values(own_key, dims, scale, most, cuts=(), kind=jnp.bfloat16):
    loudness = block_levels(own_key, dims, cuts, -0.22, 0.18) if cuts else 1.0
    result = jax.random.normal(own_key, dims, jnp.float32) * scale * loudness
    return jnp.minimum(jnp.maximum(result, -most), most).astype(kind)


def noise_with(stream_key, shape, spread, limit, shards, heavy, kind=jnp.bfloat16):
    drawn = spread * jax.random.normal(stream_key, shape, jnp.float32)
    if shards:
        drawn = drawn * block_levels(stream_key, shape, shards, -0.22, 0.18)
    return jnp.clip(with_spikes(drawn, jax.random.fold_in(stream_key, 3), *heavy), -limit, limit).astype(kind)


def setup_inputs(seed: int = 0) -> dict:
    streams_of = jax.random.split(jax.random.key(seed), 21)
    tokens = noise_with(streams_of[0], (STREAMS, SLEN, D), 1.0, 6.0, ((0, 16), (1, 2)), (0, 2, 16, 2.0))
    doc_lengths = jax.vmap(lambda own: ragged(own, NDOC, SLEN, SLEN // 4, 2))(jax.random.split(streams_of[1], STREAMS)).reshape((STREAMS, NDOC)).astype(jnp.int32)
    feature_ints = plant(jax.random.randint(streams_of[2], (H, DH, F), -128, 128), jax.random.fold_in(streams_of[2], 1), -128, 127).astype(jnp.int32)
    w_query = normal_values(streams_of[3], (D, D), D ** -0.5, 0.21875, ((0, 16),))
    b_query = normal_values(streams_of[4], (D,), 0.3, 1.75, ((0, 16),))
    w_key = normal_values(streams_of[5], (D, D), D ** -0.5, 0.21875, ((0, 16),))
    b_key = normal_values(streams_of[6], (D,), 0.3, 1.75, ((0, 16),))
    w_value = normal_values(streams_of[7], (D, D), D ** -0.5, 0.21875, ((0, 16),))
    b_value = normal_values(streams_of[8], (D,), 0.5, 3.0, ((0, 16),))
    w_out = normal_values(streams_of[9], (D, D), (D // 32) ** -0.5, 1.25, ((0, 16),))
    b_out = normal_values(streams_of[10], (D,), 0.5, 3.0, ((0, 16),))
    norm1_gain = jnp.clip(1.0 + 0.15 * jax.random.normal(streams_of[11], (D,), jnp.float32), 0.25, 1.75).astype(jnp.bfloat16)
    norm1_bias = normal_values(streams_of[12], (D,), 0.5, 3.0, ((0, 16),))
    w_in = normal_values(streams_of[13], (D, FF), D ** -0.5, 0.21875, ((0, 16),))
    b_in = normal_values(streams_of[14], (FF,), 0.5, 3.0, ((0, 16),))
    w_down = normal_values(streams_of[15], (FF, D), FF ** -0.5, 0.109375, ((0, 16),))
    b_down = normal_values(streams_of[16], (D,), 0.5, 3.0, ((0, 16),))
    norm2_gain = jnp.clip(1.0 + 0.15 * jax.random.normal(streams_of[17], (D,), jnp.float32), 0.25, 1.75).astype(jnp.bfloat16)
    norm2_bias = normal_values(streams_of[18], (D,), 0.5, 3.0, ((0, 16),))
    cotangent = normal_values(streams_of[19], (STREAMS, SLEN, D), 1.0, 6.0, ((0, 16), (1, 2)))
    return dict(tokens=tokens, doc_lengths=doc_lengths, feature_ints=feature_ints, w_query=w_query, b_query=b_query, w_key=w_key, b_key=b_key, w_value=w_value, b_value=b_value, w_out=w_out, b_out=b_out, norm1_gain=norm1_gain, norm1_bias=norm1_bias, w_in=w_in, b_in=b_in, w_down=w_down, b_down=b_down, norm2_gain=norm2_gain, norm2_bias=norm2_bias, cotangent=cotangent)


@jax.custom_vjp
def low(v):
    return lax.optimization_barrier(v.astype(jnp.bfloat16)).astype(jnp.float32)

@jax.custom_vjp
def low_back(v):
    return v

def low_keep(v):
    return (low(v), None)

def low_pass(kept, grad):
    return (grad,)

def back_keep(v):
    return (v, None)

def back_low(kept, grad):
    return (low(grad),)
low.defvjp(low_keep, low_pass)
low_back.defvjp(back_keep, back_low)
unit_spread = 0.013531646934131853
highest = lax.Precision.HIGHEST

def project(row_block, weight, bias_row):
    return jnp.dot(row_block, weight, precision=highest, preferred_element_type=jnp.float32) + bias_row

def layer_norm(residual, norm_gain, norm_bias):
    centred = residual - lax.optimization_barrier(jnp.mean(residual, axis=-1, keepdims=True))
    inverse = lax.rsqrt(lax.optimization_barrier(jnp.mean(centred * centred, axis=-1, keepdims=True)) + 1e-06)
    return centred * inverse * norm_gain + norm_bias

def gelu_value(pre_act):
    return 0.5 * pre_act * (1.0 + lax.erf(pre_act * 0.7071067811865476))

def feature_logits(head_rows, feature_matrix):
    raw_part = jnp.einsum('shd,hdf->shf', head_rows, feature_matrix, precision=highest) * (DH ** (-0.25) * unit_spread)
    half_norm = lax.optimization_barrier(jnp.sum(head_rows * head_rows, axis=2, keepdims=True)) * (0.5 * DH ** (-0.5))
    return (raw_part, half_norm)

def doc_table(length_row):
    doc_ends = jnp.cumsum(length_row)
    doc_starts = doc_ends - length_row
    position = jnp.arange(SLEN, dtype=jnp.int32)[:, None]
    return jnp.logical_and(position >= doc_starts[None, :], position < doc_ends[None, :])

def stabilizers(stream_rows, doc_mask, feature_matrix, params):
    query_heads = low(project(stream_rows, params[0], params[1])).reshape(SLEN, H, DH)
    key_heads = low(project(stream_rows, params[2], params[3])).reshape(SLEN, H, DH)
    raw_q, half_q = feature_logits(query_heads, feature_matrix)
    raw_k, half_k = feature_logits(key_heads, feature_matrix)
    query_peak = lax.optimization_barrier(jnp.max(raw_q - half_q, axis=2))
    key_rowmax = lax.optimization_barrier(jnp.max(raw_k - half_k, axis=2))
    doc_peak = lax.optimization_barrier(jnp.max(jnp.where(doc_mask[:, :, None], key_rowmax[:, None, :], -1e+30), axis=0))
    return (query_peak, doc_peak)

def stream_forward(stream_rows, doc_mask, query_peak, doc_peak, feature_matrix, params):
    query_weight, query_bias, key_weight, key_bias, value_weight, value_bias, out_weight, out_bias, gain_one, offset_one, in_weight, in_bias, down_weight, down_bias, gain_two, offset_two = params
    query_heads = low(low_back(project(stream_rows, query_weight, query_bias))).reshape(SLEN, H, DH)
    key_heads = low(low_back(project(stream_rows, key_weight, key_bias))).reshape(SLEN, H, DH)
    value_heads = low(low_back(project(stream_rows, value_weight, value_bias))).reshape(SLEN, H, DH)
    doc_float = doc_mask.astype(jnp.float32)
    raw_q, half_q = feature_logits(query_heads, feature_matrix)
    phi_query = low(jnp.exp(low_back(raw_q) - half_q - query_peak[:, :, None]))
    raw_k, half_k = feature_logits(key_heads, feature_matrix)
    key_peak = jnp.einsum('sd,dh->sh', doc_float, doc_peak, precision=highest)
    phi_key = low(jnp.exp(low_back(raw_k) - half_k - key_peak[:, :, None]))
    key_values = low(low_back(jnp.einsum('sd,shf,she->hdef', doc_float, phi_key, value_heads, precision=highest)))
    key_totals = low(low_back(jnp.einsum('sd,shf->hdf', doc_float, phi_key, precision=highest)))
    numerator = low_back(jnp.einsum('sd,shf,hdef->she', doc_float, phi_query, key_values, precision=highest))
    denominator = low_back(jnp.einsum('sd,shf,hdf->sh', doc_float, phi_query, key_totals, precision=highest))
    attended = low(low_back(numerator / denominator[:, :, None])).reshape(SLEN, D)
    residual_one = stream_rows + low_back(project(attended, out_weight, out_bias))
    hidden = low(layer_norm(residual_one, gain_one, offset_one))
    gelu_rows = low(gelu_value(low_back(project(hidden, in_weight, in_bias))))
    residual_two = hidden + low_back(project(gelu_rows, down_weight, down_bias))
    return layer_norm(residual_two, gain_two, offset_two)

def reference(tokens, doc_lengths, feature_ints, w_query, b_query, w_key, b_key, w_value, b_value, w_out, b_out, norm1_gain, norm1_bias, w_in, b_in, w_down, b_down, norm2_gain, norm2_bias, cotangent):
    feature_matrix = feature_ints.astype(jnp.float32)
    params = tuple((weight.astype(jnp.float32) for weight in (w_query, b_query, w_key, b_key, w_value, b_value, w_out, b_out, norm1_gain, norm1_bias, w_in, b_in, w_down, b_down, norm2_gain, norm2_bias)))
    all_rows = tokens.astype(jnp.float32)
    doc_masks = jax.vmap(doc_table)(doc_lengths)
    query_peaks, doc_peaks = lax.map(lambda bundle: stabilizers(bundle[0], bundle[1], feature_matrix, params), (all_rows, doc_masks))

    def forward(stream_all, weights):
        per_stream = jax.checkpoint(lambda bundle: stream_forward(bundle[0], bundle[1], bundle[2], bundle[3], feature_matrix, weights))
        return lax.map(per_stream, (stream_all, doc_masks, query_peaks, doc_peaks))
    layer_out, pullback = jax.vjp(forward, all_rows, params)
    grad_rows, grad_weights = pullback(cotangent.astype(jnp.float32))
    return (layer_out.astype(jnp.bfloat16), grad_rows, grad_weights[0], grad_weights[1], grad_weights[2], grad_weights[3], grad_weights[4], grad_weights[5], grad_weights[6], grad_weights[7], grad_weights[8], grad_weights[9], grad_weights[10], grad_weights[11], grad_weights[12], grad_weights[13], grad_weights[14], grad_weights[15])
```

```python
from functools import partial

import jax
import jax.numpy as jnp
from jax import lax
from jax.experimental import pallas as pl
from jax.experimental.pallas import tpu as pltpu
from jax.sharding import PartitionSpec as P

unit_spread = 0.013531646934131853
inv_root_two = 0.7071067811865476
inv_root_tau = 0.3989422804014327
far_below = -1e30
log2_e = 1.4426950408889634
MESH = pl.DeviceIdType.MESH
f32 = jnp.float32
bf16 = jnp.bfloat16
TAIL = 16


def layer_norm(residual, norm_gain, norm_bias):
    centred = residual - jnp.mean(residual, axis=1, keepdims=True)
    inverse = lax.rsqrt(jnp.mean(centred * centred, axis=1, keepdims=True) + 1e-06)
    normed = centred * inverse
    return (normed * norm_gain.astype(f32) + norm_bias.astype(f32), normed, inverse)


def norm_back(grad_out, normed, inverse, norm_gain):
    scaled = grad_out * norm_gain.astype(f32)
    centre_part = jnp.mean(scaled, axis=1, keepdims=True)
    slope_part = jnp.mean(scaled * normed, axis=1, keepdims=True)
    grad_resid = inverse * (scaled - centre_part - normed * slope_part)
    return (grad_resid, jnp.sum(grad_out * normed, axis=0), jnp.sum(grad_out, axis=0))


def gelu_value(pre_act):
    return 0.5 * pre_act * (1.0 + lax.erf(pre_act * inv_root_two))


def gelu_slope(pre_act):
    return (
        0.5 * (1.0 + lax.erf(pre_act * inv_root_two))
        + pre_act * jnp.exp(-0.5 * pre_act * pre_act) * inv_root_tau
    )


def mul(a, b):
    return lax.dot_general(a, b, (((1,), (0,)), ((), ())), preferred_element_type=f32)


def mul_tb(a, b):
    return lax.dot_general(a, b, (((1,), (1,)), ((), ())), preferred_element_type=f32)


def mul_ta(a, b):
    return lax.dot_general(a, b, (((0,), (0,)), ((), ())), preferred_element_type=f32)


def affine(row_block, weight, bias_row):
    return mul(row_block, weight) + bias_row.astype(f32)


def column_total(values):
    return jnp.sum(values, axis=0, dtype=f32)


def lane_ids(shape):
    return lax.broadcasted_iota(jnp.int32, shape, len(shape) - 1)


def doc_setup(lengths, place, mask_ref, onehot_ref, strad_ref, stradrow_ref):
    rows = mask_ref.shape[0]
    docs = lengths.shape[1]
    total = jnp.int32(0)
    ends = []
    for d in range(docs):
        total = total + lengths[0, d]
        ends.append(total)
    pos = lax.broadcasted_iota(jnp.int32, (rows, 128), 0) + place * rows
    pos_row = lax.broadcasted_iota(jnp.int32, (8, rows), 1) + place * rows
    did = jnp.zeros((rows, 128), jnp.int32)
    did_row = jnp.zeros((8, rows), jnp.int32)
    edge = jnp.int32(0)
    for end in ends[:-1]:
        did = did + (pos >= end).astype(jnp.int32)
        did_row = did_row + (pos_row >= end).astype(jnp.int32)
        edge = edge + (end <= rows).astype(jnp.int32)
    for j in range(rows // 128):
        cols = did_row[0:1, j * 128 : (j + 1) * 128]
        mask_ref[:, j * 128 : (j + 1) * 128] = (did == cols).astype(f32).astype(bf16)
    onehot_ref[...] = (did == lane_ids((rows, 128))).astype(f32)
    strad_ref[...] = (did == edge).astype(f32)
    one_row = (did_row[0:1] == edge).astype(f32)
    stradrow_ref[...] = jnp.broadcast_to(one_row, stradrow_ref.shape).astype(bf16)


def features_setup(ints_ref, omx_ref):
    heads, size, feats = ints_ref.shape

    @pl.loop(0, heads)
    def _(h):
        mat = ints_ref[h].astype(f32).astype(bf16)
        zero = jnp.zeros((size, feats), bf16)
        odd = lax.rem(h, 2) == 1
        omx_ref[h, 0:size] = jnp.where(odd, zero, mat)
        omx_ref[h, size : 2 * size] = jnp.where(odd, mat, zero)
        omx_ref[h, 2 * size :] = jnp.ones((2 * size, feats), bf16)


def three_terms(value):
    first = value.astype(bf16).astype(f32)
    second = (value - first).astype(bf16).astype(f32)
    return first, second, value - first - second


def forward_states(p, scale, q_ref, k_ref, v_ref, omx_ref, onehot_ref, strad_ref, stradrow_ref, pq_ref, pk_ref, peak_ref, out_ref):
    rows = q_ref.shape[1]
    lanes = lane_ids((1, 128))
    qp, kp, vp = q_ref[p], k_ref[p], v_ref[p]
    kf = kp.astype(f32)
    ksq = kf * kf
    vt = jnp.concatenate([vp.T * stradrow_ref[0:1], stradrow_ref[...]], axis=0)
    tail = jnp.zeros((TAIL, pq_ref.shape[-1]), f32)
    tail_row = lax.broadcasted_iota(jnp.int32, tail.shape, 0)
    for j in range(2):
        om = omx_ref[2 * p + j, 0:128]
        raw_q = mul(qp, om)
        raw_q = raw_q - jnp.max(raw_q, axis=1, keepdims=True)
        pq_ref[p, j] = jnp.exp2(raw_q * (scale * log2_e)).astype(bf16)
        here = (lanes >= 64) if j else (lanes < 64)
        half = jnp.sum(jnp.where(here, ksq, 0.0), axis=1, keepdims=True) * (0.0625 / scale)
        raw_k = mul(kp, om) - half
        row_peak = jnp.max(raw_k, axis=1, keepdims=True)
        doc_peak = jnp.max(jnp.where(onehot_ref[...] > 0.5, row_peak, far_below), axis=0, keepdims=True)
        back = jnp.max(jnp.where(onehot_ref[...] > 0.5, doc_peak, far_below), axis=1, keepdims=True)
        edge_peak = jnp.max(jnp.where(strad_ref[...] > 0.5, row_peak, far_below), axis=0, keepdims=True)
        phi_k = jnp.exp2((raw_k - back) * (scale * log2_e)).astype(bf16)
        pk_ref[p, j] = phi_k
        part = mul(vt, phi_k)
        out_ref[p, 64 * j : 64 * j + 64] = part[64 * j : 64 * j + 64].astype(bf16)
        edge_wide = jnp.concatenate([edge_peak, edge_peak], axis=1)
        peak_ref[p, j] = edge_wide
        tail = jnp.where(tail_row == j, part[128 : 128 + TAIL], tail)
        for t, term in enumerate(three_terms(edge_wide)):
            tail = jnp.where(tail_row == 2 + 3 * j + t, term, tail)
    out_ref[p, 128:] = tail.astype(bf16)


def edge_parts(state_ref, p, j):
    tail = state_ref[p, 128:].astype(f32)
    feats = tail.shape[1]
    totals = jnp.broadcast_to(tail[j : j + 1], (128, feats)).astype(bf16)
    peak = tail[2 + 3 * j : 3 + 3 * j] + tail[3 + 3 * j : 4 + 3 * j] + tail[4 + 3 * j : 5 + 3 * j]
    return jnp.concatenate([state_ref[p, 0:128], totals], axis=0), peak


def edge_weights(scale, own, other, strad):
    top = jnp.maximum(own, other)
    own_w = jnp.exp2((own - top) * (scale * log2_e))
    other_w = jnp.exp2((other - top) * (scale * log2_e))
    return 1.0 + strad * (own_w[:, 0:128] - 1.0), strad * other_w[:, 0:128]


def forward_finish(p, scale, v_ref, pq_ref, pk_ref, mask_ref, strad_ref, peak_ref, in_ref, att_ref, den_ref):
    rows = v_ref.shape[1]
    first_half = lane_ids((rows, 128)) < 64
    vx = jnp.concatenate([v_ref[p], jnp.ones((rows, 128), bf16)], axis=1)
    got = []
    for j in range(2):
        phi_q = pq_ref[p, j]
        pair = mul_tb(phi_q, pk_ref[p, j]).astype(bf16) * mask_ref[...]
        near = mul(pair, vx)
        state, other = edge_parts(in_ref, p, j)
        far = mul_tb(phi_q, state)
        wn, wf = edge_weights(scale, peak_ref[p, j], other, strad_ref[...])
        den = near[:, 128:] * wn + far[:, 128:] * wf
        got.append(((near[:, :128] * wn + far[:, :128] * wf) / den, den))
    att_ref[p] = jnp.where(first_half, got[0][0], got[1][0]).astype(bf16)
    den_ref[p] = jnp.where(first_half, got[0][1], got[1][1])


def numer_grads(p, att_ref, den_ref, gatt_ref):
    rows = att_ref.shape[1]
    lanes = lane_ids((rows, 128))
    gn = gatt_ref[p].astype(f32) / den_ref[p]
    prod = gn * att_ref[p].astype(f32)
    d0 = -jnp.sum(jnp.where(lanes < 64, prod, 0.0), axis=1, keepdims=True)
    d1 = -jnp.sum(jnp.where(lanes < 64, 0.0, prod), axis=1, keepdims=True)
    return gn, d0, d1, lanes


def backward_states(p, scale, att_ref, den_ref, gatt_ref, pq_ref, strad_ref, peak_ref, in_ref, out_ref):
    gn, d0, d1, lanes = numer_grads(p, att_ref, den_ref, gatt_ref)
    far = [edge_weights(scale, peak_ref[p, j], edge_parts(in_ref, p, j)[1], strad_ref[...])[1] for j in range(2)]
    left = (gn * jnp.where(lanes < 64, far[0], far[1])).astype(bf16)
    right = (jnp.where(lanes == 0, d0 * far[0], 0.0) + jnp.where(lanes == 1, d1 * far[1], 0.0)).astype(bf16)
    turned = jnp.concatenate([left.T, right.T[0:TAIL]], axis=0)
    tails = []
    for j in range(2):
        part = mul(turned, pq_ref[p, j])
        out_ref[p, 64 * j : 64 * j + 64] = part[64 * j : 64 * j + 64].astype(bf16)
        tails.append(part[128:])
    rowid = lax.broadcasted_iota(jnp.int32, tails[0].shape, 0)
    out_ref[p, 128:] = jnp.where(rowid == 0, tails[0], tails[1]).astype(bf16)


def backward_finish(
    p, scale, q_ref, k_ref, v_ref, omx_ref, pq_ref, pk_ref, mask_ref, strad_ref, peak_ref, in_ref, gin_ref,
    att_ref, den_ref, gatt_ref, gq_ref, gk_ref, gv_ref,
):
    rows = q_ref.shape[1]
    gn, d0, d1, lanes = numer_grads(p, att_ref, den_ref, gatt_ref)
    first_half = lanes < 64
    vp = v_ref[p]
    ones = jnp.ones((rows, 128), bf16)
    vx = jnp.concatenate([vp, ones], axis=1)
    strad = strad_ref[...]
    gq = jnp.zeros((rows, 128), f32)
    gk = jnp.zeros((rows, 128), f32)
    gv = jnp.zeros((rows, 128), f32)
    q_sums, k_sums = [], []
    for j in range(2):
        here = (lanes >= 64) if j else (lanes < 64)
        gd = d1 if j else d0
        state, other = edge_parts(in_ref, p, j)
        wn, wf = edge_weights(scale, peak_ref[p, j], other, strad)
        base_l = jnp.where(here, gn, 0.0)
        base_r = jnp.where(lanes == 0, gd, 0.0)
        near = jnp.concatenate([(base_l * wn).astype(bf16), (base_r * wn).astype(bf16)], axis=1)
        far = jnp.concatenate([(base_l * wf).astype(bf16), (base_r * wf).astype(bf16)], axis=1)
        phi_q, phi_k = pq_ref[p, j], pk_ref[p, j]
        turned = mul_tb(phi_k, phi_q).astype(bf16) * mask_ref[...]
        gv = gv + mul(turned, near[:, 0:128])
        gpair = mul_tb(near, vx).astype(bf16) * mask_ref[...]
        gphi_q = mul(gpair, phi_k) + mul(far, state)
        gturned = mul_tb(vx, near).astype(bf16) * mask_ref[...]
        gstate, _ = edge_parts(gin_ref, p, j)
        vs = jnp.concatenate(
            [(jnp.where(here, vp.astype(f32), 0.0) * strad).astype(bf16), jnp.where(lanes == 0, strad, 0.0).astype(bf16)],
            axis=1,
        )
        gphi_k = mul(gturned, phi_q) + mul(vs, gstate)
        gv = gv + jnp.where(here, mul_tb(phi_k, gstate[0:128]) * strad, 0.0)
        omx = omx_ref[2 * p + j]
        back_q = mul_tb((gphi_q * phi_q.astype(f32)).astype(bf16), omx)
        back_k = mul_tb((gphi_k * phi_k.astype(f32)).astype(bf16), omx)
        gq = gq + back_q[:, 0:128]
        gk = gk + back_k[:, 0:128]
        q_sums.append(back_q[:, 128:])
        k_sums.append(back_k[:, 128:])
    gq = gq * scale - jnp.where(first_half, q_sums[0], q_sums[1]) * q_ref[p].astype(f32) * 0.125
    gk = gk * scale - jnp.where(first_half, k_sums[0], k_sums[1]) * k_ref[p].astype(f32) * 0.125
    gq_ref[p] = gq.astype(bf16)
    gk_ref[p] = gk.astype(bf16)
    gv_ref[p] = gv.astype(bf16)


def peer_barrier(peers):
    barrier = pltpu.get_barrier_semaphore()
    for peer in peers:
        pl.semaphore_signal(barrier, inc=1, device_id=peer, device_id_type=MESH)
    pl.semaphore_wait(barrier, len(peers))


def forward_kernel(
    scale, x_ref, wq_ref, wk_ref, wv_ref, bias_ref, ints_ref, len_ref,
    q_ref, k_ref, v_ref, pq_ref, pk_ref, att_ref, den_ref, peak_ref, state_ref,
    omx_ref, mask_ref, onehot_ref, strad_ref, stradrow_ref, send_ref, ssem, rsem,
):
    place = lax.axis_index("seq")
    peer = {"seq": 1 - place}
    peer_barrier([peer])
    pairs = q_ref.shape[0]
    doc_setup(len_ref, place, mask_ref, onehot_ref, strad_ref, stradrow_ref)
    features_setup(ints_ref, omx_ref)
    for n, (w_ref, o_ref) in enumerate(((wq_ref, q_ref), (wk_ref, k_ref), (wv_ref, v_ref))):
        for j in range(pairs // 2):
            cols = slice(256 * j, 256 * j + 256)
            got = (mul(x_ref[...], w_ref[:, cols]) + bias_ref[n : n + 1, cols].astype(f32)).astype(bf16)
            o_ref[2 * j] = got[:, 0:128]
            o_ref[2 * j + 1] = got[:, 128:256]

    def copy(p):
        return pltpu.make_async_remote_copy(
            src_ref=send_ref.at[p], dst_ref=state_ref.at[p], send_sem=ssem.at[p], recv_sem=rsem.at[p],
            device_id=peer, device_id_type=MESH,
        )

    @pl.loop(0, pairs)
    def _(p):
        forward_states(p, scale, q_ref, k_ref, v_ref, omx_ref, onehot_ref, strad_ref, stradrow_ref, pq_ref, pk_ref, peak_ref, send_ref)
        copy(p).start()

    @pl.loop(0, pairs)
    def _(p):
        copy(p).wait()
        forward_finish(p, scale, v_ref, pq_ref, pk_ref, mask_ref, strad_ref, peak_ref, state_ref, att_ref, den_ref)


def backward_kernel(
    scale, q_ref, k_ref, v_ref, pq_ref, pk_ref, att_ref, den_ref, peak_ref, state_ref, gatt_ref, ints_ref, len_ref,
    gq_ref, gk_ref, gv_ref,
    gstate_ref, omx_ref, mask_ref, onehot_ref, strad_ref, stradrow_ref, send_ref, ssem, rsem,
):
    place = lax.axis_index("seq")
    peer = {"seq": 1 - place}
    peer_barrier([peer])
    pairs = q_ref.shape[0]
    doc_setup(len_ref, place, mask_ref, onehot_ref, strad_ref, stradrow_ref)
    features_setup(ints_ref, omx_ref)

    def copy(p):
        return pltpu.make_async_remote_copy(
            src_ref=send_ref.at[p], dst_ref=gstate_ref.at[p], send_sem=ssem.at[p], recv_sem=rsem.at[p],
            device_id=peer, device_id_type=MESH,
        )

    @pl.loop(0, pairs)
    def _(p):
        backward_states(p, scale, att_ref, den_ref, gatt_ref, pq_ref, strad_ref, peak_ref, state_ref, send_ref)
        copy(p).start()

    @pl.loop(0, pairs)
    def _(p):
        copy(p).wait()
        backward_finish(
            p, scale, q_ref, k_ref, v_ref, omx_ref, pq_ref, pk_ref, mask_ref, strad_ref, peak_ref, state_ref, gstate_ref,
            att_ref, den_ref, gatt_ref, gq_ref, gk_ref, gv_ref,
        )


def scratch_masks(rows, heads, feats):
    return [
        pltpu.VMEM((heads, 256, feats), bf16),
        pltpu.VMEM((rows, rows), bf16),
        pltpu.VMEM((rows, 128), f32),
        pltpu.VMEM((rows, 128), f32),
        pltpu.VMEM((TAIL, rows), bf16),
    ]


def vmem():
    return pl.BlockSpec(memory_space=pltpu.VMEM)


def attention_forward(x, wq, wk, wv, biases, ints, lengths):
    rows = x.shape[0]
    heads, size, feats = ints.shape
    pairs = heads // 2
    scale = size ** (-0.25) * unit_spread
    shape = jax.ShapeDtypeStruct
    return pl.pallas_call(
        partial(forward_kernel, scale),
        out_shape=[
            shape((pairs, rows, 128), bf16), shape((pairs, rows, 128), bf16), shape((pairs, rows, 128), bf16),
            shape((pairs, 2, rows, feats), bf16), shape((pairs, 2, rows, feats), bf16),
            shape((pairs, rows, 128), bf16), shape((pairs, rows, 128), f32),
            shape((pairs, 2, 1, feats), f32), shape((pairs, 128 + TAIL, feats), bf16),
        ],
        in_specs=[vmem()] * 6 + [pl.BlockSpec(memory_space=pltpu.SMEM)],
        out_specs=[vmem()] * 9,
        scratch_shapes=scratch_masks(rows, heads, feats) + [
            pltpu.VMEM((pairs, 128 + TAIL, feats), bf16),
            pltpu.SemaphoreType.DMA((pairs,)),
            pltpu.SemaphoreType.DMA((pairs,)),
        ],
        compiler_params=pltpu.CompilerParams(collective_id=0, has_side_effects=True, vmem_limit_bytes=60 << 20),
        name="attention_forward",
    )(x, wq, wk, wv, biases, ints, lengths)


def attention_backward(saved, gatt, ints, lengths):
    pairs, rows, _ = gatt.shape
    heads, size, feats = ints.shape
    scale = size ** (-0.25) * unit_spread
    shape = jax.ShapeDtypeStruct
    return pl.pallas_call(
        partial(backward_kernel, scale),
        out_shape=[shape((pairs, rows, 128), bf16)] * 3,
        in_specs=[vmem()] * 11 + [pl.BlockSpec(memory_space=pltpu.SMEM)],
        out_specs=[vmem()] * 3,
        scratch_shapes=[pltpu.VMEM((pairs, 128 + TAIL, feats), bf16)] + scratch_masks(rows, heads, feats) + [
            pltpu.VMEM((pairs, 128 + TAIL, feats), bf16),
            pltpu.SemaphoreType.DMA((pairs,)),
            pltpu.SemaphoreType.DMA((pairs,)),
        ],
        compiler_params=pltpu.CompilerParams(collective_id=1, has_side_effects=True, vmem_limit_bytes=60 << 20),
        name="attention_backward",
    )(*saved, gatt, ints, lengths)


def to_pairs(rows):
    return rows.reshape(rows.shape[0], -1, 128).transpose(1, 0, 2)


def from_pairs(pairs):
    return pairs.transpose(1, 0, 2).reshape(pairs.shape[1], -1)


def gathered(piece):
    return lax.all_gather(piece, "fsdp", axis=0, tiled=True)


def per_device(
    tokens, doc_lengths, feature_ints, w_query, b_query, w_key, b_key, w_value, b_value, w_out, b_out,
    norm1_gain, norm1_bias, w_in, b_in, w_down, b_down, norm2_gain, norm2_bias, cotangent,
):
    row_block = tokens[0]
    width = row_block.shape[1]
    fsdp = lax.axis_size("fsdp")
    me = lax.axis_index("fsdp")
    attn_stack = gathered(jnp.stack([w_query, w_key, w_value, w_out], axis=1))
    query_weight, key_weight, value_weight, out_weight = (attn_stack[:, i] for i in range(4))
    small = jnp.concatenate(
        [b_query, b_key, b_value, b_out, norm1_gain, norm1_bias, b_down, norm2_gain, norm2_bias, b_in]
    )
    small = lax.all_gather(small[None], "fsdp", axis=0, tiled=True)
    part = width // fsdp
    vectors = [small[:, part * i : part * (i + 1)].reshape(-1) for i in range(9)] + [small[:, 9 * part :].reshape(-1)]
    query_bias, key_bias, value_bias, out_bias, gain_one, offset_one, down_bias, gain_two, offset_two, in_bias = vectors
    saved = attention_forward(
        row_block, query_weight, key_weight, value_weight, jnp.stack([query_bias, key_bias, value_bias]),
        feature_ints, doc_lengths,
    )
    att_rows = from_pairs(saved[5])
    residual_one = row_block.astype(f32) + affine(att_rows, out_weight, out_bias)
    hidden_wide, normed_one, inverse_one = layer_norm(residual_one, gain_one, offset_one)
    hidden_low = hidden_wide.astype(bf16)
    in_weight = gathered(w_in)
    down_weight = gathered(w_down)
    pre_act = affine(hidden_low, in_weight, in_bias)
    gelu_low = gelu_value(pre_act).astype(bf16)
    residual_two = hidden_low.astype(f32) + affine(gelu_low, down_weight, down_bias)
    layer_wide, normed_two, inverse_two = layer_norm(residual_two, gain_two, offset_two)
    grad_out = cotangent[0].astype(f32)
    grad_resid_two, grad_gain_two, grad_offset_two = norm_back(grad_out, normed_two, inverse_two, gain_two)
    grad_down_low = grad_resid_two.astype(bf16)
    grad_down_weight = mul_ta(gelu_low, grad_down_low)
    grad_down_bias = column_total(grad_down_low)
    grad_pre_low = (mul_tb(grad_down_low, down_weight) * gelu_slope(pre_act)).astype(bf16)
    grad_in_weight = mul_ta(hidden_low, grad_pre_low)
    grad_in_bias = column_total(grad_pre_low)
    grad_hidden = mul_tb(grad_pre_low, in_weight) + grad_resid_two
    grad_resid_one, grad_gain_one, grad_offset_one = norm_back(grad_hidden, normed_one, inverse_one, gain_one)
    grad_proj_low = grad_resid_one.astype(bf16)
    grad_out_weight = mul_ta(att_rows, grad_proj_low)
    grad_out_bias = column_total(grad_proj_low)
    grad_att_rows = mul_tb(grad_proj_low, out_weight).astype(bf16)
    grads = attention_backward(saved, to_pairs(grad_att_rows), feature_ints, doc_lengths)
    grad_query_rows, grad_key_rows, grad_value_rows = (from_pairs(g) for g in grads)
    grad_query_weight = mul_ta(row_block, grad_query_rows)
    grad_key_weight = mul_ta(row_block, grad_key_rows)
    grad_value_weight = mul_ta(row_block, grad_value_rows)
    grad_input = (
        mul_tb(grad_query_rows, query_weight)
        + mul_tb(grad_key_rows, key_weight)
        + mul_tb(grad_value_rows, value_weight)
        + grad_resid_one
    )

    def owned(grad):
        shard = lax.psum_scatter(grad.astype(bf16), "fsdp", scatter_dimension=0, tiled=True)
        return lax.psum(shard, "seq").astype(f32)

    sums = jnp.stack(
        [
            column_total(grad_query_rows), column_total(grad_key_rows), column_total(grad_value_rows), grad_out_bias,
            grad_gain_one, grad_offset_one, grad_down_bias, grad_gain_two, grad_offset_two,
            *grad_in_bias.reshape(-1, width),
        ]
    )
    sums = lax.psum(sums, ("fsdp", "seq"))
    mine = [lax.dynamic_slice(sums[i], (me * part,), (part,)) for i in range(9)]
    wide = in_bias.shape[0] // fsdp
    mine_in = lax.dynamic_slice(sums[9:].reshape(-1), (me * wide,), (wide,))
    return (
        layer_wide.astype(bf16)[None],
        grad_input[None],
        owned(grad_query_weight), mine[0],
        owned(grad_key_weight), mine[1],
        owned(grad_value_weight), mine[2],
        owned(grad_out_weight), mine[3],
        mine[4], mine[5],
        owned(grad_in_weight), mine_in,
        owned(grad_down_weight), mine[6],
        mine[7], mine[8],
    )


def solution(mesh):
    rows, matrix, vector = P("fsdp", "seq", None), P("fsdp", None), P("fsdp")
    weights = (matrix, vector) * 4 + (vector, vector) + (matrix, vector) * 2 + (vector, vector)
    return jax.shard_map(
        per_device,
        mesh=mesh,
        in_specs=(rows, matrix, P(), *weights, rows),
        out_specs=(rows, rows, *weights),
        check_vma=False,
    )
```

```python
from functools import partial

import jax
import jax.numpy as jnp
from jax import lax
from jax.experimental import pallas as pl
from jax.experimental.pallas import tpu as pltpu
from jax.sharding import PartitionSpec as P

unit_spread = 0.013531646934131853
inv_root_two = 0.7071067811865476
inv_root_tau = 0.3989422804014327
far_below = -1e30
log2_e = 1.4426950408889634
MESH = pl.DeviceIdType.MESH
f32 = jnp.float32
bf16 = jnp.bfloat16
TAIL = 16
DEPTH = 4


def layer_norm(residual, norm_gain, norm_bias):
    centred = residual - jnp.mean(residual, axis=1, keepdims=True)
    inverse = lax.rsqrt(jnp.mean(centred * centred, axis=1, keepdims=True) + 1e-06)
    normed = centred * inverse
    return (normed * norm_gain.astype(f32) + norm_bias.astype(f32), normed, inverse)


def norm_back(grad_out, normed, inverse, norm_gain):
    scaled = grad_out * norm_gain.astype(f32)
    centre_part = jnp.mean(scaled, axis=1, keepdims=True)
    slope_part = jnp.mean(scaled * normed, axis=1, keepdims=True)
    grad_resid = inverse * (scaled - centre_part - normed * slope_part)
    return (grad_resid, jnp.sum(grad_out * normed, axis=0), jnp.sum(grad_out, axis=0))


def gelu_value(pre_act):
    return 0.5 * pre_act * (1.0 + lax.erf(pre_act * inv_root_two))


def gelu_slope(pre_act):
    return (
        0.5 * (1.0 + lax.erf(pre_act * inv_root_two))
        + pre_act * jnp.exp(-0.5 * pre_act * pre_act) * inv_root_tau
    )


def mul(a, b):
    return lax.dot_general(a, b, (((1,), (0,)), ((), ())), preferred_element_type=f32)


def mul_tb(a, b):
    return lax.dot_general(a, b, (((1,), (1,)), ((), ())), preferred_element_type=f32)


def mul_ta(a, b):
    return lax.dot_general(a, b, (((0,), (0,)), ((), ())), preferred_element_type=f32)


def affine(row_block, weight, bias_row):
    return mul(row_block, weight) + bias_row.astype(f32)


def column_total(values):
    return jnp.sum(values, axis=0, dtype=f32)


def lane_ids(shape):
    return lax.broadcasted_iota(jnp.int32, shape, len(shape) - 1)


def doc_setup(lengths, place, mask_ref, onehot_ref, strad_ref, stradrow_ref):
    rows = mask_ref.shape[0]
    docs = lengths.shape[1]
    total = jnp.int32(0)
    ends = []
    for d in range(docs):
        total = total + lengths[0, d]
        ends.append(total)
    pos = lax.broadcasted_iota(jnp.int32, (rows, 128), 0) + place * rows
    pos_row = lax.broadcasted_iota(jnp.int32, (8, rows), 1) + place * rows
    did = jnp.zeros((rows, 128), jnp.int32)
    did_row = jnp.zeros((8, rows), jnp.int32)
    edge = jnp.int32(0)
    for end in ends[:-1]:
        did = did + (pos >= end).astype(jnp.int32)
        did_row = did_row + (pos_row >= end).astype(jnp.int32)
        edge = edge + (end <= rows).astype(jnp.int32)
    for j in range(rows // 128):
        cols = did_row[0:1, j * 128 : (j + 1) * 128]
        mask_ref[:, j * 128 : (j + 1) * 128] = (did == cols).astype(f32).astype(bf16)
    onehot_ref[...] = (did == lane_ids((rows, 128))).astype(f32)
    strad_ref[...] = (did == edge).astype(f32)
    one_row = (did_row[0:1] == edge).astype(f32)
    stradrow_ref[...] = jnp.broadcast_to(one_row, stradrow_ref.shape).astype(bf16)


def features_setup(ints_ref, omx_ref):
    heads, size, feats = ints_ref.shape

    @pl.loop(0, heads)
    def _(h):
        mat = ints_ref[h].astype(f32).astype(bf16)
        zero = jnp.zeros((size, feats), bf16)
        odd = lax.rem(h, 2) == 1
        omx_ref[h, 0:size] = jnp.where(odd, zero, mat)
        omx_ref[h, size : 2 * size] = jnp.where(odd, mat, zero)
        omx_ref[h, 2 * size :] = jnp.ones((2 * size, feats), bf16)


def three_terms(value):
    first = value.astype(bf16).astype(f32)
    second = (value - first).astype(bf16).astype(f32)
    return first, second, value - first - second


def forward_states(p, scale, q_ref, k_ref, v_ref, omx_ref, onehot_ref, strad_ref, stradrow_ref, pq_ref, pk_ref, peak_ref, out_ref):
    rows = q_ref.shape[1]
    lanes = lane_ids((1, 128))
    qp, kp, vp = q_ref[p], k_ref[p], v_ref[p]
    kf = kp.astype(f32)
    ksq = kf * kf
    vt = jnp.concatenate([vp.T * stradrow_ref[0:1], stradrow_ref[...]], axis=0)
    tail = jnp.zeros((TAIL, pq_ref.shape[-1]), f32)
    tail_row = lax.broadcasted_iota(jnp.int32, tail.shape, 0)
    for j in range(2):
        om = omx_ref[2 * p + j, 0:128]
        raw_q = mul(qp, om)
        raw_q = raw_q - jnp.max(raw_q, axis=1, keepdims=True)
        pq_ref[p, j] = jnp.exp2(raw_q * (scale * log2_e)).astype(bf16)
        here = (lanes >= 64) if j else (lanes < 64)
        half = jnp.sum(jnp.where(here, ksq, 0.0), axis=1, keepdims=True) * (0.0625 / scale)
        raw_k = mul(kp, om) - half
        row_peak = jnp.max(raw_k, axis=1, keepdims=True)
        doc_peak = jnp.max(jnp.where(onehot_ref[...] > 0.5, row_peak, far_below), axis=0, keepdims=True)
        back = jnp.max(jnp.where(onehot_ref[...] > 0.5, doc_peak, far_below), axis=1, keepdims=True)
        edge_peak = jnp.max(jnp.where(strad_ref[...] > 0.5, row_peak, far_below), axis=0, keepdims=True)
        phi_k = jnp.exp2((raw_k - back) * (scale * log2_e)).astype(bf16)
        pk_ref[p, j] = phi_k
        part = mul(vt, phi_k)
        out_ref[p, 64 * j : 64 * j + 64] = part[64 * j : 64 * j + 64].astype(bf16)
        edge_wide = jnp.concatenate([edge_peak, edge_peak], axis=1)
        peak_ref[p, j] = edge_wide
        tail = jnp.where(tail_row == j, part[128 : 128 + TAIL], tail)
        for t, term in enumerate(three_terms(edge_wide)):
            tail = jnp.where(tail_row == 2 + 3 * j + t, term, tail)
    out_ref[p, 128:] = tail.astype(bf16)


def edge_parts(state_ref, p, j):
    tail = state_ref[p, 128:].astype(f32)
    feats = tail.shape[1]
    totals = jnp.broadcast_to(tail[j : j + 1], (128, feats)).astype(bf16)
    peak = tail[2 + 3 * j : 3 + 3 * j] + tail[3 + 3 * j : 4 + 3 * j] + tail[4 + 3 * j : 5 + 3 * j]
    return jnp.concatenate([state_ref[p, 0:128], totals], axis=0), peak


def edge_weights(scale, own, other, strad):
    top = jnp.maximum(own, other)
    own_w = jnp.exp2((own - top) * (scale * log2_e))
    other_w = jnp.exp2((other - top) * (scale * log2_e))
    return 1.0 + strad * (own_w[:, 0:128] - 1.0), strad * other_w[:, 0:128]


def forward_finish(p, scale, v_ref, pq_ref, pk_ref, mask_ref, strad_ref, peak_ref, in_ref, att_ref, den_ref):
    rows = v_ref.shape[1]
    first_half = lane_ids((rows, 128)) < 64
    vx = jnp.concatenate([v_ref[p], jnp.ones((rows, 128), bf16)], axis=1)
    got = []
    for j in range(2):
        phi_q = pq_ref[p, j]
        pair = mul_tb(phi_q, pk_ref[p, j]).astype(bf16) * mask_ref[...]
        near = mul(pair, vx)
        state, other = edge_parts(in_ref, p, j)
        far = mul_tb(phi_q, state)
        wn, wf = edge_weights(scale, peak_ref[p, j], other, strad_ref[...])
        den = near[:, 128:] * wn + far[:, 128:] * wf
        got.append(((near[:, :128] * wn + far[:, :128] * wf) / den, den))
    att_ref[p] = jnp.where(first_half, got[0][0], got[1][0]).astype(bf16)
    den_ref[p] = jnp.where(first_half, got[0][1], got[1][1])


def numer_grads(p, att_ref, den_ref, gatt_ref):
    rows = att_ref.shape[1]
    lanes = lane_ids((rows, 128))
    gn = gatt_ref[p].astype(f32) / den_ref[p]
    prod = gn * att_ref[p].astype(f32)
    d0 = -jnp.sum(jnp.where(lanes < 64, prod, 0.0), axis=1, keepdims=True)
    d1 = -jnp.sum(jnp.where(lanes < 64, 0.0, prod), axis=1, keepdims=True)
    return gn, d0, d1, lanes


def backward_states(p, scale, att_ref, den_ref, gatt_ref, pq_ref, strad_ref, peak_ref, in_ref, out_ref):
    gn, d0, d1, lanes = numer_grads(p, att_ref, den_ref, gatt_ref)
    far = [edge_weights(scale, peak_ref[p, j], edge_parts(in_ref, p, j)[1], strad_ref[...])[1] for j in range(2)]
    left = (gn * jnp.where(lanes < 64, far[0], far[1])).astype(bf16)
    right = (jnp.where(lanes == 0, d0 * far[0], 0.0) + jnp.where(lanes == 1, d1 * far[1], 0.0)).astype(bf16)
    turned = jnp.concatenate([left.T, right.T[0:TAIL]], axis=0)
    tails = []
    for j in range(2):
        part = mul(turned, pq_ref[p, j])
        out_ref[p, 64 * j : 64 * j + 64] = part[64 * j : 64 * j + 64].astype(bf16)
        tails.append(part[128:])
    rowid = lax.broadcasted_iota(jnp.int32, tails[0].shape, 0)
    out_ref[p, 128:] = jnp.where(rowid == 0, tails[0], tails[1]).astype(bf16)


def backward_finish(
    p, scale, q_ref, k_ref, v_ref, omx_ref, pq_ref, pk_ref, mask_ref, strad_ref, peak_ref, in_ref, gin_ref,
    att_ref, den_ref, gatt_ref, gq_ref, gk_ref, gv_ref,
):
    rows = q_ref.shape[1]
    gn, d0, d1, lanes = numer_grads(p, att_ref, den_ref, gatt_ref)
    first_half = lanes < 64
    vp = v_ref[p]
    ones = jnp.ones((rows, 128), bf16)
    vx = jnp.concatenate([vp, ones], axis=1)
    strad = strad_ref[...]
    gq = jnp.zeros((rows, 128), f32)
    gk = jnp.zeros((rows, 128), f32)
    gv = jnp.zeros((rows, 128), f32)
    q_sums, k_sums = [], []
    for j in range(2):
        here = (lanes >= 64) if j else (lanes < 64)
        gd = d1 if j else d0
        state, other = edge_parts(in_ref, p, j)
        wn, wf = edge_weights(scale, peak_ref[p, j], other, strad)
        base_l = jnp.where(here, gn, 0.0)
        base_r = jnp.where(lanes == 0, gd, 0.0)
        near = jnp.concatenate([(base_l * wn).astype(bf16), (base_r * wn).astype(bf16)], axis=1)
        far = jnp.concatenate([(base_l * wf).astype(bf16), (base_r * wf).astype(bf16)], axis=1)
        phi_q, phi_k = pq_ref[p, j], pk_ref[p, j]
        turned = mul_tb(phi_k, phi_q).astype(bf16) * mask_ref[...]
        gv = gv + mul(turned, near[:, 0:128])
        gpair = mul_tb(near, vx).astype(bf16) * mask_ref[...]
        gphi_q = mul(gpair, phi_k) + mul(far, state)
        gturned = mul_tb(vx, near).astype(bf16) * mask_ref[...]
        gstate, _ = edge_parts(gin_ref, p, j)
        vs = jnp.concatenate(
            [(jnp.where(here, vp.astype(f32), 0.0) * strad).astype(bf16), jnp.where(lanes == 0, strad, 0.0).astype(bf16)],
            axis=1,
        )
        gphi_k = mul(gturned, phi_q) + mul(vs, gstate)
        gv = gv + jnp.where(here, mul_tb(phi_k, gstate[0:128]) * strad, 0.0)
        omx = omx_ref[2 * p + j]
        back_q = mul_tb((gphi_q * phi_q.astype(f32)).astype(bf16), omx)
        back_k = mul_tb((gphi_k * phi_k.astype(f32)).astype(bf16), omx)
        gq = gq + back_q[:, 0:128]
        gk = gk + back_k[:, 0:128]
        q_sums.append(back_q[:, 128:])
        k_sums.append(back_k[:, 128:])
    gq = gq * scale - jnp.where(first_half, q_sums[0], q_sums[1]) * q_ref[p].astype(f32) * 0.125
    gk = gk * scale - jnp.where(first_half, k_sums[0], k_sums[1]) * k_ref[p].astype(f32) * 0.125
    gq_ref[p] = gq.astype(bf16)
    gk_ref[p] = gk.astype(bf16)
    gv_ref[p] = gv.astype(bf16)


def peer_barrier(peers):
    barrier = pltpu.get_barrier_semaphore()
    for peer in peers:
        pl.semaphore_signal(barrier, inc=1, device_id=peer, device_id_type=MESH)
    pl.semaphore_wait(barrier, len(peers))


class Place:
    def __init__(self):
        me = lax.axis_index("fsdp")
        self.y = lax.axis_index("seq")
        self.c = lax.rem(me, 2)
        self.x = lax.rem(lax.div(me, 2), 2)
        self.z = lax.div(me, 4)
        self.across = {"seq": 1 - self.y}
        self.twin = {"fsdp": self.z * 4 + self.x * 2 + 1 - self.c}
        self.beside = {"fsdp": self.z * 4 + (1 - self.x) * 2 + self.c}

    def along(self, d):
        return {"fsdp": self.other(d) * 4 + self.x * 2 + self.c}

    def other(self, d):
        return lax.rem(self.z + (d + DEPTH), DEPTH)

    def peers(self):
        return [self.twin, self.beside, self.across] + [self.along(d) for d in range(1, DEPTH)]


def cols_at(start, size):
    return pl.ds(pl.multiple_of(start, 128), size)


def remote(src, dst, ssem, rsem, peer):
    return pltpu.make_async_remote_copy(
        src_ref=src, dst_ref=dst, send_sem=ssem, recv_sem=rsem, device_id=peer, device_id_type=MESH
    )


class Gather:
    def __init__(self, at, own, full, base, width, ssem, rsem, lsem):
        self.at, self.own, self.full = at, own, full
        self.third, self.base, self.width = width // 3, base, width
        self.ssem, self.rsem, self.lsem = ssem, rsem, lsem
        self.sent = []

    def spread(self):
        return cols_at(self.base + self.third * self.at.y, 2 * self.third)

    def extra(self, y):
        return cols_at(self.base + 2 * self.third * y, self.third)

    def whole(self):
        return pl.ds(self.base, self.width)

    def go(self, n, ends):
        src, dst, peer = ends()
        remote(src, dst, self.ssem.at[n], self.rsem.at[n], peer).start()
        self.sent.append((n, ends))

    def came(self, n, ref):
        remote(ref, ref, self.ssem.at[n], self.rsem.at[n], self.at.twin).wait_recv()

    def local(self):
        at = self.at
        return pltpu.make_async_copy(
            self.own.at[:, self.whole()], self.full.at[at.z, at.x, at.c, :, self.whole()], self.lsem
        )

    def begin(self):
        at = self.at
        self.local().start()
        for d in range(1, DEPTH):
            self.go(d - 1, lambda d=d: (*self.first(), at.along(d)))

    def first(self):
        at = self.at
        return self.own.at[:, self.spread()], self.full.at[at.z, at.x, at.c, :, self.spread()]

    def piece(self, d, x, cols):
        return self.full.at[self.at.other(-d), x, self.at.c, :, cols]

    def stage_x(self):
        at = self.at
        self.go(DEPTH - 1, lambda: (*self.first(), at.beside))
        for d in range(1, DEPTH):
            self.came(d - 1, self.piece(d, at.x, self.spread()))
            self.go(DEPTH - 1 + d, lambda d=d: (*[self.piece(d, at.x, self.spread())] * 2, at.beside))
            self.go(2 * DEPTH - 2 + d, lambda d=d: (*[self.piece(d, at.x, self.extra(at.y))] * 2, at.across))

    def stage_y(self):
        at = self.at
        for d in range(DEPTH):
            self.came(DEPTH - 1 + d, self.piece(d, 1 - at.x, self.spread()))
            self.go(3 * DEPTH - 2 + d, lambda d=d: (*[self.piece(d, 1 - at.x, self.extra(at.y))] * 2, at.across))

    def stage_c(self):
        at = self.at
        for d in range(1, DEPTH):
            self.came(2 * DEPTH - 2 + d, self.piece(d, at.x, self.extra(1 - at.y)))
        for d in range(DEPTH):
            self.came(3 * DEPTH - 2 + d, self.piece(d, 1 - at.x, self.extra(1 - at.y)))
        self.local().wait()
        self.go(4 * DEPTH - 2, lambda: (*[self.full.at[:, :, at.c, :, self.whole()]] * 2, at.twin))

    def ready(self):
        self.came(4 * DEPTH - 2, self.full.at[:, :, 1 - self.at.c, :, self.whole()])

    def drain(self):
        for n, ends in self.sent:
            src, dst, peer = ends()
            remote(src, dst, self.ssem.at[n], self.rsem.at[n], peer).wait_send()


GATHER_COPIES = 4 * DEPTH - 1


class SmallSum:
    def __init__(self, at, total, land, ssem, rsem, over_seq):
        self.at, self.total, self.land, self.ssem, self.rsem, self.over_seq = at, total, land, ssem, rsem, over_seq
        self.sent = []

    def go(self, src, n, peer):
        copy = remote(self.total.at[src], self.land.at[n], self.ssem.at[n], self.rsem.at[n], peer)
        copy.start()
        self.sent.append(copy)

    def came(self, n):
        remote(self.land.at[n], self.land.at[n], self.ssem.at[n], self.rsem.at[n], self.at.twin).wait_recv()

    def begin(self):
        for d in range(1, DEPTH):
            self.go(0, d - 1, self.at.along(d))

    def step(self, k):
        if k == 0:
            got = self.total[0]
            for d in range(1, DEPTH):
                self.came(d - 1)
            order = [self.at.z] + [self.at.other(-d) for d in range(1, DEPTH)]
            parts = [got] + [self.land[d - 1] for d in range(1, DEPTH)]
            value = jnp.zeros_like(got)
            for z in range(DEPTH):
                one = jnp.zeros_like(got)
                for place, part in zip(order, parts):
                    one = jnp.where(place == z, part, one)
                value = value + one
        else:
            self.came(DEPTH - 2 + k)
            value = self.total[k] + self.land[DEPTH - 2 + k]
        self.total[k + 1] = value
        hops = [self.at.beside, self.at.twin] + ([self.at.across] if self.over_seq else [])
        if k < len(hops):
            self.go(k + 1, DEPTH - 1 + k, hops[k])

    def steps(self):
        return 4 if self.over_seq else 3

    def result(self):
        return self.total[self.steps()]

    def drain(self):
        for copy in self.sent:
            copy.wait_send()


def spread_vectors(at, pieces, wide):
    width = 768
    part = pieces[0].shape[-1]
    rows = [p[...].astype(f32).reshape(1, part) for p in pieces]
    rows = jnp.concatenate(rows + [jnp.zeros((16 - len(rows), part), f32)], axis=0)
    rows = jnp.concatenate([rows, jnp.zeros((16, width - part), f32)], axis=1)
    rows = pltpu.roll(rows, (at.z * 4 + at.x * 2 + at.c) * part, 1)
    span = wide.shape[-1]
    row = jnp.concatenate([wide[...].astype(f32).reshape(1, span), jnp.zeros((1, width - span), f32)], axis=1)
    row = pltpu.roll(jnp.broadcast_to(row, (16, width)), (at.x * 2 + at.c) * span, 1)
    here = lax.broadcasted_iota(jnp.int32, (16, width), 0)
    return jnp.where(here == len(pieces) + at.z, row, rows)


def forward_kernel(
    scale, x_ref, wq_ref, wk_ref, wv_ref, wo_ref, win_ref, wdn_ref, bq_ref, bk_ref, bv_ref, bo_ref, g1_ref, o1_ref, bd_ref,
    g2_ref, o2_ref, bin_ref, ints_ref, len_ref,
    q_ref, k_ref, v_ref, pq_ref, pk_ref, att_ref, den_ref, peak_ref, state_ref, sq_ref, fin_ref, fdn_ref, vec_ref,
    omx_ref, mask_ref, onehot_ref, strad_ref, stradrow_ref, send_ref, total_ref, land_ref,
    ssem, rsem, gs_sem, gr_sem, gl_sem, vs_sem, vr_sem,
):
    at = Place()
    pairs = q_ref.shape[0]
    blocks = []
    specs = [(w, sq_ref.at[n], 0, 768) for n, w in enumerate((wq_ref, wk_ref, wv_ref, wo_ref))]
    specs += [(win_ref, fin_ref, 1536 * h, 1536) for h in range(2)]
    half = wdn_ref.shape[0] // 2
    specs += [(wdn_ref.at[pl.ds(half * h, half)], fdn_ref.at[:, :, :, pl.ds(half * h, half)], 0, 768) for h in range(2)]
    for n, (own, full, base, width) in enumerate(specs):
        blocks.append(Gather(at, own, full, base, width, gs_sem.at[n], gr_sem.at[n], gl_sem.at[n]))
    bq, bk, bv, bo, bi0, bi1, bd0, bd1 = blocks
    peer_barrier(at.peers())
    vec = SmallSum(at, total_ref, land_ref, vs_sem, vr_sem, False)
    total_ref[0] = spread_vectors(
        at, (bq_ref, bk_ref, bv_ref, bo_ref, g1_ref, o1_ref, bd_ref, g2_ref, o2_ref), bin_ref
    ).astype(bf16)
    bq.begin()
    vec.begin()
    for b in blocks[1:]:
        b.begin()
    doc_setup(len_ref, at.y, mask_ref, onehot_ref, strad_ref, stradrow_ref)
    features_setup(ints_ref, omx_ref)

    def project(n, o_ref):
        for j in range(pairs // 2):
            cols = slice(256 * j, 256 * j + 256)
            got = mul(x_ref[...], sq_ref[n, :, :, :, :, cols].reshape(768, 256))
            got = (got + vec_ref[n : n + 1, cols].astype(f32)).astype(bf16)
            o_ref[2 * j] = got[:, 0:128]
            o_ref[2 * j + 1] = got[:, 128:256]

    bq.stage_x()
    vec.step(0)
    bk.stage_x()
    bq.stage_y()
    vec.step(1)
    bv.stage_x()
    bk.stage_y()
    bq.stage_c()
    vec.step(2)
    vec_ref[...] = vec.result()
    bo.stage_x()
    bv.stage_y()
    bk.stage_c()
    bq.ready()
    project(0, q_ref)
    bv.stage_c()
    bk.ready()
    project(1, k_ref)
    bo.stage_y()
    bv.ready()
    project(2, v_ref)

    def copy(p):
        return remote(send_ref.at[p], state_ref.at[p], ssem.at[p], rsem.at[p], at.across)

    early = {0: [bi0.stage_x], 2: [bo.stage_c, bi0.stage_y], 4: [bi1.stage_x], 5: [bi0.stage_c]}
    late = {0: [bi1.stage_y], 1: [bo.ready], 2: [bd0.stage_x, bi0.ready], 3: [bi1.stage_c], 4: [bd0.stage_y], 5: [bd1.stage_x]}

    @pl.loop(0, pairs)
    def _(p):
        forward_states(p, scale, q_ref, k_ref, v_ref, omx_ref, onehot_ref, strad_ref, stradrow_ref, pq_ref, pk_ref, peak_ref, send_ref)
        copy(p).start()
        for n, todo in early.items():
            @pl.when(p == n)
            def _(todo=todo):
                for one in todo:
                    one()

    @pl.loop(0, pairs)
    def _(p):
        copy(p).wait()
        forward_finish(p, scale, v_ref, pq_ref, pk_ref, mask_ref, strad_ref, peak_ref, state_ref, att_ref, den_ref)
        for n, todo in late.items():
            @pl.when(p == n)
            def _(todo=todo):
                for one in todo:
                    one()

    bd0.stage_c()
    bd1.stage_y()
    bi1.ready()
    bd1.stage_c()
    bd0.ready()
    bd1.ready()
    for b in blocks:
        b.drain()
    vec.drain()


class Scatter:
    def __init__(self, at, n, flip, source, acc, twin_in, wide_in, half_in, deep_in, done, done_in, put, ssem, rsem, lsem):
        self.at, self.n, self.flip, self.source, self.acc = at, n, flip, source, acc
        self.twin_in, self.wide_in, self.half_in, self.deep_in = twin_in, wide_in, half_in, deep_in
        self.done, self.done_in, self.put = done, done_in, put
        self.ssem, self.rsem, self.lsem = ssem, rsem, lsem
        self.half = acc.shape[-1] // 2
        self.sent = []

    def side(self, y):
        return cols_at(self.half * y, self.half)

    def go(self, n, ends):
        src, dst, peer = ends()
        remote(src, dst, self.ssem.at[n], self.rsem.at[n], peer).start()
        self.sent.append((n, ends))

    def came(self, n, ref):
        remote(ref, ref, self.ssem.at[n], self.rsem.at[n], self.at.twin).wait_recv()

    def local(self):
        return pltpu.make_async_copy(self.source(self.at.c), self.acc, self.lsem)

    def begin(self):
        self.go(0, lambda: (self.source(1 - self.at.c), self.twin_in, self.at.twin))
        self.local().start()

    def stage_1(self):
        at = self.at
        self.local().wait()
        self.came(0, self.twin_in)

        @pl.loop(0, DEPTH)
        def _(z):
            for x in range(2):
                self.acc[z, x] = (self.acc[z, x].astype(f32) + self.twin_in[z, x].astype(f32)).astype(bf16)

        if self.flip:
            self.go(1, lambda: (self.acc.at[:, :, :, self.side(1 - at.y)], self.wide_in, at.across))
        else:
            self.go(1, lambda: (self.acc.at[:, 1 - at.x], self.wide_in, at.beside))

    def stage_2(self):
        at = self.at
        self.came(1, self.wide_in)

        @pl.loop(0, DEPTH)
        def _(z):
            if self.flip:
                for x in range(2):
                    spot = (z, x, slice(None), self.side(at.y))
                    self.acc[spot] = (self.acc[spot].astype(f32) + self.wide_in[z, x].astype(f32)).astype(bf16)
            else:
                self.acc[z, at.x] = (self.acc[z, at.x].astype(f32) + self.wide_in[z].astype(f32)).astype(bf16)

        if self.flip:
            self.go(2, lambda: (self.acc.at[:, 1 - at.x, :, self.side(at.y)], self.half_in, at.beside))
        else:
            self.go(2, lambda: (self.acc.at[:, at.x, :, self.side(1 - at.y)], self.half_in, at.across))

    def stage_3(self):
        at = self.at
        self.came(2, self.half_in)

        @pl.loop(0, DEPTH)
        def _(z):
            spot = (z, at.x, slice(None), self.side(at.y))
            self.acc[spot] = (self.acc[spot].astype(f32) + self.half_in[z].astype(f32)).astype(bf16)

        for d in range(1, DEPTH):
            self.go(2 + d, lambda d=d: (self.acc.at[at.other(d), at.x, :, self.side(at.y)], self.deep_in.at[d - 1], at.along(d)))

    def stage_4(self):
        at = self.at
        value = self.acc[at.z, at.x, :, self.side(at.y)].astype(f32)
        for d in range(1, DEPTH):
            self.came(2 + d, self.deep_in.at[d - 1])
            value = value + self.deep_in[d - 1].astype(f32)
        low = value.astype(bf16)
        self.done[...] = low
        self.put(at.y, low.astype(f32))
        self.go(2 + DEPTH, lambda: (self.done, self.done_in, at.across))

    def stage_5(self):
        self.came(2 + DEPTH, self.done_in)
        self.put(1 - self.at.y, self.done_in[...].astype(f32))

    def drain(self):
        for n, ends in self.sent:
            src, dst, peer = ends()
            remote(src, dst, self.ssem.at[n], self.rsem.at[n], peer).wait_send()


SCATTER_COPIES = DEPTH + 3
FLIPS = (False, True, False, True, False, True, False, True, False, True, False, True)


def backward_kernel(
    scale, x_ref, q_ref, k_ref, v_ref, pq_ref, pk_ref, att_ref, den_ref, peak_ref, state_ref, sq_ref, gatt_ref, gres_ref,
    vecin_ref, ints_ref, len_ref, gdn_ref, gin_ref, go_ref,
    gx_ref, oq_ref, ok_ref, ov_ref, oo_ref, oin_ref, odn_ref, vec_ref,
    gstate_ref, omx_ref, mask_ref, onehot_ref, strad_ref, stradrow_ref, send_ref,
    xt_ref, gq_ref, gk_ref, gv_ref, gw_ref, total_ref, land_ref,
    acc_ref, twin_ref, wide0_ref, wide1_ref, half_ref, deep_ref, done_ref, donein_ref,
    ssem, rsem, ws_sem, wr_sem, wl_sem, vs_sem, vr_sem,
):
    at = Place()
    pairs = q_ref.shape[0]
    sources = [lambda c, b=b: gdn_ref.at[:, :, c, pl.ds(48 * b, 48)] for b in range(4)]
    sources += [lambda c, b=b: gin_ref.at[:, :, c, :, pl.ds(768 * b, 768)] for b in range(4)]
    sources += [lambda c: go_ref.at[:, :, c]]
    sources += [lambda c, n=n: gw_ref.at[n, :, :, c] for n in (2, 1, 0)]

    def putter(ref, row, col):
        def put(y, value):
            ref[pl.ds(row, 48), cols_at(col + 384 * y, 384)] = value

        return put

    puts = [putter(odn_ref, 48 * b, 0) for b in range(4)] + [putter(oin_ref, 0, 768 * b) for b in range(4)]
    puts += [putter(r, 0, 0) for r in (oo_ref, ov_ref, ok_ref, oq_ref)]
    units = []
    for n, (source, put) in enumerate(zip(sources, puts)):
        wide = wide1_ref.at[n // 2] if FLIPS[n] else wide0_ref.at[n // 2]
        units.append(
            Scatter(
                at, n, FLIPS[n], source, acc_ref.at[n], twin_ref.at[n], wide, half_ref.at[n], deep_ref.at[n],
                done_ref.at[n], donein_ref.at[n], put, ws_sem.at[n], wr_sem.at[n], wl_sem.at[n],
            )
        )
    early = len(units) - 3

    def step(s):
        for k in range(5):
            u = s - k
            if 0 <= u < len(units):
                getattr(units[u], "stage_" + str(k + 1))()

    peer_barrier(at.peers())
    for u in units[:early]:
        u.begin()
    doc_setup(len_ref, at.y, mask_ref, onehot_ref, strad_ref, stradrow_ref)
    features_setup(ints_ref, omx_ref)

    def copy(p):
        return remote(send_ref.at[p], gstate_ref.at[p], ssem.at[p], rsem.at[p], at.across)

    @pl.loop(0, pairs)
    def _(p):
        backward_states(p, scale, att_ref, den_ref, gatt_ref, pq_ref, strad_ref, peak_ref, state_ref, send_ref)
        copy(p).start()
        for n, s in ((2, 0), (5, 1)):
            @pl.when(p == n)
            def _(s=s):
                step(s)

    for j in range(pairs):
        xt_ref[128 * j : 128 * j + 128] = x_ref[:, 128 * j : 128 * j + 128].T
    total_ref[0] = vecin_ref[...]

    @pl.loop(0, pairs)
    def _(p):
        copy(p).wait()
        backward_finish(
            p, scale, q_ref, k_ref, v_ref, omx_ref, pq_ref, pk_ref, mask_ref, strad_ref, peak_ref, state_ref, gstate_ref,
            att_ref, den_ref, gatt_ref, gq_ref, gk_ref, gv_ref,
        )
        cols = cols_at(128 * p, 128)
        both = mul(xt_ref[...], jnp.concatenate([gq_ref[p], gk_ref[p]], axis=1)).astype(bf16)
        gw_ref[0, :, :, :, :, cols] = both[:, 0:128].reshape(DEPTH, 2, 2, 48, 128)
        gw_ref[1, :, :, :, :, cols] = both[:, 128:256].reshape(DEPTH, 2, 2, 48, 128)
        gw_ref[2, :, :, :, :, cols] = mul(xt_ref[...], gv_ref[p]).astype(bf16).reshape(DEPTH, 2, 2, 48, 128)
        for n, ref in enumerate((gq_ref, gk_ref, gv_ref)):
            total_ref[0, n : n + 1, cols] = jnp.sum(ref[p].astype(f32), axis=0, keepdims=True)
        for n in range(6):
            @pl.when(p == n)
            def _(n=n):
                step(n + 2)

    vec = SmallSum(at, total_ref, land_ref, vs_sem, vr_sem, True)
    vec.begin()
    for u in units[early:]:
        u.begin()
    step(8)

    def grad_input(j):
        cols = slice(256 * j, 256 * j + 256)
        value = gres_ref[:, cols]
        for n, ref in enumerate((gq_ref, gk_ref, gv_ref)):
            for i in range(pairs // 2):
                left = jnp.concatenate([ref[2 * i], ref[2 * i + 1]], axis=1)
                right = sq_ref[n, 256 * j : 256 * j + 256, 256 * i : 256 * i + 256]
                value = value + mul_tb(left, right)
        gx_ref[:, cols] = value

    step(9)
    vec.step(0)
    grad_input(0)
    step(10)
    vec.step(1)
    grad_input(1)
    step(11)
    vec.step(2)
    grad_input(2)
    step(12)
    vec.step(3)
    vec_ref[...] = vec.result()
    for s in range(13, 16):
        step(s)
    for u in units:
        u.drain()
    vec.drain()


def scratch_masks(rows, heads, feats):
    return [
        pltpu.VMEM((heads, 256, feats), bf16),
        pltpu.VMEM((rows, rows), bf16),
        pltpu.VMEM((rows, 128), f32),
        pltpu.VMEM((rows, 128), f32),
        pltpu.VMEM((TAIL, rows), bf16),
    ]


def vmem():
    return pl.BlockSpec(memory_space=pltpu.VMEM)


def anywhere():
    return pl.BlockSpec(memory_space=pl.ANY)


def smem():
    return pl.BlockSpec(memory_space=pltpu.SMEM)


def attention_forward(x, weights, vectors, ints, lengths):
    rows, width = x.shape
    heads, size, feats = ints.shape
    pairs = heads // 2
    hidden = weights[4].shape[1]
    part = weights[0].shape[0]
    scale = size ** (-0.25) * unit_spread
    shape = jax.ShapeDtypeStruct
    grid = (DEPTH, 2, 2)
    dma = pltpu.SemaphoreType.DMA
    return pl.pallas_call(
        partial(forward_kernel, scale),
        out_shape=[
            shape((pairs, rows, 128), bf16), shape((pairs, rows, 128), bf16), shape((pairs, rows, 128), bf16),
            shape((pairs, 2, rows, feats), bf16), shape((pairs, 2, rows, feats), bf16),
            shape((pairs, rows, 128), bf16), shape((pairs, rows, 128), f32),
            shape((pairs, 2, 1, feats), f32), shape((pairs, 128 + TAIL, feats), bf16),
            shape((4, *grid, part, width), bf16),
            shape((*grid, part, hidden), bf16), shape((*grid, weights[5].shape[0], width), bf16),
            shape((16, width), bf16),
        ],
        in_specs=[vmem()] * 18 + [smem()],
        out_specs=[vmem()] * 10 + [anywhere()] * 2 + [vmem()],
        scratch_shapes=scratch_masks(rows, heads, feats) + [
            pltpu.VMEM((pairs, 128 + TAIL, feats), bf16),
            pltpu.VMEM((4, 16, width), bf16),
            pltpu.VMEM((DEPTH + 1, 16, width), bf16),
            dma((pairs,)), dma((pairs,)),
            dma((8, GATHER_COPIES)), dma((8, GATHER_COPIES)), dma((8,)),
            dma((DEPTH + 1,)), dma((DEPTH + 1,)),
        ],
        compiler_params=pltpu.CompilerParams(collective_id=0, has_side_effects=True, vmem_limit_bytes=60 << 20),
        name="attention_forward",
    )(x, *weights, *vectors, ints, lengths)


def attention_backward(x, saved, gatt, gres, vec, ints, lengths, gdn, gin, go):
    rows, width = x.shape
    heads, size, feats = ints.shape
    pairs = heads // 2
    scale = size ** (-0.25) * unit_spread
    shape = jax.ShapeDtypeStruct
    dma = pltpu.SemaphoreType.DMA
    grid = (DEPTH, 2, 2)
    part = width // 16
    hidden = gin.shape[1]
    units = 12
    gdn = gdn.reshape(*grid, -1, width)
    gin = gin.reshape(*grid, part, hidden)
    go = go.reshape(*grid, part, width)
    return pl.pallas_call(
        partial(backward_kernel, scale),
        out_shape=[shape((rows, width), f32)]
        + [shape((part, width), f32)] * 4
        + [shape((part, hidden), f32), shape((hidden // 16, width), f32), shape((16, width), f32)],
        in_specs=[vmem()] * 15 + [smem()] + [anywhere()] * 3,
        out_specs=[vmem()] * 8,
        scratch_shapes=[pltpu.VMEM((pairs, 128 + TAIL, feats), bf16)] + scratch_masks(rows, heads, feats) + [
            pltpu.VMEM((pairs, 128 + TAIL, feats), bf16),
            pltpu.VMEM((width, rows), bf16),
            pltpu.VMEM((pairs, rows, 128), bf16), pltpu.VMEM((pairs, rows, 128), bf16), pltpu.VMEM((pairs, rows, 128), bf16),
            pltpu.VMEM((3, *grid, part, width), bf16),
            pltpu.VMEM((5, 16, width), f32),
            pltpu.VMEM((DEPTH + 2, 16, width), f32),
            pltpu.VMEM((units, DEPTH, 2, part, width), bf16),
            pltpu.VMEM((units, DEPTH, 2, part, width), bf16),
            pltpu.VMEM((units // 2, DEPTH, part, width), bf16),
            pltpu.VMEM((units // 2, DEPTH, 2, part, width // 2), bf16),
            pltpu.VMEM((units, DEPTH, part, width // 2), bf16),
            pltpu.VMEM((units, DEPTH - 1, part, width // 2), bf16),
            pltpu.VMEM((units, part, width // 2), bf16),
            pltpu.VMEM((units, part, width // 2), bf16),
            dma((pairs,)), dma((pairs,)),
            dma((units, SCATTER_COPIES)), dma((units, SCATTER_COPIES)), dma((units,)),
            dma((DEPTH + 2,)), dma((DEPTH + 2,)),
        ],
        compiler_params=pltpu.CompilerParams(collective_id=1, has_side_effects=True, vmem_limit_bytes=63 << 20),
        name="attention_backward",
    )(x, *saved, gatt, gres, vec, ints, lengths, gdn, gin, go)


def to_pairs(rows):
    return rows.reshape(rows.shape[0], -1, 128).transpose(1, 0, 2)


def from_pairs(pairs):
    return pairs.transpose(1, 0, 2).reshape(pairs.shape[1], -1)


def per_device(
    tokens, doc_lengths, feature_ints, w_query, b_query, w_key, b_key, w_value, b_value, w_out, b_out,
    norm1_gain, norm1_bias, w_in, b_in, w_down, b_down, norm2_gain, norm2_bias, cotangent,
):
    row_block = tokens[0]
    width = row_block.shape[1]
    me = lax.axis_index("fsdp")
    *saved, square, in_weight, down_weight, vec = attention_forward(
        row_block,
        (w_query, w_key, w_value, w_out, w_in, w_down),
        (b_query, b_key, b_value, b_out, norm1_gain, norm1_bias, b_down, norm2_gain, norm2_bias, b_in),
        feature_ints, doc_lengths,
    )
    in_weight = in_weight.reshape(width, -1)
    down_weight = down_weight.reshape(-1, width)
    square = square.reshape(4, width, width)
    out_weight = square[3]
    _, _, _, out_bias, gain_one, offset_one, down_bias, gain_two, offset_two = (vec[i] for i in range(9))
    in_bias = vec[9:13].reshape(-1)
    att_rows = from_pairs(saved[5])
    residual_one = row_block.astype(f32) + affine(att_rows, out_weight, out_bias)
    hidden_wide, normed_one, inverse_one = layer_norm(residual_one, gain_one, offset_one)
    hidden_low = hidden_wide.astype(bf16)
    pre_act = affine(hidden_low, in_weight, in_bias)
    gelu_low = gelu_value(pre_act).astype(bf16)
    residual_two = hidden_low.astype(f32) + affine(gelu_low, down_weight, down_bias)
    layer_wide, normed_two, inverse_two = layer_norm(residual_two, gain_two, offset_two)
    grad_out = cotangent[0].astype(f32)
    grad_resid_two, grad_gain_two, grad_offset_two = norm_back(grad_out, normed_two, inverse_two, gain_two)
    grad_down_low = grad_resid_two.astype(bf16)
    grad_down_weight = mul_ta(gelu_low, grad_down_low).astype(bf16)
    grad_down_bias = column_total(grad_down_low)
    grad_pre_low = (mul_tb(grad_down_low, down_weight) * gelu_slope(pre_act)).astype(bf16)
    grad_in_weight = mul_ta(hidden_low, grad_pre_low).astype(bf16)
    grad_in_bias = column_total(grad_pre_low)
    grad_hidden = mul_tb(grad_pre_low, in_weight) + grad_resid_two
    grad_resid_one, grad_gain_one, grad_offset_one = norm_back(grad_hidden, normed_one, inverse_one, gain_one)
    grad_proj_low = grad_resid_one.astype(bf16)
    grad_out_weight = mul_ta(att_rows, grad_proj_low).astype(bf16)
    grad_out_bias = column_total(grad_proj_low)
    grad_att_rows = mul_tb(grad_proj_low, out_weight).astype(bf16)
    nothing = jnp.zeros((width,), f32)
    sums = jnp.stack(
        [
            nothing, nothing, nothing, grad_out_bias, grad_gain_one, grad_offset_one, grad_down_bias, grad_gain_two,
            grad_offset_two, *grad_in_bias.reshape(-1, width), nothing, nothing, nothing,
        ]
    )
    grad_input, gq, gk, gv, go, gin, gdn, sums = attention_backward(
        row_block, (*saved, square), to_pairs(grad_att_rows), grad_resid_one, sums, feature_ints, doc_lengths,
        grad_down_weight, grad_in_weight, grad_out_weight,
    )
    part = b_query.shape[0]
    wide = b_in.shape[0]
    mine = lax.dynamic_slice(sums, (0, me * part), (9, part))
    mine_in = lax.dynamic_slice(sums[9:13].reshape(-1), (me * wide,), (wide,))
    return (
        layer_wide.astype(bf16)[None],
        grad_input[None],
        gq, mine[0], gk, mine[1], gv, mine[2], go, mine[3], mine[4], mine[5], gin, mine_in, gdn, mine[6], mine[7], mine[8],
    )


def forward_kernel_wide(
    scale, x_ref, wq_ref, wk_ref, wv_ref, bias_ref, ints_ref, len_ref,
    q_ref, k_ref, v_ref, pq_ref, pk_ref, att_ref, den_ref, peak_ref, state_ref,
    omx_ref, mask_ref, onehot_ref, strad_ref, stradrow_ref, send_ref, ssem, rsem,
):
    place = lax.axis_index("seq")
    peer = {"seq": 1 - place}
    peer_barrier([peer])
    pairs = q_ref.shape[0]
    doc_setup(len_ref, place, mask_ref, onehot_ref, strad_ref, stradrow_ref)
    features_setup(ints_ref, omx_ref)
    for n, (w_ref, o_ref) in enumerate(((wq_ref, q_ref), (wk_ref, k_ref), (wv_ref, v_ref))):
        for j in range(pairs // 2):
            cols = slice(256 * j, 256 * j + 256)
            got = (mul(x_ref[...], w_ref[:, cols]) + bias_ref[n : n + 1, cols].astype(f32)).astype(bf16)
            o_ref[2 * j] = got[:, 0:128]
            o_ref[2 * j + 1] = got[:, 128:256]

    def copy(p):
        return pltpu.make_async_remote_copy(
            src_ref=send_ref.at[p], dst_ref=state_ref.at[p], send_sem=ssem.at[p], recv_sem=rsem.at[p],
            device_id=peer, device_id_type=MESH,
        )

    @pl.loop(0, pairs)
    def _(p):
        forward_states(p, scale, q_ref, k_ref, v_ref, omx_ref, onehot_ref, strad_ref, stradrow_ref, pq_ref, pk_ref, peak_ref, send_ref)
        copy(p).start()

    @pl.loop(0, pairs)
    def _(p):
        copy(p).wait()
        forward_finish(p, scale, v_ref, pq_ref, pk_ref, mask_ref, strad_ref, peak_ref, state_ref, att_ref, den_ref)


def backward_kernel_wide(
    scale, q_ref, k_ref, v_ref, pq_ref, pk_ref, att_ref, den_ref, peak_ref, state_ref, gatt_ref, ints_ref, len_ref,
    gq_ref, gk_ref, gv_ref,
    gstate_ref, omx_ref, mask_ref, onehot_ref, strad_ref, stradrow_ref, send_ref, ssem, rsem,
):
    place = lax.axis_index("seq")
    peer = {"seq": 1 - place}
    peer_barrier([peer])
    pairs = q_ref.shape[0]
    doc_setup(len_ref, place, mask_ref, onehot_ref, strad_ref, stradrow_ref)
    features_setup(ints_ref, omx_ref)

    def copy(p):
        return pltpu.make_async_remote_copy(
            src_ref=send_ref.at[p], dst_ref=gstate_ref.at[p], send_sem=ssem.at[p], recv_sem=rsem.at[p],
            device_id=peer, device_id_type=MESH,
        )

    @pl.loop(0, pairs)
    def _(p):
        backward_states(p, scale, att_ref, den_ref, gatt_ref, pq_ref, strad_ref, peak_ref, state_ref, send_ref)
        copy(p).start()

    @pl.loop(0, pairs)
    def _(p):
        copy(p).wait()
        backward_finish(
            p, scale, q_ref, k_ref, v_ref, omx_ref, pq_ref, pk_ref, mask_ref, strad_ref, peak_ref, state_ref, gstate_ref,
            att_ref, den_ref, gatt_ref, gq_ref, gk_ref, gv_ref,
        )


def attention_forward_wide(x, wq, wk, wv, biases, ints, lengths):
    rows = x.shape[0]
    heads, size, feats = ints.shape
    pairs = heads // 2
    scale = size ** (-0.25) * unit_spread
    shape = jax.ShapeDtypeStruct
    return pl.pallas_call(
        partial(forward_kernel_wide, scale),
        out_shape=[
            shape((pairs, rows, 128), bf16), shape((pairs, rows, 128), bf16), shape((pairs, rows, 128), bf16),
            shape((pairs, 2, rows, feats), bf16), shape((pairs, 2, rows, feats), bf16),
            shape((pairs, rows, 128), bf16), shape((pairs, rows, 128), f32),
            shape((pairs, 2, 1, feats), f32), shape((pairs, 128 + TAIL, feats), bf16),
        ],
        in_specs=[vmem()] * 6 + [pl.BlockSpec(memory_space=pltpu.SMEM)],
        out_specs=[vmem()] * 9,
        scratch_shapes=scratch_masks(rows, heads, feats) + [
            pltpu.VMEM((pairs, 128 + TAIL, feats), bf16),
            pltpu.SemaphoreType.DMA((pairs,)),
            pltpu.SemaphoreType.DMA((pairs,)),
        ],
        compiler_params=pltpu.CompilerParams(collective_id=0, has_side_effects=True, vmem_limit_bytes=60 << 20),
        name="attention_forward",
    )(x, wq, wk, wv, biases, ints, lengths)


def attention_backward_wide(saved, gatt, ints, lengths):
    pairs, rows, _ = gatt.shape
    heads, size, feats = ints.shape
    scale = size ** (-0.25) * unit_spread
    shape = jax.ShapeDtypeStruct
    return pl.pallas_call(
        partial(backward_kernel_wide, scale),
        out_shape=[shape((pairs, rows, 128), bf16)] * 3,
        in_specs=[vmem()] * 11 + [pl.BlockSpec(memory_space=pltpu.SMEM)],
        out_specs=[vmem()] * 3,
        scratch_shapes=[pltpu.VMEM((pairs, 128 + TAIL, feats), bf16)] + scratch_masks(rows, heads, feats) + [
            pltpu.VMEM((pairs, 128 + TAIL, feats), bf16),
            pltpu.SemaphoreType.DMA((pairs,)),
            pltpu.SemaphoreType.DMA((pairs,)),
        ],
        compiler_params=pltpu.CompilerParams(collective_id=1, has_side_effects=True, vmem_limit_bytes=60 << 20),
        name="attention_backward",
    )(*saved, gatt, ints, lengths)


def gathered(piece):
    return lax.all_gather(piece, "fsdp", axis=0, tiled=True)


def per_device_wide(
    tokens, doc_lengths, feature_ints, w_query, b_query, w_key, b_key, w_value, b_value, w_out, b_out,
    norm1_gain, norm1_bias, w_in, b_in, w_down, b_down, norm2_gain, norm2_bias, cotangent,
):
    row_block = tokens[0]
    width = row_block.shape[1]
    fsdp = lax.axis_size("fsdp")
    me = lax.axis_index("fsdp")
    attn_stack = gathered(jnp.stack([w_query, w_key, w_value, w_out], axis=1))
    query_weight, key_weight, value_weight, out_weight = (attn_stack[:, i] for i in range(4))
    small = jnp.concatenate(
        [b_query, b_key, b_value, b_out, norm1_gain, norm1_bias, b_down, norm2_gain, norm2_bias, b_in]
    )
    small = lax.all_gather(small[None], "fsdp", axis=0, tiled=True)
    part = width // fsdp
    vectors = [small[:, part * i : part * (i + 1)].reshape(-1) for i in range(9)] + [small[:, 9 * part :].reshape(-1)]
    query_bias, key_bias, value_bias, out_bias, gain_one, offset_one, down_bias, gain_two, offset_two, in_bias = vectors
    saved = attention_forward_wide(
        row_block, query_weight, key_weight, value_weight, jnp.stack([query_bias, key_bias, value_bias]),
        feature_ints, doc_lengths,
    )
    att_rows = from_pairs(saved[5])
    residual_one = row_block.astype(f32) + affine(att_rows, out_weight, out_bias)
    hidden_wide, normed_one, inverse_one = layer_norm(residual_one, gain_one, offset_one)
    hidden_low = hidden_wide.astype(bf16)
    in_weight = gathered(w_in)
    down_weight = gathered(w_down)
    pre_act = affine(hidden_low, in_weight, in_bias)
    gelu_low = gelu_value(pre_act).astype(bf16)
    residual_two = hidden_low.astype(f32) + affine(gelu_low, down_weight, down_bias)
    layer_wide, normed_two, inverse_two = layer_norm(residual_two, gain_two, offset_two)
    grad_out = cotangent[0].astype(f32)
    grad_resid_two, grad_gain_two, grad_offset_two = norm_back(grad_out, normed_two, inverse_two, gain_two)
    grad_down_low = grad_resid_two.astype(bf16)
    grad_down_weight = mul_ta(gelu_low, grad_down_low)
    grad_down_bias = column_total(grad_down_low)
    grad_pre_low = (mul_tb(grad_down_low, down_weight) * gelu_slope(pre_act)).astype(bf16)
    grad_in_weight = mul_ta(hidden_low, grad_pre_low)
    grad_in_bias = column_total(grad_pre_low)
    grad_hidden = mul_tb(grad_pre_low, in_weight) + grad_resid_two
    grad_resid_one, grad_gain_one, grad_offset_one = norm_back(grad_hidden, normed_one, inverse_one, gain_one)
    grad_proj_low = grad_resid_one.astype(bf16)
    grad_out_weight = mul_ta(att_rows, grad_proj_low)
    grad_out_bias = column_total(grad_proj_low)
    grad_att_rows = mul_tb(grad_proj_low, out_weight).astype(bf16)
    grads = attention_backward_wide(saved, to_pairs(grad_att_rows), feature_ints, doc_lengths)
    grad_query_rows, grad_key_rows, grad_value_rows = (from_pairs(g) for g in grads)
    grad_query_weight = mul_ta(row_block, grad_query_rows)
    grad_key_weight = mul_ta(row_block, grad_key_rows)
    grad_value_weight = mul_ta(row_block, grad_value_rows)
    grad_input = (
        mul_tb(grad_query_rows, query_weight)
        + mul_tb(grad_key_rows, key_weight)
        + mul_tb(grad_value_rows, value_weight)
        + grad_resid_one
    )

    def owned(grad):
        shard = lax.psum_scatter(grad.astype(bf16), "fsdp", scatter_dimension=0, tiled=True)
        return lax.psum(shard, "seq").astype(f32)

    sums = jnp.stack(
        [
            column_total(grad_query_rows), column_total(grad_key_rows), column_total(grad_value_rows), grad_out_bias,
            grad_gain_one, grad_offset_one, grad_down_bias, grad_gain_two, grad_offset_two,
            *grad_in_bias.reshape(-1, width),
        ]
    )
    sums = lax.psum(sums, ("fsdp", "seq"))
    mine = [lax.dynamic_slice(sums[i], (me * part,), (part,)) for i in range(9)]
    wide = in_bias.shape[0] // fsdp
    mine_in = lax.dynamic_slice(sums[9:].reshape(-1), (me * wide,), (wide,))
    return (
        layer_wide.astype(bf16)[None],
        grad_input[None],
        owned(grad_query_weight), mine[0],
        owned(grad_key_weight), mine[1],
        owned(grad_value_weight), mine[2],
        owned(grad_out_weight), mine[3],
        mine[4], mine[5],
        owned(grad_in_weight), mine_in,
        owned(grad_down_weight), mine[6],
        mine[7], mine[8],
    )


def solution(mesh):
    rows, matrix, vector = P("fsdp", "seq", None), P("fsdp", None), P("fsdp")
    weights = (matrix, vector) * 4 + (vector, vector) + (matrix, vector) * 2 + (vector, vector)
    near = mesh.shape["fsdp"] == 4 * DEPTH and mesh.shape["seq"] == 2
    return jax.shard_map(
        per_device if near else per_device_wide,
        mesh=mesh,
        in_specs=(rows, matrix, P(), *weights, rows),
        out_specs=(rows, rows, *weights),
        check_vma=False,
    )
```

```python
from functools import partial

import jax
import jax.numpy as jnp
from jax import lax
from jax.experimental import pallas as pl
from jax.experimental.pallas import tpu as pltpu
from jax.sharding import PartitionSpec as P

unit_spread = 0.013531646934131853
inv_root_two = 0.7071067811865476
inv_root_tau = 0.3989422804014327
far_below = -1e30
log2_e = 1.4426950408889634
MESH = pl.DeviceIdType.MESH
f32 = jnp.float32
bf16 = jnp.bfloat16
TAIL = 16
DEPTH = 4
AHEAD = 1


def layer_norm(residual, norm_gain, norm_bias):
    centred = residual - jnp.mean(residual, axis=1, keepdims=True)
    inverse = lax.rsqrt(jnp.mean(centred * centred, axis=1, keepdims=True) + 1e-06)
    normed = centred * inverse
    return (normed * norm_gain.astype(f32) + norm_bias.astype(f32), normed, inverse)


def norm_back(grad_out, normed, inverse, norm_gain):
    scaled = grad_out * norm_gain.astype(f32)
    centre_part = jnp.mean(scaled, axis=1, keepdims=True)
    slope_part = jnp.mean(scaled * normed, axis=1, keepdims=True)
    grad_resid = inverse * (scaled - centre_part - normed * slope_part)
    return (grad_resid, jnp.sum(grad_out * normed, axis=0), jnp.sum(grad_out, axis=0))


def gelu_value(pre_act):
    return 0.5 * pre_act * (1.0 + lax.erf(pre_act * inv_root_two))


def gelu_slope(pre_act):
    return (
        0.5 * (1.0 + lax.erf(pre_act * inv_root_two))
        + pre_act * jnp.exp(-0.5 * pre_act * pre_act) * inv_root_tau
    )


def mul(a, b):
    return lax.dot_general(a, b, (((1,), (0,)), ((), ())), preferred_element_type=f32)


def mul_tb(a, b):
    return lax.dot_general(a, b, (((1,), (1,)), ((), ())), preferred_element_type=f32)


def mul_ta(a, b):
    return lax.dot_general(a, b, (((0,), (0,)), ((), ())), preferred_element_type=f32)


def affine(row_block, weight, bias_row):
    return mul(row_block, weight) + bias_row.astype(f32)


def column_total(values):
    return jnp.sum(values, axis=0, dtype=f32)


def lane_ids(shape):
    return lax.broadcasted_iota(jnp.int32, shape, len(shape) - 1)


def doc_setup(lengths, place, mask_ref, onehot_ref, strad_ref, stradrow_ref):
    rows = mask_ref.shape[0]
    docs = lengths.shape[1]
    total = jnp.int32(0)
    ends = []
    for d in range(docs):
        total = total + lengths[0, d]
        ends.append(total)
    pos = lax.broadcasted_iota(jnp.int32, (rows, 128), 0) + place * rows
    pos_row = lax.broadcasted_iota(jnp.int32, (8, rows), 1) + place * rows
    did = jnp.zeros((rows, 128), jnp.int32)
    did_row = jnp.zeros((8, rows), jnp.int32)
    edge = jnp.int32(0)
    for end in ends[:-1]:
        did = did + (pos >= end).astype(jnp.int32)
        did_row = did_row + (pos_row >= end).astype(jnp.int32)
        edge = edge + (end <= rows).astype(jnp.int32)
    for j in range(rows // 128):
        cols = did_row[0:1, j * 128 : (j + 1) * 128]
        mask_ref[:, j * 128 : (j + 1) * 128] = (did == cols).astype(f32).astype(bf16)
    onehot_ref[...] = (did == lane_ids((rows, 128))).astype(f32)
    strad_ref[...] = (did == edge).astype(f32)
    one_row = (did_row[0:1] == edge).astype(f32)
    stradrow_ref[...] = jnp.broadcast_to(one_row, stradrow_ref.shape).astype(bf16)


def features_setup(ints_ref, omx_ref):
    heads, size, feats = ints_ref.shape

    @pl.loop(0, heads)
    def _(h):
        mat = ints_ref[h].astype(f32).astype(bf16)
        zero = jnp.zeros((size, feats), bf16)
        odd = lax.rem(h, 2) == 1
        omx_ref[h, 0:size] = jnp.where(odd, zero, mat)
        omx_ref[h, size : 2 * size] = jnp.where(odd, mat, zero)
        omx_ref[h, 2 * size :] = jnp.ones((2 * size, feats), bf16)


def three_terms(value):
    first = value.astype(bf16).astype(f32)
    second = (value - first).astype(bf16).astype(f32)
    return first, second, value - first - second


def forward_states(p, scale, q_ref, k_ref, v_ref, omx_ref, onehot_ref, strad_ref, stradrow_ref, pq_ref, pk_ref, peak_ref, out_ref):
    rows = q_ref.shape[1]
    lanes = lane_ids((1, 128))
    qp, kp, vp = q_ref[p], k_ref[p], v_ref[p]
    kf = kp.astype(f32)
    ksq = kf * kf
    vt = jnp.concatenate([vp.T * stradrow_ref[0:1], stradrow_ref[...]], axis=0)
    tail = jnp.zeros((TAIL, pq_ref.shape[-1]), f32)
    tail_row = lax.broadcasted_iota(jnp.int32, tail.shape, 0)
    for j in range(2):
        om = omx_ref[2 * p + j, 0:128]
        raw_q = mul(qp, om)
        raw_q = raw_q - jnp.max(raw_q, axis=1, keepdims=True)
        pq_ref[p, j] = jnp.exp2(raw_q * (scale * log2_e)).astype(bf16)
        here = (lanes >= 64) if j else (lanes < 64)
        half = jnp.sum(jnp.where(here, ksq, 0.0), axis=1, keepdims=True) * (0.0625 / scale)
        raw_k = mul(kp, om) - half
        row_peak = jnp.max(raw_k, axis=1, keepdims=True)
        doc_peak = jnp.max(jnp.where(onehot_ref[...] > 0.5, row_peak, far_below), axis=0, keepdims=True)
        back = jnp.max(jnp.where(onehot_ref[...] > 0.5, doc_peak, far_below), axis=1, keepdims=True)
        edge_peak = jnp.max(jnp.where(strad_ref[...] > 0.5, row_peak, far_below), axis=0, keepdims=True)
        phi_k = jnp.exp2((raw_k - back) * (scale * log2_e)).astype(bf16)
        pk_ref[p, j] = phi_k
        part = mul(vt, phi_k)
        out_ref[p, 64 * j : 64 * j + 64] = part[64 * j : 64 * j + 64].astype(bf16)
        edge_wide = jnp.concatenate([edge_peak, edge_peak], axis=1)
        peak_ref[p, j] = edge_wide
        tail = jnp.where(tail_row == j, part[128 : 128 + TAIL], tail)
        for t, term in enumerate(three_terms(edge_wide)):
            tail = jnp.where(tail_row == 2 + 3 * j + t, term, tail)
    out_ref[p, 128:] = tail.astype(bf16)


def edge_parts(state_ref, p, j):
    tail = state_ref[p, 128:].astype(f32)
    feats = tail.shape[1]
    totals = jnp.broadcast_to(tail[j : j + 1], (128, feats)).astype(bf16)
    peak = tail[2 + 3 * j : 3 + 3 * j] + tail[3 + 3 * j : 4 + 3 * j] + tail[4 + 3 * j : 5 + 3 * j]
    return jnp.concatenate([state_ref[p, 0:128], totals], axis=0), peak


def edge_weights(scale, own, other, strad):
    top = jnp.maximum(own, other)
    own_w = jnp.exp2((own - top) * (scale * log2_e))
    other_w = jnp.exp2((other - top) * (scale * log2_e))
    return 1.0 + strad * (own_w[:, 0:128] - 1.0), strad * other_w[:, 0:128]


def forward_finish(p, scale, v_ref, pq_ref, pk_ref, mask_ref, strad_ref, peak_ref, in_ref, att_ref, den_ref):
    rows = v_ref.shape[1]
    first_half = lane_ids((rows, 128)) < 64
    vx = jnp.concatenate([v_ref[p], jnp.ones((rows, 128), bf16)], axis=1)
    got = []
    for j in range(2):
        phi_q = pq_ref[p, j]
        pair = mul_tb(phi_q, pk_ref[p, j]).astype(bf16) * mask_ref[...]
        near = mul(pair, vx)
        state, other = edge_parts(in_ref, p, j)
        far = mul_tb(phi_q, state)
        wn, wf = edge_weights(scale, peak_ref[p, j], other, strad_ref[...])
        den = near[:, 128:] * wn + far[:, 128:] * wf
        got.append(((near[:, :128] * wn + far[:, :128] * wf) / den, den))
    att_ref[p] = jnp.where(first_half, got[0][0], got[1][0]).astype(bf16)
    den_ref[p] = jnp.where(first_half, got[0][1], got[1][1])


def numer_grads(p, att_ref, den_ref, gatt_ref):
    rows = att_ref.shape[1]
    lanes = lane_ids((rows, 128))
    gn = gatt_ref[p].astype(f32) / den_ref[p]
    prod = gn * att_ref[p].astype(f32)
    d0 = -jnp.sum(jnp.where(lanes < 64, prod, 0.0), axis=1, keepdims=True)
    d1 = -jnp.sum(jnp.where(lanes < 64, 0.0, prod), axis=1, keepdims=True)
    return gn, d0, d1, lanes


def backward_states(p, scale, att_ref, den_ref, gatt_ref, pq_ref, strad_ref, peak_ref, in_ref, out_ref):
    gn, d0, d1, lanes = numer_grads(p, att_ref, den_ref, gatt_ref)
    far = [edge_weights(scale, peak_ref[p, j], edge_parts(in_ref, p, j)[1], strad_ref[...])[1] for j in range(2)]
    left = (gn * jnp.where(lanes < 64, far[0], far[1])).astype(bf16)
    right = (jnp.where(lanes == 0, d0 * far[0], 0.0) + jnp.where(lanes == 1, d1 * far[1], 0.0)).astype(bf16)
    turned = jnp.concatenate([left.T, right.T[0:TAIL]], axis=0)
    tails = []
    for j in range(2):
        part = mul(turned, pq_ref[p, j])
        out_ref[p, 64 * j : 64 * j + 64] = part[64 * j : 64 * j + 64].astype(bf16)
        tails.append(part[128:])
    rowid = lax.broadcasted_iota(jnp.int32, tails[0].shape, 0)
    out_ref[p, 128:] = jnp.where(rowid == 0, tails[0], tails[1]).astype(bf16)


def backward_finish(
    p, scale, q_ref, k_ref, v_ref, omx_ref, pq_ref, pk_ref, mask_ref, strad_ref, peak_ref, in_ref, gin_ref,
    att_ref, den_ref, gatt_ref, gq_ref, gk_ref, gv_ref,
):
    rows = q_ref.shape[1]
    gn, d0, d1, lanes = numer_grads(p, att_ref, den_ref, gatt_ref)
    first_half = lanes < 64
    vp = v_ref[p]
    ones = jnp.ones((rows, 128), bf16)
    vx = jnp.concatenate([vp, ones], axis=1)
    strad = strad_ref[...]
    gq = jnp.zeros((rows, 128), f32)
    gk = jnp.zeros((rows, 128), f32)
    gv = jnp.zeros((rows, 128), f32)
    q_sums, k_sums = [], []
    for j in range(2):
        here = (lanes >= 64) if j else (lanes < 64)
        gd = d1 if j else d0
        state, other = edge_parts(in_ref, p, j)
        wn, wf = edge_weights(scale, peak_ref[p, j], other, strad)
        base_l = jnp.where(here, gn, 0.0)
        base_r = jnp.where(lanes == 0, gd, 0.0)
        near = jnp.concatenate([(base_l * wn).astype(bf16), (base_r * wn).astype(bf16)], axis=1)
        far = jnp.concatenate([(base_l * wf).astype(bf16), (base_r * wf).astype(bf16)], axis=1)
        phi_q, phi_k = pq_ref[p, j], pk_ref[p, j]
        turned = mul_tb(phi_k, phi_q).astype(bf16) * mask_ref[...]
        gv = gv + mul(turned, near[:, 0:128])
        gpair = mul_tb(near, vx).astype(bf16) * mask_ref[...]
        gphi_q = mul(gpair, phi_k) + mul(far, state)
        gturned = mul_tb(vx, near).astype(bf16) * mask_ref[...]
        gstate, _ = edge_parts(gin_ref, p, j)
        vs = jnp.concatenate(
            [(jnp.where(here, vp.astype(f32), 0.0) * strad).astype(bf16), jnp.where(lanes == 0, strad, 0.0).astype(bf16)],
            axis=1,
        )
        gphi_k = mul(gturned, phi_q) + mul(vs, gstate)
        gv = gv + jnp.where(here, mul_tb(phi_k, gstate[0:128]) * strad, 0.0)
        omx = omx_ref[2 * p + j]
        back_q = mul_tb((gphi_q * phi_q.astype(f32)).astype(bf16), omx)
        back_k = mul_tb((gphi_k * phi_k.astype(f32)).astype(bf16), omx)
        gq = gq + back_q[:, 0:128]
        gk = gk + back_k[:, 0:128]
        q_sums.append(back_q[:, 128:])
        k_sums.append(back_k[:, 128:])
    gq = gq * scale - jnp.where(first_half, q_sums[0], q_sums[1]) * q_ref[p].astype(f32) * 0.125
    gk = gk * scale - jnp.where(first_half, k_sums[0], k_sums[1]) * k_ref[p].astype(f32) * 0.125
    gq_ref[p] = gq.astype(bf16)
    gk_ref[p] = gk.astype(bf16)
    gv_ref[p] = gv.astype(bf16)


def peer_barrier(peers):
    barrier = pltpu.get_barrier_semaphore()
    for peer in peers:
        pl.semaphore_signal(barrier, inc=1, device_id=peer, device_id_type=MESH)
    pl.semaphore_wait(barrier, len(peers))


class Place:
    def __init__(self):
        me = lax.axis_index("fsdp")
        self.y = lax.axis_index("seq")
        self.c = lax.rem(me, 2)
        self.x = lax.rem(lax.div(me, 2), 2)
        self.z = lax.div(me, 4)
        self.across = {"seq": 1 - self.y}
        self.twin = {"fsdp": self.z * 4 + self.x * 2 + 1 - self.c}
        self.beside = {"fsdp": self.z * 4 + (1 - self.x) * 2 + self.c}

    def along(self, d):
        return {"fsdp": self.other(d) * 4 + self.x * 2 + self.c}

    def other(self, d):
        return lax.rem(self.z + (d + DEPTH), DEPTH)

    def peers(self):
        return [self.twin, self.beside, self.across] + [self.along(d) for d in range(1, DEPTH)]


def cols_at(start, size):
    return pl.ds(pl.multiple_of(start, 128), size)


def remote(src, dst, ssem, rsem, peer):
    return pltpu.make_async_remote_copy(
        src_ref=src, dst_ref=dst, send_sem=ssem, recv_sem=rsem, device_id=peer, device_id_type=MESH
    )


class Gather:
    def __init__(self, at, own, full, base, width, ssem, rsem, lsem):
        self.at, self.own, self.full = at, own, full
        self.third, self.base, self.width = width // 3, base, width
        self.ssem, self.rsem, self.lsem = ssem, rsem, lsem
        self.sent = []

    def spread(self):
        return cols_at(self.base + self.third * self.at.y, 2 * self.third)

    def extra(self, y):
        return cols_at(self.base + 2 * self.third * y, self.third)

    def whole(self):
        return pl.ds(self.base, self.width)

    def go(self, n, ends):
        src, dst, peer = ends()
        remote(src, dst, self.ssem.at[n], self.rsem.at[n], peer).start()
        self.sent.append((n, ends))

    def came(self, n, ref):
        remote(ref, ref, self.ssem.at[n], self.rsem.at[n], self.at.twin).wait_recv()

    def local(self):
        at = self.at
        return pltpu.make_async_copy(
            self.own.at[:, self.whole()], self.full.at[at.z, at.x, at.c, :, self.whole()], self.lsem
        )

    def begin(self):
        at = self.at
        self.local().start()
        for d in range(1, DEPTH):
            self.go(d - 1, lambda d=d: (*self.first(), at.along(d)))

    def first(self):
        at = self.at
        return self.own.at[:, self.spread()], self.full.at[at.z, at.x, at.c, :, self.spread()]

    def piece(self, d, x, cols):
        return self.full.at[self.at.other(-d), x, self.at.c, :, cols]

    def stage_x(self):
        at = self.at
        self.go(DEPTH - 1, lambda: (*self.first(), at.beside))
        for d in range(1, DEPTH):
            self.came(d - 1, self.piece(d, at.x, self.spread()))
            self.go(DEPTH - 1 + d, lambda d=d: (*[self.piece(d, at.x, self.spread())] * 2, at.beside))
            self.go(2 * DEPTH - 2 + d, lambda d=d: (*[self.piece(d, at.x, self.extra(at.y))] * 2, at.across))

    def stage_y(self):
        at = self.at
        for d in range(DEPTH):
            self.came(DEPTH - 1 + d, self.piece(d, 1 - at.x, self.spread()))
            self.go(3 * DEPTH - 2 + d, lambda d=d: (*[self.piece(d, 1 - at.x, self.extra(at.y))] * 2, at.across))

    def stage_c(self):
        at = self.at
        for d in range(1, DEPTH):
            self.came(2 * DEPTH - 2 + d, self.piece(d, at.x, self.extra(1 - at.y)))
        for d in range(DEPTH):
            self.came(3 * DEPTH - 2 + d, self.piece(d, 1 - at.x, self.extra(1 - at.y)))
        self.local().wait()
        self.go(4 * DEPTH - 2, lambda: (*[self.full.at[:, :, at.c, :, self.whole()]] * 2, at.twin))

    def ready(self):
        self.came(4 * DEPTH - 2, self.full.at[:, :, 1 - self.at.c, :, self.whole()])

    def drain(self):
        for n, ends in self.sent:
            src, dst, peer = ends()
            remote(src, dst, self.ssem.at[n], self.rsem.at[n], peer).wait_send()


GATHER_COPIES = 4 * DEPTH - 1


class SmallSum:
    def __init__(self, at, total, land, ssem, rsem, over_seq):
        self.at, self.total, self.land, self.ssem, self.rsem, self.over_seq = at, total, land, ssem, rsem, over_seq
        self.sent = []

    def go(self, src, n, peer):
        copy = remote(self.total.at[src], self.land.at[n], self.ssem.at[n], self.rsem.at[n], peer)
        copy.start()
        self.sent.append(copy)

    def came(self, n):
        remote(self.land.at[n], self.land.at[n], self.ssem.at[n], self.rsem.at[n], self.at.twin).wait_recv()

    def begin(self):
        for d in range(1, DEPTH):
            self.go(0, d - 1, self.at.along(d))

    def step(self, k):
        if k == 0:
            got = self.total[0]
            for d in range(1, DEPTH):
                self.came(d - 1)
            order = [self.at.z] + [self.at.other(-d) for d in range(1, DEPTH)]
            parts = [got] + [self.land[d - 1] for d in range(1, DEPTH)]
            value = jnp.zeros_like(got)
            for z in range(DEPTH):
                one = jnp.zeros_like(got)
                for place, part in zip(order, parts):
                    one = jnp.where(place == z, part, one)
                value = value + one
        else:
            self.came(DEPTH - 2 + k)
            value = self.total[k] + self.land[DEPTH - 2 + k]
        self.total[k + 1] = value
        hops = [self.at.beside, self.at.twin] + ([self.at.across] if self.over_seq else [])
        if k < len(hops):
            self.go(k + 1, DEPTH - 1 + k, hops[k])

    def steps(self):
        return 4 if self.over_seq else 3

    def result(self):
        return self.total[self.steps()]

    def drain(self):
        for copy in self.sent:
            copy.wait_send()


def spread_vectors(at, pieces, wide):
    width = 768
    part = pieces[0].shape[-1]
    rows = [p[...].astype(f32).reshape(1, part) for p in pieces]
    rows = jnp.concatenate(rows + [jnp.zeros((16 - len(rows), part), f32)], axis=0)
    rows = jnp.concatenate([rows, jnp.zeros((16, width - part), f32)], axis=1)
    rows = pltpu.roll(rows, (at.z * 4 + at.x * 2 + at.c) * part, 1)
    span = wide.shape[-1]
    row = jnp.concatenate([wide[...].astype(f32).reshape(1, span), jnp.zeros((1, width - span), f32)], axis=1)
    row = pltpu.roll(jnp.broadcast_to(row, (16, width)), (at.x * 2 + at.c) * span, 1)
    here = lax.broadcasted_iota(jnp.int32, (16, width), 0)
    return jnp.where(here == len(pieces) + at.z, row, rows)


def forward_kernel(
    scale, x_ref, wq_ref, wk_ref, wv_ref, wo_ref, win_ref, wdn_ref, bq_ref, bk_ref, bv_ref, bo_ref, g1_ref, o1_ref, bd_ref,
    g2_ref, o2_ref, bin_ref, ints_ref, len_ref,
    q_ref, k_ref, v_ref, pq_ref, pk_ref, att_ref, den_ref, peak_ref, state_ref, omx_ref, sq_ref, fin_ref, fdn_ref, vec_ref,
    mask_ref, onehot_ref, strad_ref, stradrow_ref, send_ref, total_ref, land_ref,
    ssem, rsem, gs_sem, gr_sem, gl_sem, vs_sem, vr_sem,
):
    at = Place()
    pairs = q_ref.shape[0]
    blocks = []
    specs = [(w, sq_ref.at[n], 0, 768) for n, w in enumerate((wq_ref, wk_ref, wv_ref, wo_ref))]
    specs += [(win_ref, fin_ref, 768 * h, 768) for h in range(4)]
    specs += [(wdn_ref.at[pl.ds(48 * h, 48)], fdn_ref.at[:, :, :, pl.ds(48 * h, 48)], 0, 768) for h in range(4)]
    for n, (own, full, base, width) in enumerate(specs):
        blocks.append(Gather(at, own, full, base, width, gs_sem.at[n], gr_sem.at[n], gl_sem.at[n]))
    peer_barrier(at.peers())
    vec = SmallSum(at, total_ref, land_ref, vs_sem, vr_sem, False)
    total_ref[0] = spread_vectors(
        at, (bq_ref, bk_ref, bv_ref, bo_ref, g1_ref, o1_ref, bd_ref, g2_ref, o2_ref), bin_ref
    ).astype(bf16)
    blocks[0].begin()
    vec.begin()
    for b in blocks[1:AHEAD]:
        b.begin()
    doc_setup(len_ref, at.y, mask_ref, onehot_ref, strad_ref, stradrow_ref)
    features_setup(ints_ref, omx_ref)

    def project(n, o_ref):
        for j in range(pairs // 2):
            cols = slice(256 * j, 256 * j + 256)
            got = mul(x_ref[...], sq_ref[n, :, :, :, :, cols].reshape(768, 256))
            got = (got + vec_ref[n : n + 1, cols].astype(f32)).astype(bf16)
            o_ref[2 * j] = got[:, 0:128]
            o_ref[2 * j + 1] = got[:, 128:256]

    def tick(t):
        if t + AHEAD < len(blocks):
            blocks[t + AHEAD].begin()
        for k, name in enumerate(("stage_x", "stage_y", "stage_c", "ready")):
            if 0 <= t - k < len(blocks):
                getattr(blocks[t - k], name)()

    for t in range(3):
        tick(t)
        vec.step(t)
    vec_ref[...] = vec.result()
    for n, ref in enumerate((q_ref, k_ref, v_ref)):
        tick(3 + n)
        project(n, ref)

    def copy(p):
        return remote(send_ref.at[p], state_ref.at[p], ssem.at[p], rsem.at[p], at.across)

    early = {0: 6, 2: 7, 4: 8}
    late = {0: 9, 1: 10, 2: 11, 3: 12, 4: 13, 5: 14}

    @pl.loop(0, pairs)
    def _(p):
        forward_states(p, scale, q_ref, k_ref, v_ref, omx_ref, onehot_ref, strad_ref, stradrow_ref, pq_ref, pk_ref, peak_ref, send_ref)
        copy(p).start()
        for n, t in early.items():
            @pl.when(p == n)
            def _(t=t):
                tick(t)

    @pl.loop(0, pairs)
    def _(p):
        copy(p).wait()
        forward_finish(p, scale, v_ref, pq_ref, pk_ref, mask_ref, strad_ref, peak_ref, state_ref, att_ref, den_ref)
        for n, t in late.items():
            @pl.when(p == n)
            def _(t=t):
                tick(t)

    for b in blocks:
        b.drain()
    vec.drain()


class Scatter:
    def __init__(self, at, order, source, twin_in, lands, done, done_in, put, ssem, rsem):
        self.at, self.order, self.source, self.acc = at, order, source, source(at.c)
        self.twin_in, self.lands = twin_in, lands
        self.done, self.done_in, self.put = done, done_in, put
        self.ssem, self.rsem = ssem, rsem
        self.half = twin_in.shape[-1] // 2
        self.sent = []

    def go(self, n, ends):
        src, dst, peer = ends()
        remote(src, dst, self.ssem.at[n], self.rsem.at[n], peer).start()
        self.sent.append((n, ends))

    def came(self, n, ref):
        remote(ref, ref, self.ssem.at[n], self.rsem.at[n], self.at.twin).wait_recv()

    def side(self, y):
        return cols_at(self.half * y, self.half)

    def spot(self, fixed, **other):
        at = self.at
        z = other.get("z", at.z if "z" in fixed else slice(None))
        x = other.get("x", at.x if "x" in fixed else slice(None))
        cols = self.side(other.get("y", at.y)) if "y" in fixed or "y" in other else slice(None)
        return z, x, slice(None), cols

    def first(self, i):
        return 1 + sum(DEPTH - 1 if kind == "z" else 1 for kind in self.order[:i])

    def send(self, i):
        at, kind, fixed = self.at, self.order[i], self.order[:i]
        if kind == "z":
            for d in range(1, DEPTH):
                self.go(
                    self.first(i) + d - 1,
                    lambda d=d: (self.acc.at[self.spot(fixed, z=at.other(d))], self.lands[i].at[d - 1], at.along(d)),
                )
        elif kind == "x":
            self.go(self.first(i), lambda: (self.acc.at[self.spot(fixed, x=1 - at.x)], self.lands[i], at.beside))
        else:
            self.go(self.first(i), lambda: (self.acc.at[self.spot(fixed, y=1 - at.y)], self.lands[i], at.across))

    def add(self, parts, fixed, store):
        def at_z(z):
            for x in [None] if "x" in fixed else range(2):
                spot = list(self.spot(fixed))
                inner = ()
                if z is not None:
                    spot[0] = z
                    inner += (z,)
                if x is not None:
                    spot[1] = x
                    inner += (x,)
                value = self.acc[tuple(spot)].astype(f32)
                for part in parts:
                    value = value + part[inner + (slice(None), slice(None))].astype(f32)
                store(tuple(spot), value)

        if "z" in fixed:
            at_z(None)
        else:
            pl.loop(0, DEPTH)(at_z)

    def keep(self, spot, value):
        self.acc[spot] = value.astype(bf16)

    def finish(self, spot, value):
        low = value.astype(bf16)
        self.done[...] = low
        self.put(self.at.y, low.astype(f32))

    def arrived(self, i):
        if self.order[i] != "z":
            self.came(self.first(i), self.lands[i])
            return [self.lands[i]]
        for d in range(1, DEPTH):
            self.came(self.first(i) + d - 1, self.lands[i].at[d - 1])
        return [self.lands[i].at[d - 1] for d in range(1, DEPTH)]

    def begin(self):
        self.go(0, lambda: (self.source(1 - self.at.c), self.twin_in, self.at.twin))

    def stage_1(self):
        self.came(0, self.twin_in)
        self.add([self.twin_in], "", self.keep)
        self.send(0)

    def stage_2(self):
        self.add(self.arrived(0), self.order[:1], self.keep)
        self.send(1)

    def stage_3(self):
        self.add(self.arrived(1), self.order[:2], self.keep)
        self.send(2)

    def stage_4(self):
        self.add(self.arrived(2), self.order, self.finish)
        self.go(2 + DEPTH, lambda: (self.done, self.done_in, self.at.across))

    def stage_5(self):
        self.came(2 + DEPTH, self.done_in)
        self.put(1 - self.at.y, self.done_in[...].astype(f32))

    def drain(self):
        for n, ends in self.sent:
            src, dst, peer = ends()
            remote(src, dst, self.ssem.at[n], self.rsem.at[n], peer).wait_send()


def landing(order, part, width):
    shapes = []
    for i, kind in enumerate(order):
        kept = order[: i + 1]
        shape = [] if "z" in kept else [DEPTH]
        shape += [] if "x" in kept else [2]
        shape += [part, width // 2 if "y" in kept else width]
        shapes.append(pltpu.VMEM(tuple([DEPTH - 1] + shape if kind == "z" else shape), bf16))
    return shapes


SCATTER_COPIES = DEPTH + 3
FEED_STEPS = (3, 7)
HEAD_STEPS = (0, 1, 2, 3, 4, 5)
PACE = ((0, 2, 4, 6, 8),) * 6 + ((0, 2, 3, 4, 5),) * 3 + ((0, 1, 2, 3, 4),) * 3
ORDERS = ("xyz", "yxz") * 6


def backward_kernel(
    scale, x_ref, q_ref, k_ref, v_ref, pq_ref, pk_ref, att_ref, den_ref, peak_ref, state_ref, omx_ref, hid_ref, norm_ref,
    inv_ref, res_ref, gain_ref, vecin_ref, len_ref, gel_ref, slope_ref, win_ref, wdn_ref, sq_ref,
    gx_ref, oq_ref, ok_ref, ov_ref, oo_ref, oin_ref, odn_ref, vec_ref,
    gstate_ref, mask_ref, onehot_ref, strad_ref, stradrow_ref, send_ref,
    xt_ref, gq_ref, gk_ref, gv_ref, gatt_ref, low_ref, wide_ref, gelbuf_ref, slopebuf_ref,
    gdn_ref, gin_ref, go_ref, gw_ref, total_ref, land_ref,
    twin_ref, done_ref, donein_ref,
    ssem, rsem, load_sem, late_sem, ws_sem, wr_sem, vs_sem, vr_sem, *land_refs,
):
    at = Place()
    pairs = q_ref.shape[0]
    rows, width = x_ref.shape
    span = width // 2
    chunks = win_ref.shape[1] // span
    sources = [lambda c, b=b: gdn_ref.at[:, :, c, pl.ds(48 * b, 48)] for b in range(4)]
    sources += [lambda c, b=b: gin_ref.at[:, :, c, :, pl.ds(768 * b, 768)] for b in range(4)]
    sources += [lambda c: go_ref.at[:, :, c]]
    sources += [lambda c, n=n: gw_ref.at[n, :, :, c] for n in (2, 1, 0)]

    def putter(ref, row, col):
        def put(y, value):
            ref[pl.ds(row, 48), cols_at(col + 384 * y, 384)] = value

        return put

    puts = [putter(odn_ref, 48 * b, 0) for b in range(4)] + [putter(oin_ref, 0, 768 * b) for b in range(4)]
    puts += [putter(r, 0, 0) for r in (oo_ref, ov_ref, ok_ref, oq_ref)]
    units = []
    for n, (source, put) in enumerate(zip(sources, puts)):
        lands = land_refs[3 * n : 3 * n + 3]
        units.append(
            Scatter(
                at, ORDERS[n], source, twin_ref.at[n], lands, done_ref.at[n], donein_ref.at[n], put, ws_sem.at[n], wr_sem.at[n]
            )
        )
    early = len(units) - 3

    def step(s):
        for k in range(5):
            for u, unit in enumerate(units):
                if u + PACE[u][k] == s:
                    getattr(unit, "stage_" + str(k + 1))()


    def load(src, dst, sem):
        return pltpu.make_async_copy(src, dst, sem)

    def slot(m):
        return lax.rem(m, 2)

    def load_gelu(m):
        return load(gel_ref.at[:, cols_at(span * m, span)], gelbuf_ref.at[slot(m)], load_sem.at[0, slot(m)])

    def load_chunk(m):
        start = pl.multiple_of(span * slot(m), 128)
        return [
            load(slope_ref.at[:, cols_at(span * m, span)], slopebuf_ref.at[slot(m)], load_sem.at[1, slot(m)]),
            load(wdn_ref.at[pl.ds(pl.multiple_of(span * m, 128), span)], wide_ref.at[0, pl.ds(start, span)], load_sem.at[2, slot(m)]),
            load(win_ref.at[:, cols_at(span * m, span)], wide_ref.at[1, :, pl.ds(start, span)], load_sem.at[3, slot(m)]),
        ]

    def load_square(n, to):
        return load(sq_ref.at[n], wide_ref.at[to], late_sem.at[to])

    peer_barrier(at.peers())
    load_gelu(jnp.int32(0)).start()
    for one in load_chunk(jnp.int32(0)):
        one.start()
    load_square(3, 2).start()
    total_ref[0] = vecin_ref[...]

    @pl.loop(0, rows // 128)
    def _(r):
        here = pl.ds(pl.multiple_of(128 * r, 128), 128)
        low_ref[here] = res_ref[here].astype(bf16)
        gx_ref[here] = res_ref[here]


    @pl.loop(0, chunks)
    def _(m):
        load_gelu(m).wait()

        @pl.when(m < chunks - 1)
        def _():
            load_gelu(m + 1).start()

        turned = gelbuf_ref[slot(m)].T
        for n in range(3):
            cols = slice(256 * n, 256 * n + 256)
            got = mul(turned, low_ref[:, cols]).astype(bf16)
            gdn_ref[lax.div(m, 2), slot(m), :, :, cols] = got.reshape(2, span // 2, 256)

    units[0].begin()
    units[1].begin()
    for j in range(pairs):
        xt_ref[128 * j : 128 * j + 128] = hid_ref[:, 128 * j : 128 * j + 128].T

    @pl.loop(0, chunks)
    def _(m):
        for one in load_chunk(m):
            one.wait()

        @pl.when(m < chunks - 1)
        def _():
            for one in load_chunk(m + 1):
                one.start()

        start = pl.multiple_of(span * slot(m), 128)
        gpre = mul_tb(low_ref[...], wide_ref[0, pl.ds(start, span)]) * slopebuf_ref[slot(m)].astype(f32)
        gpre = gpre.astype(bf16)
        total_ref[0, pl.ds(9 + lax.div(m, 2), 1), cols_at(start, span)] = jnp.sum(gpre.astype(f32), axis=0, keepdims=True)
        got = mul(xt_ref[...], gpre).astype(bf16)
        gin_ref[:, :, :, :, cols_at(span * m, span)] = got.reshape(DEPTH, 2, 2, 48, span)
        for n in range(3):
            cols = slice(256 * n, 256 * n + 256)
            gx_ref[:, cols] = gx_ref[:, cols] + mul_tb(gpre, wide_ref[1, cols, pl.ds(start, span)])
        for n in range(8):
            @pl.when(m == n)
            def _(n=n):
                if n < 2:
                    units[2 + n].begin()
                if n % 2:
                    units[4 + n // 2].begin()
                if n in FEED_STEPS:
                    step(FEED_STEPS.index(n))

    done_steps = len(FEED_STEPS)

    @pl.loop(0, rows // 128)
    def _(r):
        here = pl.ds(pl.multiple_of(128 * r, 128), 128)
        grad = gx_ref[here]
        normed = norm_ref[here].astype(f32)
        scaled = grad * gain_ref[...]
        centre = jnp.mean(scaled, axis=1, keepdims=True)
        slope = jnp.mean(scaled * normed, axis=1, keepdims=True)
        resid = inv_ref[here] * (scaled - centre - normed * slope)
        gx_ref[here] = resid
        low = resid.astype(bf16)
        low_ref[here] = low
        total_ref[0, 3:4] = total_ref[0, 3:4] + jnp.sum(low.astype(f32), axis=0, keepdims=True)
        total_ref[0, 4:5] = total_ref[0, 4:5] + jnp.sum(grad * normed, axis=0, keepdims=True)
        total_ref[0, 5:6] = total_ref[0, 5:6] + jnp.sum(grad, axis=0, keepdims=True)

    load_square(3, 2).wait()
    for h in range(2):
        turned = jnp.concatenate([att_ref[3 * h + i].T for i in range(3)], axis=0)
        for n in range(3):
            cols = slice(256 * n, 256 * n + 256)
            go_ref[2 * h : 2 * h + 2, :, :, :, cols] = mul(turned, low_ref[:, cols]).astype(bf16).reshape(2, 2, 2, 48, 256)
    units[8].begin()
    for j in range(pairs // 2):
        got = mul_tb(low_ref[...], wide_ref[2, 256 * j : 256 * j + 256]).astype(bf16)
        gatt_ref[2 * j] = got[:, 0:128]
        gatt_ref[2 * j + 1] = got[:, 128:256]
    for n in range(3):
        load_square(n, n).start()
    step(done_steps)
    done_steps += 1


    doc_setup(len_ref, at.y, mask_ref, onehot_ref, strad_ref, stradrow_ref)

    def copy(p):
        return remote(send_ref.at[p], gstate_ref.at[p], ssem.at[p], rsem.at[p], at.across)

    @pl.loop(0, pairs)
    def _(p):
        backward_states(p, scale, att_ref, den_ref, gatt_ref, pq_ref, strad_ref, peak_ref, state_ref, send_ref)
        copy(p).start()

    for j in range(pairs):
        xt_ref[128 * j : 128 * j + 128] = x_ref[:, 128 * j : 128 * j + 128].T

    @pl.loop(0, pairs)
    def _(p):
        copy(p).wait()
        backward_finish(
            p, scale, q_ref, k_ref, v_ref, omx_ref, pq_ref, pk_ref, mask_ref, strad_ref, peak_ref, state_ref, gstate_ref,
            att_ref, den_ref, gatt_ref, gq_ref, gk_ref, gv_ref,
        )
        cols = cols_at(128 * p, 128)
        both = mul(xt_ref[...], jnp.concatenate([gq_ref[p], gk_ref[p]], axis=1)).astype(bf16)
        gw_ref[0, :, :, :, :, cols] = both[:, 0:128].reshape(DEPTH, 2, 2, 48, 128)
        gw_ref[1, :, :, :, :, cols] = both[:, 128:256].reshape(DEPTH, 2, 2, 48, 128)
        gw_ref[2, :, :, :, :, cols] = mul(xt_ref[...], gv_ref[p]).astype(bf16).reshape(DEPTH, 2, 2, 48, 128)
        for n, ref in enumerate((gq_ref, gk_ref, gv_ref)):
            total_ref[0, n : n + 1, cols] = jnp.sum(ref[p].astype(f32), axis=0, keepdims=True)
        for n, at_pair in enumerate(HEAD_STEPS):
            @pl.when(p == at_pair)
            def _(n=n):
                step(n + done_steps)

    vec = SmallSum(at, total_ref, land_ref, vs_sem, vr_sem, True)
    vec.begin()
    for u in units[early:]:
        u.begin()
    for n in range(3):
        load_square(n, n).wait()

    def grad_input(j):
        cols = slice(256 * j, 256 * j + 256)
        value = gx_ref[:, cols]
        for n, ref in enumerate((gq_ref, gk_ref, gv_ref)):
            for i in range(pairs // 2):
                left = jnp.concatenate([ref[2 * i], ref[2 * i + 1]], axis=1)
                right = wide_ref[n, 256 * j : 256 * j + 256, 256 * i : 256 * i + 256]
                value = value + mul_tb(left, right)
        gx_ref[:, cols] = value

    done_steps += len(HEAD_STEPS)
    for n, s in enumerate(range(done_steps, len(units) + PACE[-1][-1])):
        step(s)
        if n < 4:
            vec.step(n)
        if n < 3:
            grad_input(n)
    vec_ref[...] = vec.result()
    for u in units:
        u.drain()
    vec.drain()


def scratch_masks(rows, heads, feats):
    return [
        pltpu.VMEM((heads, 256, feats), bf16),
        pltpu.VMEM((rows, rows), bf16),
        pltpu.VMEM((rows, 128), f32),
        pltpu.VMEM((rows, 128), f32),
        pltpu.VMEM((TAIL, rows), bf16),
    ]


def vmem():
    return pl.BlockSpec(memory_space=pltpu.VMEM)


def anywhere():
    return pl.BlockSpec(memory_space=pl.ANY)


def smem():
    return pl.BlockSpec(memory_space=pltpu.SMEM)


def attention_forward(x, weights, vectors, ints, lengths):
    rows, width = x.shape
    heads, size, feats = ints.shape
    pairs = heads // 2
    hidden = weights[4].shape[1]
    part = weights[0].shape[0]
    scale = size ** (-0.25) * unit_spread
    shape = jax.ShapeDtypeStruct
    grid = (DEPTH, 2, 2)
    dma = pltpu.SemaphoreType.DMA
    return pl.pallas_call(
        partial(forward_kernel, scale),
        out_shape=[
            shape((pairs, rows, 128), bf16), shape((pairs, rows, 128), bf16), shape((pairs, rows, 128), bf16),
            shape((pairs, 2, rows, feats), bf16), shape((pairs, 2, rows, feats), bf16),
            shape((pairs, rows, 128), bf16), shape((pairs, rows, 128), f32),
            shape((pairs, 2, 1, feats), f32), shape((pairs, 128 + TAIL, feats), bf16), shape((heads, 256, feats), bf16),
            shape((4, *grid, part, width), bf16),
            shape((*grid, part, hidden), bf16), shape((*grid, weights[5].shape[0], width), bf16),
            shape((16, width), bf16),
        ],
        in_specs=[vmem()] * 18 + [smem()],
        out_specs=[vmem()] * 11 + [anywhere()] * 2 + [vmem()],
        scratch_shapes=scratch_masks(rows, heads, feats)[1:] + [
            pltpu.VMEM((pairs, 128 + TAIL, feats), bf16),
            pltpu.VMEM((4, 16, width), bf16),
            pltpu.VMEM((DEPTH + 1, 16, width), bf16),
            dma((pairs,)), dma((pairs,)),
            dma((12, GATHER_COPIES)), dma((12, GATHER_COPIES)), dma((12,)),
            dma((DEPTH + 1,)), dma((DEPTH + 1,)),
        ],
        compiler_params=pltpu.CompilerParams(collective_id=0, has_side_effects=True, vmem_limit_bytes=60 << 20),
        name="attention_forward",
    )(x, *weights, *vectors, ints, lengths)


def attention_backward(x, saved, hidden_low, normed, inverse, grad_resid, gain, vec, lengths, gelu_low, slope, win, wdn, square):
    rows, width = x.shape
    pairs, _, _, feats = saved[3].shape
    heads, hidden = 2 * pairs, win.shape[1]
    scale = (width // heads) ** (-0.25) * unit_spread
    shape = jax.ShapeDtypeStruct
    dma = pltpu.SemaphoreType.DMA
    grid = (DEPTH, 2, 2)
    part = width // 16
    units = 12
    return pl.pallas_call(
        partial(backward_kernel, scale),
        out_shape=[shape((rows, width), f32)]
        + [shape((part, width), f32)] * 4
        + [shape((part, hidden), f32), shape((hidden // 16, width), f32), shape((16, width), f32)],
        in_specs=[vmem()] * 17 + [smem()] + [anywhere()] * 5,
        out_specs=[vmem()] * 8,
        scratch_shapes=[pltpu.VMEM((pairs, 128 + TAIL, feats), bf16)] + scratch_masks(rows, heads, feats)[1:] + [
            pltpu.VMEM((pairs, 128 + TAIL, feats), bf16),
            pltpu.VMEM((width, rows), bf16),
            pltpu.VMEM((pairs, rows, 128), bf16), pltpu.VMEM((pairs, rows, 128), bf16), pltpu.VMEM((pairs, rows, 128), bf16),
            pltpu.VMEM((pairs, rows, 128), bf16),
            pltpu.VMEM((rows, width), bf16),
            pltpu.VMEM((3, width, width), bf16),
            pltpu.VMEM((2, rows, width // 2), bf16), pltpu.VMEM((2, rows, width // 2), bf16),
            pltpu.VMEM((*grid, hidden // 16, width), bf16),
            pltpu.VMEM((*grid, part, hidden), bf16),
            pltpu.VMEM((*grid, part, width), bf16),
            pltpu.VMEM((3, *grid, part, width), bf16),
            pltpu.VMEM((5, 16, width), f32),
            pltpu.VMEM((DEPTH + 2, 16, width), f32),
            pltpu.VMEM((units, DEPTH, 2, part, width), bf16),
            pltpu.VMEM((units, part, width // 2), bf16),
            pltpu.VMEM((units, part, width // 2), bf16),
            dma((pairs,)), dma((pairs,)), dma((4, 2)), dma((3,)),
            dma((units, SCATTER_COPIES)), dma((units, SCATTER_COPIES)),
            dma((DEPTH + 2,)), dma((DEPTH + 2,)),
        ] + [land for order in ORDERS for land in landing(order, part, width)],
        compiler_params=pltpu.CompilerParams(collective_id=1, has_side_effects=True, vmem_limit_bytes=65200 << 10),
        name="attention_backward",
    )(
        x, *saved, hidden_low, normed, inverse, grad_resid, gain, vec, lengths, gelu_low, slope, win, wdn, square
    )


def to_pairs(rows):
    return rows.reshape(rows.shape[0], -1, 128).transpose(1, 0, 2)


def from_pairs(pairs):
    return pairs.transpose(1, 0, 2).reshape(pairs.shape[1], -1)


def per_device(
    tokens, doc_lengths, feature_ints, w_query, b_query, w_key, b_key, w_value, b_value, w_out, b_out,
    norm1_gain, norm1_bias, w_in, b_in, w_down, b_down, norm2_gain, norm2_bias, cotangent,
):
    row_block = tokens[0]
    width = row_block.shape[1]
    me = lax.axis_index("fsdp")
    *saved, square, in_weight, down_weight, vec = attention_forward(
        row_block,
        (w_query, w_key, w_value, w_out, w_in, w_down),
        (b_query, b_key, b_value, b_out, norm1_gain, norm1_bias, b_down, norm2_gain, norm2_bias, b_in),
        feature_ints, doc_lengths,
    )
    in_weight = in_weight.reshape(width, -1)
    down_weight = down_weight.reshape(-1, width)
    square = square.reshape(4, width, width)
    out_weight = square[3]
    _, _, _, out_bias, gain_one, offset_one, down_bias, gain_two, offset_two = (vec[i] for i in range(9))
    in_bias = vec[9:13].reshape(-1)
    att_rows = from_pairs(saved[5])
    residual_one = row_block.astype(f32) + affine(att_rows, out_weight, out_bias)
    hidden_wide, normed_one, inverse_one = layer_norm(residual_one, gain_one, offset_one)
    hidden_low = hidden_wide.astype(bf16)
    pre_act = affine(hidden_low, in_weight, in_bias)
    gelu_low = gelu_value(pre_act).astype(bf16)
    slope_low = gelu_slope(pre_act).astype(bf16)
    residual_two = hidden_low.astype(f32) + affine(gelu_low, down_weight, down_bias)
    layer_wide, normed_two, inverse_two = layer_norm(residual_two, gain_two, offset_two)
    grad_out = cotangent[0].astype(f32)
    grad_resid_two, grad_gain_two, grad_offset_two = norm_back(grad_out, normed_two, inverse_two, gain_two)
    grad_down_bias = column_total(grad_resid_two.astype(bf16))
    nothing = jnp.zeros((6, width), f32)
    sums = jnp.concatenate(
        [nothing, jnp.stack([grad_down_bias, grad_gain_two, grad_offset_two]), nothing, nothing[0:1]], axis=0
    )
    grad_input, gq, gk, gv, go, gin, gdn, sums = attention_backward(
        row_block, saved, hidden_low, normed_one.astype(bf16), inverse_one, grad_resid_two, gain_one.astype(f32)[None],
        sums, doc_lengths, gelu_low, slope_low, in_weight, down_weight, square,
    )
    part = b_query.shape[0]
    wide = b_in.shape[0]
    mine = lax.dynamic_slice(sums, (0, me * part), (9, part))
    mine_in = lax.dynamic_slice(sums[9:13].reshape(-1), (me * wide,), (wide,))
    return (
        layer_wide.astype(bf16)[None],
        grad_input[None],
        gq, mine[0], gk, mine[1], gv, mine[2], go, mine[3], mine[4], mine[5], gin, mine_in, gdn, mine[6], mine[7], mine[8],
    )


def forward_kernel_wide(
    scale, x_ref, wq_ref, wk_ref, wv_ref, bias_ref, ints_ref, len_ref,
    q_ref, k_ref, v_ref, pq_ref, pk_ref, att_ref, den_ref, peak_ref, state_ref,
    omx_ref, mask_ref, onehot_ref, strad_ref, stradrow_ref, send_ref, ssem, rsem,
):
    place = lax.axis_index("seq")
    peer = {"seq": 1 - place}
    peer_barrier([peer])
    pairs = q_ref.shape[0]
    doc_setup(len_ref, place, mask_ref, onehot_ref, strad_ref, stradrow_ref)
    features_setup(ints_ref, omx_ref)
    for n, (w_ref, o_ref) in enumerate(((wq_ref, q_ref), (wk_ref, k_ref), (wv_ref, v_ref))):
        for j in range(pairs // 2):
            cols = slice(256 * j, 256 * j + 256)
            got = (mul(x_ref[...], w_ref[:, cols]) + bias_ref[n : n + 1, cols].astype(f32)).astype(bf16)
            o_ref[2 * j] = got[:, 0:128]
            o_ref[2 * j + 1] = got[:, 128:256]

    def copy(p):
        return pltpu.make_async_remote_copy(
            src_ref=send_ref.at[p], dst_ref=state_ref.at[p], send_sem=ssem.at[p], recv_sem=rsem.at[p],
            device_id=peer, device_id_type=MESH,
        )

    @pl.loop(0, pairs)
    def _(p):
        forward_states(p, scale, q_ref, k_ref, v_ref, omx_ref, onehot_ref, strad_ref, stradrow_ref, pq_ref, pk_ref, peak_ref, send_ref)
        copy(p).start()

    @pl.loop(0, pairs)
    def _(p):
        copy(p).wait()
        forward_finish(p, scale, v_ref, pq_ref, pk_ref, mask_ref, strad_ref, peak_ref, state_ref, att_ref, den_ref)


def backward_kernel_wide(
    scale, q_ref, k_ref, v_ref, pq_ref, pk_ref, att_ref, den_ref, peak_ref, state_ref, gatt_ref, ints_ref, len_ref,
    gq_ref, gk_ref, gv_ref,
    gstate_ref, omx_ref, mask_ref, onehot_ref, strad_ref, stradrow_ref, send_ref, ssem, rsem,
):
    place = lax.axis_index("seq")
    peer = {"seq": 1 - place}
    peer_barrier([peer])
    pairs = q_ref.shape[0]
    doc_setup(len_ref, place, mask_ref, onehot_ref, strad_ref, stradrow_ref)
    features_setup(ints_ref, omx_ref)

    def copy(p):
        return pltpu.make_async_remote_copy(
            src_ref=send_ref.at[p], dst_ref=gstate_ref.at[p], send_sem=ssem.at[p], recv_sem=rsem.at[p],
            device_id=peer, device_id_type=MESH,
        )

    @pl.loop(0, pairs)
    def _(p):
        backward_states(p, scale, att_ref, den_ref, gatt_ref, pq_ref, strad_ref, peak_ref, state_ref, send_ref)
        copy(p).start()

    @pl.loop(0, pairs)
    def _(p):
        copy(p).wait()
        backward_finish(
            p, scale, q_ref, k_ref, v_ref, omx_ref, pq_ref, pk_ref, mask_ref, strad_ref, peak_ref, state_ref, gstate_ref,
            att_ref, den_ref, gatt_ref, gq_ref, gk_ref, gv_ref,
        )


def attention_forward_wide(x, wq, wk, wv, biases, ints, lengths):
    rows = x.shape[0]
    heads, size, feats = ints.shape
    pairs = heads // 2
    scale = size ** (-0.25) * unit_spread
    shape = jax.ShapeDtypeStruct
    return pl.pallas_call(
        partial(forward_kernel_wide, scale),
        out_shape=[
            shape((pairs, rows, 128), bf16), shape((pairs, rows, 128), bf16), shape((pairs, rows, 128), bf16),
            shape((pairs, 2, rows, feats), bf16), shape((pairs, 2, rows, feats), bf16),
            shape((pairs, rows, 128), bf16), shape((pairs, rows, 128), f32),
            shape((pairs, 2, 1, feats), f32), shape((pairs, 128 + TAIL, feats), bf16),
        ],
        in_specs=[vmem()] * 6 + [pl.BlockSpec(memory_space=pltpu.SMEM)],
        out_specs=[vmem()] * 9,
        scratch_shapes=scratch_masks(rows, heads, feats) + [
            pltpu.VMEM((pairs, 128 + TAIL, feats), bf16),
            pltpu.SemaphoreType.DMA((pairs,)),
            pltpu.SemaphoreType.DMA((pairs,)),
        ],
        compiler_params=pltpu.CompilerParams(collective_id=0, has_side_effects=True, vmem_limit_bytes=60 << 20),
        name="attention_forward",
    )(x, wq, wk, wv, biases, ints, lengths)


def attention_backward_wide(saved, gatt, ints, lengths):
    pairs, rows, _ = gatt.shape
    heads, size, feats = ints.shape
    scale = size ** (-0.25) * unit_spread
    shape = jax.ShapeDtypeStruct
    return pl.pallas_call(
        partial(backward_kernel_wide, scale),
        out_shape=[shape((pairs, rows, 128), bf16)] * 3,
        in_specs=[vmem()] * 11 + [pl.BlockSpec(memory_space=pltpu.SMEM)],
        out_specs=[vmem()] * 3,
        scratch_shapes=[pltpu.VMEM((pairs, 128 + TAIL, feats), bf16)] + scratch_masks(rows, heads, feats) + [
            pltpu.VMEM((pairs, 128 + TAIL, feats), bf16),
            pltpu.SemaphoreType.DMA((pairs,)),
            pltpu.SemaphoreType.DMA((pairs,)),
        ],
        compiler_params=pltpu.CompilerParams(collective_id=1, has_side_effects=True, vmem_limit_bytes=60 << 20),
        name="attention_backward",
    )(*saved, gatt, ints, lengths)


def gathered(piece):
    return lax.all_gather(piece, "fsdp", axis=0, tiled=True)


def per_device_wide(
    tokens, doc_lengths, feature_ints, w_query, b_query, w_key, b_key, w_value, b_value, w_out, b_out,
    norm1_gain, norm1_bias, w_in, b_in, w_down, b_down, norm2_gain, norm2_bias, cotangent,
):
    row_block = tokens[0]
    width = row_block.shape[1]
    fsdp = lax.axis_size("fsdp")
    me = lax.axis_index("fsdp")
    attn_stack = gathered(jnp.stack([w_query, w_key, w_value, w_out], axis=1))
    query_weight, key_weight, value_weight, out_weight = (attn_stack[:, i] for i in range(4))
    small = jnp.concatenate(
        [b_query, b_key, b_value, b_out, norm1_gain, norm1_bias, b_down, norm2_gain, norm2_bias, b_in]
    )
    small = lax.all_gather(small[None], "fsdp", axis=0, tiled=True)
    part = width // fsdp
    vectors = [small[:, part * i : part * (i + 1)].reshape(-1) for i in range(9)] + [small[:, 9 * part :].reshape(-1)]
    query_bias, key_bias, value_bias, out_bias, gain_one, offset_one, down_bias, gain_two, offset_two, in_bias = vectors
    saved = attention_forward_wide(
        row_block, query_weight, key_weight, value_weight, jnp.stack([query_bias, key_bias, value_bias]),
        feature_ints, doc_lengths,
    )
    att_rows = from_pairs(saved[5])
    residual_one = row_block.astype(f32) + affine(att_rows, out_weight, out_bias)
    hidden_wide, normed_one, inverse_one = layer_norm(residual_one, gain_one, offset_one)
    hidden_low = hidden_wide.astype(bf16)
    in_weight = gathered(w_in)
    down_weight = gathered(w_down)
    pre_act = affine(hidden_low, in_weight, in_bias)
    gelu_low = gelu_value(pre_act).astype(bf16)
    residual_two = hidden_low.astype(f32) + affine(gelu_low, down_weight, down_bias)
    layer_wide, normed_two, inverse_two = layer_norm(residual_two, gain_two, offset_two)
    grad_out = cotangent[0].astype(f32)
    grad_resid_two, grad_gain_two, grad_offset_two = norm_back(grad_out, normed_two, inverse_two, gain_two)
    grad_down_low = grad_resid_two.astype(bf16)
    grad_down_weight = mul_ta(gelu_low, grad_down_low)
    grad_down_bias = column_total(grad_down_low)
    grad_pre_low = (mul_tb(grad_down_low, down_weight) * gelu_slope(pre_act)).astype(bf16)
    grad_in_weight = mul_ta(hidden_low, grad_pre_low)
    grad_in_bias = column_total(grad_pre_low)
    grad_hidden = mul_tb(grad_pre_low, in_weight) + grad_resid_two
    grad_resid_one, grad_gain_one, grad_offset_one = norm_back(grad_hidden, normed_one, inverse_one, gain_one)
    grad_proj_low = grad_resid_one.astype(bf16)
    grad_out_weight = mul_ta(att_rows, grad_proj_low)
    grad_out_bias = column_total(grad_proj_low)
    grad_att_rows = mul_tb(grad_proj_low, out_weight).astype(bf16)
    grads = attention_backward_wide(saved, to_pairs(grad_att_rows), feature_ints, doc_lengths)
    grad_query_rows, grad_key_rows, grad_value_rows = (from_pairs(g) for g in grads)
    grad_query_weight = mul_ta(row_block, grad_query_rows)
    grad_key_weight = mul_ta(row_block, grad_key_rows)
    grad_value_weight = mul_ta(row_block, grad_value_rows)
    grad_input = (
        mul_tb(grad_query_rows, query_weight)
        + mul_tb(grad_key_rows, key_weight)
        + mul_tb(grad_value_rows, value_weight)
        + grad_resid_one
    )

    def owned(grad):
        shard = lax.psum_scatter(grad.astype(bf16), "fsdp", scatter_dimension=0, tiled=True)
        return lax.psum(shard, "seq").astype(f32)

    sums = jnp.stack(
        [
            column_total(grad_query_rows), column_total(grad_key_rows), column_total(grad_value_rows), grad_out_bias,
            grad_gain_one, grad_offset_one, grad_down_bias, grad_gain_two, grad_offset_two,
            *grad_in_bias.reshape(-1, width),
        ]
    )
    sums = lax.psum(sums, ("fsdp", "seq"))
    mine = [lax.dynamic_slice(sums[i], (me * part,), (part,)) for i in range(9)]
    wide = in_bias.shape[0] // fsdp
    mine_in = lax.dynamic_slice(sums[9:].reshape(-1), (me * wide,), (wide,))
    return (
        layer_wide.astype(bf16)[None],
        grad_input[None],
        owned(grad_query_weight), mine[0],
        owned(grad_key_weight), mine[1],
        owned(grad_value_weight), mine[2],
        owned(grad_out_weight), mine[3],
        mine[4], mine[5],
        owned(grad_in_weight), mine_in,
        owned(grad_down_weight), mine[6],
        mine[7], mine[8],
    )


def solution(mesh):
    rows, matrix, vector = P("fsdp", "seq", None), P("fsdp", None), P("fsdp")
    weights = (matrix, vector) * 4 + (vector, vector) + (matrix, vector) * 2 + (vector, vector)
    near = mesh.shape["fsdp"] == 4 * DEPTH and mesh.shape["seq"] == 2
    return jax.shard_map(
        per_device if near else per_device_wide,
        mesh=mesh,
        in_specs=(rows, matrix, P(), *weights, rows),
        out_specs=(rows, rows, *weights),
        check_vma=False,
    )
```

```python
from functools import partial

import jax
import jax.numpy as jnp
from jax import lax
from jax.experimental import pallas as pl
from jax.experimental.pallas import tpu as pltpu
from jax.sharding import PartitionSpec as P

unit_spread = 0.013531646934131853
inv_root_two = 0.7071067811865476
inv_root_tau = 0.3989422804014327
far_below = -1e30
log2_e = 1.4426950408889634
MESH = pl.DeviceIdType.MESH
f32 = jnp.float32
bf16 = jnp.bfloat16
TAIL = 16
DEPTH = 4
AHEAD = 1


def layer_norm(residual, norm_gain, norm_bias):
    centred = residual - jnp.mean(residual, axis=1, keepdims=True)
    inverse = lax.rsqrt(jnp.mean(centred * centred, axis=1, keepdims=True) + 1e-06)
    normed = centred * inverse
    return (normed * norm_gain.astype(f32) + norm_bias.astype(f32), normed, inverse)


def norm_back(grad_out, normed, inverse, norm_gain):
    scaled = grad_out * norm_gain.astype(f32)
    centre_part = jnp.mean(scaled, axis=1, keepdims=True)
    slope_part = jnp.mean(scaled * normed, axis=1, keepdims=True)
    grad_resid = inverse * (scaled - centre_part - normed * slope_part)
    return (grad_resid, jnp.sum(grad_out * normed, axis=0), jnp.sum(grad_out, axis=0))


def gelu_value(pre_act):
    return 0.5 * pre_act * (1.0 + lax.erf(pre_act * inv_root_two))


def gelu_slope(pre_act):
    return (
        0.5 * (1.0 + lax.erf(pre_act * inv_root_two))
        + pre_act * jnp.exp(-0.5 * pre_act * pre_act) * inv_root_tau
    )


def mul(a, b):
    return lax.dot_general(a, b, (((1,), (0,)), ((), ())), preferred_element_type=f32)


def mul_tb(a, b):
    return lax.dot_general(a, b, (((1,), (1,)), ((), ())), preferred_element_type=f32)


def mul_ta(a, b):
    return lax.dot_general(a, b, (((0,), (0,)), ((), ())), preferred_element_type=f32)


def affine(row_block, weight, bias_row):
    return mul(row_block, weight) + bias_row.astype(f32)


def column_total(values):
    return jnp.sum(values, axis=0, dtype=f32)


def lane_ids(shape):
    return lax.broadcasted_iota(jnp.int32, shape, len(shape) - 1)


def doc_setup(lengths, place, mask_ref, onehot_ref, strad_ref, stradrow_ref):
    rows = mask_ref.shape[0]
    docs = lengths.shape[1]
    total = jnp.int32(0)
    ends = []
    for d in range(docs):
        total = total + lengths[0, d]
        ends.append(total)
    pos = lax.broadcasted_iota(jnp.int32, (rows, 128), 0) + place * rows
    pos_row = lax.broadcasted_iota(jnp.int32, (8, rows), 1) + place * rows
    did = jnp.zeros((rows, 128), jnp.int32)
    did_row = jnp.zeros((8, rows), jnp.int32)
    edge = jnp.int32(0)
    for end in ends[:-1]:
        did = did + (pos >= end).astype(jnp.int32)
        did_row = did_row + (pos_row >= end).astype(jnp.int32)
        edge = edge + (end <= rows).astype(jnp.int32)
    for j in range(rows // 128):
        cols = did_row[0:1, j * 128 : (j + 1) * 128]
        mask_ref[:, j * 128 : (j + 1) * 128] = (did == cols).astype(f32).astype(bf16)
    onehot_ref[...] = (did == lane_ids((rows, 128))).astype(f32)
    strad_ref[...] = (did == edge).astype(f32)
    one_row = (did_row[0:1] == edge).astype(f32)
    stradrow_ref[...] = jnp.broadcast_to(one_row, stradrow_ref.shape).astype(bf16)


def features_setup(ints_ref, omx_ref):
    heads, size, feats = ints_ref.shape

    @pl.loop(0, heads)
    def _(h):
        mat = ints_ref[h].astype(f32).astype(bf16)
        zero = jnp.zeros((size, feats), bf16)
        odd = lax.rem(h, 2) == 1
        omx_ref[h, 0:size] = jnp.where(odd, zero, mat)
        omx_ref[h, size : 2 * size] = jnp.where(odd, mat, zero)
        omx_ref[h, 2 * size :] = jnp.ones((2 * size, feats), bf16)


def three_terms(value):
    first = value.astype(bf16).astype(f32)
    second = (value - first).astype(bf16).astype(f32)
    return first, second, value - first - second


def forward_states(p, scale, q_ref, k_ref, v_ref, omx_ref, onehot_ref, strad_ref, stradrow_ref, pq_ref, pk_ref, peak_ref, out_ref):
    rows = q_ref.shape[1]
    lanes = lane_ids((1, 128))
    qp, kp, vp = q_ref[p], k_ref[p], v_ref[p]
    kf = kp.astype(f32)
    ksq = kf * kf
    vt = jnp.concatenate([vp.T * stradrow_ref[0:1], stradrow_ref[...]], axis=0)
    tail = jnp.zeros((TAIL, pq_ref.shape[-1]), f32)
    tail_row = lax.broadcasted_iota(jnp.int32, tail.shape, 0)
    for j in range(2):
        om = omx_ref[2 * p + j, 0:128]
        raw_q = mul(qp, om)
        raw_q = raw_q - jnp.max(raw_q, axis=1, keepdims=True)
        pq_ref[p, j] = jnp.exp2(raw_q * (scale * log2_e)).astype(bf16)
        here = (lanes >= 64) if j else (lanes < 64)
        half = jnp.sum(jnp.where(here, ksq, 0.0), axis=1, keepdims=True) * (0.0625 / scale)
        raw_k = mul(kp, om) - half
        row_peak = jnp.max(raw_k, axis=1, keepdims=True)
        doc_peak = jnp.max(jnp.where(onehot_ref[...] > 0.5, row_peak, far_below), axis=0, keepdims=True)
        back = jnp.max(jnp.where(onehot_ref[...] > 0.5, doc_peak, far_below), axis=1, keepdims=True)
        edge_peak = jnp.max(jnp.where(strad_ref[...] > 0.5, row_peak, far_below), axis=0, keepdims=True)
        phi_k = jnp.exp2((raw_k - back) * (scale * log2_e)).astype(bf16)
        pk_ref[p, j] = phi_k
        part = mul(vt, phi_k)
        out_ref[p, 64 * j : 64 * j + 64] = part[64 * j : 64 * j + 64].astype(bf16)
        edge_wide = jnp.concatenate([edge_peak, edge_peak], axis=1)
        peak_ref[p, j] = edge_wide
        tail = jnp.where(tail_row == j, part[128 : 128 + TAIL], tail)
        for t, term in enumerate(three_terms(edge_wide)):
            tail = jnp.where(tail_row == 2 + 3 * j + t, term, tail)
    out_ref[p, 128:] = tail.astype(bf16)


def edge_parts(state_ref, p, j):
    tail = state_ref[p, 128:].astype(f32)
    feats = tail.shape[1]
    totals = jnp.broadcast_to(tail[j : j + 1], (128, feats)).astype(bf16)
    peak = tail[2 + 3 * j : 3 + 3 * j] + tail[3 + 3 * j : 4 + 3 * j] + tail[4 + 3 * j : 5 + 3 * j]
    return jnp.concatenate([state_ref[p, 0:128], totals], axis=0), peak


def edge_weights(scale, own, other, strad):
    top = jnp.maximum(own, other)
    own_w = jnp.exp2((own - top) * (scale * log2_e))
    other_w = jnp.exp2((other - top) * (scale * log2_e))
    return 1.0 + strad * (own_w[:, 0:128] - 1.0), strad * other_w[:, 0:128]


def forward_finish(p, scale, v_ref, pq_ref, pk_ref, mask_ref, strad_ref, peak_ref, in_ref, att_ref, den_ref):
    rows = v_ref.shape[1]
    first_half = lane_ids((rows, 128)) < 64
    vx = jnp.concatenate([v_ref[p], jnp.ones((rows, 128), bf16)], axis=1)
    got = []
    for j in range(2):
        phi_q = pq_ref[p, j]
        pair = mul_tb(phi_q, pk_ref[p, j]).astype(bf16) * mask_ref[...]
        near = mul(pair, vx)
        state, other = edge_parts(in_ref, p, j)
        far = mul_tb(phi_q, state)
        wn, wf = edge_weights(scale, peak_ref[p, j], other, strad_ref[...])
        den = near[:, 128:] * wn + far[:, 128:] * wf
        got.append(((near[:, :128] * wn + far[:, :128] * wf) / den, den))
    att_ref[p] = jnp.where(first_half, got[0][0], got[1][0]).astype(bf16)
    den_ref[p] = jnp.where(first_half, got[0][1], got[1][1])


def numer_grads(p, att_ref, den_ref, gatt_ref):
    rows = att_ref.shape[1]
    lanes = lane_ids((rows, 128))
    gn = gatt_ref[p].astype(f32) / den_ref[p]
    prod = gn * att_ref[p].astype(f32)
    d0 = -jnp.sum(jnp.where(lanes < 64, prod, 0.0), axis=1, keepdims=True)
    d1 = -jnp.sum(jnp.where(lanes < 64, 0.0, prod), axis=1, keepdims=True)
    return gn, d0, d1, lanes


def backward_states(p, scale, att_ref, den_ref, gatt_ref, pq_ref, strad_ref, peak_ref, in_ref, out_ref):
    gn, d0, d1, lanes = numer_grads(p, att_ref, den_ref, gatt_ref)
    far = [edge_weights(scale, peak_ref[p, j], edge_parts(in_ref, p, j)[1], strad_ref[...])[1] for j in range(2)]
    left = (gn * jnp.where(lanes < 64, far[0], far[1])).astype(bf16)
    right = (jnp.where(lanes == 0, d0 * far[0], 0.0) + jnp.where(lanes == 1, d1 * far[1], 0.0)).astype(bf16)
    turned = jnp.concatenate([left.T, right.T[0:TAIL]], axis=0)
    tails = []
    for j in range(2):
        part = mul(turned, pq_ref[p, j])
        out_ref[p, 64 * j : 64 * j + 64] = part[64 * j : 64 * j + 64].astype(bf16)
        tails.append(part[128:])
    rowid = lax.broadcasted_iota(jnp.int32, tails[0].shape, 0)
    out_ref[p, 128:] = jnp.where(rowid == 0, tails[0], tails[1]).astype(bf16)


def backward_finish(
    p, scale, q_ref, k_ref, v_ref, omx_ref, pq_ref, pk_ref, mask_ref, strad_ref, peak_ref, in_ref, gin_ref,
    att_ref, den_ref, gatt_ref, gq_ref, gk_ref, gv_ref,
):
    rows = q_ref.shape[1]
    gn, d0, d1, lanes = numer_grads(p, att_ref, den_ref, gatt_ref)
    first_half = lanes < 64
    vp = v_ref[p]
    ones = jnp.ones((rows, 128), bf16)
    vx = jnp.concatenate([vp, ones], axis=1)
    strad = strad_ref[...]
    gq = jnp.zeros((rows, 128), f32)
    gk = jnp.zeros((rows, 128), f32)
    gv = jnp.zeros((rows, 128), f32)
    q_sums, k_sums = [], []
    for j in range(2):
        here = (lanes >= 64) if j else (lanes < 64)
        gd = d1 if j else d0
        state, other = edge_parts(in_ref, p, j)
        wn, wf = edge_weights(scale, peak_ref[p, j], other, strad)
        base_l = jnp.where(here, gn, 0.0)
        base_r = jnp.where(lanes == 0, gd, 0.0)
        near = jnp.concatenate([(base_l * wn).astype(bf16), (base_r * wn).astype(bf16)], axis=1)
        far = jnp.concatenate([(base_l * wf).astype(bf16), (base_r * wf).astype(bf16)], axis=1)
        phi_q, phi_k = pq_ref[p, j], pk_ref[p, j]
        turned = mul_tb(phi_k, phi_q).astype(bf16) * mask_ref[...]
        gv = gv + mul(turned, near[:, 0:128])
        gpair = mul_tb(near, vx).astype(bf16) * mask_ref[...]
        gphi_q = mul(gpair, phi_k) + mul(far, state)
        gturned = mul_tb(vx, near).astype(bf16) * mask_ref[...]
        gstate, _ = edge_parts(gin_ref, p, j)
        vs = jnp.concatenate(
            [(jnp.where(here, vp.astype(f32), 0.0) * strad).astype(bf16), jnp.where(lanes == 0, strad, 0.0).astype(bf16)],
            axis=1,
        )
        gphi_k = mul(gturned, phi_q) + mul(vs, gstate)
        gv = gv + jnp.where(here, mul_tb(phi_k, gstate[0:128]) * strad, 0.0)
        omx = omx_ref[2 * p + j]
        back_q = mul_tb((gphi_q * phi_q.astype(f32)).astype(bf16), omx)
        back_k = mul_tb((gphi_k * phi_k.astype(f32)).astype(bf16), omx)
        gq = gq + back_q[:, 0:128]
        gk = gk + back_k[:, 0:128]
        q_sums.append(back_q[:, 128:])
        k_sums.append(back_k[:, 128:])
    gq = gq * scale - jnp.where(first_half, q_sums[0], q_sums[1]) * q_ref[p].astype(f32) * 0.125
    gk = gk * scale - jnp.where(first_half, k_sums[0], k_sums[1]) * k_ref[p].astype(f32) * 0.125
    gq_ref[p] = gq.astype(bf16)
    gk_ref[p] = gk.astype(bf16)
    gv_ref[p] = gv.astype(bf16)


def peer_barrier(peers):
    barrier = pltpu.get_barrier_semaphore()
    for peer in peers:
        pl.semaphore_signal(barrier, inc=1, device_id=peer, device_id_type=MESH)
    pl.semaphore_wait(barrier, len(peers))


class Place:
    def __init__(self):
        me = lax.axis_index("fsdp")
        self.y = lax.axis_index("seq")
        self.c = lax.rem(me, 2)
        self.x = lax.rem(lax.div(me, 2), 2)
        self.z = lax.div(me, 4)
        self.across = {"seq": 1 - self.y}
        self.twin = {"fsdp": self.z * 4 + self.x * 2 + 1 - self.c}
        self.beside = {"fsdp": self.z * 4 + (1 - self.x) * 2 + self.c}

    def along(self, d):
        return {"fsdp": self.other(d) * 4 + self.x * 2 + self.c}

    def other(self, d):
        return lax.rem(self.z + (d + DEPTH), DEPTH)

    def peers(self):
        return [self.twin, self.beside, self.across] + [self.along(d) for d in range(1, DEPTH)]


def cols_at(start, size):
    return pl.ds(pl.multiple_of(start, 128), size)


def remote(src, dst, ssem, rsem, peer):
    return pltpu.make_async_remote_copy(
        src_ref=src, dst_ref=dst, send_sem=ssem, recv_sem=rsem, device_id=peer, device_id_type=MESH
    )


class Gather:
    def __init__(self, at, own, full, base, width, ssem, rsem, lsem):
        self.at, self.own, self.full = at, own, full
        self.third, self.base, self.width = width // 3, base, width
        self.ssem, self.rsem, self.lsem = ssem, rsem, lsem
        self.sent = []

    def spread(self):
        return cols_at(self.base + self.third * self.at.y, 2 * self.third)

    def extra(self, y):
        return cols_at(self.base + 2 * self.third * y, self.third)

    def whole(self):
        return pl.ds(self.base, self.width)

    def go(self, n, ends):
        src, dst, peer = ends()
        remote(src, dst, self.ssem.at[n], self.rsem.at[n], peer).start()
        self.sent.append((n, ends))

    def came(self, n, ref):
        remote(ref, ref, self.ssem.at[n], self.rsem.at[n], self.at.twin).wait_recv()

    def local(self):
        at = self.at
        return pltpu.make_async_copy(
            self.own.at[:, self.whole()], self.full.at[at.z, at.x, at.c, :, self.whole()], self.lsem
        )

    def begin(self):
        at = self.at
        self.local().start()
        for d in range(1, DEPTH):
            self.go(d - 1, lambda d=d: (*self.first(), at.along(d)))

    def first(self):
        at = self.at
        return self.own.at[:, self.spread()], self.full.at[at.z, at.x, at.c, :, self.spread()]

    def piece(self, d, x, cols):
        return self.full.at[self.at.other(-d), x, self.at.c, :, cols]

    def stage_x(self):
        at = self.at
        self.go(DEPTH - 1, lambda: (*self.first(), at.beside))
        for d in range(1, DEPTH):
            self.came(d - 1, self.piece(d, at.x, self.spread()))
            self.go(DEPTH - 1 + d, lambda d=d: (*[self.piece(d, at.x, self.spread())] * 2, at.beside))
            self.go(2 * DEPTH - 2 + d, lambda d=d: (*[self.piece(d, at.x, self.extra(at.y))] * 2, at.across))

    def stage_y(self):
        at = self.at
        for d in range(DEPTH):
            self.came(DEPTH - 1 + d, self.piece(d, 1 - at.x, self.spread()))
            self.go(3 * DEPTH - 2 + d, lambda d=d: (*[self.piece(d, 1 - at.x, self.extra(at.y))] * 2, at.across))

    def stage_c(self):
        at = self.at
        for d in range(1, DEPTH):
            self.came(2 * DEPTH - 2 + d, self.piece(d, at.x, self.extra(1 - at.y)))
        for d in range(DEPTH):
            self.came(3 * DEPTH - 2 + d, self.piece(d, 1 - at.x, self.extra(1 - at.y)))
        self.local().wait()
        self.go(4 * DEPTH - 2, lambda: (*[self.full.at[:, :, at.c, :, self.whole()]] * 2, at.twin))

    def ready(self):
        self.came(4 * DEPTH - 2, self.full.at[:, :, 1 - self.at.c, :, self.whole()])

    def drain(self):
        for n, ends in self.sent:
            src, dst, peer = ends()
            remote(src, dst, self.ssem.at[n], self.rsem.at[n], peer).wait_send()


GATHER_COPIES = 4 * DEPTH - 1


class SmallSum:
    def __init__(self, at, total, land, ssem, rsem, over_seq):
        self.at, self.total, self.land, self.ssem, self.rsem, self.over_seq = at, total, land, ssem, rsem, over_seq
        self.sent = []

    def go(self, src, n, peer):
        copy = remote(self.total.at[src], self.land.at[n], self.ssem.at[n], self.rsem.at[n], peer)
        copy.start()
        self.sent.append(copy)

    def came(self, n):
        remote(self.land.at[n], self.land.at[n], self.ssem.at[n], self.rsem.at[n], self.at.twin).wait_recv()

    def begin(self):
        for d in range(1, DEPTH):
            self.go(0, d - 1, self.at.along(d))

    def step(self, k):
        if k == 0:
            got = self.total[0]
            for d in range(1, DEPTH):
                self.came(d - 1)
            order = [self.at.z] + [self.at.other(-d) for d in range(1, DEPTH)]
            parts = [got] + [self.land[d - 1] for d in range(1, DEPTH)]
            value = jnp.zeros_like(got)
            for z in range(DEPTH):
                one = jnp.zeros_like(got)
                for place, part in zip(order, parts):
                    one = jnp.where(place == z, part, one)
                value = value + one
        else:
            self.came(DEPTH - 2 + k)
            value = self.total[k] + self.land[DEPTH - 2 + k]
        self.total[k + 1] = value
        hops = [self.at.beside, self.at.twin] + ([self.at.across] if self.over_seq else [])
        if k < len(hops):
            self.go(k + 1, DEPTH - 1 + k, hops[k])

    def steps(self):
        return 4 if self.over_seq else 3

    def result(self):
        return self.total[self.steps()]

    def drain(self):
        for copy in self.sent:
            copy.wait_send()


def spread_vectors(at, pieces, wide):
    width = 768
    part = pieces[0].shape[-1]
    rows = [p[...].astype(f32).reshape(1, part) for p in pieces]
    rows = jnp.concatenate(rows + [jnp.zeros((16 - len(rows), part), f32)], axis=0)
    rows = jnp.concatenate([rows, jnp.zeros((16, width - part), f32)], axis=1)
    rows = pltpu.roll(rows, (at.z * 4 + at.x * 2 + at.c) * part, 1)
    span = wide.shape[-1]
    row = jnp.concatenate([wide[...].astype(f32).reshape(1, span), jnp.zeros((1, width - span), f32)], axis=1)
    row = pltpu.roll(jnp.broadcast_to(row, (16, width)), (at.x * 2 + at.c) * span, 1)
    here = lax.broadcasted_iota(jnp.int32, (16, width), 0)
    return jnp.where(here == len(pieces) + at.z, row, rows)


HOLD = (
    "omx", "xt", "mask", "strad", "q", "k", "v", "pq", "pk", "att", "attt", "den", "sq", "hidt", "norm", "fin", "gelt", "slope", "fdn",
)
LATE = ("xt", "q", "k", "v", "pq", "pk", "att", "attt", "den", "omx", "mask", "strad")


def forward_kernel(
    scale, x_ref, wq_ref, wk_ref, wv_ref, wo_ref, win_ref, wdn_ref, bq_ref, bk_ref, bv_ref, bo_ref, g1_ref, o1_ref, bd_ref,
    g2_ref, o2_ref, bin_ref, ints_ref, cot_ref, len_ref, layer_ref, peak_ref, state_ref, inv_ref, res_ref, vec_ref, sums_ref, *rest,
):
    outs, rest = rest[: len(HOLD)], rest[len(HOLD) :]
    hold, rest = rest[: len(HOLD)], rest[len(HOLD) :]
    (
        omx_ref, xt_ref, mask_ref, strad_ref, q_ref, k_ref, v_ref, pq_ref, pk_ref, att_ref, attt_ref, den_ref, sq_ref, hidt_ref,
        norm_ref, fin_ref, gelt_ref, slope_ref, fdn_ref,
    ) = hold
    hid_ref, gel_ref, onehot_ref, stradrow_ref, send_ref, total_ref, land_ref = rest[:7]
    ssem, rsem, gs_sem, gr_sem, gl_sem, vs_sem, vr_sem, out_sem = rest[7:]
    at = Place()
    pairs = q_ref.shape[0]
    rows, width = x_ref.shape

    def stash(*names):
        return [pltpu.make_async_copy(hold[n], outs[n], out_sem.at[n]) for n in map(HOLD.index, names)]

    def give(*names):
        for copy in stash(*names):
            copy.start()

    blocks = []
    specs = [(w, sq_ref.at[n], 0, 768) for n, w in enumerate((wq_ref, wk_ref, wv_ref, wo_ref))]
    specs += [(win_ref, fin_ref, 768 * h, 768) for h in range(4)]
    specs += [
        (wdn_ref.at[pl.ds(96 * r, 96)], fdn_ref.at[:, :, :, pl.ds(96 * r, 96)], 384 * h, 384) for h in range(2) for r in range(2)
    ]
    for n, (own, full, base, span) in enumerate(specs):
        blocks.append(Gather(at, own, full, base, span, gs_sem.at[n], gr_sem.at[n], gl_sem.at[n]))
    peer_barrier(at.peers())
    vec = SmallSum(at, total_ref, land_ref, vs_sem, vr_sem, False)
    total_ref[0] = spread_vectors(
        at, (bq_ref, bk_ref, bv_ref, bo_ref, g1_ref, o1_ref, bd_ref, g2_ref, o2_ref), bin_ref
    ).astype(bf16)
    blocks[0].begin()
    vec.begin()
    for b in blocks[1:AHEAD]:
        b.begin()
    doc_setup(len_ref, at.y, mask_ref, onehot_ref, strad_ref, stradrow_ref)
    features_setup(ints_ref, omx_ref)
    for j in range(pairs):
        xt_ref[128 * j : 128 * j + 128] = x_ref[:, 128 * j : 128 * j + 128].T
    give("omx", "xt", "mask", "strad")
    sums_ref[...] = jnp.zeros_like(sums_ref)

    def vector(n, cols=slice(None)):
        return vec_ref[n : n + 1, cols].astype(f32)

    def project(n, o_ref):
        for j in range(pairs // 2):
            cols = slice(256 * j, 256 * j + 256)
            got = mul(x_ref[...], sq_ref[n, :, :, :, :, cols].reshape(768, 256))
            got = (got + vector(n, cols)).astype(bf16)
            o_ref[2 * j] = got[:, 0:128]
            o_ref[2 * j + 1] = got[:, 128:256]

    def tick(t):
        if t + AHEAD < len(blocks):
            blocks[t + AHEAD].begin()
        for k, name in enumerate(("stage_x", "stage_y", "stage_c", "ready")):
            if 0 <= t - k < len(blocks):
                getattr(blocks[t - k], name)()

    for t in range(3):
        tick(t)
        vec.step(t)
    vec_ref[...] = vec.result()
    for n, ref in enumerate((q_ref, k_ref, v_ref)):
        tick(3 + n)
        project(n, ref)
        give("qkv"[n])

    def copy(p):
        return remote(send_ref.at[p], state_ref.at[p], ssem.at[p], rsem.at[p], at.across)

    def ticks_at(p, plan):
        for n, t in plan.items():
            @pl.when(p == n)
            def _(t=t):
                tick(t)

    @pl.loop(0, pairs)
    def _(p):
        forward_states(p, scale, q_ref, k_ref, v_ref, omx_ref, onehot_ref, strad_ref, stradrow_ref, pq_ref, pk_ref, peak_ref, send_ref)
        copy(p).start()
        ticks_at(p, {0: 6, 2: 7, 4: 8})

    give("pq", "pk", "sq")

    @pl.loop(0, pairs)
    def _(p):
        copy(p).wait()
        forward_finish(p, scale, v_ref, pq_ref, pk_ref, mask_ref, strad_ref, peak_ref, state_ref, att_ref, den_ref)
        attt_ref[p] = att_ref[p].T
        ticks_at(p, {0: 9, 3: 10})

    give("att", "attt", "den", "fin")


    whole = jnp.concatenate([att_ref[p] for p in range(pairs)], axis=1)
    for j in range(pairs // 2):
        cols = slice(256 * j, 256 * j + 256)
        got = mul(whole, sq_ref[3, :, :, :, :, cols].reshape(768, 256))
        res_ref[:, cols] = got + vector(3, cols) + x_ref[:, cols].astype(f32)

    def centred(value):
        value = value - jnp.mean(value, axis=1, keepdims=True)
        inverse = lax.rsqrt(jnp.mean(value * value, axis=1, keepdims=True) + 1e-06)
        return value * inverse, inverse

    def here(r):
        return pl.ds(pl.multiple_of(128 * r, 128), 128)

    @pl.loop(0, rows // 128)
    def _(r):
        normed, inverse = centred(res_ref[here(r)])
        inv_ref[here(r)] = inverse
        norm_ref[here(r)] = normed.astype(bf16)
        hid_ref[here(r)] = (normed * vector(4) + vector(5)).astype(bf16)

    for j in range(pairs):
        hidt_ref[128 * j : 128 * j + 128] = hid_ref[:, 128 * j : 128 * j + 128].T
    give("hidt", "norm")


    @pl.loop(0, 4)
    def _(b):
        ticks_at(b, {0: 11, 2: 12})
        for j in range(3):
            cols = cols_at(768 * b + 256 * j, 256)
            pre = mul(hid_ref[...], fin_ref[:, :, :, :, cols].reshape(768, 256))
            bias = jnp.zeros((1, 256), f32)
            for n in range(4):
                bias = jnp.where(b == n, vector(9 + n, slice(256 * j, 256 * j + 256)), bias)
            pre = pre + bias
            share = 0.5 * (1.0 + lax.erf(pre * inv_root_two))
            gel = (pre * share).astype(bf16)
            gel_ref[:, cols] = gel
            gelt_ref[cols] = gel.T
            slope_ref[:, cols] = (share + pre * (jnp.exp(-0.5 * pre * pre) * inv_root_tau)).astype(bf16)

    give("gelt", "slope")

    def down(h):
        cols = slice(384 * h, 384 * h + 384)
        res_ref[:, cols] = hid_ref[:, cols].astype(f32) + vector(6, cols)

        @pl.loop(0, DEPTH)
        def _(z):
            got = mul(gel_ref[:, cols_at(768 * z, 768)], fdn_ref[z, :, :, :, cols].reshape(768, 384))
            res_ref[:, cols] = res_ref[:, cols] + got

    down(0)
    tick(13)
    tick(14)
    give("fdn")
    down(1)


    @pl.loop(0, rows // 128)
    def _(r):
        normed, inverse = centred(res_ref[here(r)])
        layer_ref[here(r)] = (normed * vector(7) + vector(8)).astype(bf16)
        grad = cot_ref[here(r)].astype(f32)
        scaled = grad * vector(7)
        centre = jnp.mean(scaled, axis=1, keepdims=True)
        lean = jnp.mean(scaled * normed, axis=1, keepdims=True)
        resid = inverse * (scaled - centre - normed * lean)
        res_ref[here(r)] = resid
        sums_ref[6:7] = sums_ref[6:7] + jnp.sum(resid.astype(bf16).astype(f32), axis=0, keepdims=True)
        sums_ref[7:8] = sums_ref[7:8] + jnp.sum(grad * normed, axis=0, keepdims=True)
        sums_ref[8:9] = sums_ref[8:9] + jnp.sum(grad, axis=0, keepdims=True)

    for b in blocks:
        b.drain()
    vec.drain()
    for one in stash(*HOLD):
        one.wait()


class Scatter:
    def __init__(self, at, order, source, twin_in, lands, done, done_in, put, ssem, rsem):
        self.at, self.order, self.source, self.acc = at, order, source, source(at.c)
        self.twin_in, self.lands = twin_in, lands
        self.done, self.done_in, self.put = done, done_in, put
        self.ssem, self.rsem = ssem, rsem
        self.half = twin_in.shape[-1] // 2
        self.sent = []

    def go(self, n, ends):
        src, dst, peer = ends()
        remote(src, dst, self.ssem.at[n], self.rsem.at[n], peer).start()
        self.sent.append((n, ends))

    def came(self, n, ref):
        remote(ref, ref, self.ssem.at[n], self.rsem.at[n], self.at.twin).wait_recv()

    def side(self, y):
        return cols_at(self.half * y, self.half)

    def spot(self, fixed, **other):
        at = self.at
        z = other.get("z", at.z if "z" in fixed else slice(None))
        x = other.get("x", at.x if "x" in fixed else slice(None))
        cols = self.side(other.get("y", at.y)) if "y" in fixed or "y" in other else slice(None)
        return z, x, slice(None), cols

    def first(self, i):
        return 1 + sum(DEPTH - 1 if kind == "z" else 1 for kind in self.order[:i])

    def send(self, i):
        at, kind, fixed = self.at, self.order[i], self.order[:i]
        if kind == "z":
            for d in range(1, DEPTH):
                self.go(
                    self.first(i) + d - 1,
                    lambda d=d: (self.acc.at[self.spot(fixed, z=at.other(d))], self.lands[i].at[d - 1], at.along(d)),
                )
        elif kind == "x":
            self.go(self.first(i), lambda: (self.acc.at[self.spot(fixed, x=1 - at.x)], self.lands[i], at.beside))
        else:
            self.go(self.first(i), lambda: (self.acc.at[self.spot(fixed, y=1 - at.y)], self.lands[i], at.across))

    def add(self, parts, fixed, store):
        def at_z(z):
            for x in [None] if "x" in fixed else range(2):
                spot = list(self.spot(fixed))
                inner = ()
                if z is not None:
                    spot[0] = z
                    inner += (z,)
                if x is not None:
                    spot[1] = x
                    inner += (x,)
                value = self.acc[tuple(spot)].astype(f32)
                for part in parts:
                    value = value + part[inner + (slice(None), slice(None))].astype(f32)
                store(tuple(spot), value)

        if "z" in fixed:
            at_z(None)
        else:
            pl.loop(0, DEPTH)(at_z)

    def keep(self, spot, value):
        self.acc[spot] = value.astype(bf16)

    def finish(self, spot, value):
        low = value.astype(bf16)
        self.done[...] = low
        self.put(self.at.y, low.astype(f32))

    def arrived(self, i):
        if self.order[i] != "z":
            self.came(self.first(i), self.lands[i])
            return [self.lands[i]]
        for d in range(1, DEPTH):
            self.came(self.first(i) + d - 1, self.lands[i].at[d - 1])
        return [self.lands[i].at[d - 1] for d in range(1, DEPTH)]

    def begin(self):
        self.go(0, lambda: (self.source(1 - self.at.c), self.twin_in, self.at.twin))

    def stage_1(self):
        self.came(0, self.twin_in)
        self.add([self.twin_in], "", self.keep)
        self.send(0)

    def stage_2(self):
        self.add(self.arrived(0), self.order[:1], self.keep)
        self.send(1)

    def stage_3(self):
        self.add(self.arrived(1), self.order[:2], self.keep)
        self.send(2)

    def stage_4(self):
        self.add(self.arrived(2), self.order, self.finish)
        self.go(2 + DEPTH, lambda: (self.done, self.done_in, self.at.across))

    def stage_5(self):
        self.came(2 + DEPTH, self.done_in)
        self.put(1 - self.at.y, self.done_in[...].astype(f32))

    def drain(self):
        for n, ends in self.sent:
            src, dst, peer = ends()
            remote(src, dst, self.ssem.at[n], self.rsem.at[n], peer).wait_send()


def landing(order, part, width):
    shapes = []
    for i, kind in enumerate(order):
        kept = order[: i + 1]
        shape = [] if "z" in kept else [DEPTH]
        shape += [] if "x" in kept else [2]
        shape += [part, width // 2 if "y" in kept else width]
        shapes.append(pltpu.VMEM(tuple([DEPTH - 1] + shape if kind == "z" else shape), bf16))
    return shapes


SCATTER_COPIES = DEPTH + 3
FEED_STEPS = (3, 7)
HEAD_STEPS = (0, 1, 2, 3, 4, 5)
PACE = ((0, 2, 4, 6, 8),) * 6 + ((0, 2, 3, 4, 5),) * 3 + ((0, 1, 2, 3, 4),) * 3
ORDERS = ("xyz", "yxz") * 6


def backward_kernel(
    scale, peak_ref, state_ref, hidt_ref, norm_ref, inv_ref, res_ref, gain_ref, vecin_ref, gel_ref, slope_ref, win_ref, wdn_ref,
    sq_ref, *rest,
):
    late_refs, rest = rest[: len(LATE)], rest[len(LATE) :]
    gx_ref, oq_ref, ok_ref, ov_ref, oo_ref, oin_ref, odn_ref, vec_ref = rest[:8]
    kept_refs, rest = rest[8 : 8 + len(LATE)], rest[8 + len(LATE) :]
    xt_ref, q_ref, k_ref, v_ref, pq_ref, pk_ref, att_ref, attt_ref, den_ref, omx_ref, mask_ref, strad_ref = kept_refs
    gstate_ref, send_ref, gq_ref, gk_ref, gv_ref, gatt_ref, low_ref, wide_ref, gelbuf_ref, slopebuf_ref = rest[:10]
    gdn_ref, gin_ref, go_ref, gw_ref, total_ref, land_ref, twin_ref, done_ref, donein_ref = rest[10:19]
    ssem, rsem, load_sem, late_sem, keep_sem, ws_sem, wr_sem, vs_sem, vr_sem = rest[19:28]
    land_refs = rest[28:]
    at = Place()
    pairs = q_ref.shape[0]
    rows, width = res_ref.shape
    span = width // 2
    chunks = win_ref.shape[1] // span
    sources = [lambda c, b=b: gdn_ref.at[:, :, c, pl.ds(48 * b, 48)] for b in range(4)]
    sources += [lambda c, b=b: gin_ref.at[:, :, c, :, pl.ds(768 * b, 768)] for b in range(4)]
    sources += [lambda c: go_ref.at[:, :, c]]
    sources += [lambda c, n=n: gw_ref.at[n, :, :, c] for n in (2, 1, 0)]

    def putter(ref, row, col):
        def put(y, value):
            ref[pl.ds(row, 48), cols_at(col + 384 * y, 384)] = value

        return put

    puts = [putter(odn_ref, 48 * b, 0) for b in range(4)] + [putter(oin_ref, 0, 768 * b) for b in range(4)]
    puts += [putter(r, 0, 0) for r in (oo_ref, ov_ref, ok_ref, oq_ref)]
    units = []
    for n, (source, put) in enumerate(zip(sources, puts)):
        lands = land_refs[3 * n : 3 * n + 3]
        units.append(
            Scatter(
                at, ORDERS[n], source, twin_ref.at[n], lands, done_ref.at[n], donein_ref.at[n], put, ws_sem.at[n], wr_sem.at[n]
            )
        )
    early = len(units) - 3

    def step(s):
        for k in range(5):
            for u, unit in enumerate(units):
                if u + PACE[u][k] == s:
                    getattr(unit, "stage_" + str(k + 1))()


    def load(src, dst, sem):
        return pltpu.make_async_copy(src, dst, sem)

    def slot(m):
        return lax.rem(m, 2)

    def load_gelu(m):
        return load(gel_ref.at[pl.ds(pl.multiple_of(span * m, 128), span)], gelbuf_ref.at[slot(m)], load_sem.at[0, slot(m)])

    def load_chunk(m):
        start = pl.multiple_of(span * slot(m), 128)
        return [
            load(slope_ref.at[:, cols_at(span * m, span)], slopebuf_ref.at[slot(m)], load_sem.at[1, slot(m)]),
            load(wdn_ref.at[pl.ds(pl.multiple_of(span * m, 128), span)], wide_ref.at[0, pl.ds(start, span)], load_sem.at[2, slot(m)]),
            load(win_ref.at[:, cols_at(span * m, span)], wide_ref.at[1, :, pl.ds(start, span)], load_sem.at[3, slot(m)]),
        ]

    def load_square(n, to):
        return load(sq_ref.at[n], wide_ref.at[to], late_sem.at[to])

    peer_barrier(at.peers())
    load_gelu(jnp.int32(0)).start()
    for one in load_chunk(jnp.int32(0)):
        one.start()
    load_square(3, 2).start()
    kept = [load(src, dst, keep_sem.at[n]) for n, (src, dst) in enumerate(zip(late_refs, kept_refs))]
    for one in kept:
        one.start()
    total_ref[0] = vecin_ref[...]

    @pl.loop(0, rows // 128)
    def _(r):
        here = pl.ds(pl.multiple_of(128 * r, 128), 128)
        low_ref[here] = res_ref[here].astype(bf16)
        gx_ref[here] = res_ref[here]


    @pl.loop(0, chunks)
    def _(m):
        load_gelu(m).wait()

        @pl.when(m < chunks - 1)
        def _():
            load_gelu(m + 1).start()

        turned = gelbuf_ref[slot(m)]
        for n in range(3):
            cols = slice(256 * n, 256 * n + 256)
            got = mul(turned, low_ref[:, cols]).astype(bf16)
            gdn_ref[lax.div(m, 2), slot(m), :, :, cols] = got.reshape(2, span // 2, 256)

    units[0].begin()
    units[1].begin()
    @pl.loop(0, chunks)
    def _(m):
        for one in load_chunk(m):
            one.wait()

        @pl.when(m < chunks - 1)
        def _():
            for one in load_chunk(m + 1):
                one.start()

        start = pl.multiple_of(span * slot(m), 128)
        gpre = mul_tb(low_ref[...], wide_ref[0, pl.ds(start, span)]) * slopebuf_ref[slot(m)].astype(f32)
        gpre = gpre.astype(bf16)
        total_ref[0, pl.ds(9 + lax.div(m, 2), 1), cols_at(start, span)] = jnp.sum(gpre.astype(f32), axis=0, keepdims=True)
        got = mul(hidt_ref[...], gpre).astype(bf16)
        gin_ref[:, :, :, :, cols_at(span * m, span)] = got.reshape(DEPTH, 2, 2, 48, span)
        for n in range(3):
            cols = slice(256 * n, 256 * n + 256)
            gx_ref[:, cols] = gx_ref[:, cols] + mul_tb(gpre, wide_ref[1, cols, pl.ds(start, span)])
        for n in range(8):
            @pl.when(m == n)
            def _(n=n):
                if n < 2:
                    units[2 + n].begin()
                if n % 2:
                    units[4 + n // 2].begin()
                if n in FEED_STEPS:
                    step(FEED_STEPS.index(n))

    done_steps = len(FEED_STEPS)

    @pl.loop(0, rows // 128)
    def _(r):
        here = pl.ds(pl.multiple_of(128 * r, 128), 128)
        grad = gx_ref[here]
        normed = norm_ref[here].astype(f32)
        scaled = grad * gain_ref[4:5].astype(f32)
        centre = jnp.mean(scaled, axis=1, keepdims=True)
        slope = jnp.mean(scaled * normed, axis=1, keepdims=True)
        resid = inv_ref[here] * (scaled - centre - normed * slope)
        gx_ref[here] = resid
        low = resid.astype(bf16)
        low_ref[here] = low
        total_ref[0, 3:4] = total_ref[0, 3:4] + jnp.sum(low.astype(f32), axis=0, keepdims=True)
        total_ref[0, 4:5] = total_ref[0, 4:5] + jnp.sum(grad * normed, axis=0, keepdims=True)
        total_ref[0, 5:6] = total_ref[0, 5:6] + jnp.sum(grad, axis=0, keepdims=True)

    load_square(3, 2).wait()
    for one in kept:
        one.wait()
    for h in range(2):
        turned = attt_ref[3 * h : 3 * h + 3].reshape(384, rows)
        for n in range(3):
            cols = slice(256 * n, 256 * n + 256)
            go_ref[2 * h : 2 * h + 2, :, :, :, cols] = mul(turned, low_ref[:, cols]).astype(bf16).reshape(2, 2, 2, 48, 256)
    units[8].begin()
    for j in range(pairs // 2):
        got = mul_tb(low_ref[...], wide_ref[2, 256 * j : 256 * j + 256]).astype(bf16)
        gatt_ref[2 * j] = got[:, 0:128]
        gatt_ref[2 * j + 1] = got[:, 128:256]
    for n in range(3):
        load_square(n, n).start()
    step(done_steps)
    done_steps += 1


    def copy(p):
        return remote(send_ref.at[p], gstate_ref.at[p], ssem.at[p], rsem.at[p], at.across)

    @pl.loop(0, pairs)
    def _(p):
        backward_states(p, scale, att_ref, den_ref, gatt_ref, pq_ref, strad_ref, peak_ref, state_ref, send_ref)
        copy(p).start()

    @pl.loop(0, pairs)
    def _(p):
        copy(p).wait()
        backward_finish(
            p, scale, q_ref, k_ref, v_ref, omx_ref, pq_ref, pk_ref, mask_ref, strad_ref, peak_ref, state_ref, gstate_ref,
            att_ref, den_ref, gatt_ref, gq_ref, gk_ref, gv_ref,
        )
        cols = cols_at(128 * p, 128)
        both = mul(xt_ref[...], jnp.concatenate([gq_ref[p], gk_ref[p]], axis=1)).astype(bf16)
        gw_ref[0, :, :, :, :, cols] = both[:, 0:128].reshape(DEPTH, 2, 2, 48, 128)
        gw_ref[1, :, :, :, :, cols] = both[:, 128:256].reshape(DEPTH, 2, 2, 48, 128)
        gw_ref[2, :, :, :, :, cols] = mul(xt_ref[...], gv_ref[p]).astype(bf16).reshape(DEPTH, 2, 2, 48, 128)
        for n, ref in enumerate((gq_ref, gk_ref, gv_ref)):
            total_ref[0, n : n + 1, cols] = jnp.sum(ref[p].astype(f32), axis=0, keepdims=True)
        for n, at_pair in enumerate(HEAD_STEPS):
            @pl.when(p == at_pair)
            def _(n=n):
                step(n + done_steps)

    vec = SmallSum(at, total_ref, land_ref, vs_sem, vr_sem, True)
    vec.begin()
    for u in units[early:]:
        u.begin()
    for n in range(3):
        load_square(n, n).wait()

    def grad_input(j):
        cols = slice(256 * j, 256 * j + 256)
        value = gx_ref[:, cols]
        for n, ref in enumerate((gq_ref, gk_ref, gv_ref)):
            for i in range(pairs // 2):
                left = jnp.concatenate([ref[2 * i], ref[2 * i + 1]], axis=1)
                right = wide_ref[n, 256 * j : 256 * j + 256, 256 * i : 256 * i + 256]
                value = value + mul_tb(left, right)
        gx_ref[:, cols] = value

    done_steps += len(HEAD_STEPS)
    for n, s in enumerate(range(done_steps, len(units) + PACE[-1][-1])):
        step(s)
        if n < 4:
            vec.step(n)
        if n < 3:
            grad_input(n)
    vec_ref[...] = vec.result()
    for u in units:
        u.drain()
    vec.drain()


def scratch_masks(rows, heads, feats):
    return [
        pltpu.VMEM((heads, 256, feats), bf16),
        pltpu.VMEM((rows, rows), bf16),
        pltpu.VMEM((rows, 128), f32),
        pltpu.VMEM((rows, 128), f32),
        pltpu.VMEM((TAIL, rows), bf16),
    ]


def vmem():
    return pl.BlockSpec(memory_space=pltpu.VMEM)


def anywhere():
    return pl.BlockSpec(memory_space=pl.ANY)


def smem():
    return pl.BlockSpec(memory_space=pltpu.SMEM)


def attention_forward(x, weights, vectors, ints, cot, lengths):
    rows, width = x.shape
    heads, size, feats = ints.shape
    pairs = heads // 2
    hidden = weights[4].shape[1]
    part = weights[0].shape[0]
    scale = size ** (-0.25) * unit_spread
    shape = jax.ShapeDtypeStruct
    grid = (DEPTH, 2, 2)
    dma = pltpu.SemaphoreType.DMA
    pair, phi, full, tall = (pairs, rows, 128), (pairs, 2, rows, feats), (rows, width), (rows, hidden)
    held = {
        "omx": (heads, 256, feats), "xt": (width, rows), "mask": (rows, rows), "strad": (rows, 128), "q": pair, "k": pair, "v": pair, "pq": phi, "pk": phi, "att": pair,
        "attt": (pairs, 128, rows), "den": pair, "sq": (4, *grid, part, width), "hidt": (width, rows), "norm": full,
        "fin": (*grid, part, hidden), "gelt": (hidden, rows), "slope": tall,
        "fdn": (*grid, weights[5].shape[0], width),
    }
    kind = {name: f32 if name in ("den", "strad") else bf16 for name in HOLD}
    layer, peak, state, inverse, resid, vec, sums, *rest = pl.pallas_call(
        partial(forward_kernel, scale),
        out_shape=[
            shape(full, bf16), shape((pairs, 2, 1, feats), f32), shape((pairs, 128 + TAIL, feats), bf16),
            shape((rows, 1), f32), shape(full, f32), shape((16, width), bf16), shape((16, width), f32),
        ] + [shape(held[name], kind[name]) for name in HOLD],
        in_specs=[vmem()] * 19 + [smem()],
        out_specs=[vmem()] * 7 + [anywhere()] * len(HOLD),
        scratch_shapes=[pltpu.VMEM(held[name], kind[name]) for name in HOLD] + [
            pltpu.VMEM(full, bf16), pltpu.VMEM(tall, bf16),
            pltpu.VMEM((rows, 128), f32), pltpu.VMEM((TAIL, rows), bf16),
            pltpu.VMEM((pairs, 128 + TAIL, feats), bf16),
            pltpu.VMEM((4, 16, width), bf16),
            pltpu.VMEM((DEPTH + 1, 16, width), bf16),
            dma((pairs,)), dma((pairs,)),
            dma((12, GATHER_COPIES)), dma((12, GATHER_COPIES)), dma((12,)),
            dma((DEPTH + 1,)), dma((DEPTH + 1,)), dma((len(HOLD),)),
        ],
        compiler_params=pltpu.CompilerParams(collective_id=0, has_side_effects=True, vmem_limit_bytes=65200 << 10),
        name="attention_forward",
    )(x, *weights, *vectors, ints, cot, lengths)
    got = dict(zip(HOLD, rest))
    inner = (peak, state, got["hidt"], got["norm"], inverse, resid, vec, sums)
    late = (
        got["gelt"], got["slope"], got["fin"].reshape(width, hidden), got["fdn"].reshape(hidden, width),
        got["sq"].reshape(4, width, width), *(got[name] for name in LATE),
    )
    return layer, inner, late


def attention_backward(inner, late):
    rows, width = inner[5].shape
    pairs, _, _, feats = inner[0].shape
    heads, hidden = 2 * pairs, late[0].shape[0]
    scale = (width // heads) ** (-0.25) * unit_spread
    shape = jax.ShapeDtypeStruct
    dma = pltpu.SemaphoreType.DMA
    grid = (DEPTH, 2, 2)
    part = width // 16
    units = 12
    return pl.pallas_call(
        partial(backward_kernel, scale),
        out_shape=[shape((rows, width), f32)]
        + [shape((part, width), f32)] * 4
        + [shape((part, hidden), f32), shape((hidden // 16, width), f32), shape((16, width), f32)],
        in_specs=[vmem()] * 8 + [anywhere()] * (5 + len(LATE)),
        out_specs=[vmem()] * 8,
        scratch_shapes=[pltpu.VMEM(one.shape, one.dtype) for one in late[5:]] + [
            pltpu.VMEM((pairs, 128 + TAIL, feats), bf16), pltpu.VMEM((pairs, 128 + TAIL, feats), bf16),
            pltpu.VMEM((pairs, rows, 128), bf16), pltpu.VMEM((pairs, rows, 128), bf16), pltpu.VMEM((pairs, rows, 128), bf16),
            pltpu.VMEM((pairs, rows, 128), bf16),
            pltpu.VMEM((rows, width), bf16),
            pltpu.VMEM((3, width, width), bf16),
            pltpu.VMEM((2, width // 2, rows), bf16), pltpu.VMEM((2, rows, width // 2), bf16),
            pltpu.VMEM((*grid, hidden // 16, width), bf16),
            pltpu.VMEM((*grid, part, hidden), bf16),
            pltpu.VMEM((*grid, part, width), bf16),
            pltpu.VMEM((3, *grid, part, width), bf16),
            pltpu.VMEM((5, 16, width), f32),
            pltpu.VMEM((DEPTH + 2, 16, width), f32),
            pltpu.VMEM((units, DEPTH, 2, part, width), bf16),
            pltpu.VMEM((units, part, width // 2), bf16),
            pltpu.VMEM((units, part, width // 2), bf16),
            dma((pairs,)), dma((pairs,)), dma((4, 2)), dma((3,)), dma((len(LATE),)),
            dma((units, SCATTER_COPIES)), dma((units, SCATTER_COPIES)),
            dma((DEPTH + 2,)), dma((DEPTH + 2,)),
        ] + [land for order in ORDERS for land in landing(order, part, width)],
        compiler_params=pltpu.CompilerParams(collective_id=1, has_side_effects=True, vmem_limit_bytes=65200 << 10),
        name="attention_backward",
    )(*inner, *late)


def finish_kernel(sums_ref, *refs):
    big = BIG
    ins, outs, vectors, sem = refs[:big], refs[big : 2 * big], refs[2 * big : -1], refs[-1]
    copies = [pltpu.make_async_copy(src, dst, sem.at[n]) for n, (src, dst) in enumerate(zip(ins, outs))]
    for one in copies:
        one.start()
    me = lax.axis_index("fsdp")
    part, wide = vectors[0].shape[1], vectors[9].shape[1]
    width = sums_ref.shape[1]
    sums = sums_ref[...]
    turned = pltpu.roll(sums, lax.rem(width - part * me, width), 1)
    for n in range(9):
        vectors[n][...] = turned[n : n + 1, 0:part]
    inner = pltpu.roll(sums, lax.rem(width - wide * lax.rem(me, 4), width), 1)
    row = jnp.zeros((1, width), f32)
    for n in range(DEPTH):
        row = jnp.where(lax.div(me, 4) == n, inner[9 + n : 10 + n], row)
    vectors[9][...] = row[:, 0:wide]
    for one in copies:
        one.wait()


BIG = 8


def finish(arrays, sums, part, wide):
    shape = jax.ShapeDtypeStruct
    return pl.pallas_call(
        finish_kernel,
        out_shape=[shape(a.shape, a.dtype) for a in arrays] + [shape((1, part), f32)] * 9 + [shape((1, wide), f32)],
        in_specs=[vmem()] + [anywhere()] * BIG,
        out_specs=[vmem()] * (BIG + 10),
        scratch_shapes=[pltpu.SemaphoreType.DMA((BIG,))],
        name="finish",
    )(sums, *arrays)


def to_pairs(rows):
    return rows.reshape(rows.shape[0], -1, 128).transpose(1, 0, 2)


def from_pairs(pairs):
    return pairs.transpose(1, 0, 2).reshape(pairs.shape[1], -1)


def per_device(
    tokens, doc_lengths, feature_ints, w_query, b_query, w_key, b_key, w_value, b_value, w_out, b_out,
    norm1_gain, norm1_bias, w_in, b_in, w_down, b_down, norm2_gain, norm2_bias, cotangent,
):
    layer_out, inner, late = attention_forward(
        tokens[0],
        (w_query, w_key, w_value, w_out, w_in, w_down),
        (b_query, b_key, b_value, b_out, norm1_gain, norm1_bias, b_down, norm2_gain, norm2_bias, b_in),
        feature_ints, cotangent[0], doc_lengths,
    )
    *grads, sums = attention_backward(inner, late)
    done = finish((layer_out, *grads), sums, b_query.shape[0], b_in.shape[0])
    layer_out, grad_input, gq, gk, gv, go, gin, gdn = done[:BIG]
    bq, bk, bv, bo, g1, o1, bd, g2, o2, bi = (one.reshape(-1) for one in done[BIG:])
    return (
        layer_out[None], grad_input[None],
        gq, bq, gk, bk, gv, bv, go, bo, g1, o1, gin, bi, gdn, bd, g2, o2,
    )


def forward_kernel_wide(
    scale, x_ref, wq_ref, wk_ref, wv_ref, bias_ref, ints_ref, len_ref,
    q_ref, k_ref, v_ref, pq_ref, pk_ref, att_ref, den_ref, peak_ref, state_ref,
    omx_ref, mask_ref, onehot_ref, strad_ref, stradrow_ref, send_ref, ssem, rsem,
):
    place = lax.axis_index("seq")
    peer = {"seq": 1 - place}
    peer_barrier([peer])
    pairs = q_ref.shape[0]
    doc_setup(len_ref, place, mask_ref, onehot_ref, strad_ref, stradrow_ref)
    features_setup(ints_ref, omx_ref)
    for n, (w_ref, o_ref) in enumerate(((wq_ref, q_ref), (wk_ref, k_ref), (wv_ref, v_ref))):
        for j in range(pairs // 2):
            cols = slice(256 * j, 256 * j + 256)
            got = (mul(x_ref[...], w_ref[:, cols]) + bias_ref[n : n + 1, cols].astype(f32)).astype(bf16)
            o_ref[2 * j] = got[:, 0:128]
            o_ref[2 * j + 1] = got[:, 128:256]

    def copy(p):
        return pltpu.make_async_remote_copy(
            src_ref=send_ref.at[p], dst_ref=state_ref.at[p], send_sem=ssem.at[p], recv_sem=rsem.at[p],
            device_id=peer, device_id_type=MESH,
        )

    @pl.loop(0, pairs)
    def _(p):
        forward_states(p, scale, q_ref, k_ref, v_ref, omx_ref, onehot_ref, strad_ref, stradrow_ref, pq_ref, pk_ref, peak_ref, send_ref)
        copy(p).start()

    @pl.loop(0, pairs)
    def _(p):
        copy(p).wait()
        forward_finish(p, scale, v_ref, pq_ref, pk_ref, mask_ref, strad_ref, peak_ref, state_ref, att_ref, den_ref)


def backward_kernel_wide(
    scale, q_ref, k_ref, v_ref, pq_ref, pk_ref, att_ref, den_ref, peak_ref, state_ref, gatt_ref, ints_ref, len_ref,
    gq_ref, gk_ref, gv_ref,
    gstate_ref, omx_ref, mask_ref, onehot_ref, strad_ref, stradrow_ref, send_ref, ssem, rsem,
):
    place = lax.axis_index("seq")
    peer = {"seq": 1 - place}
    peer_barrier([peer])
    pairs = q_ref.shape[0]
    doc_setup(len_ref, place, mask_ref, onehot_ref, strad_ref, stradrow_ref)
    features_setup(ints_ref, omx_ref)

    def copy(p):
        return pltpu.make_async_remote_copy(
            src_ref=send_ref.at[p], dst_ref=gstate_ref.at[p], send_sem=ssem.at[p], recv_sem=rsem.at[p],
            device_id=peer, device_id_type=MESH,
        )

    @pl.loop(0, pairs)
    def _(p):
        backward_states(p, scale, att_ref, den_ref, gatt_ref, pq_ref, strad_ref, peak_ref, state_ref, send_ref)
        copy(p).start()

    @pl.loop(0, pairs)
    def _(p):
        copy(p).wait()
        backward_finish(
            p, scale, q_ref, k_ref, v_ref, omx_ref, pq_ref, pk_ref, mask_ref, strad_ref, peak_ref, state_ref, gstate_ref,
            att_ref, den_ref, gatt_ref, gq_ref, gk_ref, gv_ref,
        )


def attention_forward_wide(x, wq, wk, wv, biases, ints, lengths):
    rows = x.shape[0]
    heads, size, feats = ints.shape
    pairs = heads // 2
    scale = size ** (-0.25) * unit_spread
    shape = jax.ShapeDtypeStruct
    return pl.pallas_call(
        partial(forward_kernel_wide, scale),
        out_shape=[
            shape((pairs, rows, 128), bf16), shape((pairs, rows, 128), bf16), shape((pairs, rows, 128), bf16),
            shape((pairs, 2, rows, feats), bf16), shape((pairs, 2, rows, feats), bf16),
            shape((pairs, rows, 128), bf16), shape((pairs, rows, 128), f32),
            shape((pairs, 2, 1, feats), f32), shape((pairs, 128 + TAIL, feats), bf16),
        ],
        in_specs=[vmem()] * 6 + [pl.BlockSpec(memory_space=pltpu.SMEM)],
        out_specs=[vmem()] * 9,
        scratch_shapes=scratch_masks(rows, heads, feats) + [
            pltpu.VMEM((pairs, 128 + TAIL, feats), bf16),
            pltpu.SemaphoreType.DMA((pairs,)),
            pltpu.SemaphoreType.DMA((pairs,)),
        ],
        compiler_params=pltpu.CompilerParams(collective_id=0, has_side_effects=True, vmem_limit_bytes=60 << 20),
        name="attention_forward",
    )(x, wq, wk, wv, biases, ints, lengths)


def attention_backward_wide(saved, gatt, ints, lengths):
    pairs, rows, _ = gatt.shape
    heads, size, feats = ints.shape
    scale = size ** (-0.25) * unit_spread
    shape = jax.ShapeDtypeStruct
    return pl.pallas_call(
        partial(backward_kernel_wide, scale),
        out_shape=[shape((pairs, rows, 128), bf16)] * 3,
        in_specs=[vmem()] * 11 + [pl.BlockSpec(memory_space=pltpu.SMEM)],
        out_specs=[vmem()] * 3,
        scratch_shapes=[pltpu.VMEM((pairs, 128 + TAIL, feats), bf16)] + scratch_masks(rows, heads, feats) + [
            pltpu.VMEM((pairs, 128 + TAIL, feats), bf16),
            pltpu.SemaphoreType.DMA((pairs,)),
            pltpu.SemaphoreType.DMA((pairs,)),
        ],
        compiler_params=pltpu.CompilerParams(collective_id=1, has_side_effects=True, vmem_limit_bytes=60 << 20),
        name="attention_backward",
    )(*saved, gatt, ints, lengths)


def gathered(piece):
    return lax.all_gather(piece, "fsdp", axis=0, tiled=True)


def per_device_wide(
    tokens, doc_lengths, feature_ints, w_query, b_query, w_key, b_key, w_value, b_value, w_out, b_out,
    norm1_gain, norm1_bias, w_in, b_in, w_down, b_down, norm2_gain, norm2_bias, cotangent,
):
    row_block = tokens[0]
    width = row_block.shape[1]
    fsdp = lax.axis_size("fsdp")
    me = lax.axis_index("fsdp")
    attn_stack = gathered(jnp.stack([w_query, w_key, w_value, w_out], axis=1))
    query_weight, key_weight, value_weight, out_weight = (attn_stack[:, i] for i in range(4))
    small = jnp.concatenate(
        [b_query, b_key, b_value, b_out, norm1_gain, norm1_bias, b_down, norm2_gain, norm2_bias, b_in]
    )
    small = lax.all_gather(small[None], "fsdp", axis=0, tiled=True)
    part = width // fsdp
    vectors = [small[:, part * i : part * (i + 1)].reshape(-1) for i in range(9)] + [small[:, 9 * part :].reshape(-1)]
    query_bias, key_bias, value_bias, out_bias, gain_one, offset_one, down_bias, gain_two, offset_two, in_bias = vectors
    saved = attention_forward_wide(
        row_block, query_weight, key_weight, value_weight, jnp.stack([query_bias, key_bias, value_bias]),
        feature_ints, doc_lengths,
    )
    att_rows = from_pairs(saved[5])
    residual_one = row_block.astype(f32) + affine(att_rows, out_weight, out_bias)
    hidden_wide, normed_one, inverse_one = layer_norm(residual_one, gain_one, offset_one)
    hidden_low = hidden_wide.astype(bf16)
    in_weight = gathered(w_in)
    down_weight = gathered(w_down)
    pre_act = affine(hidden_low, in_weight, in_bias)
    gelu_low = gelu_value(pre_act).astype(bf16)
    residual_two = hidden_low.astype(f32) + affine(gelu_low, down_weight, down_bias)
    layer_wide, normed_two, inverse_two = layer_norm(residual_two, gain_two, offset_two)
    grad_out = cotangent[0].astype(f32)
    grad_resid_two, grad_gain_two, grad_offset_two = norm_back(grad_out, normed_two, inverse_two, gain_two)
    grad_down_low = grad_resid_two.astype(bf16)
    grad_down_weight = mul_ta(gelu_low, grad_down_low)
    grad_down_bias = column_total(grad_down_low)
    grad_pre_low = (mul_tb(grad_down_low, down_weight) * gelu_slope(pre_act)).astype(bf16)
    grad_in_weight = mul_ta(hidden_low, grad_pre_low)
    grad_in_bias = column_total(grad_pre_low)
    grad_hidden = mul_tb(grad_pre_low, in_weight) + grad_resid_two
    grad_resid_one, grad_gain_one, grad_offset_one = norm_back(grad_hidden, normed_one, inverse_one, gain_one)
    grad_proj_low = grad_resid_one.astype(bf16)
    grad_out_weight = mul_ta(att_rows, grad_proj_low)
    grad_out_bias = column_total(grad_proj_low)
    grad_att_rows = mul_tb(grad_proj_low, out_weight).astype(bf16)
    grads = attention_backward_wide(saved, to_pairs(grad_att_rows), feature_ints, doc_lengths)
    grad_query_rows, grad_key_rows, grad_value_rows = (from_pairs(g) for g in grads)
    grad_query_weight = mul_ta(row_block, grad_query_rows)
    grad_key_weight = mul_ta(row_block, grad_key_rows)
    grad_value_weight = mul_ta(row_block, grad_value_rows)
    grad_input = (
        mul_tb(grad_query_rows, query_weight)
        + mul_tb(grad_key_rows, key_weight)
        + mul_tb(grad_value_rows, value_weight)
        + grad_resid_one
    )

    def owned(grad):
        shard = lax.psum_scatter(grad.astype(bf16), "fsdp", scatter_dimension=0, tiled=True)
        return lax.psum(shard, "seq").astype(f32)

    sums = jnp.stack(
        [
            column_total(grad_query_rows), column_total(grad_key_rows), column_total(grad_value_rows), grad_out_bias,
            grad_gain_one, grad_offset_one, grad_down_bias, grad_gain_two, grad_offset_two,
            *grad_in_bias.reshape(-1, width),
        ]
    )
    sums = lax.psum(sums, ("fsdp", "seq"))
    mine = [lax.dynamic_slice(sums[i], (me * part,), (part,)) for i in range(9)]
    wide = in_bias.shape[0] // fsdp
    mine_in = lax.dynamic_slice(sums[9:].reshape(-1), (me * wide,), (wide,))
    return (
        layer_wide.astype(bf16)[None],
        grad_input[None],
        owned(grad_query_weight), mine[0],
        owned(grad_key_weight), mine[1],
        owned(grad_value_weight), mine[2],
        owned(grad_out_weight), mine[3],
        mine[4], mine[5],
        owned(grad_in_weight), mine_in,
        owned(grad_down_weight), mine[6],
        mine[7], mine[8],
    )


def solution(mesh):
    rows, matrix, vector = P("fsdp", "seq", None), P("fsdp", None), P("fsdp")
    weights = (matrix, vector) * 4 + (vector, vector) + (matrix, vector) * 2 + (vector, vector)
    near = mesh.shape["fsdp"] == 4 * DEPTH and mesh.shape["seq"] == 2
    return jax.shard_map(
        per_device if near else per_device_wide,
        mesh=mesh,
        in_specs=(rows, matrix, P(), *weights, rows),
        out_specs=(rows, rows, *weights),
        check_vma=False,
    )
```

```python
from functools import partial

import jax
import jax.numpy as jnp
from jax import lax
from jax.experimental import pallas as pl
from jax.experimental.pallas import tpu as pltpu
from jax.sharding import PartitionSpec as P

unit_spread = 0.013531646934131853
inv_root_two = 0.7071067811865476
inv_root_tau = 0.3989422804014327
far_below = -1e30
log2_e = 1.4426950408889634
MESH = pl.DeviceIdType.MESH
f32 = jnp.float32
bf16 = jnp.bfloat16
TAIL = 16
DEPTH = 4
AHEAD = 1


def layer_norm(residual, norm_gain, norm_bias):
    centred = residual - jnp.mean(residual, axis=1, keepdims=True)
    inverse = lax.rsqrt(jnp.mean(centred * centred, axis=1, keepdims=True) + 1e-06)
    normed = centred * inverse
    return (normed * norm_gain.astype(f32) + norm_bias.astype(f32), normed, inverse)


def norm_back(grad_out, normed, inverse, norm_gain):
    scaled = grad_out * norm_gain.astype(f32)
    centre_part = jnp.mean(scaled, axis=1, keepdims=True)
    slope_part = jnp.mean(scaled * normed, axis=1, keepdims=True)
    grad_resid = inverse * (scaled - centre_part - normed * slope_part)
    return (grad_resid, jnp.sum(grad_out * normed, axis=0), jnp.sum(grad_out, axis=0))


def gelu_value(pre_act):
    return 0.5 * pre_act * (1.0 + lax.erf(pre_act * inv_root_two))


def gelu_slope(pre_act):
    return (
        0.5 * (1.0 + lax.erf(pre_act * inv_root_two))
        + pre_act * jnp.exp(-0.5 * pre_act * pre_act) * inv_root_tau
    )


def mul(a, b):
    return lax.dot_general(a, b, (((1,), (0,)), ((), ())), preferred_element_type=f32)


def mul_tb(a, b):
    return lax.dot_general(a, b, (((1,), (1,)), ((), ())), preferred_element_type=f32)


def mul_ta(a, b):
    return lax.dot_general(a, b, (((0,), (0,)), ((), ())), preferred_element_type=f32)


def affine(row_block, weight, bias_row):
    return mul(row_block, weight) + bias_row.astype(f32)


def column_total(values):
    return jnp.sum(values, axis=0, dtype=f32)


def lane_ids(shape):
    return lax.broadcasted_iota(jnp.int32, shape, len(shape) - 1)


def doc_setup(lengths, place, mask_ref, onehot_ref, strad_ref, stradrow_ref):
    rows = mask_ref.shape[0]
    docs = lengths.shape[1]
    total = jnp.int32(0)
    ends = []
    for d in range(docs):
        total = total + lengths[0, d]
        ends.append(total)
    pos = lax.broadcasted_iota(jnp.int32, (rows, 128), 0) + place * rows
    pos_row = lax.broadcasted_iota(jnp.int32, (8, rows), 1) + place * rows
    did = jnp.zeros((rows, 128), jnp.int32)
    did_row = jnp.zeros((8, rows), jnp.int32)
    edge = jnp.int32(0)
    for end in ends[:-1]:
        did = did + (pos >= end).astype(jnp.int32)
        did_row = did_row + (pos_row >= end).astype(jnp.int32)
        edge = edge + (end <= rows).astype(jnp.int32)
    for j in range(rows // 128):
        cols = did_row[0:1, j * 128 : (j + 1) * 128]
        mask_ref[:, j * 128 : (j + 1) * 128] = (did == cols).astype(f32).astype(bf16)
    onehot_ref[...] = (did == lane_ids((rows, 128))).astype(f32)
    strad_ref[...] = (did == edge).astype(f32)
    one_row = (did_row[0:1] == edge).astype(f32)
    stradrow_ref[...] = jnp.broadcast_to(one_row, stradrow_ref.shape).astype(bf16)


def features_setup(ints_ref, omx_ref):
    heads, size, feats = ints_ref.shape

    @pl.loop(0, heads)
    def _(h):
        mat = ints_ref[h].astype(f32).astype(bf16)
        zero = jnp.zeros((size, feats), bf16)
        odd = lax.rem(h, 2) == 1
        omx_ref[h, 0:size] = jnp.where(odd, zero, mat)
        omx_ref[h, size : 2 * size] = jnp.where(odd, mat, zero)
        omx_ref[h, 2 * size :] = jnp.ones((2 * size, feats), bf16)


def three_terms(value):
    first = value.astype(bf16).astype(f32)
    second = (value - first).astype(bf16).astype(f32)
    return first, second, value - first - second


def forward_states(p, scale, q_ref, k_ref, v_ref, omx_ref, onehot_ref, strad_ref, stradrow_ref, pq_ref, pk_ref, peak_ref, out_ref):
    rows = q_ref.shape[1]
    lanes = lane_ids((1, 128))
    qp, kp, vp = q_ref[p], k_ref[p], v_ref[p]
    kf = kp.astype(f32)
    ksq = kf * kf
    vt = jnp.concatenate([vp.T * stradrow_ref[0:1], stradrow_ref[...]], axis=0)
    tail = jnp.zeros((TAIL, pq_ref.shape[-1]), f32)
    tail_row = lax.broadcasted_iota(jnp.int32, tail.shape, 0)
    for j in range(2):
        om = omx_ref[2 * p + j, 0:128]
        raw_q = mul(qp, om)
        raw_q = raw_q - jnp.max(raw_q, axis=1, keepdims=True)
        pq_ref[p, j] = jnp.exp2(raw_q * (scale * log2_e)).astype(bf16)
        here = (lanes >= 64) if j else (lanes < 64)
        half = jnp.sum(jnp.where(here, ksq, 0.0), axis=1, keepdims=True) * (0.0625 / scale)
        raw_k = mul(kp, om) - half
        row_peak = jnp.max(raw_k, axis=1, keepdims=True)
        doc_peak = jnp.max(jnp.where(onehot_ref[...] > 0.5, row_peak, far_below), axis=0, keepdims=True)
        back = jnp.max(jnp.where(onehot_ref[...] > 0.5, doc_peak, far_below), axis=1, keepdims=True)
        edge_peak = jnp.max(jnp.where(strad_ref[...] > 0.5, row_peak, far_below), axis=0, keepdims=True)
        phi_k = jnp.exp2((raw_k - back) * (scale * log2_e)).astype(bf16)
        pk_ref[p, j] = phi_k
        part = mul(vt, phi_k)
        out_ref[p, 64 * j : 64 * j + 64] = part[64 * j : 64 * j + 64].astype(bf16)
        edge_wide = jnp.concatenate([edge_peak, edge_peak], axis=1)
        peak_ref[p, j] = edge_wide
        tail = jnp.where(tail_row == j, part[128 : 128 + TAIL], tail)
        for t, term in enumerate(three_terms(edge_wide)):
            tail = jnp.where(tail_row == 2 + 3 * j + t, term, tail)
    out_ref[p, 128:] = tail.astype(bf16)


def edge_parts(state_ref, p, j):
    tail = state_ref[p, 128:].astype(f32)
    feats = tail.shape[1]
    totals = jnp.broadcast_to(tail[j : j + 1], (128, feats)).astype(bf16)
    peak = tail[2 + 3 * j : 3 + 3 * j] + tail[3 + 3 * j : 4 + 3 * j] + tail[4 + 3 * j : 5 + 3 * j]
    return jnp.concatenate([state_ref[p, 0:128], totals], axis=0), peak


def edge_weights(scale, own, other, strad):
    top = jnp.maximum(own, other)
    own_w = jnp.exp2((own - top) * (scale * log2_e))
    other_w = jnp.exp2((other - top) * (scale * log2_e))
    return 1.0 + strad * (own_w[:, 0:128] - 1.0), strad * other_w[:, 0:128]


def forward_finish(p, scale, v_ref, pq_ref, pk_ref, mask_ref, strad_ref, peak_ref, in_ref, att_ref, den_ref):
    rows = v_ref.shape[1]
    first_half = lane_ids((rows, 128)) < 64
    vx = jnp.concatenate([v_ref[p], jnp.ones((rows, 128), bf16)], axis=1)
    got = []
    for j in range(2):
        phi_q = pq_ref[p, j]
        pair = mul_tb(phi_q, pk_ref[p, j]).astype(bf16) * mask_ref[...]
        near = mul(pair, vx)
        state, other = edge_parts(in_ref, p, j)
        far = mul_tb(phi_q, state)
        wn, wf = edge_weights(scale, peak_ref[p, j], other, strad_ref[...])
        den = near[:, 128:] * wn + far[:, 128:] * wf
        got.append(((near[:, :128] * wn + far[:, :128] * wf) / den, den))
    att_ref[p] = jnp.where(first_half, got[0][0], got[1][0]).astype(bf16)
    den_ref[p] = jnp.where(first_half, got[0][1], got[1][1])


def numer_grads(p, att_ref, den_ref, gatt_ref):
    rows = att_ref.shape[1]
    lanes = lane_ids((rows, 128))
    gn = gatt_ref[p].astype(f32) / den_ref[p]
    prod = gn * att_ref[p].astype(f32)
    d0 = -jnp.sum(jnp.where(lanes < 64, prod, 0.0), axis=1, keepdims=True)
    d1 = -jnp.sum(jnp.where(lanes < 64, 0.0, prod), axis=1, keepdims=True)
    return gn, d0, d1, lanes


def backward_states(p, scale, att_ref, den_ref, gatt_ref, pq_ref, strad_ref, peak_ref, in_ref, out_ref):
    gn, d0, d1, lanes = numer_grads(p, att_ref, den_ref, gatt_ref)
    far = [edge_weights(scale, peak_ref[p, j], edge_parts(in_ref, p, j)[1], strad_ref[...])[1] for j in range(2)]
    left = (gn * jnp.where(lanes < 64, far[0], far[1])).astype(bf16)
    right = (jnp.where(lanes == 0, d0 * far[0], 0.0) + jnp.where(lanes == 1, d1 * far[1], 0.0)).astype(bf16)
    turned = jnp.concatenate([left.T, right.T[0:TAIL]], axis=0)
    tails = []
    for j in range(2):
        part = mul(turned, pq_ref[p, j])
        out_ref[p, 64 * j : 64 * j + 64] = part[64 * j : 64 * j + 64].astype(bf16)
        tails.append(part[128:])
    rowid = lax.broadcasted_iota(jnp.int32, tails[0].shape, 0)
    out_ref[p, 128:] = jnp.where(rowid == 0, tails[0], tails[1]).astype(bf16)


def backward_finish(
    p, scale, q_ref, k_ref, v_ref, omx_ref, pq_ref, pk_ref, mask_ref, strad_ref, peak_ref, in_ref, gin_ref,
    att_ref, den_ref, gatt_ref, gq_ref, gk_ref, gv_ref,
):
    rows = q_ref.shape[1]
    gn, d0, d1, lanes = numer_grads(p, att_ref, den_ref, gatt_ref)
    first_half = lanes < 64
    vp = v_ref[p]
    ones = jnp.ones((rows, 128), bf16)
    vx = jnp.concatenate([vp, ones], axis=1)
    strad = strad_ref[...]
    gq = jnp.zeros((rows, 128), f32)
    gk = jnp.zeros((rows, 128), f32)
    gv = jnp.zeros((rows, 128), f32)
    q_sums, k_sums = [], []
    for j in range(2):
        here = (lanes >= 64) if j else (lanes < 64)
        gd = d1 if j else d0
        state, other = edge_parts(in_ref, p, j)
        wn, wf = edge_weights(scale, peak_ref[p, j], other, strad)
        base_l = jnp.where(here, gn, 0.0)
        base_r = jnp.where(lanes == 0, gd, 0.0)
        near = jnp.concatenate([(base_l * wn).astype(bf16), (base_r * wn).astype(bf16)], axis=1)
        far = jnp.concatenate([(base_l * wf).astype(bf16), (base_r * wf).astype(bf16)], axis=1)
        phi_q, phi_k = pq_ref[p, j], pk_ref[p, j]
        turned = mul_tb(phi_k, phi_q).astype(bf16) * mask_ref[...]
        gv = gv + mul(turned, near[:, 0:128])
        gpair = mul_tb(near, vx).astype(bf16) * mask_ref[...]
        gphi_q = mul(gpair, phi_k) + mul(far, state)
        gturned = mul_tb(vx, near).astype(bf16) * mask_ref[...]
        gstate, _ = edge_parts(gin_ref, p, j)
        vs = jnp.concatenate(
            [(jnp.where(here, vp.astype(f32), 0.0) * strad).astype(bf16), jnp.where(lanes == 0, strad, 0.0).astype(bf16)],
            axis=1,
        )
        gphi_k = mul(gturned, phi_q) + mul(vs, gstate)
        gv = gv + jnp.where(here, mul_tb(phi_k, gstate[0:128]) * strad, 0.0)
        omx = omx_ref[2 * p + j]
        back_q = mul_tb((gphi_q * phi_q.astype(f32)).astype(bf16), omx)
        back_k = mul_tb((gphi_k * phi_k.astype(f32)).astype(bf16), omx)
        gq = gq + back_q[:, 0:128]
        gk = gk + back_k[:, 0:128]
        q_sums.append(back_q[:, 128:])
        k_sums.append(back_k[:, 128:])
    gq = gq * scale - jnp.where(first_half, q_sums[0], q_sums[1]) * q_ref[p].astype(f32) * 0.125
    gk = gk * scale - jnp.where(first_half, k_sums[0], k_sums[1]) * k_ref[p].astype(f32) * 0.125
    gq_ref[p] = gq.astype(bf16)
    gk_ref[p] = gk.astype(bf16)
    gv_ref[p] = gv.astype(bf16)


def peer_barrier(peers):
    barrier = pltpu.get_barrier_semaphore()
    for peer in peers:
        pl.semaphore_signal(barrier, inc=1, device_id=peer, device_id_type=MESH)
    pl.semaphore_wait(barrier, len(peers))


class Place:
    def __init__(self):
        me = lax.axis_index("fsdp")
        self.y = lax.axis_index("seq")
        self.c = lax.rem(me, 2)
        self.x = lax.rem(lax.div(me, 2), 2)
        self.z = lax.div(me, 4)
        self.across = {"seq": 1 - self.y}
        self.twin = {"fsdp": self.z * 4 + self.x * 2 + 1 - self.c}
        self.beside = {"fsdp": self.z * 4 + (1 - self.x) * 2 + self.c}

    def along(self, d):
        return {"fsdp": self.other(d) * 4 + self.x * 2 + self.c}

    def other(self, d):
        return lax.rem(self.z + (d + DEPTH), DEPTH)

    def peers(self):
        return [self.twin, self.beside, self.across] + [self.along(d) for d in range(1, DEPTH)]


def cols_at(start, size):
    return pl.ds(pl.multiple_of(start, 128), size)


def remote(src, dst, ssem, rsem, peer):
    return pltpu.make_async_remote_copy(
        src_ref=src, dst_ref=dst, send_sem=ssem, recv_sem=rsem, device_id=peer, device_id_type=MESH
    )


class Gather:
    def __init__(self, at, own, full, base, width, ssem, rsem, lsem):
        self.at, self.own, self.full = at, own, full
        self.third, self.base, self.width = width // 3, base, width
        self.ssem, self.rsem, self.lsem = ssem, rsem, lsem
        self.sent = []

    def spread(self):
        return cols_at(self.base + self.third * self.at.y, 2 * self.third)

    def extra(self, y):
        return cols_at(self.base + 2 * self.third * y, self.third)

    def whole(self):
        return pl.ds(self.base, self.width)

    def go(self, n, ends):
        src, dst, peer = ends()
        remote(src, dst, self.ssem.at[n], self.rsem.at[n], peer).start()
        self.sent.append((n, ends))

    def came(self, n, ref):
        remote(ref, ref, self.ssem.at[n], self.rsem.at[n], self.at.twin).wait_recv()

    def local(self):
        at = self.at
        return pltpu.make_async_copy(
            self.own.at[:, self.whole()], self.full.at[at.z, at.x, at.c, :, self.whole()], self.lsem
        )

    def begin(self):
        at = self.at
        self.local().start()
        for d in range(1, DEPTH):
            self.go(d - 1, lambda d=d: (*self.first(), at.along(d)))

    def first(self):
        at = self.at
        return self.own.at[:, self.spread()], self.full.at[at.z, at.x, at.c, :, self.spread()]

    def piece(self, d, x, cols):
        return self.full.at[self.at.other(-d), x, self.at.c, :, cols]

    def stage_x(self):
        at = self.at
        self.go(DEPTH - 1, lambda: (*self.first(), at.beside))
        for d in range(1, DEPTH):
            self.came(d - 1, self.piece(d, at.x, self.spread()))
            self.go(DEPTH - 1 + d, lambda d=d: (*[self.piece(d, at.x, self.spread())] * 2, at.beside))
            self.go(2 * DEPTH - 2 + d, lambda d=d: (*[self.piece(d, at.x, self.extra(at.y))] * 2, at.across))

    def stage_y(self):
        at = self.at
        for d in range(DEPTH):
            self.came(DEPTH - 1 + d, self.piece(d, 1 - at.x, self.spread()))
            self.go(3 * DEPTH - 2 + d, lambda d=d: (*[self.piece(d, 1 - at.x, self.extra(at.y))] * 2, at.across))

    def stage_c(self):
        at = self.at
        for d in range(1, DEPTH):
            self.came(2 * DEPTH - 2 + d, self.piece(d, at.x, self.extra(1 - at.y)))
        for d in range(DEPTH):
            self.came(3 * DEPTH - 2 + d, self.piece(d, 1 - at.x, self.extra(1 - at.y)))
        self.local().wait()
        self.go(4 * DEPTH - 2, lambda: (*[self.full.at[:, :, at.c, :, self.whole()]] * 2, at.twin))

    def ready(self):
        self.came(4 * DEPTH - 2, self.full.at[:, :, 1 - self.at.c, :, self.whole()])

    def drain(self):
        for n, ends in self.sent:
            src, dst, peer = ends()
            remote(src, dst, self.ssem.at[n], self.rsem.at[n], peer).wait_send()


GATHER_COPIES = 4 * DEPTH - 1


class SmallSum:
    def __init__(self, at, total, land, ssem, rsem, over_seq):
        self.at, self.total, self.land, self.ssem, self.rsem, self.over_seq = at, total, land, ssem, rsem, over_seq
        self.sent = []

    def go(self, src, n, peer):
        copy = remote(self.total.at[src], self.land.at[n], self.ssem.at[n], self.rsem.at[n], peer)
        copy.start()
        self.sent.append(copy)

    def came(self, n):
        remote(self.land.at[n], self.land.at[n], self.ssem.at[n], self.rsem.at[n], self.at.twin).wait_recv()

    def begin(self):
        for d in range(1, DEPTH):
            self.go(0, d - 1, self.at.along(d))

    def step(self, k):
        if k == 0:
            got = self.total[0]
            for d in range(1, DEPTH):
                self.came(d - 1)
            order = [self.at.z] + [self.at.other(-d) for d in range(1, DEPTH)]
            parts = [got] + [self.land[d - 1] for d in range(1, DEPTH)]
            value = jnp.zeros_like(got)
            for z in range(DEPTH):
                one = jnp.zeros_like(got)
                for place, part in zip(order, parts):
                    one = jnp.where(place == z, part, one)
                value = value + one
        else:
            self.came(DEPTH - 2 + k)
            value = self.total[k] + self.land[DEPTH - 2 + k]
        self.total[k + 1] = value
        hops = [self.at.beside, self.at.twin] + ([self.at.across] if self.over_seq else [])
        if k < len(hops):
            self.go(k + 1, DEPTH - 1 + k, hops[k])

    def steps(self):
        return 4 if self.over_seq else 3

    def result(self):
        return self.total[self.steps()]

    def drain(self):
        for copy in self.sent:
            copy.wait_send()


def spread_vectors(at, pieces, wide):
    width = 768
    part = pieces[0].shape[-1]
    rows = [p[...].astype(f32).reshape(1, part) for p in pieces]
    rows = jnp.concatenate(rows + [jnp.zeros((16 - len(rows), part), f32)], axis=0)
    rows = jnp.concatenate([rows, jnp.zeros((16, width - part), f32)], axis=1)
    rows = pltpu.roll(rows, (at.z * 4 + at.x * 2 + at.c) * part, 1)
    span = wide.shape[-1]
    row = jnp.concatenate([wide[...].astype(f32).reshape(1, span), jnp.zeros((1, width - span), f32)], axis=1)
    row = pltpu.roll(jnp.broadcast_to(row, (16, width)), (at.x * 2 + at.c) * span, 1)
    here = lax.broadcasted_iota(jnp.int32, (16, width), 0)
    return jnp.where(here == len(pieces) + at.z, row, rows)


HOLD = (
    "omx", "xt", "mask", "strad", "q", "k", "v", "pq", "pk", "att", "attt", "den", "sq", "hidt", "norm", "fin", "gelt", "slope", "fdn",
)
LATE = ("xt", "q", "k", "v", "pq", "pk", "att", "attt", "den", "omx", "mask", "strad")


def forward_kernel(
    scale, x_ref, wq_ref, wk_ref, wv_ref, wo_ref, win_ref, wdn_ref, bq_ref, bk_ref, bv_ref, bo_ref, g1_ref, o1_ref, bd_ref,
    g2_ref, o2_ref, bin_ref, ints_ref, cot_ref, len_ref, layer_ref, peak_ref, state_ref, inv_ref, res_ref, vec_ref, sums_ref, *rest,
):
    outs, rest = rest[: len(HOLD)], rest[len(HOLD) :]
    hold, rest = rest[: len(HOLD)], rest[len(HOLD) :]
    (
        omx_ref, xt_ref, mask_ref, strad_ref, q_ref, k_ref, v_ref, pq_ref, pk_ref, att_ref, attt_ref, den_ref, sq_ref, hidt_ref,
        norm_ref, fin_ref, gelt_ref, slope_ref, fdn_ref,
    ) = hold
    hid_ref, gel_ref, onehot_ref, stradrow_ref, send_ref, total_ref, land_ref = rest[:7]
    ssem, rsem, gs_sem, gr_sem, gl_sem, vs_sem, vr_sem, out_sem = rest[7:]
    at = Place()
    pairs = q_ref.shape[0]
    rows, width = x_ref.shape

    def stash(*names):
        return [pltpu.make_async_copy(hold[n], outs[n], out_sem.at[n]) for n in map(HOLD.index, names)]

    def give(*names):
        for copy in stash(*names):
            copy.start()

    blocks = []
    specs = [(w, sq_ref.at[n], 0, 768) for n, w in enumerate((wq_ref, wk_ref, wv_ref, wo_ref))]
    specs += [(win_ref, fin_ref, 768 * h, 768) for h in range(4)]
    specs += [
        (wdn_ref.at[pl.ds(96 * r, 96)], fdn_ref.at[:, :, :, pl.ds(96 * r, 96)], 384 * h, 384) for h in range(2) for r in range(2)
    ]
    for n, (own, full, base, span) in enumerate(specs):
        blocks.append(Gather(at, own, full, base, span, gs_sem.at[n], gr_sem.at[n], gl_sem.at[n]))
    peer_barrier(at.peers())
    vec = SmallSum(at, total_ref, land_ref, vs_sem, vr_sem, False)
    total_ref[0] = spread_vectors(
        at, (bq_ref, bk_ref, bv_ref, bo_ref, g1_ref, o1_ref, bd_ref, g2_ref, o2_ref), bin_ref
    ).astype(bf16)
    blocks[0].begin()
    vec.begin()
    for b in blocks[1:AHEAD]:
        b.begin()
    doc_setup(len_ref, at.y, mask_ref, onehot_ref, strad_ref, stradrow_ref)
    features_setup(ints_ref, omx_ref)
    for j in range(pairs):
        xt_ref[128 * j : 128 * j + 128] = x_ref[:, 128 * j : 128 * j + 128].T
    give("omx", "xt", "mask", "strad")
    sums_ref[...] = jnp.zeros_like(sums_ref)

    def vector(n, cols=slice(None)):
        return vec_ref[n : n + 1, cols].astype(f32)

    def project(n, o_ref):
        for j in range(pairs // 2):
            cols = slice(256 * j, 256 * j + 256)
            got = mul(x_ref[...], sq_ref[n, :, :, :, :, cols].reshape(768, 256))
            got = (got + vector(n, cols)).astype(bf16)
            o_ref[2 * j] = got[:, 0:128]
            o_ref[2 * j + 1] = got[:, 128:256]

    def tick(t):
        if t + AHEAD < len(blocks):
            blocks[t + AHEAD].begin()
        for k, name in enumerate(("stage_x", "stage_y", "stage_c", "ready")):
            if 0 <= t - k < len(blocks):
                getattr(blocks[t - k], name)()

    for t in range(3):
        tick(t)
        vec.step(t)
    vec_ref[...] = vec.result()
    for n, ref in enumerate((q_ref, k_ref, v_ref)):
        tick(3 + n)
        project(n, ref)
        give("qkv"[n])

    def copy(p):
        return remote(send_ref.at[p], state_ref.at[p], ssem.at[p], rsem.at[p], at.across)

    def ticks_at(p, plan):
        for n, t in plan.items():
            @pl.when(p == n)
            def _(t=t):
                tick(t)

    @pl.loop(0, pairs)
    def _(p):
        forward_states(p, scale, q_ref, k_ref, v_ref, omx_ref, onehot_ref, strad_ref, stradrow_ref, pq_ref, pk_ref, peak_ref, send_ref)
        copy(p).start()
        ticks_at(p, {0: 6, 2: 7, 4: 8})

    give("pq", "pk", "sq")

    @pl.loop(0, pairs)
    def _(p):
        copy(p).wait()
        forward_finish(p, scale, v_ref, pq_ref, pk_ref, mask_ref, strad_ref, peak_ref, state_ref, att_ref, den_ref)
        attt_ref[p] = att_ref[p].T
        ticks_at(p, {0: 9, 3: 10})

    give("att", "attt", "den", "fin")


    whole = jnp.concatenate([att_ref[p] for p in range(pairs)], axis=1)
    for j in range(pairs // 2):
        cols = slice(256 * j, 256 * j + 256)
        got = mul(whole, sq_ref[3, :, :, :, :, cols].reshape(768, 256))
        res_ref[:, cols] = got + vector(3, cols) + x_ref[:, cols].astype(f32)

    def centred(value):
        value = value - jnp.mean(value, axis=1, keepdims=True)
        inverse = lax.rsqrt(jnp.mean(value * value, axis=1, keepdims=True) + 1e-06)
        return value * inverse, inverse

    def here(r):
        return pl.ds(pl.multiple_of(128 * r, 128), 128)

    @pl.loop(0, rows // 128)
    def _(r):
        normed, inverse = centred(res_ref[here(r)])
        inv_ref[here(r)] = inverse
        norm_ref[here(r)] = normed.astype(bf16)
        hid_ref[here(r)] = (normed * vector(4) + vector(5)).astype(bf16)

    for j in range(pairs):
        hidt_ref[128 * j : 128 * j + 128] = hid_ref[:, 128 * j : 128 * j + 128].T
    give("hidt", "norm")


    @pl.loop(0, 4)
    def _(b):
        ticks_at(b, {0: 11, 2: 12})
        for j in range(3):
            cols = cols_at(768 * b + 256 * j, 256)
            pre = mul(hid_ref[...], fin_ref[:, :, :, :, cols].reshape(768, 256))
            bias = jnp.zeros((1, 256), f32)
            for n in range(4):
                bias = jnp.where(b == n, vector(9 + n, slice(256 * j, 256 * j + 256)), bias)
            pre = pre + bias
            share = 0.5 * (1.0 + lax.erf(pre * inv_root_two))
            gel = (pre * share).astype(bf16)
            gel_ref[:, cols] = gel
            gelt_ref[cols] = gel.T
            slope_ref[:, cols] = (share + pre * (jnp.exp(-0.5 * pre * pre) * inv_root_tau)).astype(bf16)

    give("gelt", "slope")

    def down(h):
        cols = slice(384 * h, 384 * h + 384)
        res_ref[:, cols] = hid_ref[:, cols].astype(f32) + vector(6, cols)

        @pl.loop(0, DEPTH)
        def _(z):
            got = mul(gel_ref[:, cols_at(768 * z, 768)], fdn_ref[z, :, :, :, cols].reshape(768, 384))
            res_ref[:, cols] = res_ref[:, cols] + got

    down(0)
    tick(13)
    tick(14)
    give("fdn")
    down(1)


    @pl.loop(0, rows // 128)
    def _(r):
        normed, inverse = centred(res_ref[here(r)])
        layer_ref[here(r)] = (normed * vector(7) + vector(8)).astype(bf16)
        grad = cot_ref[here(r)].astype(f32)
        scaled = grad * vector(7)
        centre = jnp.mean(scaled, axis=1, keepdims=True)
        lean = jnp.mean(scaled * normed, axis=1, keepdims=True)
        resid = inverse * (scaled - centre - normed * lean)
        res_ref[here(r)] = resid
        sums_ref[6:7] = sums_ref[6:7] + jnp.sum(resid.astype(bf16).astype(f32), axis=0, keepdims=True)
        sums_ref[7:8] = sums_ref[7:8] + jnp.sum(grad * normed, axis=0, keepdims=True)
        sums_ref[8:9] = sums_ref[8:9] + jnp.sum(grad, axis=0, keepdims=True)

    for b in blocks:
        b.drain()
    vec.drain()
    for one in stash(*HOLD):
        one.wait()


class Scatter:
    def __init__(self, at, order, source, twin_in, lands, done, done_in, put, ssem, rsem):
        self.at, self.order, self.source, self.acc = at, order, source, source(at.c)
        self.twin_in, self.lands = twin_in, lands
        self.done, self.done_in, self.put = done, done_in, put
        self.ssem, self.rsem = ssem, rsem
        self.half = twin_in.shape[-1] // 2
        self.sent = []

    def go(self, n, ends):
        src, dst, peer = ends()
        remote(src, dst, self.ssem.at[n], self.rsem.at[n], peer).start()
        self.sent.append((n, ends))

    def came(self, n, ref):
        remote(ref, ref, self.ssem.at[n], self.rsem.at[n], self.at.twin).wait_recv()

    def side(self, y):
        return cols_at(self.half * y, self.half)

    def spot(self, fixed, **other):
        at = self.at
        z = other.get("z", at.z if "z" in fixed else slice(None))
        x = other.get("x", at.x if "x" in fixed else slice(None))
        cols = self.side(other.get("y", at.y)) if "y" in fixed or "y" in other else slice(None)
        return z, x, slice(None), cols

    def first(self, i):
        return 1 + sum(DEPTH - 1 if kind == "z" else 1 for kind in self.order[:i])

    def send(self, i):
        at, kind, fixed = self.at, self.order[i], self.order[:i]
        if kind == "z":
            for d in range(1, DEPTH):
                self.go(
                    self.first(i) + d - 1,
                    lambda d=d: (self.acc.at[self.spot(fixed, z=at.other(d))], self.lands[i].at[d - 1], at.along(d)),
                )
        elif kind == "x":
            self.go(self.first(i), lambda: (self.acc.at[self.spot(fixed, x=1 - at.x)], self.lands[i], at.beside))
        else:
            self.go(self.first(i), lambda: (self.acc.at[self.spot(fixed, y=1 - at.y)], self.lands[i], at.across))

    def add(self, parts, fixed, store):
        def at_z(z):
            for x in [None] if "x" in fixed else range(2):
                spot = list(self.spot(fixed))
                inner = ()
                if z is not None:
                    spot[0] = z
                    inner += (z,)
                if x is not None:
                    spot[1] = x
                    inner += (x,)
                value = self.acc[tuple(spot)].astype(f32)
                for part in parts:
                    value = value + part[inner + (slice(None), slice(None))].astype(f32)
                store(tuple(spot), value)

        if "z" in fixed:
            at_z(None)
        else:
            pl.loop(0, DEPTH)(at_z)

    def keep(self, spot, value):
        self.acc[spot] = value.astype(bf16)

    def finish(self, spot, value):
        low = value.astype(bf16)
        self.done[...] = low
        self.put(self.at.y, low.astype(f32))

    def arrived(self, i):
        if self.order[i] != "z":
            self.came(self.first(i), self.lands[i])
            return [self.lands[i]]
        for d in range(1, DEPTH):
            self.came(self.first(i) + d - 1, self.lands[i].at[d - 1])
        return [self.lands[i].at[d - 1] for d in range(1, DEPTH)]

    def begin(self):
        self.go(0, lambda: (self.source(1 - self.at.c), self.twin_in, self.at.twin))

    def stage_1(self):
        self.came(0, self.twin_in)
        self.add([self.twin_in], "", self.keep)
        self.send(0)

    def stage_2(self):
        self.add(self.arrived(0), self.order[:1], self.keep)
        self.send(1)

    def stage_3(self):
        self.add(self.arrived(1), self.order[:2], self.keep)
        self.send(2)

    def stage_4(self):
        self.add(self.arrived(2), self.order, self.finish)
        self.go(2 + DEPTH, lambda: (self.done, self.done_in, self.at.across))

    def stage_5(self):
        self.came(2 + DEPTH, self.done_in)
        self.put(1 - self.at.y, self.done_in[...].astype(f32))

    def drain(self):
        for n, ends in self.sent:
            src, dst, peer = ends()
            remote(src, dst, self.ssem.at[n], self.rsem.at[n], peer).wait_send()


def landing(order, part, width):
    shapes = []
    for i, kind in enumerate(order):
        kept = order[: i + 1]
        shape = [] if "z" in kept else [DEPTH]
        shape += [] if "x" in kept else [2]
        shape += [part, width // 2 if "y" in kept else width]
        shapes.append(pltpu.VMEM(tuple([DEPTH - 1] + shape if kind == "z" else shape), bf16))
    return shapes


SCATTER_COPIES = DEPTH + 3
GELU_SLOTS = 4
FEED_SLOTS = 3
FEED_STEPS = (3, 7)
HEAD_STEPS = (0, 1, 2, 3, 4, 5)
PACE = ((0, 2, 4, 6, 8),) * 6 + ((0, 2, 3, 4, 5),) * 3 + ((0, 1, 2, 3, 4),) * 3
ORDERS = ("yxz", "xyz", "xyz") * 4


def backward_kernel(
    scale, peak_ref, state_ref, hidt_ref, norm_ref, inv_ref, res_ref, gain_ref, vecin_ref, gel_ref, slope_ref, win_ref, wdn_ref,
    sq_ref, *rest,
):
    late_refs, rest = rest[: len(LATE)], rest[len(LATE) :]
    gx_ref, oq_ref, ok_ref, ov_ref, oo_ref, oin_ref, odn_ref, vec_ref = rest[:8]
    kept_refs, rest = rest[8 : 8 + len(LATE)], rest[8 + len(LATE) :]
    xt_ref, q_ref, k_ref, v_ref, pq_ref, pk_ref, att_ref, attt_ref, den_ref, omx_ref, mask_ref, strad_ref = kept_refs
    gstate_ref, send_ref, gq_ref, gk_ref, gv_ref, gatt_ref, low_ref, wide_ref, gelbuf_ref, slopebuf_ref, winbuf_ref = rest[:11]
    gdn_ref, gin_ref, go_ref, gw_ref, total_ref, land_ref, twin_ref, done_ref, donein_ref = rest[11:20]
    ssem, rsem, load_sem, late_sem, keep_sem, ws_sem, wr_sem, vs_sem, vr_sem = rest[20:29]
    land_refs = rest[29:]
    at = Place()
    pairs = q_ref.shape[0]
    rows, width = res_ref.shape
    span = width // 2
    chunks = win_ref.shape[1] // span
    sources = [lambda c, b=b: gdn_ref.at[:, :, c, pl.ds(48 * b, 48)] for b in range(4)]
    sources += [lambda c, b=b: gin_ref.at[:, :, c, :, pl.ds(768 * b, 768)] for b in range(4)]
    sources += [lambda c: go_ref.at[:, :, c]]
    sources += [lambda c, n=n: gw_ref.at[n, :, :, c] for n in (2, 1, 0)]

    def putter(ref, row, col):
        def put(y, value):
            ref[pl.ds(row, 48), cols_at(col + 384 * y, 384)] = value

        return put

    puts = [putter(odn_ref, 48 * b, 0) for b in range(4)] + [putter(oin_ref, 0, 768 * b) for b in range(4)]
    puts += [putter(r, 0, 0) for r in (oo_ref, ov_ref, ok_ref, oq_ref)]
    units = []
    for n, (source, put) in enumerate(zip(sources, puts)):
        lands = land_refs[3 * n : 3 * n + 3]
        units.append(
            Scatter(
                at, ORDERS[n], source, twin_ref.at[n], lands, done_ref.at[n], donein_ref.at[n], put, ws_sem.at[n], wr_sem.at[n]
            )
        )
    early = len(units) - 3

    def step(s):
        for k in range(5):
            for u, unit in enumerate(units):
                if u + PACE[u][k] == s:
                    getattr(unit, "stage_" + str(k + 1))()


    def load(src, dst, sem):
        return pltpu.make_async_copy(src, dst, sem)

    def gelu_at(m):
        return lax.rem(m, GELU_SLOTS)

    def load_gelu(m):
        return load(
            gel_ref.at[pl.ds(pl.multiple_of(span * m, 128), span)], gelbuf_ref.at[gelu_at(m)], load_sem.at[0, gelu_at(m)]
        )

    def slot(m):
        return lax.rem(m, FEED_SLOTS)

    def down_at(m):
        n = slot(m)
        return 2 * lax.div(n, 2), pl.ds(pl.multiple_of(span * lax.rem(n, 2), 128), span)

    def load_chunk(m):
        return [
            load(slope_ref.at[:, cols_at(span * m, span)], slopebuf_ref.at[slot(m)], load_sem.at[1, slot(m)]),
            load(wdn_ref.at[pl.ds(pl.multiple_of(span * m, 128), span)], wide_ref.at[down_at(m)], load_sem.at[2, slot(m)]),
            load(win_ref.at[:, cols_at(span * m, span)], winbuf_ref.at[slot(m)], load_sem.at[3, slot(m)]),
        ]

    def load_square(n, to):
        return load(sq_ref.at[n], wide_ref.at[to], late_sem.at[to])

    peer_barrier(at.peers())
    first = load(res_ref, gx_ref, late_sem.at[0])
    first.start()
    for m in range(GELU_SLOTS - 1):
        load_gelu(jnp.int32(m)).start()
    for m in range(FEED_SLOTS - 1):
        for one in load_chunk(jnp.int32(m)):
            one.start()
    load_square(3, 1).start()
    kept = [load(src, dst, keep_sem.at[n]) for n, (src, dst) in enumerate(zip(late_refs, kept_refs))]
    for one in kept:
        one.start()
    total_ref[0] = vecin_ref[...]

    first.wait()

    @pl.loop(0, rows // 128)
    def _(r):
        here = pl.ds(pl.multiple_of(128 * r, 128), 128)
        low_ref[here] = gx_ref[here].astype(bf16)


    @pl.loop(0, chunks)
    def _(m):
        load_gelu(m).wait()

        @pl.when(m < chunks - (GELU_SLOTS - 1))
        def _():
            load_gelu(m + GELU_SLOTS - 1).start()

        turned = gelbuf_ref[gelu_at(m)]
        for n in range(3):
            cols = slice(256 * n, 256 * n + 256)
            got = mul(turned, low_ref[:, cols]).astype(bf16)
            gdn_ref[lax.div(m, 2), lax.rem(m, 2), :, :, cols] = got.reshape(2, span // 2, 256)

    units[0].begin()
    units[1].begin()
    @pl.loop(0, chunks)
    def _(m):
        for one in load_chunk(m):
            one.wait()

        @pl.when(m < chunks - (FEED_SLOTS - 1))
        def _():
            for one in load_chunk(m + FEED_SLOTS - 1):
                one.start()

        start = pl.multiple_of(span * lax.rem(m, 2), 128)
        gpre = mul_tb(low_ref[...], wide_ref[down_at(m)]) * slopebuf_ref[slot(m)].astype(f32)
        gpre = gpre.astype(bf16)
        total_ref[0, pl.ds(9 + lax.div(m, 2), 1), cols_at(start, span)] = jnp.sum(gpre.astype(f32), axis=0, keepdims=True)
        got = mul(hidt_ref[...], gpre).astype(bf16)
        gin_ref[:, :, :, :, cols_at(span * m, span)] = got.reshape(DEPTH, 2, 2, 48, span)
        for n in range(3):
            cols = slice(256 * n, 256 * n + 256)
            gx_ref[:, cols] = gx_ref[:, cols] + mul_tb(gpre, winbuf_ref[slot(m), cols])
        for n in range(8):
            @pl.when(m == n)
            def _(n=n):
                if n < 2:
                    units[2 + n].begin()
                if n % 2:
                    units[4 + n // 2].begin()
                if n in FEED_STEPS:
                    step(FEED_STEPS.index(n))

    done_steps = len(FEED_STEPS)

    @pl.loop(0, rows // 128)
    def _(r):
        here = pl.ds(pl.multiple_of(128 * r, 128), 128)
        grad = gx_ref[here]
        normed = norm_ref[here].astype(f32)
        scaled = grad * gain_ref[4:5].astype(f32)
        centre = jnp.mean(scaled, axis=1, keepdims=True)
        slope = jnp.mean(scaled * normed, axis=1, keepdims=True)
        resid = inv_ref[here] * (scaled - centre - normed * slope)
        gx_ref[here] = resid
        low = resid.astype(bf16)
        low_ref[here] = low
        total_ref[0, 3:4] = total_ref[0, 3:4] + jnp.sum(low.astype(f32), axis=0, keepdims=True)
        total_ref[0, 4:5] = total_ref[0, 4:5] + jnp.sum(grad * normed, axis=0, keepdims=True)
        total_ref[0, 5:6] = total_ref[0, 5:6] + jnp.sum(grad, axis=0, keepdims=True)

    load_square(3, 1).wait()
    for one in kept:
        one.wait()
    for h in range(2):
        turned = attt_ref[3 * h : 3 * h + 3].reshape(384, rows)
        for n in range(3):
            cols = slice(256 * n, 256 * n + 256)
            go_ref[2 * h : 2 * h + 2, :, :, :, cols] = mul(turned, low_ref[:, cols]).astype(bf16).reshape(2, 2, 2, 48, 256)
    units[8].begin()
    for j in range(pairs // 2):
        got = mul_tb(low_ref[...], wide_ref[1, 256 * j : 256 * j + 256]).astype(bf16)
        gatt_ref[2 * j] = got[:, 0:128]
        gatt_ref[2 * j + 1] = got[:, 128:256]
    for n in range(3):
        load_square(n, n).start()
    step(done_steps)
    done_steps += 1


    def copy(p):
        return remote(send_ref.at[p], gstate_ref.at[p], ssem.at[p], rsem.at[p], at.across)

    @pl.loop(0, pairs)
    def _(p):
        backward_states(p, scale, att_ref, den_ref, gatt_ref, pq_ref, strad_ref, peak_ref, state_ref, send_ref)
        copy(p).start()

    @pl.loop(0, pairs)
    def _(p):
        copy(p).wait()
        backward_finish(
            p, scale, q_ref, k_ref, v_ref, omx_ref, pq_ref, pk_ref, mask_ref, strad_ref, peak_ref, state_ref, gstate_ref,
            att_ref, den_ref, gatt_ref, gq_ref, gk_ref, gv_ref,
        )
        cols = cols_at(128 * p, 128)
        both = mul(xt_ref[...], jnp.concatenate([gq_ref[p], gk_ref[p]], axis=1)).astype(bf16)
        gw_ref[0, :, :, :, :, cols] = both[:, 0:128].reshape(DEPTH, 2, 2, 48, 128)
        gw_ref[1, :, :, :, :, cols] = both[:, 128:256].reshape(DEPTH, 2, 2, 48, 128)
        gw_ref[2, :, :, :, :, cols] = mul(xt_ref[...], gv_ref[p]).astype(bf16).reshape(DEPTH, 2, 2, 48, 128)
        for n, ref in enumerate((gq_ref, gk_ref, gv_ref)):
            total_ref[0, n : n + 1, cols] = jnp.sum(ref[p].astype(f32), axis=0, keepdims=True)
        for n, at_pair in enumerate(HEAD_STEPS):
            @pl.when(p == at_pair)
            def _(n=n):
                step(n + done_steps)

    vec = SmallSum(at, total_ref, land_ref, vs_sem, vr_sem, True)
    vec.begin()
    for u in units[early:]:
        u.begin()
    for n in range(3):
        load_square(n, n).wait()

    def grad_input(j):
        cols = slice(256 * j, 256 * j + 256)
        value = gx_ref[:, cols]
        for n, ref in enumerate((gq_ref, gk_ref, gv_ref)):
            for i in range(pairs // 2):
                left = jnp.concatenate([ref[2 * i], ref[2 * i + 1]], axis=1)
                right = wide_ref[n, 256 * j : 256 * j + 256, 256 * i : 256 * i + 256]
                value = value + mul_tb(left, right)
        gx_ref[:, cols] = value

    done_steps += len(HEAD_STEPS)
    for n, s in enumerate(range(done_steps, len(units) + PACE[-1][-1])):
        step(s)
        if n < 4:
            vec.step(n)
        if n < 3:
            grad_input(n)
    vec_ref[...] = vec.result()
    for u in units:
        u.drain()
    vec.drain()


def scratch_masks(rows, heads, feats):
    return [
        pltpu.VMEM((heads, 256, feats), bf16),
        pltpu.VMEM((rows, rows), bf16),
        pltpu.VMEM((rows, 128), f32),
        pltpu.VMEM((rows, 128), f32),
        pltpu.VMEM((TAIL, rows), bf16),
    ]


def vmem():
    return pl.BlockSpec(memory_space=pltpu.VMEM)


def anywhere():
    return pl.BlockSpec(memory_space=pl.ANY)


def smem():
    return pl.BlockSpec(memory_space=pltpu.SMEM)


def attention_forward(x, weights, vectors, ints, cot, lengths):
    rows, width = x.shape
    heads, size, feats = ints.shape
    pairs = heads // 2
    hidden = weights[4].shape[1]
    part = weights[0].shape[0]
    scale = size ** (-0.25) * unit_spread
    shape = jax.ShapeDtypeStruct
    grid = (DEPTH, 2, 2)
    dma = pltpu.SemaphoreType.DMA
    pair, phi, full, tall = (pairs, rows, 128), (pairs, 2, rows, feats), (rows, width), (rows, hidden)
    held = {
        "omx": (heads, 256, feats), "xt": (width, rows), "mask": (rows, rows), "strad": (rows, 128), "q": pair, "k": pair, "v": pair, "pq": phi, "pk": phi, "att": pair,
        "attt": (pairs, 128, rows), "den": pair, "sq": (4, *grid, part, width), "hidt": (width, rows), "norm": full,
        "fin": (*grid, part, hidden), "gelt": (hidden, rows), "slope": tall,
        "fdn": (*grid, weights[5].shape[0], width),
    }
    kind = {name: f32 if name in ("den", "strad") else bf16 for name in HOLD}
    layer, peak, state, inverse, resid, vec, sums, *rest = pl.pallas_call(
        partial(forward_kernel, scale),
        out_shape=[
            shape(full, bf16), shape((pairs, 2, 1, feats), f32), shape((pairs, 128 + TAIL, feats), bf16),
            shape((rows, 1), f32), shape(full, f32), shape((16, width), bf16), shape((16, width), f32),
        ] + [shape(held[name], kind[name]) for name in HOLD],
        in_specs=[vmem()] * 19 + [smem()],
        out_specs=[vmem()] * 7 + [anywhere()] * len(HOLD),
        scratch_shapes=[pltpu.VMEM(held[name], kind[name]) for name in HOLD] + [
            pltpu.VMEM(full, bf16), pltpu.VMEM(tall, bf16),
            pltpu.VMEM((rows, 128), f32), pltpu.VMEM((TAIL, rows), bf16),
            pltpu.VMEM((pairs, 128 + TAIL, feats), bf16),
            pltpu.VMEM((4, 16, width), bf16),
            pltpu.VMEM((DEPTH + 1, 16, width), bf16),
            dma((pairs,)), dma((pairs,)),
            dma((12, GATHER_COPIES)), dma((12, GATHER_COPIES)), dma((12,)),
            dma((DEPTH + 1,)), dma((DEPTH + 1,)), dma((len(HOLD),)),
        ],
        compiler_params=pltpu.CompilerParams(collective_id=0, has_side_effects=True, vmem_limit_bytes=65200 << 10),
        name="attention_forward",
    )(x, *weights, *vectors, ints, cot, lengths)
    got = dict(zip(HOLD, rest))
    inner = (peak, state, got["hidt"], got["norm"], inverse, resid, vec, sums)
    late = (
        got["gelt"], got["slope"], got["fin"].reshape(width, hidden), got["fdn"].reshape(hidden, width),
        got["sq"].reshape(4, width, width), *(got[name] for name in LATE),
    )
    return layer, inner, late


def attention_backward(inner, late):
    rows, width = inner[5].shape
    pairs, _, _, feats = inner[0].shape
    heads, hidden = 2 * pairs, late[0].shape[0]
    scale = (width // heads) ** (-0.25) * unit_spread
    shape = jax.ShapeDtypeStruct
    dma = pltpu.SemaphoreType.DMA
    grid = (DEPTH, 2, 2)
    part = width // 16
    units = 12
    return pl.pallas_call(
        partial(backward_kernel, scale),
        out_shape=[shape((rows, width), f32)]
        + [shape((part, width), f32)] * 4
        + [shape((part, hidden), f32), shape((hidden // 16, width), f32), shape((16, width), f32)],
        in_specs=[vmem()] * 5 + [anywhere()] + [vmem()] * 2 + [anywhere()] * (5 + len(LATE)),
        out_specs=[vmem()] * 8,
        scratch_shapes=[pltpu.VMEM(one.shape, one.dtype) for one in late[5:]] + [
            pltpu.VMEM((pairs, 128 + TAIL, feats), bf16), pltpu.VMEM((pairs, 128 + TAIL, feats), bf16),
            pltpu.VMEM((pairs, rows, 128), bf16), pltpu.VMEM((pairs, rows, 128), bf16), pltpu.VMEM((pairs, rows, 128), bf16),
            pltpu.VMEM((pairs, rows, 128), bf16),
            pltpu.VMEM((rows, width), bf16),
            pltpu.VMEM((3, width, width), bf16),
            pltpu.VMEM((GELU_SLOTS, width // 2, rows), bf16), pltpu.VMEM((FEED_SLOTS, rows, width // 2), bf16),
            pltpu.VMEM((FEED_SLOTS, width, width // 2), bf16),
            pltpu.VMEM((*grid, hidden // 16, width), bf16),
            pltpu.VMEM((*grid, part, hidden), bf16),
            pltpu.VMEM((*grid, part, width), bf16),
            pltpu.VMEM((3, *grid, part, width), bf16),
            pltpu.VMEM((5, 16, width), f32),
            pltpu.VMEM((DEPTH + 2, 16, width), f32),
            pltpu.VMEM((units, DEPTH, 2, part, width), bf16),
            pltpu.VMEM((units, part, width // 2), bf16),
            pltpu.VMEM((units, part, width // 2), bf16),
            dma((pairs,)), dma((pairs,)), dma((4, GELU_SLOTS)), dma((3,)), dma((len(LATE),)),
            dma((units, SCATTER_COPIES)), dma((units, SCATTER_COPIES)),
            dma((DEPTH + 2,)), dma((DEPTH + 2,)),
        ] + [land for order in ORDERS for land in landing(order, part, width)],
        compiler_params=pltpu.CompilerParams(collective_id=1, has_side_effects=True, vmem_limit_bytes=65200 << 10),
        name="attention_backward",
    )(*inner, *late)


def finish_kernel(sums_ref, *refs):
    big = BIG
    ins, outs, vectors, sem = refs[:big], refs[big : 2 * big], refs[2 * big : -1], refs[-1]
    copies = [pltpu.make_async_copy(src, dst, sem.at[n]) for n, (src, dst) in enumerate(zip(ins, outs))]
    for one in copies:
        one.start()
    me = lax.axis_index("fsdp")
    part, wide = vectors[0].shape[1], vectors[9].shape[1]
    width = sums_ref.shape[1]
    sums = sums_ref[...]
    turned = pltpu.roll(sums, lax.rem(width - part * me, width), 1)
    for n in range(9):
        vectors[n][...] = turned[n : n + 1, 0:part]
    inner = pltpu.roll(sums, lax.rem(width - wide * lax.rem(me, 4), width), 1)
    row = jnp.zeros((1, width), f32)
    for n in range(DEPTH):
        row = jnp.where(lax.div(me, 4) == n, inner[9 + n : 10 + n], row)
    vectors[9][...] = row[:, 0:wide]
    for one in copies:
        one.wait()


BIG = 8


def finish(arrays, sums, part, wide):
    shape = jax.ShapeDtypeStruct
    return pl.pallas_call(
        finish_kernel,
        out_shape=[shape(a.shape, a.dtype) for a in arrays] + [shape((1, part), f32)] * 9 + [shape((1, wide), f32)],
        in_specs=[vmem()] + [anywhere()] * BIG,
        out_specs=[vmem()] * (BIG + 10),
        scratch_shapes=[pltpu.SemaphoreType.DMA((BIG,))],
        name="finish",
    )(sums, *arrays)


def to_pairs(rows):
    return rows.reshape(rows.shape[0], -1, 128).transpose(1, 0, 2)


def from_pairs(pairs):
    return pairs.transpose(1, 0, 2).reshape(pairs.shape[1], -1)


def per_device(
    tokens, doc_lengths, feature_ints, w_query, b_query, w_key, b_key, w_value, b_value, w_out, b_out,
    norm1_gain, norm1_bias, w_in, b_in, w_down, b_down, norm2_gain, norm2_bias, cotangent,
):
    layer_out, inner, late = attention_forward(
        tokens[0],
        (w_query, w_key, w_value, w_out, w_in, w_down),
        (b_query, b_key, b_value, b_out, norm1_gain, norm1_bias, b_down, norm2_gain, norm2_bias, b_in),
        feature_ints, cotangent[0], doc_lengths,
    )
    *grads, sums = attention_backward(inner, late)
    done = finish((layer_out, *grads), sums, b_query.shape[0], b_in.shape[0])
    layer_out, grad_input, gq, gk, gv, go, gin, gdn = done[:BIG]
    bq, bk, bv, bo, g1, o1, bd, g2, o2, bi = (one.reshape(-1) for one in done[BIG:])
    return (
        layer_out[None], grad_input[None],
        gq, bq, gk, bk, gv, bv, go, bo, g1, o1, gin, bi, gdn, bd, g2, o2,
    )


def forward_kernel_wide(
    scale, x_ref, wq_ref, wk_ref, wv_ref, bias_ref, ints_ref, len_ref,
    q_ref, k_ref, v_ref, pq_ref, pk_ref, att_ref, den_ref, peak_ref, state_ref,
    omx_ref, mask_ref, onehot_ref, strad_ref, stradrow_ref, send_ref, ssem, rsem,
):
    place = lax.axis_index("seq")
    peer = {"seq": 1 - place}
    peer_barrier([peer])
    pairs = q_ref.shape[0]
    doc_setup(len_ref, place, mask_ref, onehot_ref, strad_ref, stradrow_ref)
    features_setup(ints_ref, omx_ref)
    for n, (w_ref, o_ref) in enumerate(((wq_ref, q_ref), (wk_ref, k_ref), (wv_ref, v_ref))):
        for j in range(pairs // 2):
            cols = slice(256 * j, 256 * j + 256)
            got = (mul(x_ref[...], w_ref[:, cols]) + bias_ref[n : n + 1, cols].astype(f32)).astype(bf16)
            o_ref[2 * j] = got[:, 0:128]
            o_ref[2 * j + 1] = got[:, 128:256]

    def copy(p):
        return pltpu.make_async_remote_copy(
            src_ref=send_ref.at[p], dst_ref=state_ref.at[p], send_sem=ssem.at[p], recv_sem=rsem.at[p],
            device_id=peer, device_id_type=MESH,
        )

    @pl.loop(0, pairs)
    def _(p):
        forward_states(p, scale, q_ref, k_ref, v_ref, omx_ref, onehot_ref, strad_ref, stradrow_ref, pq_ref, pk_ref, peak_ref, send_ref)
        copy(p).start()

    @pl.loop(0, pairs)
    def _(p):
        copy(p).wait()
        forward_finish(p, scale, v_ref, pq_ref, pk_ref, mask_ref, strad_ref, peak_ref, state_ref, att_ref, den_ref)


def backward_kernel_wide(
    scale, q_ref, k_ref, v_ref, pq_ref, pk_ref, att_ref, den_ref, peak_ref, state_ref, gatt_ref, ints_ref, len_ref,
    gq_ref, gk_ref, gv_ref,
    gstate_ref, omx_ref, mask_ref, onehot_ref, strad_ref, stradrow_ref, send_ref, ssem, rsem,
):
    place = lax.axis_index("seq")
    peer = {"seq": 1 - place}
    peer_barrier([peer])
    pairs = q_ref.shape[0]
    doc_setup(len_ref, place, mask_ref, onehot_ref, strad_ref, stradrow_ref)
    features_setup(ints_ref, omx_ref)

    def copy(p):
        return pltpu.make_async_remote_copy(
            src_ref=send_ref.at[p], dst_ref=gstate_ref.at[p], send_sem=ssem.at[p], recv_sem=rsem.at[p],
            device_id=peer, device_id_type=MESH,
        )

    @pl.loop(0, pairs)
    def _(p):
        backward_states(p, scale, att_ref, den_ref, gatt_ref, pq_ref, strad_ref, peak_ref, state_ref, send_ref)
        copy(p).start()

    @pl.loop(0, pairs)
    def _(p):
        copy(p).wait()
        backward_finish(
            p, scale, q_ref, k_ref, v_ref, omx_ref, pq_ref, pk_ref, mask_ref, strad_ref, peak_ref, state_ref, gstate_ref,
            att_ref, den_ref, gatt_ref, gq_ref, gk_ref, gv_ref,
        )


def attention_forward_wide(x, wq, wk, wv, biases, ints, lengths):
    rows = x.shape[0]
    heads, size, feats = ints.shape
    pairs = heads // 2
    scale = size ** (-0.25) * unit_spread
    shape = jax.ShapeDtypeStruct
    return pl.pallas_call(
        partial(forward_kernel_wide, scale),
        out_shape=[
            shape((pairs, rows, 128), bf16), shape((pairs, rows, 128), bf16), shape((pairs, rows, 128), bf16),
            shape((pairs, 2, rows, feats), bf16), shape((pairs, 2, rows, feats), bf16),
            shape((pairs, rows, 128), bf16), shape((pairs, rows, 128), f32),
            shape((pairs, 2, 1, feats), f32), shape((pairs, 128 + TAIL, feats), bf16),
        ],
        in_specs=[vmem()] * 6 + [pl.BlockSpec(memory_space=pltpu.SMEM)],
        out_specs=[vmem()] * 9,
        scratch_shapes=scratch_masks(rows, heads, feats) + [
            pltpu.VMEM((pairs, 128 + TAIL, feats), bf16),
            pltpu.SemaphoreType.DMA((pairs,)),
            pltpu.SemaphoreType.DMA((pairs,)),
        ],
        compiler_params=pltpu.CompilerParams(collective_id=0, has_side_effects=True, vmem_limit_bytes=60 << 20),
        name="attention_forward",
    )(x, wq, wk, wv, biases, ints, lengths)


def attention_backward_wide(saved, gatt, ints, lengths):
    pairs, rows, _ = gatt.shape
    heads, size, feats = ints.shape
    scale = size ** (-0.25) * unit_spread
    shape = jax.ShapeDtypeStruct
    return pl.pallas_call(
        partial(backward_kernel_wide, scale),
        out_shape=[shape((pairs, rows, 128), bf16)] * 3,
        in_specs=[vmem()] * 11 + [pl.BlockSpec(memory_space=pltpu.SMEM)],
        out_specs=[vmem()] * 3,
        scratch_shapes=[pltpu.VMEM((pairs, 128 + TAIL, feats), bf16)] + scratch_masks(rows, heads, feats) + [
            pltpu.VMEM((pairs, 128 + TAIL, feats), bf16),
            pltpu.SemaphoreType.DMA((pairs,)),
            pltpu.SemaphoreType.DMA((pairs,)),
        ],
        compiler_params=pltpu.CompilerParams(collective_id=1, has_side_effects=True, vmem_limit_bytes=60 << 20),
        name="attention_backward",
    )(*saved, gatt, ints, lengths)


def gathered(piece):
    return lax.all_gather(piece, "fsdp", axis=0, tiled=True)


def per_device_wide(
    tokens, doc_lengths, feature_ints, w_query, b_query, w_key, b_key, w_value, b_value, w_out, b_out,
    norm1_gain, norm1_bias, w_in, b_in, w_down, b_down, norm2_gain, norm2_bias, cotangent,
):
    row_block = tokens[0]
    width = row_block.shape[1]
    fsdp = lax.axis_size("fsdp")
    me = lax.axis_index("fsdp")
    attn_stack = gathered(jnp.stack([w_query, w_key, w_value, w_out], axis=1))
    query_weight, key_weight, value_weight, out_weight = (attn_stack[:, i] for i in range(4))
    small = jnp.concatenate(
        [b_query, b_key, b_value, b_out, norm1_gain, norm1_bias, b_down, norm2_gain, norm2_bias, b_in]
    )
    small = lax.all_gather(small[None], "fsdp", axis=0, tiled=True)
    part = width // fsdp
    vectors = [small[:, part * i : part * (i + 1)].reshape(-1) for i in range(9)] + [small[:, 9 * part :].reshape(-1)]
    query_bias, key_bias, value_bias, out_bias, gain_one, offset_one, down_bias, gain_two, offset_two, in_bias = vectors
    saved = attention_forward_wide(
        row_block, query_weight, key_weight, value_weight, jnp.stack([query_bias, key_bias, value_bias]),
        feature_ints, doc_lengths,
    )
    att_rows = from_pairs(saved[5])
    residual_one = row_block.astype(f32) + affine(att_rows, out_weight, out_bias)
    hidden_wide, normed_one, inverse_one = layer_norm(residual_one, gain_one, offset_one)
    hidden_low = hidden_wide.astype(bf16)
    in_weight = gathered(w_in)
    down_weight = gathered(w_down)
    pre_act = affine(hidden_low, in_weight, in_bias)
    gelu_low = gelu_value(pre_act).astype(bf16)
    residual_two = hidden_low.astype(f32) + affine(gelu_low, down_weight, down_bias)
    layer_wide, normed_two, inverse_two = layer_norm(residual_two, gain_two, offset_two)
    grad_out = cotangent[0].astype(f32)
    grad_resid_two, grad_gain_two, grad_offset_two = norm_back(grad_out, normed_two, inverse_two, gain_two)
    grad_down_low = grad_resid_two.astype(bf16)
    grad_down_weight = mul_ta(gelu_low, grad_down_low)
    grad_down_bias = column_total(grad_down_low)
    grad_pre_low = (mul_tb(grad_down_low, down_weight) * gelu_slope(pre_act)).astype(bf16)
    grad_in_weight = mul_ta(hidden_low, grad_pre_low)
    grad_in_bias = column_total(grad_pre_low)
    grad_hidden = mul_tb(grad_pre_low, in_weight) + grad_resid_two
    grad_resid_one, grad_gain_one, grad_offset_one = norm_back(grad_hidden, normed_one, inverse_one, gain_one)
    grad_proj_low = grad_resid_one.astype(bf16)
    grad_out_weight = mul_ta(att_rows, grad_proj_low)
    grad_out_bias = column_total(grad_proj_low)
    grad_att_rows = mul_tb(grad_proj_low, out_weight).astype(bf16)
    grads = attention_backward_wide(saved, to_pairs(grad_att_rows), feature_ints, doc_lengths)
    grad_query_rows, grad_key_rows, grad_value_rows = (from_pairs(g) for g in grads)
    grad_query_weight = mul_ta(row_block, grad_query_rows)
    grad_key_weight = mul_ta(row_block, grad_key_rows)
    grad_value_weight = mul_ta(row_block, grad_value_rows)
    grad_input = (
        mul_tb(grad_query_rows, query_weight)
        + mul_tb(grad_key_rows, key_weight)
        + mul_tb(grad_value_rows, value_weight)
        + grad_resid_one
    )

    def owned(grad):
        shard = lax.psum_scatter(grad.astype(bf16), "fsdp", scatter_dimension=0, tiled=True)
        return lax.psum(shard, "seq").astype(f32)

    sums = jnp.stack(
        [
            column_total(grad_query_rows), column_total(grad_key_rows), column_total(grad_value_rows), grad_out_bias,
            grad_gain_one, grad_offset_one, grad_down_bias, grad_gain_two, grad_offset_two,
            *grad_in_bias.reshape(-1, width),
        ]
    )
    sums = lax.psum(sums, ("fsdp", "seq"))
    mine = [lax.dynamic_slice(sums[i], (me * part,), (part,)) for i in range(9)]
    wide = in_bias.shape[0] // fsdp
    mine_in = lax.dynamic_slice(sums[9:].reshape(-1), (me * wide,), (wide,))
    return (
        layer_wide.astype(bf16)[None],
        grad_input[None],
        owned(grad_query_weight), mine[0],
        owned(grad_key_weight), mine[1],
        owned(grad_value_weight), mine[2],
        owned(grad_out_weight), mine[3],
        mine[4], mine[5],
        owned(grad_in_weight), mine_in,
        owned(grad_down_weight), mine[6],
        mine[7], mine[8],
    )


def solution(mesh):
    rows, matrix, vector = P("fsdp", "seq", None), P("fsdp", None), P("fsdp")
    weights = (matrix, vector) * 4 + (vector, vector) + (matrix, vector) * 2 + (vector, vector)
    near = mesh.shape["fsdp"] == 4 * DEPTH and mesh.shape["seq"] == 2
    return jax.shard_map(
        per_device if near else per_device_wide,
        mesh=mesh,
        in_specs=(rows, matrix, P(), *weights, rows),
        out_specs=(rows, rows, *weights),
        check_vma=False,
    )
```

```python
from functools import partial

import jax
import jax.numpy as jnp
from jax import lax
from jax.experimental import pallas as pl
from jax.experimental.pallas import tpu as pltpu
from jax.sharding import PartitionSpec as P

unit_spread = 0.013531646934131853
inv_root_two = 0.7071067811865476
inv_root_tau = 0.3989422804014327
far_below = -1e30
log2_e = 1.4426950408889634
MESH = pl.DeviceIdType.MESH
f32 = jnp.float32
bf16 = jnp.bfloat16
TAIL = 16
DEPTH = 4
AHEAD = 1


def layer_norm(residual, norm_gain, norm_bias):
    centred = residual - jnp.mean(residual, axis=1, keepdims=True)
    inverse = lax.rsqrt(jnp.mean(centred * centred, axis=1, keepdims=True) + 1e-06)
    normed = centred * inverse
    return (normed * norm_gain.astype(f32) + norm_bias.astype(f32), normed, inverse)


def norm_back(grad_out, normed, inverse, norm_gain):
    scaled = grad_out * norm_gain.astype(f32)
    centre_part = jnp.mean(scaled, axis=1, keepdims=True)
    slope_part = jnp.mean(scaled * normed, axis=1, keepdims=True)
    grad_resid = inverse * (scaled - centre_part - normed * slope_part)
    return (grad_resid, jnp.sum(grad_out * normed, axis=0), jnp.sum(grad_out, axis=0))


def gelu_value(pre_act):
    return 0.5 * pre_act * (1.0 + lax.erf(pre_act * inv_root_two))


def gelu_slope(pre_act):
    return (
        0.5 * (1.0 + lax.erf(pre_act * inv_root_two))
        + pre_act * jnp.exp(-0.5 * pre_act * pre_act) * inv_root_tau
    )


def mul(a, b):
    return lax.dot_general(a, b, (((1,), (0,)), ((), ())), preferred_element_type=f32)


def mul_tb(a, b):
    return lax.dot_general(a, b, (((1,), (1,)), ((), ())), preferred_element_type=f32)


def mul_ta(a, b):
    return lax.dot_general(a, b, (((0,), (0,)), ((), ())), preferred_element_type=f32)


def affine(row_block, weight, bias_row):
    return mul(row_block, weight) + bias_row.astype(f32)


def column_total(values):
    return jnp.sum(values, axis=0, dtype=f32)


def lane_ids(shape):
    return lax.broadcasted_iota(jnp.int32, shape, len(shape) - 1)


def doc_setup(lengths, place, mask_ref, onehot_ref, strad_ref, stradrow_ref):
    rows = mask_ref.shape[0]
    docs = lengths.shape[1]
    total = jnp.int32(0)
    ends = []
    for d in range(docs):
        total = total + lengths[0, d]
        ends.append(total)
    pos = lax.broadcasted_iota(jnp.int32, (rows, 128), 0) + place * rows
    pos_row = lax.broadcasted_iota(jnp.int32, (8, rows), 1) + place * rows
    did = jnp.zeros((rows, 128), jnp.int32)
    did_row = jnp.zeros((8, rows), jnp.int32)
    edge = jnp.int32(0)
    for end in ends[:-1]:
        did = did + (pos >= end).astype(jnp.int32)
        did_row = did_row + (pos_row >= end).astype(jnp.int32)
        edge = edge + (end <= rows).astype(jnp.int32)
    for j in range(rows // 128):
        cols = did_row[0:1, j * 128 : (j + 1) * 128]
        mask_ref[:, j * 128 : (j + 1) * 128] = (did == cols).astype(f32).astype(bf16)
    onehot_ref[...] = (did == lane_ids((rows, 128))).astype(f32)
    strad_ref[...] = (did == edge).astype(f32)
    one_row = (did_row[0:1] == edge).astype(f32)
    stradrow_ref[...] = jnp.broadcast_to(one_row, stradrow_ref.shape).astype(bf16)


def features_setup(ints_ref, omx_ref):
    heads, size, feats = ints_ref.shape

    @pl.loop(0, heads)
    def _(h):
        mat = ints_ref[h].astype(f32).astype(bf16)
        zero = jnp.zeros((size, feats), bf16)
        odd = lax.rem(h, 2) == 1
        omx_ref[h, 0:size] = jnp.where(odd, zero, mat)
        omx_ref[h, size : 2 * size] = jnp.where(odd, mat, zero)
        omx_ref[h, 2 * size :] = jnp.ones((2 * size, feats), bf16)


def three_terms(value):
    first = value.astype(bf16).astype(f32)
    second = (value - first).astype(bf16).astype(f32)
    return first, second, value - first - second


def forward_states(p, scale, q_ref, k_ref, v_ref, omx_ref, onehot_ref, strad_ref, stradrow_ref, pq_ref, pk_ref, peak_ref, out_ref):
    rows = q_ref.shape[1]
    lanes = lane_ids((1, 128))
    qp, kp, vp = q_ref[p], k_ref[p], v_ref[p]
    kf = kp.astype(f32)
    ksq = kf * kf
    vt = jnp.concatenate([vp.T * stradrow_ref[0:1], stradrow_ref[...]], axis=0)
    tail = jnp.zeros((TAIL, pq_ref.shape[-1]), f32)
    tail_row = lax.broadcasted_iota(jnp.int32, tail.shape, 0)
    for j in range(2):
        om = omx_ref[2 * p + j, 0:128]
        raw_q = mul(qp, om)
        raw_q = raw_q - jnp.max(raw_q, axis=1, keepdims=True)
        pq_ref[p, j] = jnp.exp2(raw_q * (scale * log2_e)).astype(bf16)
        here = (lanes >= 64) if j else (lanes < 64)
        half = jnp.sum(jnp.where(here, ksq, 0.0), axis=1, keepdims=True) * (0.0625 / scale)
        raw_k = mul(kp, om) - half
        row_peak = jnp.max(raw_k, axis=1, keepdims=True)
        doc_peak = jnp.max(jnp.where(onehot_ref[...] > 0.5, row_peak, far_below), axis=0, keepdims=True)
        back = jnp.max(jnp.where(onehot_ref[...] > 0.5, doc_peak, far_below), axis=1, keepdims=True)
        edge_peak = jnp.max(jnp.where(strad_ref[...] > 0.5, row_peak, far_below), axis=0, keepdims=True)
        phi_k = jnp.exp2((raw_k - back) * (scale * log2_e)).astype(bf16)
        pk_ref[p, j] = phi_k
        part = mul(vt, phi_k)
        out_ref[p, 64 * j : 64 * j + 64] = part[64 * j : 64 * j + 64].astype(bf16)
        edge_wide = jnp.concatenate([edge_peak, edge_peak], axis=1)
        peak_ref[p, j] = edge_wide
        tail = jnp.where(tail_row == j, part[128 : 128 + TAIL], tail)
        for t, term in enumerate(three_terms(edge_wide)):
            tail = jnp.where(tail_row == 2 + 3 * j + t, term, tail)
    out_ref[p, 128:] = tail.astype(bf16)


def edge_parts(state_ref, p, j):
    tail = state_ref[p, 128:].astype(f32)
    feats = tail.shape[1]
    totals = jnp.broadcast_to(tail[j : j + 1], (128, feats)).astype(bf16)
    peak = tail[2 + 3 * j : 3 + 3 * j] + tail[3 + 3 * j : 4 + 3 * j] + tail[4 + 3 * j : 5 + 3 * j]
    return jnp.concatenate([state_ref[p, 0:128], totals], axis=0), peak


def edge_weights(scale, own, other, strad):
    top = jnp.maximum(own, other)
    own_w = jnp.exp2((own - top) * (scale * log2_e))
    other_w = jnp.exp2((other - top) * (scale * log2_e))
    return 1.0 + strad * (own_w[:, 0:128] - 1.0), strad * other_w[:, 0:128]


def forward_finish(p, scale, v_ref, pq_ref, pk_ref, mask_ref, strad_ref, peak_ref, in_ref, att_ref, den_ref):
    rows = v_ref.shape[1]
    first_half = lane_ids((rows, 128)) < 64
    vx = jnp.concatenate([v_ref[p], jnp.ones((rows, 128), bf16)], axis=1)
    got = []
    for j in range(2):
        phi_q = pq_ref[p, j]
        pair = mul_tb(phi_q, pk_ref[p, j]).astype(bf16) * mask_ref[...]
        near = mul(pair, vx)
        state, other = edge_parts(in_ref, p, j)
        far = mul_tb(phi_q, state)
        wn, wf = edge_weights(scale, peak_ref[p, j], other, strad_ref[...])
        den = near[:, 128:] * wn + far[:, 128:] * wf
        got.append(((near[:, :128] * wn + far[:, :128] * wf) / den, den))
    att_ref[p] = jnp.where(first_half, got[0][0], got[1][0]).astype(bf16)
    den_ref[p] = jnp.where(first_half, got[0][1], got[1][1])


def numer_grads(p, att_ref, den_ref, gatt_ref):
    rows = att_ref.shape[1]
    lanes = lane_ids((rows, 128))
    gn = gatt_ref[p].astype(f32) / den_ref[p]
    prod = gn * att_ref[p].astype(f32)
    d0 = -jnp.sum(jnp.where(lanes < 64, prod, 0.0), axis=1, keepdims=True)
    d1 = -jnp.sum(jnp.where(lanes < 64, 0.0, prod), axis=1, keepdims=True)
    return gn, d0, d1, lanes


def backward_states(p, scale, att_ref, den_ref, gatt_ref, pq_ref, strad_ref, peak_ref, in_ref, out_ref):
    gn, d0, d1, lanes = numer_grads(p, att_ref, den_ref, gatt_ref)
    far = [edge_weights(scale, peak_ref[p, j], edge_parts(in_ref, p, j)[1], strad_ref[...])[1] for j in range(2)]
    left = (gn * jnp.where(lanes < 64, far[0], far[1])).astype(bf16)
    right = (jnp.where(lanes == 0, d0 * far[0], 0.0) + jnp.where(lanes == 1, d1 * far[1], 0.0)).astype(bf16)
    turned = jnp.concatenate([left.T, right.T[0:TAIL]], axis=0)
    tails = []
    for j in range(2):
        part = mul(turned, pq_ref[p, j])
        out_ref[p, 64 * j : 64 * j + 64] = part[64 * j : 64 * j + 64].astype(bf16)
        tails.append(part[128:])
    rowid = lax.broadcasted_iota(jnp.int32, tails[0].shape, 0)
    out_ref[p, 128:] = jnp.where(rowid == 0, tails[0], tails[1]).astype(bf16)


def backward_finish(
    p, scale, q_ref, k_ref, v_ref, omx_ref, pq_ref, pk_ref, mask_ref, strad_ref, peak_ref, in_ref, gin_ref,
    att_ref, den_ref, gatt_ref, gq_ref, gk_ref, gv_ref,
):
    rows = q_ref.shape[1]
    gn, d0, d1, lanes = numer_grads(p, att_ref, den_ref, gatt_ref)
    first_half = lanes < 64
    vp = v_ref[p]
    ones = jnp.ones((rows, 128), bf16)
    vx = jnp.concatenate([vp, ones], axis=1)
    strad = strad_ref[...]
    gq = jnp.zeros((rows, 128), f32)
    gk = jnp.zeros((rows, 128), f32)
    gv = jnp.zeros((rows, 128), f32)
    q_sums, k_sums = [], []
    for j in range(2):
        here = (lanes >= 64) if j else (lanes < 64)
        gd = d1 if j else d0
        state, other = edge_parts(in_ref, p, j)
        wn, wf = edge_weights(scale, peak_ref[p, j], other, strad)
        base_l = jnp.where(here, gn, 0.0)
        base_r = jnp.where(lanes == 0, gd, 0.0)
        near = jnp.concatenate([(base_l * wn).astype(bf16), (base_r * wn).astype(bf16)], axis=1)
        far = jnp.concatenate([(base_l * wf).astype(bf16), (base_r * wf).astype(bf16)], axis=1)
        phi_q, phi_k = pq_ref[p, j], pk_ref[p, j]
        turned = mul_tb(phi_k, phi_q).astype(bf16) * mask_ref[...]
        gv = gv + mul(turned, near[:, 0:128])
        gpair = mul_tb(near, vx).astype(bf16) * mask_ref[...]
        gphi_q = mul(gpair, phi_k) + mul(far, state)
        gturned = mul_tb(vx, near).astype(bf16) * mask_ref[...]
        gstate, _ = edge_parts(gin_ref, p, j)
        vs = jnp.concatenate(
            [(jnp.where(here, vp.astype(f32), 0.0) * strad).astype(bf16), jnp.where(lanes == 0, strad, 0.0).astype(bf16)],
            axis=1,
        )
        gphi_k = mul(gturned, phi_q) + mul(vs, gstate)
        gv = gv + jnp.where(here, mul_tb(phi_k, gstate[0:128]) * strad, 0.0)
        omx = omx_ref[2 * p + j]
        back_q = mul_tb((gphi_q * phi_q.astype(f32)).astype(bf16), omx)
        back_k = mul_tb((gphi_k * phi_k.astype(f32)).astype(bf16), omx)
        gq = gq + back_q[:, 0:128]
        gk = gk + back_k[:, 0:128]
        q_sums.append(back_q[:, 128:])
        k_sums.append(back_k[:, 128:])
    gq = gq * scale - jnp.where(first_half, q_sums[0], q_sums[1]) * q_ref[p].astype(f32) * 0.125
    gk = gk * scale - jnp.where(first_half, k_sums[0], k_sums[1]) * k_ref[p].astype(f32) * 0.125
    gq_ref[p] = gq.astype(bf16)
    gk_ref[p] = gk.astype(bf16)
    gv_ref[p] = gv.astype(bf16)


def peer_barrier(peers):
    barrier = pltpu.get_barrier_semaphore()
    for peer in peers:
        pl.semaphore_signal(barrier, inc=1, device_id=peer, device_id_type=MESH)
    pl.semaphore_wait(barrier, len(peers))


class Place:
    def __init__(self):
        me = lax.axis_index("fsdp")
        self.y = lax.axis_index("seq")
        self.c = lax.rem(me, 2)
        self.x = lax.rem(lax.div(me, 2), 2)
        self.z = lax.div(me, 4)
        self.across = {"seq": 1 - self.y}
        self.twin = {"fsdp": self.z * 4 + self.x * 2 + 1 - self.c}
        self.beside = {"fsdp": self.z * 4 + (1 - self.x) * 2 + self.c}

    def along(self, d):
        return {"fsdp": self.other(d) * 4 + self.x * 2 + self.c}

    def other(self, d):
        return lax.rem(self.z + (d + DEPTH), DEPTH)

    def peers(self):
        return [self.twin, self.beside, self.across] + [self.along(d) for d in range(1, DEPTH)]


def cols_at(start, size):
    return pl.ds(pl.multiple_of(start, 128), size)


def remote(src, dst, ssem, rsem, peer):
    return pltpu.make_async_remote_copy(
        src_ref=src, dst_ref=dst, send_sem=ssem, recv_sem=rsem, device_id=peer, device_id_type=MESH
    )


class Gather:
    def __init__(self, at, own, full, base, width, ssem, rsem, lsem):
        self.at, self.own, self.full = at, own, full
        self.third, self.base, self.width = width // 3, base, width
        self.ssem, self.rsem, self.lsem = ssem, rsem, lsem
        self.sent = []

    def spread(self):
        return cols_at(self.base + self.third * self.at.y, 2 * self.third)

    def extra(self, y):
        return cols_at(self.base + 2 * self.third * y, self.third)

    def whole(self):
        return pl.ds(self.base, self.width)

    def go(self, n, ends):
        src, dst, peer = ends()
        remote(src, dst, self.ssem.at[n], self.rsem.at[n], peer).start()
        self.sent.append((n, ends))

    def came(self, n, ref):
        remote(ref, ref, self.ssem.at[n], self.rsem.at[n], self.at.twin).wait_recv()

    def local(self):
        at = self.at
        return pltpu.make_async_copy(
            self.own.at[:, self.whole()], self.full.at[at.z, at.x, at.c, :, self.whole()], self.lsem
        )

    def begin(self):
        at = self.at
        self.local().start()
        for d in range(1, DEPTH):
            self.go(d - 1, lambda d=d: (*self.first(), at.along(d)))

    def first(self):
        at = self.at
        return self.own.at[:, self.spread()], self.full.at[at.z, at.x, at.c, :, self.spread()]

    def piece(self, d, x, cols):
        return self.full.at[self.at.other(-d), x, self.at.c, :, cols]

    def stage_x(self):
        at = self.at
        self.go(DEPTH - 1, lambda: (*self.first(), at.beside))
        for d in range(1, DEPTH):
            self.came(d - 1, self.piece(d, at.x, self.spread()))
            self.go(DEPTH - 1 + d, lambda d=d: (*[self.piece(d, at.x, self.spread())] * 2, at.beside))
            self.go(2 * DEPTH - 2 + d, lambda d=d: (*[self.piece(d, at.x, self.extra(at.y))] * 2, at.across))

    def stage_y(self):
        at = self.at
        for d in range(DEPTH):
            self.came(DEPTH - 1 + d, self.piece(d, 1 - at.x, self.spread()))
            self.go(3 * DEPTH - 2 + d, lambda d=d: (*[self.piece(d, 1 - at.x, self.extra(at.y))] * 2, at.across))

    def stage_c(self):
        at = self.at
        for d in range(1, DEPTH):
            self.came(2 * DEPTH - 2 + d, self.piece(d, at.x, self.extra(1 - at.y)))
        for d in range(DEPTH):
            self.came(3 * DEPTH - 2 + d, self.piece(d, 1 - at.x, self.extra(1 - at.y)))
        self.local().wait()
        self.go(4 * DEPTH - 2, lambda: (*[self.full.at[:, :, at.c, :, self.whole()]] * 2, at.twin))

    def ready(self):
        self.came(4 * DEPTH - 2, self.full.at[:, :, 1 - self.at.c, :, self.whole()])

    def drain(self):
        for n, ends in self.sent:
            src, dst, peer = ends()
            remote(src, dst, self.ssem.at[n], self.rsem.at[n], peer).wait_send()


GATHER_COPIES = 4 * DEPTH - 1


class SmallSum:
    def __init__(self, at, total, land, ssem, rsem, over_seq):
        self.at, self.total, self.land, self.ssem, self.rsem, self.over_seq = at, total, land, ssem, rsem, over_seq
        self.sent = []

    def go(self, src, n, peer):
        copy = remote(self.total.at[src], self.land.at[n], self.ssem.at[n], self.rsem.at[n], peer)
        copy.start()
        self.sent.append(copy)

    def came(self, n):
        remote(self.land.at[n], self.land.at[n], self.ssem.at[n], self.rsem.at[n], self.at.twin).wait_recv()

    def begin(self):
        for d in range(1, DEPTH):
            self.go(0, d - 1, self.at.along(d))

    def step(self, k):
        if k == 0:
            got = self.total[0]
            for d in range(1, DEPTH):
                self.came(d - 1)
            order = [self.at.z] + [self.at.other(-d) for d in range(1, DEPTH)]
            parts = [got] + [self.land[d - 1] for d in range(1, DEPTH)]
            value = jnp.zeros_like(got)
            for z in range(DEPTH):
                one = jnp.zeros_like(got)
                for place, part in zip(order, parts):
                    one = jnp.where(place == z, part, one)
                value = value + one
        else:
            self.came(DEPTH - 2 + k)
            value = self.total[k] + self.land[DEPTH - 2 + k]
        self.total[k + 1] = value
        hops = [self.at.beside, self.at.twin] + ([self.at.across] if self.over_seq else [])
        if k < len(hops):
            self.go(k + 1, DEPTH - 1 + k, hops[k])

    def steps(self):
        return 4 if self.over_seq else 3

    def result(self):
        return self.total[self.steps()]

    def drain(self):
        for copy in self.sent:
            copy.wait_send()


def spread_vectors(at, pieces, wide):
    width = 768
    part = pieces[0].shape[-1]
    rows = [p[...].astype(f32).reshape(1, part) for p in pieces]
    rows = jnp.concatenate(rows + [jnp.zeros((16 - len(rows), part), f32)], axis=0)
    rows = jnp.concatenate([rows, jnp.zeros((16, width - part), f32)], axis=1)
    rows = pltpu.roll(rows, (at.z * 4 + at.x * 2 + at.c) * part, 1)
    span = wide.shape[-1]
    row = jnp.concatenate([wide[...].astype(f32).reshape(1, span), jnp.zeros((1, width - span), f32)], axis=1)
    row = pltpu.roll(jnp.broadcast_to(row, (16, width)), (at.x * 2 + at.c) * span, 1)
    here = lax.broadcasted_iota(jnp.int32, (16, width), 0)
    return jnp.where(here == len(pieces) + at.z, row, rows)


HOLD = (
    "omx", "xt", "mask", "strad", "q", "k", "v", "pq", "pk", "att", "attt", "den", "sq", "hidt", "norm", "fin", "gelt", "slope", "fdn",
)
LATE = ("xt", "q", "k", "v", "pq", "pk", "att", "attt", "den", "omx", "mask", "strad")


def forward_kernel(
    scale, x_ref, wq_ref, wk_ref, wv_ref, wo_ref, win_ref, wdn_ref, bq_ref, bk_ref, bv_ref, bo_ref, g1_ref, o1_ref, bd_ref,
    g2_ref, o2_ref, bin_ref, ints_ref, cot_ref, len_ref, layer_ref, peak_ref, state_ref, inv_ref, res_ref, vec_ref, sums_ref, *rest,
):
    outs, rest = rest[: len(HOLD)], rest[len(HOLD) :]
    hold, rest = rest[: len(HOLD)], rest[len(HOLD) :]
    (
        omx_ref, xt_ref, mask_ref, strad_ref, q_ref, k_ref, v_ref, pq_ref, pk_ref, att_ref, attt_ref, den_ref, sq_ref, hidt_ref,
        norm_ref, fin_ref, gelt_ref, slope_ref, fdn_ref,
    ) = hold
    hid_ref, gel_ref, onehot_ref, stradrow_ref, send_ref, total_ref, land_ref = rest[:7]
    ssem, rsem, gs_sem, gr_sem, gl_sem, vs_sem, vr_sem, out_sem = rest[7:]
    at = Place()
    pairs = q_ref.shape[0]
    rows, width = x_ref.shape

    def stash(*names):
        return [pltpu.make_async_copy(hold[n], outs[n], out_sem.at[n]) for n in map(HOLD.index, names)]

    def give(*names):
        for copy in stash(*names):
            copy.start()

    blocks = []
    specs = [(w, sq_ref.at[n], 0, 768) for n, w in enumerate((wq_ref, wk_ref, wv_ref, wo_ref))]
    specs += [(win_ref, fin_ref, 768 * h, 768) for h in range(4)]
    specs += [
        (wdn_ref.at[pl.ds(96 * r, 96)], fdn_ref.at[:, :, :, pl.ds(96 * r, 96)], 384 * h, 384) for h in range(2) for r in range(2)
    ]
    for n, (own, full, base, span) in enumerate(specs):
        blocks.append(Gather(at, own, full, base, span, gs_sem.at[n], gr_sem.at[n], gl_sem.at[n]))
    peer_barrier(at.peers())
    vec = SmallSum(at, total_ref, land_ref, vs_sem, vr_sem, False)
    total_ref[0] = spread_vectors(
        at, (bq_ref, bk_ref, bv_ref, bo_ref, g1_ref, o1_ref, bd_ref, g2_ref, o2_ref), bin_ref
    ).astype(bf16)
    blocks[0].begin()
    vec.begin()
    for b in blocks[1:AHEAD]:
        b.begin()
    doc_setup(len_ref, at.y, mask_ref, onehot_ref, strad_ref, stradrow_ref)
    features_setup(ints_ref, omx_ref)
    for j in range(pairs):
        xt_ref[128 * j : 128 * j + 128] = x_ref[:, 128 * j : 128 * j + 128].T
    give("omx", "xt", "mask", "strad")
    sums_ref[...] = jnp.zeros_like(sums_ref)

    def vector(n, cols=slice(None)):
        return vec_ref[n : n + 1, cols].astype(f32)

    def project(n, o_ref):
        for j in range(pairs // 2):
            cols = slice(256 * j, 256 * j + 256)
            got = mul(x_ref[...], sq_ref[n, :, :, :, :, cols].reshape(768, 256))
            got = (got + vector(n, cols)).astype(bf16)
            o_ref[2 * j] = got[:, 0:128]
            o_ref[2 * j + 1] = got[:, 128:256]

    def tick(t):
        if t + AHEAD < len(blocks):
            blocks[t + AHEAD].begin()
        for k, name in enumerate(("stage_x", "stage_y", "stage_c", "ready")):
            if 0 <= t - k < len(blocks):
                getattr(blocks[t - k], name)()

    for t in range(3):
        tick(t)
        vec.step(t)
    vec_ref[...] = vec.result()
    for n, ref in enumerate((q_ref, k_ref, v_ref)):
        tick(3 + n)
        project(n, ref)
        give("qkv"[n])

    def copy(p):
        return remote(send_ref.at[p], state_ref.at[p], ssem.at[p], rsem.at[p], at.across)

    def ticks_at(p, plan):
        for n, t in plan.items():
            @pl.when(p == n)
            def _(t=t):
                tick(t)

    @pl.loop(0, pairs)
    def _(p):
        forward_states(p, scale, q_ref, k_ref, v_ref, omx_ref, onehot_ref, strad_ref, stradrow_ref, pq_ref, pk_ref, peak_ref, send_ref)
        copy(p).start()
        ticks_at(p, {0: 6, 2: 7, 4: 8})

    give("pq", "pk", "sq")

    @pl.loop(0, pairs)
    def _(p):
        copy(p).wait()
        forward_finish(p, scale, v_ref, pq_ref, pk_ref, mask_ref, strad_ref, peak_ref, state_ref, att_ref, den_ref)
        attt_ref[p] = att_ref[p].T
        ticks_at(p, {0: 9, 3: 10})

    give("att", "attt", "den", "fin")


    whole = jnp.concatenate([att_ref[p] for p in range(pairs)], axis=1)
    for j in range(pairs // 2):
        cols = slice(256 * j, 256 * j + 256)
        got = mul(whole, sq_ref[3, :, :, :, :, cols].reshape(768, 256))
        res_ref[:, cols] = got + vector(3, cols) + x_ref[:, cols].astype(f32)

    def centred(value):
        value = value - jnp.mean(value, axis=1, keepdims=True)
        inverse = lax.rsqrt(jnp.mean(value * value, axis=1, keepdims=True) + 1e-06)
        return value * inverse, inverse

    def here(r):
        return pl.ds(pl.multiple_of(128 * r, 128), 128)

    @pl.loop(0, rows // 128)
    def _(r):
        normed, inverse = centred(res_ref[here(r)])
        inv_ref[here(r)] = inverse
        norm_ref[here(r)] = normed.astype(bf16)
        hid_ref[here(r)] = (normed * vector(4) + vector(5)).astype(bf16)

    for j in range(pairs):
        hidt_ref[128 * j : 128 * j + 128] = hid_ref[:, 128 * j : 128 * j + 128].T
    give("hidt", "norm")


    @pl.loop(0, 4)
    def _(b):
        ticks_at(b, {0: 11, 2: 12})
        for j in range(3):
            cols = cols_at(768 * b + 256 * j, 256)
            pre = mul(hid_ref[...], fin_ref[:, :, :, :, cols].reshape(768, 256))
            bias = jnp.zeros((1, 256), f32)
            for n in range(4):
                bias = jnp.where(b == n, vector(9 + n, slice(256 * j, 256 * j + 256)), bias)
            pre = pre + bias
            share = 0.5 * (1.0 + lax.erf(pre * inv_root_two))
            gel = (pre * share).astype(bf16)
            gel_ref[:, cols] = gel
            gelt_ref[cols] = gel.T
            slope_ref[:, cols] = (share + pre * (jnp.exp(-0.5 * pre * pre) * inv_root_tau)).astype(bf16)

    give("gelt", "slope")

    def down(h):
        cols = slice(384 * h, 384 * h + 384)
        res_ref[:, cols] = hid_ref[:, cols].astype(f32) + vector(6, cols)

        @pl.loop(0, DEPTH)
        def _(z):
            got = mul(gel_ref[:, cols_at(768 * z, 768)], fdn_ref[z, :, :, :, cols].reshape(768, 384))
            res_ref[:, cols] = res_ref[:, cols] + got

    down(0)
    tick(13)
    tick(14)
    give("fdn")
    down(1)


    @pl.loop(0, rows // 128)
    def _(r):
        normed, inverse = centred(res_ref[here(r)])
        layer_ref[here(r)] = (normed * vector(7) + vector(8)).astype(bf16)
        grad = cot_ref[here(r)].astype(f32)
        scaled = grad * vector(7)
        centre = jnp.mean(scaled, axis=1, keepdims=True)
        lean = jnp.mean(scaled * normed, axis=1, keepdims=True)
        resid = inverse * (scaled - centre - normed * lean)
        res_ref[here(r)] = resid
        sums_ref[6:7] = sums_ref[6:7] + jnp.sum(resid.astype(bf16).astype(f32), axis=0, keepdims=True)
        sums_ref[7:8] = sums_ref[7:8] + jnp.sum(grad * normed, axis=0, keepdims=True)
        sums_ref[8:9] = sums_ref[8:9] + jnp.sum(grad, axis=0, keepdims=True)

    for b in blocks:
        b.drain()
    vec.drain()
    for one in stash(*HOLD):
        one.wait()


class Scatter:
    def __init__(self, at, order, source, twin_in, lands, done, done_in, put, ssem, rsem):
        self.at, self.order, self.source, self.acc = at, order, source, source(at.c)
        self.twin_in, self.lands = twin_in, lands
        self.done, self.done_in, self.put = done, done_in, put
        self.ssem, self.rsem = ssem, rsem
        self.half = twin_in.shape[-1] // 2
        self.sent = []

    def go(self, n, ends):
        src, dst, peer = ends()
        remote(src, dst, self.ssem.at[n], self.rsem.at[n], peer).start()
        self.sent.append((n, ends))

    def came(self, n, ref):
        remote(ref, ref, self.ssem.at[n], self.rsem.at[n], self.at.twin).wait_recv()

    def side(self, y):
        return cols_at(self.half * y, self.half)

    def spot(self, fixed, **other):
        at = self.at
        z = other.get("z", at.z if "z" in fixed else slice(None))
        x = other.get("x", at.x if "x" in fixed else slice(None))
        cols = self.side(other.get("y", at.y)) if "y" in fixed or "y" in other else slice(None)
        return z, x, slice(None), cols

    def first(self, i):
        return 1 + sum(DEPTH - 1 if kind == "z" else 1 for kind in self.order[:i])

    def send(self, i):
        at, kind, fixed = self.at, self.order[i], self.order[:i]
        if kind == "z":
            for d in range(1, DEPTH):
                self.go(
                    self.first(i) + d - 1,
                    lambda d=d: (self.acc.at[self.spot(fixed, z=at.other(d))], self.lands[i].at[d - 1], at.along(d)),
                )
        elif kind == "x":
            self.go(self.first(i), lambda: (self.acc.at[self.spot(fixed, x=1 - at.x)], self.lands[i], at.beside))
        else:
            self.go(self.first(i), lambda: (self.acc.at[self.spot(fixed, y=1 - at.y)], self.lands[i], at.across))

    def add(self, parts, fixed, store):
        def at_z(z):
            for x in [None] if "x" in fixed else range(2):
                spot = list(self.spot(fixed))
                inner = ()
                if z is not None:
                    spot[0] = z
                    inner += (z,)
                if x is not None:
                    spot[1] = x
                    inner += (x,)
                value = self.acc[tuple(spot)].astype(f32)
                for part in parts:
                    value = value + part[inner + (slice(None), slice(None))].astype(f32)
                store(tuple(spot), value)

        if "z" in fixed:
            at_z(None)
        else:
            pl.loop(0, DEPTH)(at_z)

    def keep(self, spot, value):
        self.acc[spot] = value.astype(bf16)

    def finish(self, spot, value):
        low = value.astype(bf16)
        self.done[...] = low
        self.put(self.at.y, low.astype(f32))

    def arrived(self, i):
        if self.order[i] != "z":
            self.came(self.first(i), self.lands[i])
            return [self.lands[i]]
        for d in range(1, DEPTH):
            self.came(self.first(i) + d - 1, self.lands[i].at[d - 1])
        return [self.lands[i].at[d - 1] for d in range(1, DEPTH)]

    def begin(self):
        self.go(0, lambda: (self.source(1 - self.at.c), self.twin_in, self.at.twin))

    def stage_1(self):
        self.came(0, self.twin_in)
        self.add([self.twin_in], "", self.keep)
        self.send(0)

    def stage_2(self):
        self.add(self.arrived(0), self.order[:1], self.keep)
        self.send(1)

    def stage_3(self):
        self.add(self.arrived(1), self.order[:2], self.keep)
        self.send(2)

    def stage_4(self):
        self.add(self.arrived(2), self.order, self.finish)
        self.go(2 + DEPTH, lambda: (self.done, self.done_in, self.at.across))

    def stage_5(self):
        self.came(2 + DEPTH, self.done_in)
        self.put(1 - self.at.y, self.done_in[...].astype(f32))

    def drain(self):
        for n, ends in self.sent:
            src, dst, peer = ends()
            remote(src, dst, self.ssem.at[n], self.rsem.at[n], peer).wait_send()


def landing(order, part, width):
    shapes = []
    for i, kind in enumerate(order):
        kept = order[: i + 1]
        shape = [] if "z" in kept else [DEPTH]
        shape += [] if "x" in kept else [2]
        shape += [part, width // 2 if "y" in kept else width]
        shapes.append(pltpu.VMEM(tuple([DEPTH - 1] + shape if kind == "z" else shape), bf16))
    return shapes


SCATTER_COPIES = DEPTH + 3
GELU_SLOTS = 4
FEED_SLOTS = 3
FEED_STEPS = (2, 6)
HEAD_STEPS = (0, 1, 2, 3, 4, 5)
PACE = ((0, 2, 4, 6, 8),) * 8 + ((0, 2, 3, 4, 5),) + ((0, 1, 2, 3, 4),) * 3
ORDERS = ("yxz", "xyz", "xyz") * 4


def backward_kernel(
    scale, peak_ref, state_ref, hidt_ref, norm_ref, inv_ref, res_ref, gain_ref, vecin_ref, gel_ref, slope_ref, win_ref, wdn_ref,
    sq_ref, *rest,
):
    late_refs, rest = rest[: len(LATE)], rest[len(LATE) :]
    gx_ref, oq_ref, ok_ref, ov_ref, oo_ref, oin_ref, odn_ref, vec_ref = rest[:8]
    kept_refs, rest = rest[8 : 8 + len(LATE)], rest[8 + len(LATE) :]
    xt_ref, q_ref, k_ref, v_ref, pq_ref, pk_ref, att_ref, attt_ref, den_ref, omx_ref, mask_ref, strad_ref = kept_refs
    gstate_ref, send_ref, gq_ref, gk_ref, gv_ref, gatt_ref, low_ref, wide_ref, gelbuf_ref, slopebuf_ref, winbuf_ref = rest[:11]
    gdn_ref, gin_ref, go_ref, gw_ref, total_ref, land_ref, twin_ref, done_ref, donein_ref = rest[11:20]
    ssem, rsem, load_sem, late_sem, keep_sem, ws_sem, wr_sem, vs_sem, vr_sem = rest[20:29]
    land_refs = rest[29:]
    at = Place()
    pairs = q_ref.shape[0]
    rows, width = res_ref.shape
    span = width // 2
    chunks = win_ref.shape[1] // span
    sources = [lambda c, b=b: gdn_ref.at[:, :, c, pl.ds(48 * b, 48)] for b in range(4)]
    sources += [lambda c, b=b: gin_ref.at[:, :, c, :, pl.ds(768 * b, 768)] for b in range(4)]
    sources += [lambda c: go_ref.at[:, :, c]]
    sources += [lambda c, n=n: gw_ref.at[n, :, :, c] for n in (2, 1, 0)]

    def putter(ref, row, col):
        def put(y, value):
            ref[pl.ds(row, 48), cols_at(col + 384 * y, 384)] = value

        return put

    puts = [putter(odn_ref, 48 * b, 0) for b in range(4)] + [putter(oin_ref, 0, 768 * b) for b in range(4)]
    puts += [putter(r, 0, 0) for r in (oo_ref, ov_ref, ok_ref, oq_ref)]
    units = []
    for n, (source, put) in enumerate(zip(sources, puts)):
        lands = land_refs[3 * n : 3 * n + 3]
        units.append(
            Scatter(
                at, ORDERS[n], source, twin_ref.at[n], lands, done_ref.at[n], donein_ref.at[n], put, ws_sem.at[n], wr_sem.at[n]
            )
        )
    early = len(units) - 3

    def step(s):
        for k in range(5):
            for u, unit in enumerate(units):
                if u + PACE[u][k] == s:
                    getattr(unit, "stage_" + str(k + 1))()


    def load(src, dst, sem):
        return pltpu.make_async_copy(src, dst, sem)

    def gelu_at(m):
        return lax.rem(m, GELU_SLOTS)

    def load_gelu(m):
        return load(
            gel_ref.at[pl.ds(pl.multiple_of(span * m, 128), span)], gelbuf_ref.at[gelu_at(m)], load_sem.at[0, gelu_at(m)]
        )

    def slot(m):
        return lax.rem(m, FEED_SLOTS)

    def down_at(m):
        n = slot(m)
        return 2 * lax.div(n, 2), pl.ds(pl.multiple_of(span * lax.rem(n, 2), 128), span)

    def load_chunk(m):
        return [
            load(slope_ref.at[:, cols_at(span * m, span)], slopebuf_ref.at[slot(m)], load_sem.at[1, slot(m)]),
            load(wdn_ref.at[pl.ds(pl.multiple_of(span * m, 128), span)], wide_ref.at[down_at(m)], load_sem.at[2, slot(m)]),
            load(win_ref.at[:, cols_at(span * m, span)], winbuf_ref.at[slot(m)], load_sem.at[3, slot(m)]),
        ]

    def load_square(n, to):
        return load(sq_ref.at[n], wide_ref.at[to], late_sem.at[to])

    peer_barrier(at.peers())
    first = load(res_ref, gx_ref, late_sem.at[0])
    first.start()
    for m in range(GELU_SLOTS - 1):
        load_gelu(jnp.int32(m)).start()
    for m in range(FEED_SLOTS - 1):
        for one in load_chunk(jnp.int32(m)):
            one.start()
    load_square(3, 1).start()
    kept = [load(src, dst, keep_sem.at[n]) for n, (src, dst) in enumerate(zip(late_refs, kept_refs))]
    for one in kept:
        one.start()
    total_ref[0] = vecin_ref[...]

    first.wait()

    @pl.loop(0, rows // 128)
    def _(r):
        here = pl.ds(pl.multiple_of(128 * r, 128), 128)
        low_ref[here] = gx_ref[here].astype(bf16)


    @pl.loop(0, chunks)
    def _(m):
        load_gelu(m).wait()

        @pl.when(m < chunks - (GELU_SLOTS - 1))
        def _():
            load_gelu(m + GELU_SLOTS - 1).start()

        turned = gelbuf_ref[gelu_at(m)]
        for n in range(3):
            cols = slice(256 * n, 256 * n + 256)
            got = mul(turned, low_ref[:, cols]).astype(bf16)
            gdn_ref[lax.div(m, 2), lax.rem(m, 2), :, :, cols] = got.reshape(2, span // 2, 256)

    units[0].begin()
    units[1].begin()
    @pl.loop(0, chunks)
    def _(m):
        for one in load_chunk(m):
            one.wait()

        @pl.when(m < chunks - (FEED_SLOTS - 1))
        def _():
            for one in load_chunk(m + FEED_SLOTS - 1):
                one.start()

        start = pl.multiple_of(span * lax.rem(m, 2), 128)
        gpre = mul_tb(low_ref[...], wide_ref[down_at(m)]) * slopebuf_ref[slot(m)].astype(f32)
        gpre = gpre.astype(bf16)
        total_ref[0, pl.ds(9 + lax.div(m, 2), 1), cols_at(start, span)] = jnp.sum(gpre.astype(f32), axis=0, keepdims=True)
        got = mul(hidt_ref[...], gpre).astype(bf16)
        gin_ref[:, :, :, :, cols_at(span * m, span)] = got.reshape(DEPTH, 2, 2, 48, span)
        for n in range(3):
            cols = slice(256 * n, 256 * n + 256)
            gx_ref[:, cols] = gx_ref[:, cols] + mul_tb(gpre, winbuf_ref[slot(m), cols])
        for n in range(8):
            @pl.when(m == n)
            def _(n=n):
                if n < 2:
                    units[2 + n].begin()
                if n % 2:
                    units[4 + n // 2].begin()
                if n in FEED_STEPS:
                    step(FEED_STEPS.index(n))

    done_steps = len(FEED_STEPS)

    @pl.loop(0, rows // 128)
    def _(r):
        here = pl.ds(pl.multiple_of(128 * r, 128), 128)
        grad = gx_ref[here]
        normed = norm_ref[here].astype(f32)
        scaled = grad * gain_ref[4:5].astype(f32)
        centre = jnp.mean(scaled, axis=1, keepdims=True)
        slope = jnp.mean(scaled * normed, axis=1, keepdims=True)
        resid = inv_ref[here] * (scaled - centre - normed * slope)
        gx_ref[here] = resid
        low = resid.astype(bf16)
        low_ref[here] = low
        total_ref[0, 3:4] = total_ref[0, 3:4] + jnp.sum(low.astype(f32), axis=0, keepdims=True)
        total_ref[0, 4:5] = total_ref[0, 4:5] + jnp.sum(grad * normed, axis=0, keepdims=True)
        total_ref[0, 5:6] = total_ref[0, 5:6] + jnp.sum(grad, axis=0, keepdims=True)

    load_square(3, 1).wait()
    for one in kept:
        one.wait()
    for h in range(2):
        turned = attt_ref[3 * h : 3 * h + 3].reshape(384, rows)
        for n in range(3):
            cols = slice(256 * n, 256 * n + 256)
            go_ref[2 * h : 2 * h + 2, :, :, :, cols] = mul(turned, low_ref[:, cols]).astype(bf16).reshape(2, 2, 2, 48, 256)
    units[8].begin()
    for j in range(pairs // 2):
        got = mul_tb(low_ref[...], wide_ref[1, 256 * j : 256 * j + 256]).astype(bf16)
        gatt_ref[2 * j] = got[:, 0:128]
        gatt_ref[2 * j + 1] = got[:, 128:256]
    for n in range(3):
        load_square(n, n).start()
    step(done_steps)
    done_steps += 1


    def copy(p):
        return remote(send_ref.at[p], gstate_ref.at[p], ssem.at[p], rsem.at[p], at.across)

    @pl.loop(0, pairs)
    def _(p):
        backward_states(p, scale, att_ref, den_ref, gatt_ref, pq_ref, strad_ref, peak_ref, state_ref, send_ref)
        copy(p).start()

    @pl.loop(0, pairs)
    def _(p):
        copy(p).wait()
        backward_finish(
            p, scale, q_ref, k_ref, v_ref, omx_ref, pq_ref, pk_ref, mask_ref, strad_ref, peak_ref, state_ref, gstate_ref,
            att_ref, den_ref, gatt_ref, gq_ref, gk_ref, gv_ref,
        )
        cols = cols_at(128 * p, 128)
        both = mul(xt_ref[...], jnp.concatenate([gq_ref[p], gk_ref[p]], axis=1)).astype(bf16)
        gw_ref[0, :, :, :, :, cols] = both[:, 0:128].reshape(DEPTH, 2, 2, 48, 128)
        gw_ref[1, :, :, :, :, cols] = both[:, 128:256].reshape(DEPTH, 2, 2, 48, 128)
        gw_ref[2, :, :, :, :, cols] = mul(xt_ref[...], gv_ref[p]).astype(bf16).reshape(DEPTH, 2, 2, 48, 128)
        for n, ref in enumerate((gq_ref, gk_ref, gv_ref)):
            total_ref[0, n : n + 1, cols] = jnp.sum(ref[p].astype(f32), axis=0, keepdims=True)
        for n, at_pair in enumerate(HEAD_STEPS):
            @pl.when(p == at_pair)
            def _(n=n):
                step(n + done_steps)

    vec = SmallSum(at, total_ref, land_ref, vs_sem, vr_sem, True)
    vec.begin()
    for u in units[early:]:
        u.begin()
    for n in range(3):
        load_square(n, n).wait()

    def grad_input(j):
        cols = slice(256 * j, 256 * j + 256)
        value = gx_ref[:, cols]
        for n, ref in enumerate((gq_ref, gk_ref, gv_ref)):
            for i in range(pairs // 2):
                left = jnp.concatenate([ref[2 * i], ref[2 * i + 1]], axis=1)
                right = wide_ref[n, 256 * j : 256 * j + 256, 256 * i : 256 * i + 256]
                value = value + mul_tb(left, right)
        gx_ref[:, cols] = value

    done_steps += len(HEAD_STEPS)
    for n, s in enumerate(range(done_steps, len(units) + PACE[-1][-1])):
        step(s)
        if n < 4:
            vec.step(n)
        if n < 3:
            grad_input(n)
    vec_ref[...] = vec.result()
    for u in units:
        u.drain()
    vec.drain()


def scratch_masks(rows, heads, feats):
    return [
        pltpu.VMEM((heads, 256, feats), bf16),
        pltpu.VMEM((rows, rows), bf16),
        pltpu.VMEM((rows, 128), f32),
        pltpu.VMEM((rows, 128), f32),
        pltpu.VMEM((TAIL, rows), bf16),
    ]


def vmem():
    return pl.BlockSpec(memory_space=pltpu.VMEM)


def anywhere():
    return pl.BlockSpec(memory_space=pl.ANY)


def smem():
    return pl.BlockSpec(memory_space=pltpu.SMEM)


def attention_forward(x, weights, vectors, ints, cot, lengths):
    rows, width = x.shape
    heads, size, feats = ints.shape
    pairs = heads // 2
    hidden = weights[4].shape[1]
    part = weights[0].shape[0]
    scale = size ** (-0.25) * unit_spread
    shape = jax.ShapeDtypeStruct
    grid = (DEPTH, 2, 2)
    dma = pltpu.SemaphoreType.DMA
    pair, phi, full, tall = (pairs, rows, 128), (pairs, 2, rows, feats), (rows, width), (rows, hidden)
    held = {
        "omx": (heads, 256, feats), "xt": (width, rows), "mask": (rows, rows), "strad": (rows, 128), "q": pair, "k": pair, "v": pair, "pq": phi, "pk": phi, "att": pair,
        "attt": (pairs, 128, rows), "den": pair, "sq": (4, *grid, part, width), "hidt": (width, rows), "norm": full,
        "fin": (*grid, part, hidden), "gelt": (hidden, rows), "slope": tall,
        "fdn": (*grid, weights[5].shape[0], width),
    }
    kind = {name: f32 if name in ("den", "strad") else bf16 for name in HOLD}
    layer, peak, state, inverse, resid, vec, sums, *rest = pl.pallas_call(
        partial(forward_kernel, scale),
        out_shape=[
            shape(full, bf16), shape((pairs, 2, 1, feats), f32), shape((pairs, 128 + TAIL, feats), bf16),
            shape((rows, 1), f32), shape(full, f32), shape((16, width), bf16), shape((16, width), f32),
        ] + [shape(held[name], kind[name]) for name in HOLD],
        in_specs=[vmem()] * 19 + [smem()],
        out_specs=[vmem()] * 7 + [anywhere()] * len(HOLD),
        scratch_shapes=[pltpu.VMEM(held[name], kind[name]) for name in HOLD] + [
            pltpu.VMEM(full, bf16), pltpu.VMEM(tall, bf16),
            pltpu.VMEM((rows, 128), f32), pltpu.VMEM((TAIL, rows), bf16),
            pltpu.VMEM((pairs, 128 + TAIL, feats), bf16),
            pltpu.VMEM((4, 16, width), bf16),
            pltpu.VMEM((DEPTH + 1, 16, width), bf16),
            dma((pairs,)), dma((pairs,)),
            dma((12, GATHER_COPIES)), dma((12, GATHER_COPIES)), dma((12,)),
            dma((DEPTH + 1,)), dma((DEPTH + 1,)), dma((len(HOLD),)),
        ],
        compiler_params=pltpu.CompilerParams(collective_id=0, has_side_effects=True, vmem_limit_bytes=65200 << 10),
        name="attention_forward",
    )(x, *weights, *vectors, ints, cot, lengths)
    got = dict(zip(HOLD, rest))
    inner = (peak, state, got["hidt"], got["norm"], inverse, resid, vec, sums)
    late = (
        got["gelt"], got["slope"], got["fin"].reshape(width, hidden), got["fdn"].reshape(hidden, width),
        got["sq"].reshape(4, width, width), *(got[name] for name in LATE),
    )
    return layer, inner, late


def attention_backward(inner, late):
    rows, width = inner[5].shape
    pairs, _, _, feats = inner[0].shape
    heads, hidden = 2 * pairs, late[0].shape[0]
    scale = (width // heads) ** (-0.25) * unit_spread
    shape = jax.ShapeDtypeStruct
    dma = pltpu.SemaphoreType.DMA
    grid = (DEPTH, 2, 2)
    part = width // 16
    units = 12
    return pl.pallas_call(
        partial(backward_kernel, scale),
        out_shape=[shape((rows, width), f32)]
        + [shape((part, width), f32)] * 4
        + [shape((part, hidden), f32), shape((hidden // 16, width), f32), shape((16, width), f32)],
        in_specs=[vmem()] * 5 + [anywhere()] + [vmem()] * 2 + [anywhere()] * (5 + len(LATE)),
        out_specs=[vmem()] * 8,
        scratch_shapes=[pltpu.VMEM(one.shape, one.dtype) for one in late[5:]] + [
            pltpu.VMEM((pairs, 128 + TAIL, feats), bf16), pltpu.VMEM((pairs, 128 + TAIL, feats), bf16),
            pltpu.VMEM((pairs, rows, 128), bf16), pltpu.VMEM((pairs, rows, 128), bf16), pltpu.VMEM((pairs, rows, 128), bf16),
            pltpu.VMEM((pairs, rows, 128), bf16),
            pltpu.VMEM((rows, width), bf16),
            pltpu.VMEM((3, width, width), bf16),
            pltpu.VMEM((GELU_SLOTS, width // 2, rows), bf16), pltpu.VMEM((FEED_SLOTS, rows, width // 2), bf16),
            pltpu.VMEM((FEED_SLOTS, width, width // 2), bf16),
            pltpu.VMEM((*grid, hidden // 16, width), bf16),
            pltpu.VMEM((*grid, part, hidden), bf16),
            pltpu.VMEM((*grid, part, width), bf16),
            pltpu.VMEM((3, *grid, part, width), bf16),
            pltpu.VMEM((5, 16, width), f32),
            pltpu.VMEM((DEPTH + 2, 16, width), f32),
            pltpu.VMEM((units, DEPTH, 2, part, width), bf16),
            pltpu.VMEM((units, part, width // 2), bf16),
            pltpu.VMEM((units, part, width // 2), bf16),
            dma((pairs,)), dma((pairs,)), dma((4, GELU_SLOTS)), dma((3,)), dma((len(LATE),)),
            dma((units, SCATTER_COPIES)), dma((units, SCATTER_COPIES)),
            dma((DEPTH + 2,)), dma((DEPTH + 2,)),
        ] + [land for order in ORDERS for land in landing(order, part, width)],
        compiler_params=pltpu.CompilerParams(collective_id=1, has_side_effects=True, vmem_limit_bytes=65200 << 10),
        name="attention_backward",
    )(*inner, *late)


def finish_kernel(sums_ref, *refs):
    big = BIG
    ins, outs, vectors, mids, sem = refs[:big], refs[big : 2 * big], refs[2 * big : -1 - big], refs[-1 - big : -1], refs[-1]
    taken = [pltpu.make_async_copy(src, dst, sem.at[0, n]) for n, (src, dst) in enumerate(zip(ins, mids))]
    given = [pltpu.make_async_copy(src, dst, sem.at[1, n]) for n, (src, dst) in enumerate(zip(mids, outs))]
    for one in taken:
        one.start()
    me = lax.axis_index("fsdp")
    part, wide = vectors[0].shape[1], vectors[9].shape[1]
    width = sums_ref.shape[1]
    sums = sums_ref[...]
    turned = pltpu.roll(sums, lax.rem(width - part * me, width), 1)
    for n in range(9):
        vectors[n][...] = turned[n : n + 1, 0:part]
    inner = pltpu.roll(sums, lax.rem(width - wide * lax.rem(me, 4), width), 1)
    row = jnp.zeros((1, width), f32)
    for n in range(DEPTH):
        row = jnp.where(lax.div(me, 4) == n, inner[9 + n : 10 + n], row)
    vectors[9][...] = row[:, 0:wide]
    for one, two in zip(taken, given):
        one.wait()
        two.start()
    for two in given:
        two.wait()


BIG = 8


def finish(arrays, sums, part, wide):
    shape = jax.ShapeDtypeStruct
    return pl.pallas_call(
        finish_kernel,
        out_shape=[shape(a.shape, a.dtype) for a in arrays] + [shape((1, part), f32)] * 9 + [shape((1, wide), f32)],
        in_specs=[vmem()] + [anywhere()] * BIG,
        out_specs=[anywhere()] * BIG + [vmem()] * 10,
        scratch_shapes=[pltpu.VMEM(a.shape, a.dtype) for a in arrays] + [pltpu.SemaphoreType.DMA((2, BIG))],
        name="finish",
    )(sums, *arrays)


def to_pairs(rows):
    return rows.reshape(rows.shape[0], -1, 128).transpose(1, 0, 2)


def from_pairs(pairs):
    return pairs.transpose(1, 0, 2).reshape(pairs.shape[1], -1)


def per_device(
    tokens, doc_lengths, feature_ints, w_query, b_query, w_key, b_key, w_value, b_value, w_out, b_out,
    norm1_gain, norm1_bias, w_in, b_in, w_down, b_down, norm2_gain, norm2_bias, cotangent,
):
    layer_out, inner, late = attention_forward(
        tokens[0],
        (w_query, w_key, w_value, w_out, w_in, w_down),
        (b_query, b_key, b_value, b_out, norm1_gain, norm1_bias, b_down, norm2_gain, norm2_bias, b_in),
        feature_ints, cotangent[0], doc_lengths,
    )
    *grads, sums = attention_backward(inner, late)
    done = finish((layer_out, *grads), sums, b_query.shape[0], b_in.shape[0])
    layer_out, grad_input, gq, gk, gv, go, gin, gdn = done[:BIG]
    bq, bk, bv, bo, g1, o1, bd, g2, o2, bi = (one.reshape(-1) for one in done[BIG:])
    return (
        layer_out[None], grad_input[None],
        gq, bq, gk, bk, gv, bv, go, bo, g1, o1, gin, bi, gdn, bd, g2, o2,
    )


def forward_kernel_wide(
    scale, x_ref, wq_ref, wk_ref, wv_ref, bias_ref, ints_ref, len_ref,
    q_ref, k_ref, v_ref, pq_ref, pk_ref, att_ref, den_ref, peak_ref, state_ref,
    omx_ref, mask_ref, onehot_ref, strad_ref, stradrow_ref, send_ref, ssem, rsem,
):
    place = lax.axis_index("seq")
    peer = {"seq": 1 - place}
    peer_barrier([peer])
    pairs = q_ref.shape[0]
    doc_setup(len_ref, place, mask_ref, onehot_ref, strad_ref, stradrow_ref)
    features_setup(ints_ref, omx_ref)
    for n, (w_ref, o_ref) in enumerate(((wq_ref, q_ref), (wk_ref, k_ref), (wv_ref, v_ref))):
        for j in range(pairs // 2):
            cols = slice(256 * j, 256 * j + 256)
            got = (mul(x_ref[...], w_ref[:, cols]) + bias_ref[n : n + 1, cols].astype(f32)).astype(bf16)
            o_ref[2 * j] = got[:, 0:128]
            o_ref[2 * j + 1] = got[:, 128:256]

    def copy(p):
        return pltpu.make_async_remote_copy(
            src_ref=send_ref.at[p], dst_ref=state_ref.at[p], send_sem=ssem.at[p], recv_sem=rsem.at[p],
            device_id=peer, device_id_type=MESH,
        )

    @pl.loop(0, pairs)
    def _(p):
        forward_states(p, scale, q_ref, k_ref, v_ref, omx_ref, onehot_ref, strad_ref, stradrow_ref, pq_ref, pk_ref, peak_ref, send_ref)
        copy(p).start()

    @pl.loop(0, pairs)
    def _(p):
        copy(p).wait()
        forward_finish(p, scale, v_ref, pq_ref, pk_ref, mask_ref, strad_ref, peak_ref, state_ref, att_ref, den_ref)


def backward_kernel_wide(
    scale, q_ref, k_ref, v_ref, pq_ref, pk_ref, att_ref, den_ref, peak_ref, state_ref, gatt_ref, ints_ref, len_ref,
    gq_ref, gk_ref, gv_ref,
    gstate_ref, omx_ref, mask_ref, onehot_ref, strad_ref, stradrow_ref, send_ref, ssem, rsem,
):
    place = lax.axis_index("seq")
    peer = {"seq": 1 - place}
    peer_barrier([peer])
    pairs = q_ref.shape[0]
    doc_setup(len_ref, place, mask_ref, onehot_ref, strad_ref, stradrow_ref)
    features_setup(ints_ref, omx_ref)

    def copy(p):
        return pltpu.make_async_remote_copy(
            src_ref=send_ref.at[p], dst_ref=gstate_ref.at[p], send_sem=ssem.at[p], recv_sem=rsem.at[p],
            device_id=peer, device_id_type=MESH,
        )

    @pl.loop(0, pairs)
    def _(p):
        backward_states(p, scale, att_ref, den_ref, gatt_ref, pq_ref, strad_ref, peak_ref, state_ref, send_ref)
        copy(p).start()

    @pl.loop(0, pairs)
    def _(p):
        copy(p).wait()
        backward_finish(
            p, scale, q_ref, k_ref, v_ref, omx_ref, pq_ref, pk_ref, mask_ref, strad_ref, peak_ref, state_ref, gstate_ref,
            att_ref, den_ref, gatt_ref, gq_ref, gk_ref, gv_ref,
        )


def attention_forward_wide(x, wq, wk, wv, biases, ints, lengths):
    rows = x.shape[0]
    heads, size, feats = ints.shape
    pairs = heads // 2
    scale = size ** (-0.25) * unit_spread
    shape = jax.ShapeDtypeStruct
    return pl.pallas_call(
        partial(forward_kernel_wide, scale),
        out_shape=[
            shape((pairs, rows, 128), bf16), shape((pairs, rows, 128), bf16), shape((pairs, rows, 128), bf16),
            shape((pairs, 2, rows, feats), bf16), shape((pairs, 2, rows, feats), bf16),
            shape((pairs, rows, 128), bf16), shape((pairs, rows, 128), f32),
            shape((pairs, 2, 1, feats), f32), shape((pairs, 128 + TAIL, feats), bf16),
        ],
        in_specs=[vmem()] * 6 + [pl.BlockSpec(memory_space=pltpu.SMEM)],
        out_specs=[vmem()] * 9,
        scratch_shapes=scratch_masks(rows, heads, feats) + [
            pltpu.VMEM((pairs, 128 + TAIL, feats), bf16),
            pltpu.SemaphoreType.DMA((pairs,)),
            pltpu.SemaphoreType.DMA((pairs,)),
        ],
        compiler_params=pltpu.CompilerParams(collective_id=0, has_side_effects=True, vmem_limit_bytes=60 << 20),
        name="attention_forward",
    )(x, wq, wk, wv, biases, ints, lengths)


def attention_backward_wide(saved, gatt, ints, lengths):
    pairs, rows, _ = gatt.shape
    heads, size, feats = ints.shape
    scale = size ** (-0.25) * unit_spread
    shape = jax.ShapeDtypeStruct
    return pl.pallas_call(
        partial(backward_kernel_wide, scale),
        out_shape=[shape((pairs, rows, 128), bf16)] * 3,
        in_specs=[vmem()] * 11 + [pl.BlockSpec(memory_space=pltpu.SMEM)],
        out_specs=[vmem()] * 3,
        scratch_shapes=[pltpu.VMEM((pairs, 128 + TAIL, feats), bf16)] + scratch_masks(rows, heads, feats) + [
            pltpu.VMEM((pairs, 128 + TAIL, feats), bf16),
            pltpu.SemaphoreType.DMA((pairs,)),
            pltpu.SemaphoreType.DMA((pairs,)),
        ],
        compiler_params=pltpu.CompilerParams(collective_id=1, has_side_effects=True, vmem_limit_bytes=60 << 20),
        name="attention_backward",
    )(*saved, gatt, ints, lengths)


def gathered(piece):
    return lax.all_gather(piece, "fsdp", axis=0, tiled=True)


def per_device_wide(
    tokens, doc_lengths, feature_ints, w_query, b_query, w_key, b_key, w_value, b_value, w_out, b_out,
    norm1_gain, norm1_bias, w_in, b_in, w_down, b_down, norm2_gain, norm2_bias, cotangent,
):
    row_block = tokens[0]
    width = row_block.shape[1]
    fsdp = lax.axis_size("fsdp")
    me = lax.axis_index("fsdp")
    attn_stack = gathered(jnp.stack([w_query, w_key, w_value, w_out], axis=1))
    query_weight, key_weight, value_weight, out_weight = (attn_stack[:, i] for i in range(4))
    small = jnp.concatenate(
        [b_query, b_key, b_value, b_out, norm1_gain, norm1_bias, b_down, norm2_gain, norm2_bias, b_in]
    )
    small = lax.all_gather(small[None], "fsdp", axis=0, tiled=True)
    part = width // fsdp
    vectors = [small[:, part * i : part * (i + 1)].reshape(-1) for i in range(9)] + [small[:, 9 * part :].reshape(-1)]
    query_bias, key_bias, value_bias, out_bias, gain_one, offset_one, down_bias, gain_two, offset_two, in_bias = vectors
    saved = attention_forward_wide(
        row_block, query_weight, key_weight, value_weight, jnp.stack([query_bias, key_bias, value_bias]),
        feature_ints, doc_lengths,
    )
    att_rows = from_pairs(saved[5])
    residual_one = row_block.astype(f32) + affine(att_rows, out_weight, out_bias)
    hidden_wide, normed_one, inverse_one = layer_norm(residual_one, gain_one, offset_one)
    hidden_low = hidden_wide.astype(bf16)
    in_weight = gathered(w_in)
    down_weight = gathered(w_down)
    pre_act = affine(hidden_low, in_weight, in_bias)
    gelu_low = gelu_value(pre_act).astype(bf16)
    residual_two = hidden_low.astype(f32) + affine(gelu_low, down_weight, down_bias)
    layer_wide, normed_two, inverse_two = layer_norm(residual_two, gain_two, offset_two)
    grad_out = cotangent[0].astype(f32)
    grad_resid_two, grad_gain_two, grad_offset_two = norm_back(grad_out, normed_two, inverse_two, gain_two)
    grad_down_low = grad_resid_two.astype(bf16)
    grad_down_weight = mul_ta(gelu_low, grad_down_low)
    grad_down_bias = column_total(grad_down_low)
    grad_pre_low = (mul_tb(grad_down_low, down_weight) * gelu_slope(pre_act)).astype(bf16)
    grad_in_weight = mul_ta(hidden_low, grad_pre_low)
    grad_in_bias = column_total(grad_pre_low)
    grad_hidden = mul_tb(grad_pre_low, in_weight) + grad_resid_two
    grad_resid_one, grad_gain_one, grad_offset_one = norm_back(grad_hidden, normed_one, inverse_one, gain_one)
    grad_proj_low = grad_resid_one.astype(bf16)
    grad_out_weight = mul_ta(att_rows, grad_proj_low)
    grad_out_bias = column_total(grad_proj_low)
    grad_att_rows = mul_tb(grad_proj_low, out_weight).astype(bf16)
    grads = attention_backward_wide(saved, to_pairs(grad_att_rows), feature_ints, doc_lengths)
    grad_query_rows, grad_key_rows, grad_value_rows = (from_pairs(g) for g in grads)
    grad_query_weight = mul_ta(row_block, grad_query_rows)
    grad_key_weight = mul_ta(row_block, grad_key_rows)
    grad_value_weight = mul_ta(row_block, grad_value_rows)
    grad_input = (
        mul_tb(grad_query_rows, query_weight)
        + mul_tb(grad_key_rows, key_weight)
        + mul_tb(grad_value_rows, value_weight)
        + grad_resid_one
    )

    def owned(grad):
        shard = lax.psum_scatter(grad.astype(bf16), "fsdp", scatter_dimension=0, tiled=True)
        return lax.psum(shard, "seq").astype(f32)

    sums = jnp.stack(
        [
            column_total(grad_query_rows), column_total(grad_key_rows), column_total(grad_value_rows), grad_out_bias,
            grad_gain_one, grad_offset_one, grad_down_bias, grad_gain_two, grad_offset_two,
            *grad_in_bias.reshape(-1, width),
        ]
    )
    sums = lax.psum(sums, ("fsdp", "seq"))
    mine = [lax.dynamic_slice(sums[i], (me * part,), (part,)) for i in range(9)]
    wide = in_bias.shape[0] // fsdp
    mine_in = lax.dynamic_slice(sums[9:].reshape(-1), (me * wide,), (wide,))
    return (
        layer_wide.astype(bf16)[None],
        grad_input[None],
        owned(grad_query_weight), mine[0],
        owned(grad_key_weight), mine[1],
        owned(grad_value_weight), mine[2],
        owned(grad_out_weight), mine[3],
        mine[4], mine[5],
        owned(grad_in_weight), mine_in,
        owned(grad_down_weight), mine[6],
        mine[7], mine[8],
    )


def solution(mesh):
    rows, matrix, vector = P("fsdp", "seq", None), P("fsdp", None), P("fsdp")
    weights = (matrix, vector) * 4 + (vector, vector) + (matrix, vector) * 2 + (vector, vector)
    near = mesh.shape["fsdp"] == 4 * DEPTH and mesh.shape["seq"] == 2
    return jax.shard_map(
        per_device if near else per_device_wide,
        mesh=mesh,
        in_specs=(rows, matrix, P(), *weights, rows),
        out_specs=(rows, rows, *weights),
        check_vma=False,
    )
```

```python
from functools import partial

import jax
import jax.numpy as jnp
from jax import lax
from jax.experimental import pallas as pl
from jax.experimental.pallas import tpu as pltpu
from jax.sharding import PartitionSpec as P

unit_spread = 0.013531646934131853
inv_root_two = 0.7071067811865476
inv_root_tau = 0.3989422804014327
far_below = -1e30
log2_e = 1.4426950408889634
MESH = pl.DeviceIdType.MESH
f32 = jnp.float32
bf16 = jnp.bfloat16
TAIL = 16
DEPTH = 4
AHEAD = 1


def layer_norm(residual, norm_gain, norm_bias):
    centred = residual - jnp.mean(residual, axis=1, keepdims=True)
    inverse = lax.rsqrt(jnp.mean(centred * centred, axis=1, keepdims=True) + 1e-06)
    normed = centred * inverse
    return (normed * norm_gain.astype(f32) + norm_bias.astype(f32), normed, inverse)


def norm_back(grad_out, normed, inverse, norm_gain):
    scaled = grad_out * norm_gain.astype(f32)
    centre_part = jnp.mean(scaled, axis=1, keepdims=True)
    slope_part = jnp.mean(scaled * normed, axis=1, keepdims=True)
    grad_resid = inverse * (scaled - centre_part - normed * slope_part)
    return (grad_resid, jnp.sum(grad_out * normed, axis=0), jnp.sum(grad_out, axis=0))


def gelu_value(pre_act):
    return 0.5 * pre_act * (1.0 + lax.erf(pre_act * inv_root_two))


def gelu_slope(pre_act):
    return (
        0.5 * (1.0 + lax.erf(pre_act * inv_root_two))
        + pre_act * jnp.exp(-0.5 * pre_act * pre_act) * inv_root_tau
    )


def mul(a, b):
    return lax.dot_general(a, b, (((1,), (0,)), ((), ())), preferred_element_type=f32)


def mul_tb(a, b):
    return lax.dot_general(a, b, (((1,), (1,)), ((), ())), preferred_element_type=f32)


def mul_ta(a, b):
    return lax.dot_general(a, b, (((0,), (0,)), ((), ())), preferred_element_type=f32)


def affine(row_block, weight, bias_row):
    return mul(row_block, weight) + bias_row.astype(f32)


def column_total(values):
    return jnp.sum(values, axis=0, dtype=f32)


def lane_ids(shape):
    return lax.broadcasted_iota(jnp.int32, shape, len(shape) - 1)


def doc_setup(lengths, place, mask_ref, onehot_ref, strad_ref, stradrow_ref):
    rows = mask_ref.shape[0]
    docs = lengths.shape[1]
    total = jnp.int32(0)
    ends = []
    for d in range(docs):
        total = total + lengths[0, d]
        ends.append(total)
    pos = lax.broadcasted_iota(jnp.int32, (rows, 128), 0) + place * rows
    pos_row = lax.broadcasted_iota(jnp.int32, (8, rows), 1) + place * rows
    did = jnp.zeros((rows, 128), jnp.int32)
    did_row = jnp.zeros((8, rows), jnp.int32)
    edge = jnp.int32(0)
    for end in ends[:-1]:
        did = did + (pos >= end).astype(jnp.int32)
        did_row = did_row + (pos_row >= end).astype(jnp.int32)
        edge = edge + (end <= rows).astype(jnp.int32)
    for j in range(rows // 128):
        cols = did_row[0:1, j * 128 : (j + 1) * 128]
        mask_ref[:, j * 128 : (j + 1) * 128] = (did == cols).astype(f32).astype(bf16)
    onehot_ref[...] = (did == lane_ids((rows, 128))).astype(f32)
    strad_ref[...] = (did == edge).astype(f32)
    one_row = (did_row[0:1] == edge).astype(f32)
    stradrow_ref[...] = jnp.broadcast_to(one_row, stradrow_ref.shape).astype(bf16)


def features_setup(ints_ref, omx_ref):
    heads, size, feats = ints_ref.shape

    @pl.loop(0, heads)
    def _(h):
        mat = ints_ref[h].astype(f32).astype(bf16)
        zero = jnp.zeros((size, feats), bf16)
        odd = lax.rem(h, 2) == 1
        omx_ref[h, 0:size] = jnp.where(odd, zero, mat)
        omx_ref[h, size : 2 * size] = jnp.where(odd, mat, zero)
        omx_ref[h, 2 * size :] = jnp.ones((2 * size, feats), bf16)


def three_terms(value):
    first = value.astype(bf16).astype(f32)
    second = (value - first).astype(bf16).astype(f32)
    return first, second, value - first - second


def forward_states(p, scale, q_ref, k_ref, v_ref, omx_ref, onehot_ref, strad_ref, stradrow_ref, pq_ref, pk_ref, peak_ref, out_ref):
    rows = q_ref.shape[1]
    lanes = lane_ids((1, 128))
    qp, kp, vp = q_ref[p], k_ref[p], v_ref[p]
    kf = kp.astype(f32)
    ksq = kf * kf
    vt = jnp.concatenate([vp.T * stradrow_ref[0:1], stradrow_ref[...]], axis=0)
    tail = jnp.zeros((TAIL, pq_ref.shape[-1]), f32)
    tail_row = lax.broadcasted_iota(jnp.int32, tail.shape, 0)
    for j in range(2):
        om = omx_ref[2 * p + j, 0:128]
        raw_q = mul(qp, om)
        raw_q = raw_q - jnp.max(raw_q, axis=1, keepdims=True)
        pq_ref[p, j] = jnp.exp2(raw_q * (scale * log2_e)).astype(bf16)
        here = (lanes >= 64) if j else (lanes < 64)
        half = jnp.sum(jnp.where(here, ksq, 0.0), axis=1, keepdims=True) * (0.0625 / scale)
        raw_k = mul(kp, om) - half
        row_peak = jnp.max(raw_k, axis=1, keepdims=True)
        doc_peak = jnp.max(jnp.where(onehot_ref[...] > 0.5, row_peak, far_below), axis=0, keepdims=True)
        back = jnp.max(jnp.where(onehot_ref[...] > 0.5, doc_peak, far_below), axis=1, keepdims=True)
        edge_peak = jnp.max(jnp.where(strad_ref[...] > 0.5, row_peak, far_below), axis=0, keepdims=True)
        phi_k = jnp.exp2((raw_k - back) * (scale * log2_e)).astype(bf16)
        pk_ref[p, j] = phi_k
        part = mul(vt, phi_k)
        out_ref[p, 64 * j : 64 * j + 64] = part[64 * j : 64 * j + 64].astype(bf16)
        edge_wide = jnp.concatenate([edge_peak, edge_peak], axis=1)
        peak_ref[p, j] = edge_wide
        tail = jnp.where(tail_row == j, part[128 : 128 + TAIL], tail)
        for t, term in enumerate(three_terms(edge_wide)):
            tail = jnp.where(tail_row == 2 + 3 * j + t, term, tail)
    out_ref[p, 128:] = tail.astype(bf16)


def edge_parts(state_ref, p, j):
    tail = state_ref[p, 128:].astype(f32)
    feats = tail.shape[1]
    totals = jnp.broadcast_to(tail[j : j + 1], (128, feats)).astype(bf16)
    peak = tail[2 + 3 * j : 3 + 3 * j] + tail[3 + 3 * j : 4 + 3 * j] + tail[4 + 3 * j : 5 + 3 * j]
    return jnp.concatenate([state_ref[p, 0:128], totals], axis=0), peak


def edge_weights(scale, own, other, strad):
    top = jnp.maximum(own, other)
    own_w = jnp.exp2((own - top) * (scale * log2_e))
    other_w = jnp.exp2((other - top) * (scale * log2_e))
    return 1.0 + strad * (own_w[:, 0:128] - 1.0), strad * other_w[:, 0:128]


def forward_finish(p, scale, v_ref, pq_ref, pk_ref, mask_ref, strad_ref, peak_ref, in_ref, att_ref, den_ref):
    rows = v_ref.shape[1]
    first_half = lane_ids((rows, 128)) < 64
    vx = jnp.concatenate([v_ref[p], jnp.ones((rows, 128), bf16)], axis=1)
    got = []
    for j in range(2):
        phi_q = pq_ref[p, j]
        pair = mul_tb(phi_q, pk_ref[p, j]).astype(bf16) * mask_ref[...]
        near = mul(pair, vx)
        state, other = edge_parts(in_ref, p, j)
        far = mul_tb(phi_q, state)
        wn, wf = edge_weights(scale, peak_ref[p, j], other, strad_ref[...])
        den = near[:, 128:] * wn + far[:, 128:] * wf
        got.append(((near[:, :128] * wn + far[:, :128] * wf) / den, den))
    att_ref[p] = jnp.where(first_half, got[0][0], got[1][0]).astype(bf16)
    den_ref[p] = jnp.where(first_half, got[0][1], got[1][1])


def numer_grads(p, att_ref, den_ref, gatt_ref):
    rows = att_ref.shape[1]
    lanes = lane_ids((rows, 128))
    gn = gatt_ref[p].astype(f32) / den_ref[p]
    prod = gn * att_ref[p].astype(f32)
    d0 = -jnp.sum(jnp.where(lanes < 64, prod, 0.0), axis=1, keepdims=True)
    d1 = -jnp.sum(jnp.where(lanes < 64, 0.0, prod), axis=1, keepdims=True)
    return gn, d0, d1, lanes


def backward_states(p, scale, att_ref, den_ref, gatt_ref, pq_ref, strad_ref, peak_ref, in_ref, out_ref):
    gn, d0, d1, lanes = numer_grads(p, att_ref, den_ref, gatt_ref)
    far = [edge_weights(scale, peak_ref[p, j], edge_parts(in_ref, p, j)[1], strad_ref[...])[1] for j in range(2)]
    left = (gn * jnp.where(lanes < 64, far[0], far[1])).astype(bf16)
    right = (jnp.where(lanes == 0, d0 * far[0], 0.0) + jnp.where(lanes == 1, d1 * far[1], 0.0)).astype(bf16)
    turned = jnp.concatenate([left.T, right.T[0:TAIL]], axis=0)
    tails = []
    for j in range(2):
        part = mul(turned, pq_ref[p, j])
        out_ref[p, 64 * j : 64 * j + 64] = part[64 * j : 64 * j + 64].astype(bf16)
        tails.append(part[128:])
    rowid = lax.broadcasted_iota(jnp.int32, tails[0].shape, 0)
    out_ref[p, 128:] = jnp.where(rowid == 0, tails[0], tails[1]).astype(bf16)


def backward_finish(
    p, scale, q_ref, k_ref, v_ref, omx_ref, pq_ref, pk_ref, mask_ref, strad_ref, peak_ref, in_ref, gin_ref,
    att_ref, den_ref, gatt_ref, gq_ref, gk_ref, gv_ref,
):
    rows = q_ref.shape[1]
    gn, d0, d1, lanes = numer_grads(p, att_ref, den_ref, gatt_ref)
    first_half = lanes < 64
    vp = v_ref[p]
    ones = jnp.ones((rows, 128), bf16)
    vx = jnp.concatenate([vp, ones], axis=1)
    strad = strad_ref[...]
    gq = jnp.zeros((rows, 128), f32)
    gk = jnp.zeros((rows, 128), f32)
    gv = jnp.zeros((rows, 128), f32)
    q_sums, k_sums = [], []
    for j in range(2):
        here = (lanes >= 64) if j else (lanes < 64)
        gd = d1 if j else d0
        state, other = edge_parts(in_ref, p, j)
        wn, wf = edge_weights(scale, peak_ref[p, j], other, strad)
        base_l = jnp.where(here, gn, 0.0)
        base_r = jnp.where(lanes == 0, gd, 0.0)
        near = jnp.concatenate([(base_l * wn).astype(bf16), (base_r * wn).astype(bf16)], axis=1)
        far = jnp.concatenate([(base_l * wf).astype(bf16), (base_r * wf).astype(bf16)], axis=1)
        phi_q, phi_k = pq_ref[p, j], pk_ref[p, j]
        turned = mul_tb(phi_k, phi_q).astype(bf16) * mask_ref[...]
        gv = gv + mul(turned, near[:, 0:128])
        gpair = mul_tb(near, vx).astype(bf16) * mask_ref[...]
        gphi_q = mul(gpair, phi_k) + mul(far, state)
        gturned = mul_tb(vx, near).astype(bf16) * mask_ref[...]
        gstate, _ = edge_parts(gin_ref, p, j)
        vs = jnp.concatenate(
            [(jnp.where(here, vp.astype(f32), 0.0) * strad).astype(bf16), jnp.where(lanes == 0, strad, 0.0).astype(bf16)],
            axis=1,
        )
        gphi_k = mul(gturned, phi_q) + mul(vs, gstate)
        gv = gv + jnp.where(here, mul_tb(phi_k, gstate[0:128]) * strad, 0.0)
        omx = omx_ref[2 * p + j]
        back_q = mul_tb((gphi_q * phi_q.astype(f32)).astype(bf16), omx)
        back_k = mul_tb((gphi_k * phi_k.astype(f32)).astype(bf16), omx)
        gq = gq + back_q[:, 0:128]
        gk = gk + back_k[:, 0:128]
        q_sums.append(back_q[:, 128:])
        k_sums.append(back_k[:, 128:])
    gq = gq * scale - jnp.where(first_half, q_sums[0], q_sums[1]) * q_ref[p].astype(f32) * 0.125
    gk = gk * scale - jnp.where(first_half, k_sums[0], k_sums[1]) * k_ref[p].astype(f32) * 0.125
    gq_ref[p] = gq.astype(bf16)
    gk_ref[p] = gk.astype(bf16)
    gv_ref[p] = gv.astype(bf16)


def peer_barrier(peers):
    barrier = pltpu.get_barrier_semaphore()
    for peer in peers:
        pl.semaphore_signal(barrier, inc=1, device_id=peer, device_id_type=MESH)
    pl.semaphore_wait(barrier, len(peers))


class Place:
    def __init__(self):
        me = lax.axis_index("fsdp")
        self.y = lax.axis_index("seq")
        self.c = lax.rem(me, 2)
        self.x = lax.rem(lax.div(me, 2), 2)
        self.z = lax.div(me, 4)
        self.across = {"seq": 1 - self.y}
        self.twin = {"fsdp": self.z * 4 + self.x * 2 + 1 - self.c}
        self.beside = {"fsdp": self.z * 4 + (1 - self.x) * 2 + self.c}

    def along(self, d):
        return {"fsdp": self.other(d) * 4 + self.x * 2 + self.c}

    def other(self, d):
        return lax.rem(self.z + (d + DEPTH), DEPTH)

    def peers(self):
        return [self.twin, self.beside, self.across] + [self.along(d) for d in range(1, DEPTH)]


def cols_at(start, size):
    return pl.ds(pl.multiple_of(start, 128), size)


def remote(src, dst, ssem, rsem, peer):
    return pltpu.make_async_remote_copy(
        src_ref=src, dst_ref=dst, send_sem=ssem, recv_sem=rsem, device_id=peer, device_id_type=MESH
    )


class Gather:
    def __init__(self, at, own, full, base, width, ssem, rsem, lsem):
        self.at, self.own, self.full = at, own, full
        self.third, self.base, self.width = width // 3, base, width
        self.ssem, self.rsem, self.lsem = ssem, rsem, lsem
        self.sent = []

    def spread(self):
        return cols_at(self.base + self.third * self.at.y, 2 * self.third)

    def extra(self, y):
        return cols_at(self.base + 2 * self.third * y, self.third)

    def whole(self):
        return pl.ds(self.base, self.width)

    def go(self, n, ends):
        src, dst, peer = ends()
        remote(src, dst, self.ssem.at[n], self.rsem.at[n], peer).start()
        self.sent.append((n, ends))

    def came(self, n, ref):
        remote(ref, ref, self.ssem.at[n], self.rsem.at[n], self.at.twin).wait_recv()

    def local(self):
        at = self.at
        return pltpu.make_async_copy(
            self.own.at[:, self.whole()], self.full.at[at.z, at.x, at.c, :, self.whole()], self.lsem
        )

    def begin(self):
        at = self.at
        self.local().start()
        for d in range(1, DEPTH):
            self.go(d - 1, lambda d=d: (*self.first(), at.along(d)))

    def first(self):
        at = self.at
        return self.own.at[:, self.spread()], self.full.at[at.z, at.x, at.c, :, self.spread()]

    def piece(self, d, x, cols):
        return self.full.at[self.at.other(-d), x, self.at.c, :, cols]

    def stage_x(self):
        at = self.at
        self.go(DEPTH - 1, lambda: (*self.first(), at.beside))
        for d in range(1, DEPTH):
            self.came(d - 1, self.piece(d, at.x, self.spread()))
            self.go(DEPTH - 1 + d, lambda d=d: (*[self.piece(d, at.x, self.spread())] * 2, at.beside))
            self.go(2 * DEPTH - 2 + d, lambda d=d: (*[self.piece(d, at.x, self.extra(at.y))] * 2, at.across))

    def stage_y(self):
        at = self.at
        for d in range(DEPTH):
            self.came(DEPTH - 1 + d, self.piece(d, 1 - at.x, self.spread()))
            self.go(3 * DEPTH - 2 + d, lambda d=d: (*[self.piece(d, 1 - at.x, self.extra(at.y))] * 2, at.across))

    def stage_c(self):
        at = self.at
        for d in range(1, DEPTH):
            self.came(2 * DEPTH - 2 + d, self.piece(d, at.x, self.extra(1 - at.y)))
        for d in range(DEPTH):
            self.came(3 * DEPTH - 2 + d, self.piece(d, 1 - at.x, self.extra(1 - at.y)))
        self.local().wait()
        self.go(4 * DEPTH - 2, lambda: (*[self.full.at[:, :, at.c, :, self.whole()]] * 2, at.twin))

    def ready(self):
        self.came(4 * DEPTH - 2, self.full.at[:, :, 1 - self.at.c, :, self.whole()])

    def drain(self):
        for n, ends in self.sent:
            src, dst, peer = ends()
            remote(src, dst, self.ssem.at[n], self.rsem.at[n], peer).wait_send()


GATHER_COPIES = 4 * DEPTH - 1


class SmallSum:
    def __init__(self, at, total, land, ssem, rsem, over_seq):
        self.at, self.total, self.land, self.ssem, self.rsem, self.over_seq = at, total, land, ssem, rsem, over_seq
        self.sent = []

    def go(self, src, n, peer):
        copy = remote(self.total.at[src], self.land.at[n], self.ssem.at[n], self.rsem.at[n], peer)
        copy.start()
        self.sent.append(copy)

    def came(self, n):
        remote(self.land.at[n], self.land.at[n], self.ssem.at[n], self.rsem.at[n], self.at.twin).wait_recv()

    def begin(self):
        for d in range(1, DEPTH):
            self.go(0, d - 1, self.at.along(d))

    def step(self, k):
        if k == 0:
            got = self.total[0]
            for d in range(1, DEPTH):
                self.came(d - 1)
            order = [self.at.z] + [self.at.other(-d) for d in range(1, DEPTH)]
            parts = [got] + [self.land[d - 1] for d in range(1, DEPTH)]
            value = jnp.zeros_like(got)
            for z in range(DEPTH):
                one = jnp.zeros_like(got)
                for place, part in zip(order, parts):
                    one = jnp.where(place == z, part, one)
                value = value + one
        else:
            self.came(DEPTH - 2 + k)
            value = self.total[k] + self.land[DEPTH - 2 + k]
        self.total[k + 1] = value
        hops = [self.at.beside, self.at.twin] + ([self.at.across] if self.over_seq else [])
        if k < len(hops):
            self.go(k + 1, DEPTH - 1 + k, hops[k])

    def steps(self):
        return 4 if self.over_seq else 3

    def result(self):
        return self.total[self.steps()]

    def drain(self):
        for copy in self.sent:
            copy.wait_send()


def spread_vectors(at, pieces, wide):
    width = 768
    part = pieces[0].shape[-1]
    rows = [p[...].astype(f32).reshape(1, part) for p in pieces]
    rows = jnp.concatenate(rows + [jnp.zeros((16 - len(rows), part), f32)], axis=0)
    rows = jnp.concatenate([rows, jnp.zeros((16, width - part), f32)], axis=1)
    rows = pltpu.roll(rows, (at.z * 4 + at.x * 2 + at.c) * part, 1)
    span = wide.shape[-1]
    row = jnp.concatenate([wide[...].astype(f32).reshape(1, span), jnp.zeros((1, width - span), f32)], axis=1)
    row = pltpu.roll(jnp.broadcast_to(row, (16, width)), (at.x * 2 + at.c) * span, 1)
    here = lax.broadcasted_iota(jnp.int32, (16, width), 0)
    return jnp.where(here == len(pieces) + at.z, row, rows)


HOLD = (
    "omx", "xt", "mask", "strad", "q", "k", "v", "pq", "pk", "att", "attt", "den", "sq", "hidt", "norm", "fin", "gelt", "slope", "fdn",
)
LATE = ("xt", "q", "k", "v", "pq", "pk", "att", "attt", "den", "omx", "mask", "strad")


def forward_kernel(
    scale, x_ref, wq_ref, wk_ref, wv_ref, wo_ref, win_ref, wdn_ref, bq_ref, bk_ref, bv_ref, bo_ref, g1_ref, o1_ref, bd_ref,
    g2_ref, o2_ref, bin_ref, ints_ref, cot_ref, len_ref, layer_ref, peak_ref, state_ref, inv_ref, res_ref, vec_ref, sums_ref, *rest,
):
    outs, rest = rest[: len(HOLD)], rest[len(HOLD) :]
    hold, rest = rest[: len(HOLD)], rest[len(HOLD) :]
    (
        omx_ref, xt_ref, mask_ref, strad_ref, q_ref, k_ref, v_ref, pq_ref, pk_ref, att_ref, attt_ref, den_ref, sq_ref, hidt_ref,
        norm_ref, fin_ref, gelt_ref, slope_ref, fdn_ref,
    ) = hold
    hid_ref, gel_ref, onehot_ref, stradrow_ref, send_ref, total_ref, land_ref = rest[:7]
    ssem, rsem, gs_sem, gr_sem, gl_sem, vs_sem, vr_sem, out_sem = rest[7:]
    at = Place()
    pairs = q_ref.shape[0]
    rows, width = x_ref.shape

    def stash(*names):
        return [pltpu.make_async_copy(hold[n], outs[n], out_sem.at[n]) for n in map(HOLD.index, names)]

    def give(*names):
        for copy in stash(*names):
            copy.start()

    blocks = []
    specs = [(w, sq_ref.at[n], 0, 768) for n, w in enumerate((wq_ref, wk_ref, wv_ref, wo_ref))]
    specs += [(win_ref, fin_ref, 768 * h, 768) for h in range(4)]
    specs += [
        (wdn_ref.at[pl.ds(96 * r, 96)], fdn_ref.at[:, :, :, pl.ds(96 * r, 96)], 384 * h, 384) for h in range(2) for r in range(2)
    ]
    for n, (own, full, base, span) in enumerate(specs):
        blocks.append(Gather(at, own, full, base, span, gs_sem.at[n], gr_sem.at[n], gl_sem.at[n]))
    peer_barrier(at.peers())
    vec = SmallSum(at, total_ref, land_ref, vs_sem, vr_sem, False)
    total_ref[0] = spread_vectors(
        at, (bq_ref, bk_ref, bv_ref, bo_ref, g1_ref, o1_ref, bd_ref, g2_ref, o2_ref), bin_ref
    ).astype(bf16)
    blocks[0].begin()
    vec.begin()
    for b in blocks[1:AHEAD]:
        b.begin()
    doc_setup(len_ref, at.y, mask_ref, onehot_ref, strad_ref, stradrow_ref)
    features_setup(ints_ref, omx_ref)
    for j in range(pairs):
        xt_ref[128 * j : 128 * j + 128] = x_ref[:, 128 * j : 128 * j + 128].T
    give("omx", "xt", "mask", "strad")
    sums_ref[...] = jnp.zeros_like(sums_ref)

    def vector(n, cols=slice(None)):
        return vec_ref[n : n + 1, cols].astype(f32)

    def project(n, o_ref):
        for j in range(pairs // 2):
            cols = slice(256 * j, 256 * j + 256)
            got = mul(x_ref[...], sq_ref[n, :, :, :, :, cols].reshape(768, 256))
            got = (got + vector(n, cols)).astype(bf16)
            o_ref[2 * j] = got[:, 0:128]
            o_ref[2 * j + 1] = got[:, 128:256]

    def tick(t):
        if t + AHEAD < len(blocks):
            blocks[t + AHEAD].begin()
        for k, name in enumerate(("stage_x", "stage_y", "stage_c", "ready")):
            if 0 <= t - k < len(blocks):
                getattr(blocks[t - k], name)()

    for t in range(3):
        tick(t)
        vec.step(t)
    vec_ref[...] = vec.result()
    for n, ref in enumerate((q_ref, k_ref, v_ref)):
        tick(3 + n)
        project(n, ref)
        give("qkv"[n])

    def copy(p):
        return remote(send_ref.at[p], state_ref.at[p], ssem.at[p], rsem.at[p], at.across)

    def ticks_at(p, plan):
        for n, t in plan.items():
            @pl.when(p == n)
            def _(t=t):
                tick(t)

    @pl.loop(0, pairs)
    def _(p):
        forward_states(p, scale, q_ref, k_ref, v_ref, omx_ref, onehot_ref, strad_ref, stradrow_ref, pq_ref, pk_ref, peak_ref, send_ref)
        copy(p).start()
        ticks_at(p, {0: 6, 2: 7, 4: 8})

    give("pq", "pk", "sq")

    @pl.loop(0, pairs)
    def _(p):
        copy(p).wait()
        forward_finish(p, scale, v_ref, pq_ref, pk_ref, mask_ref, strad_ref, peak_ref, state_ref, att_ref, den_ref)
        attt_ref[p] = att_ref[p].T
        ticks_at(p, {0: 9, 3: 10})

    give("att", "attt", "den", "fin")


    whole = jnp.concatenate([att_ref[p] for p in range(pairs)], axis=1)
    for j in range(pairs // 2):
        cols = slice(256 * j, 256 * j + 256)
        got = mul(whole, sq_ref[3, :, :, :, :, cols].reshape(768, 256))
        res_ref[:, cols] = got + vector(3, cols) + x_ref[:, cols].astype(f32)

    def centred(value):
        value = value - jnp.mean(value, axis=1, keepdims=True)
        inverse = lax.rsqrt(jnp.mean(value * value, axis=1, keepdims=True) + 1e-06)
        return value * inverse, inverse

    def here(r):
        return pl.ds(pl.multiple_of(128 * r, 128), 128)

    @pl.loop(0, rows // 128)
    def _(r):
        normed, inverse = centred(res_ref[here(r)])
        inv_ref[here(r)] = inverse
        norm_ref[here(r)] = normed.astype(bf16)
        hid_ref[here(r)] = (normed * vector(4) + vector(5)).astype(bf16)

    for j in range(pairs):
        hidt_ref[128 * j : 128 * j + 128] = hid_ref[:, 128 * j : 128 * j + 128].T
    give("hidt", "norm")


    @pl.loop(0, 4)
    def _(b):
        ticks_at(b, {0: 11, 2: 12})
        for j in range(3):
            cols = cols_at(768 * b + 256 * j, 256)
            pre = mul(hid_ref[...], fin_ref[:, :, :, :, cols].reshape(768, 256))
            bias = jnp.zeros((1, 256), f32)
            for n in range(4):
                bias = jnp.where(b == n, vector(9 + n, slice(256 * j, 256 * j + 256)), bias)
            pre = pre + bias
            share = 0.5 * (1.0 + lax.erf(pre * inv_root_two))
            gel = (pre * share).astype(bf16)
            gel_ref[:, cols] = gel
            gelt_ref[cols] = gel.T
            slope_ref[:, cols] = (share + pre * (jnp.exp(-0.5 * pre * pre) * inv_root_tau)).astype(bf16)

    give("gelt", "slope")

    def down(h):
        cols = slice(384 * h, 384 * h + 384)
        res_ref[:, cols] = hid_ref[:, cols].astype(f32) + vector(6, cols)

        @pl.loop(0, DEPTH)
        def _(z):
            got = mul(gel_ref[:, cols_at(768 * z, 768)], fdn_ref[z, :, :, :, cols].reshape(768, 384))
            res_ref[:, cols] = res_ref[:, cols] + got

    down(0)
    tick(13)
    tick(14)
    give("fdn")
    down(1)


    @pl.loop(0, rows // 128)
    def _(r):
        normed, inverse = centred(res_ref[here(r)])
        layer_ref[here(r)] = (normed * vector(7) + vector(8)).astype(bf16)
        grad = cot_ref[here(r)].astype(f32)
        scaled = grad * vector(7)
        centre = jnp.mean(scaled, axis=1, keepdims=True)
        lean = jnp.mean(scaled * normed, axis=1, keepdims=True)
        resid = inverse * (scaled - centre - normed * lean)
        res_ref[here(r)] = resid
        sums_ref[6:7] = sums_ref[6:7] + jnp.sum(resid.astype(bf16).astype(f32), axis=0, keepdims=True)
        sums_ref[7:8] = sums_ref[7:8] + jnp.sum(grad * normed, axis=0, keepdims=True)
        sums_ref[8:9] = sums_ref[8:9] + jnp.sum(grad, axis=0, keepdims=True)

    for b in blocks:
        b.drain()
    vec.drain()
    for one in stash(*HOLD):
        one.wait()


class Scatter:
    def __init__(self, at, order, source, twin_in, lands, done, done_in, put, ssem, rsem):
        self.at, self.order, self.source, self.acc = at, order, source, source(at.c)
        self.twin_in, self.lands = twin_in, lands
        self.done, self.done_in, self.put = done, done_in, put
        self.ssem, self.rsem = ssem, rsem
        self.half = twin_in.shape[-1] // 2
        self.sent = []

    def go(self, n, ends):
        src, dst, peer = ends()
        remote(src, dst, self.ssem.at[n], self.rsem.at[n], peer).start()
        self.sent.append((n, ends))

    def came(self, n, ref):
        remote(ref, ref, self.ssem.at[n], self.rsem.at[n], self.at.twin).wait_recv()

    def side(self, y):
        return cols_at(self.half * y, self.half)

    def spot(self, fixed, **other):
        at = self.at
        z = other.get("z", at.z if "z" in fixed else slice(None))
        x = other.get("x", at.x if "x" in fixed else slice(None))
        cols = self.side(other.get("y", at.y)) if "y" in fixed or "y" in other else slice(None)
        return z, x, slice(None), cols

    def first(self, i):
        return 1 + sum(DEPTH - 1 if kind == "z" else 1 for kind in self.order[:i])

    def send(self, i):
        at, kind, fixed = self.at, self.order[i], self.order[:i]
        if kind == "z":
            for d in range(1, DEPTH):
                self.go(
                    self.first(i) + d - 1,
                    lambda d=d: (self.acc.at[self.spot(fixed, z=at.other(d))], self.lands[i].at[d - 1], at.along(d)),
                )
        elif kind == "x":
            self.go(self.first(i), lambda: (self.acc.at[self.spot(fixed, x=1 - at.x)], self.lands[i], at.beside))
        else:
            self.go(self.first(i), lambda: (self.acc.at[self.spot(fixed, y=1 - at.y)], self.lands[i], at.across))

    def add(self, parts, fixed, store):
        def at_z(z):
            for x in [None] if "x" in fixed else range(2):
                spot = list(self.spot(fixed))
                inner = ()
                if z is not None:
                    spot[0] = z
                    inner += (z,)
                if x is not None:
                    spot[1] = x
                    inner += (x,)
                value = self.acc[tuple(spot)].astype(f32)
                for part in parts:
                    value = value + part[inner + (slice(None), slice(None))].astype(f32)
                store(tuple(spot), value)

        if "z" in fixed:
            at_z(None)
        else:
            pl.loop(0, DEPTH)(at_z)

    def keep(self, spot, value):
        self.acc[spot] = value.astype(bf16)

    def finish(self, spot, value):
        low = value.astype(bf16)
        self.done[...] = low
        self.put(self.at.y, low.astype(f32))

    def arrived(self, i):
        if self.order[i] != "z":
            self.came(self.first(i), self.lands[i])
            return [self.lands[i]]
        for d in range(1, DEPTH):
            self.came(self.first(i) + d - 1, self.lands[i].at[d - 1])
        return [self.lands[i].at[d - 1] for d in range(1, DEPTH)]

    def begin(self):
        self.go(0, lambda: (self.source(1 - self.at.c), self.twin_in, self.at.twin))

    def stage_1(self):
        self.came(0, self.twin_in)
        self.add([self.twin_in], "", self.keep)
        self.send(0)

    def stage_2(self):
        self.add(self.arrived(0), self.order[:1], self.keep)
        self.send(1)

    def stage_3(self):
        self.add(self.arrived(1), self.order[:2], self.keep)
        self.send(2)

    def stage_4(self):
        self.add(self.arrived(2), self.order, self.finish)
        self.go(2 + DEPTH, lambda: (self.done, self.done_in, self.at.across))

    def stage_5(self):
        self.came(2 + DEPTH, self.done_in)
        self.put(1 - self.at.y, self.done_in[...].astype(f32))

    def drain(self):
        for n, ends in self.sent:
            src, dst, peer = ends()
            remote(src, dst, self.ssem.at[n], self.rsem.at[n], peer).wait_send()


def landing(order, part, width):
    shapes = []
    for i, kind in enumerate(order):
        kept = order[: i + 1]
        shape = [] if "z" in kept else [DEPTH]
        shape += [] if "x" in kept else [2]
        shape += [part, width // 2 if "y" in kept else width]
        shapes.append(pltpu.VMEM(tuple([DEPTH - 1] + shape if kind == "z" else shape), bf16))
    return shapes


SCATTER_COPIES = DEPTH + 3
GELU_SLOTS = 4
FEED_SLOTS = 3
FEED_STEPS = (1, 5)
HEAD_STEPS = (0, 1, 2, 3, 4, 5)
PACE = ((0, 2, 4, 6, 8),) * 8 + ((0, 2, 3, 4, 5),) + ((0, 1, 2, 3, 4),) * 3
ORDERS = ("yxz", "xyz", "xyz") * 4


def backward_kernel(
    scale, peak_ref, state_ref, hidt_ref, norm_ref, inv_ref, res_ref, gain_ref, vecin_ref, gel_ref, slope_ref, win_ref, wdn_ref,
    sq_ref, *rest,
):
    late_refs, rest = rest[: len(LATE)], rest[len(LATE) :]
    gx_ref, oq_ref, ok_ref, ov_ref, oo_ref, oin_ref, odn_ref, vec_ref = rest[:8]
    kept_refs, rest = rest[8 : 8 + len(LATE)], rest[8 + len(LATE) :]
    xt_ref, q_ref, k_ref, v_ref, pq_ref, pk_ref, att_ref, attt_ref, den_ref, omx_ref, mask_ref, strad_ref = kept_refs
    gstate_ref, send_ref, gq_ref, gk_ref, gv_ref, gatt_ref, low_ref, wide_ref, gelbuf_ref, slopebuf_ref, winbuf_ref = rest[:11]
    gdn_ref, gin_ref, go_ref, gw_ref, total_ref, land_ref, twin_ref, done_ref, donein_ref = rest[11:20]
    ssem, rsem, load_sem, late_sem, keep_sem, ws_sem, wr_sem, vs_sem, vr_sem = rest[20:29]
    land_refs = rest[29:]
    at = Place()
    pairs = q_ref.shape[0]
    rows, width = res_ref.shape
    span = width // 2
    chunks = win_ref.shape[1] // span
    sources = [lambda c, b=b: gdn_ref.at[:, :, c, pl.ds(48 * b, 48)] for b in range(4)]
    sources += [lambda c, b=b: gin_ref.at[:, :, c, :, pl.ds(768 * b, 768)] for b in range(4)]
    sources += [lambda c: go_ref.at[:, :, c]]
    sources += [lambda c, n=n: gw_ref.at[n, :, :, c] for n in (2, 1, 0)]

    def putter(ref, row, col):
        def put(y, value):
            ref[pl.ds(row, 48), cols_at(col + 384 * y, 384)] = value

        return put

    puts = [putter(odn_ref, 48 * b, 0) for b in range(4)] + [putter(oin_ref, 0, 768 * b) for b in range(4)]
    puts += [putter(r, 0, 0) for r in (oo_ref, ov_ref, ok_ref, oq_ref)]
    units = []
    for n, (source, put) in enumerate(zip(sources, puts)):
        lands = land_refs[3 * n : 3 * n + 3]
        units.append(
            Scatter(
                at, ORDERS[n], source, twin_ref.at[n], lands, done_ref.at[n], donein_ref.at[n], put, ws_sem.at[n], wr_sem.at[n]
            )
        )
    early = len(units) - 3

    def step(s):
        for k in range(5):
            for u, unit in enumerate(units):
                if u + PACE[u][k] == s:
                    getattr(unit, "stage_" + str(k + 1))()


    def load(src, dst, sem):
        return pltpu.make_async_copy(src, dst, sem)

    def gelu_at(m):
        return lax.rem(m, GELU_SLOTS)

    def load_gelu(m):
        return load(
            gel_ref.at[pl.ds(pl.multiple_of(span * m, 128), span)], gelbuf_ref.at[gelu_at(m)], load_sem.at[0, gelu_at(m)]
        )

    def slot(m):
        return lax.rem(m, FEED_SLOTS)

    def down_at(m):
        n = slot(m)
        return 2 * lax.div(n, 2), pl.ds(pl.multiple_of(span * lax.rem(n, 2), 128), span)

    def load_chunk(m):
        return [
            load(slope_ref.at[:, cols_at(span * m, span)], slopebuf_ref.at[slot(m)], load_sem.at[1, slot(m)]),
            load(wdn_ref.at[pl.ds(pl.multiple_of(span * m, 128), span)], wide_ref.at[down_at(m)], load_sem.at[2, slot(m)]),
            load(win_ref.at[:, cols_at(span * m, span)], winbuf_ref.at[slot(m)], load_sem.at[3, slot(m)]),
        ]

    def load_square(n, to):
        return load(sq_ref.at[n], wide_ref.at[to], late_sem.at[to])

    peer_barrier(at.peers())
    first = load(res_ref, gx_ref, late_sem.at[0])
    first.start()
    for m in range(GELU_SLOTS - 1):
        load_gelu(jnp.int32(m)).start()
    for m in range(FEED_SLOTS - 1):
        for one in load_chunk(jnp.int32(m)):
            one.start()
    load_square(3, 1).start()
    kept = [load(src, dst, keep_sem.at[n]) for n, (src, dst) in enumerate(zip(late_refs, kept_refs))]
    for one in kept:
        one.start()
    total_ref[0] = vecin_ref[...]

    first.wait()

    @pl.loop(0, rows // 128)
    def _(r):
        here = pl.ds(pl.multiple_of(128 * r, 128), 128)
        low_ref[here] = gx_ref[here].astype(bf16)


    @pl.loop(0, chunks)
    def _(m):
        load_gelu(m).wait()

        @pl.when(m < chunks - (GELU_SLOTS - 1))
        def _():
            load_gelu(m + GELU_SLOTS - 1).start()

        turned = gelbuf_ref[gelu_at(m)]
        for n in range(3):
            cols = slice(256 * n, 256 * n + 256)
            got = mul(turned, low_ref[:, cols]).astype(bf16)
            gdn_ref[lax.div(m, 2), lax.rem(m, 2), :, :, cols] = got.reshape(2, span // 2, 256)

    units[0].begin()
    units[1].begin()
    @pl.loop(0, chunks)
    def _(m):
        for one in load_chunk(m):
            one.wait()

        @pl.when(m < chunks - (FEED_SLOTS - 1))
        def _():
            for one in load_chunk(m + FEED_SLOTS - 1):
                one.start()

        start = pl.multiple_of(span * lax.rem(m, 2), 128)
        gpre = mul_tb(low_ref[...], wide_ref[down_at(m)]) * slopebuf_ref[slot(m)].astype(f32)
        gpre = gpre.astype(bf16)
        total_ref[0, pl.ds(9 + lax.div(m, 2), 1), cols_at(start, span)] = jnp.sum(gpre.astype(f32), axis=0, keepdims=True)
        got = mul(hidt_ref[...], gpre).astype(bf16)
        gin_ref[:, :, :, :, cols_at(span * m, span)] = got.reshape(DEPTH, 2, 2, 48, span)
        for n in range(3):
            cols = slice(256 * n, 256 * n + 256)
            gx_ref[:, cols] = gx_ref[:, cols] + mul_tb(gpre, winbuf_ref[slot(m), cols])
        for n in range(8):
            @pl.when(m == n)
            def _(n=n):
                if n < 2:
                    units[2 + n].begin()
                if n % 2:
                    units[4 + n // 2].begin()
                if n in FEED_STEPS:
                    step(FEED_STEPS.index(n))

    done_steps = len(FEED_STEPS)

    @pl.loop(0, rows // 128)
    def _(r):
        here = pl.ds(pl.multiple_of(128 * r, 128), 128)
        grad = gx_ref[here]
        normed = norm_ref[here].astype(f32)
        scaled = grad * gain_ref[4:5].astype(f32)
        centre = jnp.mean(scaled, axis=1, keepdims=True)
        slope = jnp.mean(scaled * normed, axis=1, keepdims=True)
        resid = inv_ref[here] * (scaled - centre - normed * slope)
        gx_ref[here] = resid
        low = resid.astype(bf16)
        low_ref[here] = low
        total_ref[0, 3:4] = total_ref[0, 3:4] + jnp.sum(low.astype(f32), axis=0, keepdims=True)
        total_ref[0, 4:5] = total_ref[0, 4:5] + jnp.sum(grad * normed, axis=0, keepdims=True)
        total_ref[0, 5:6] = total_ref[0, 5:6] + jnp.sum(grad, axis=0, keepdims=True)

    load_square(3, 1).wait()
    for one in kept:
        one.wait()
    for h in range(2):
        turned = attt_ref[3 * h : 3 * h + 3].reshape(384, rows)
        for n in range(3):
            cols = slice(256 * n, 256 * n + 256)
            go_ref[2 * h : 2 * h + 2, :, :, :, cols] = mul(turned, low_ref[:, cols]).astype(bf16).reshape(2, 2, 2, 48, 256)
    units[8].begin()
    for j in range(pairs // 2):
        got = mul_tb(low_ref[...], wide_ref[1, 256 * j : 256 * j + 256]).astype(bf16)
        gatt_ref[2 * j] = got[:, 0:128]
        gatt_ref[2 * j + 1] = got[:, 128:256]
    for n in range(3):
        load_square(n, n).start()
    step(done_steps)
    done_steps += 1


    def copy(p):
        return remote(send_ref.at[p], gstate_ref.at[p], ssem.at[p], rsem.at[p], at.across)

    @pl.loop(0, pairs)
    def _(p):
        backward_states(p, scale, att_ref, den_ref, gatt_ref, pq_ref, strad_ref, peak_ref, state_ref, send_ref)
        copy(p).start()

    @pl.loop(0, pairs)
    def _(p):
        copy(p).wait()
        backward_finish(
            p, scale, q_ref, k_ref, v_ref, omx_ref, pq_ref, pk_ref, mask_ref, strad_ref, peak_ref, state_ref, gstate_ref,
            att_ref, den_ref, gatt_ref, gq_ref, gk_ref, gv_ref,
        )
        cols = cols_at(128 * p, 128)
        both = mul(xt_ref[...], jnp.concatenate([gq_ref[p], gk_ref[p]], axis=1)).astype(bf16)
        gw_ref[0, :, :, :, :, cols] = both[:, 0:128].reshape(DEPTH, 2, 2, 48, 128)
        gw_ref[1, :, :, :, :, cols] = both[:, 128:256].reshape(DEPTH, 2, 2, 48, 128)
        gw_ref[2, :, :, :, :, cols] = mul(xt_ref[...], gv_ref[p]).astype(bf16).reshape(DEPTH, 2, 2, 48, 128)
        for n, ref in enumerate((gq_ref, gk_ref, gv_ref)):
            total_ref[0, n : n + 1, cols] = jnp.sum(ref[p].astype(f32), axis=0, keepdims=True)
        for n, at_pair in enumerate(HEAD_STEPS):
            @pl.when(p == at_pair)
            def _(n=n):
                step(n + done_steps)

    vec = SmallSum(at, total_ref, land_ref, vs_sem, vr_sem, True)
    vec.begin()
    for u in units[early:]:
        u.begin()
    for n in range(3):
        load_square(n, n).wait()

    def grad_input(j):
        cols = slice(256 * j, 256 * j + 256)
        value = gx_ref[:, cols]
        for n, ref in enumerate((gq_ref, gk_ref, gv_ref)):
            for i in range(pairs // 2):
                left = jnp.concatenate([ref[2 * i], ref[2 * i + 1]], axis=1)
                right = wide_ref[n, 256 * j : 256 * j + 256, 256 * i : 256 * i + 256]
                value = value + mul_tb(left, right)
        gx_ref[:, cols] = value

    done_steps += len(HEAD_STEPS)
    for n, s in enumerate(range(done_steps, len(units) + PACE[-1][-1])):
        step(s)
        if n < 4:
            vec.step(n)
        if n < 3:
            grad_input(n)
    vec_ref[...] = vec.result()
    for u in units:
        u.drain()
    vec.drain()


def scratch_masks(rows, heads, feats):
    return [
        pltpu.VMEM((heads, 256, feats), bf16),
        pltpu.VMEM((rows, rows), bf16),
        pltpu.VMEM((rows, 128), f32),
        pltpu.VMEM((rows, 128), f32),
        pltpu.VMEM((TAIL, rows), bf16),
    ]


def vmem():
    return pl.BlockSpec(memory_space=pltpu.VMEM)


def anywhere():
    return pl.BlockSpec(memory_space=pl.ANY)


def smem():
    return pl.BlockSpec(memory_space=pltpu.SMEM)


def attention_forward(x, weights, vectors, ints, cot, lengths):
    rows, width = x.shape
    heads, size, feats = ints.shape
    pairs = heads // 2
    hidden = weights[4].shape[1]
    part = weights[0].shape[0]
    scale = size ** (-0.25) * unit_spread
    shape = jax.ShapeDtypeStruct
    grid = (DEPTH, 2, 2)
    dma = pltpu.SemaphoreType.DMA
    pair, phi, full, tall = (pairs, rows, 128), (pairs, 2, rows, feats), (rows, width), (rows, hidden)
    held = {
        "omx": (heads, 256, feats), "xt": (width, rows), "mask": (rows, rows), "strad": (rows, 128), "q": pair, "k": pair, "v": pair, "pq": phi, "pk": phi, "att": pair,
        "attt": (pairs, 128, rows), "den": pair, "sq": (4, *grid, part, width), "hidt": (width, rows), "norm": full,
        "fin": (*grid, part, hidden), "gelt": (hidden, rows), "slope": tall,
        "fdn": (*grid, weights[5].shape[0], width),
    }
    kind = {name: f32 if name in ("den", "strad") else bf16 for name in HOLD}
    layer, peak, state, inverse, resid, vec, sums, *rest = pl.pallas_call(
        partial(forward_kernel, scale),
        out_shape=[
            shape(full, bf16), shape((pairs, 2, 1, feats), f32), shape((pairs, 128 + TAIL, feats), bf16),
            shape((rows, 1), f32), shape(full, f32), shape((16, width), bf16), shape((16, width), f32),
        ] + [shape(held[name], kind[name]) for name in HOLD],
        in_specs=[vmem()] * 19 + [smem()],
        out_specs=[vmem()] * 7 + [anywhere()] * len(HOLD),
        scratch_shapes=[pltpu.VMEM(held[name], kind[name]) for name in HOLD] + [
            pltpu.VMEM(full, bf16), pltpu.VMEM(tall, bf16),
            pltpu.VMEM((rows, 128), f32), pltpu.VMEM((TAIL, rows), bf16),
            pltpu.VMEM((pairs, 128 + TAIL, feats), bf16),
            pltpu.VMEM((4, 16, width), bf16),
            pltpu.VMEM((DEPTH + 1, 16, width), bf16),
            dma((pairs,)), dma((pairs,)),
            dma((12, GATHER_COPIES)), dma((12, GATHER_COPIES)), dma((12,)),
            dma((DEPTH + 1,)), dma((DEPTH + 1,)), dma((len(HOLD),)),
        ],
        compiler_params=pltpu.CompilerParams(collective_id=0, has_side_effects=True, vmem_limit_bytes=65200 << 10),
        name="attention_forward",
    )(x, *weights, *vectors, ints, cot, lengths)
    got = dict(zip(HOLD, rest))
    inner = (peak, state, got["hidt"], got["norm"], inverse, resid, vec, sums)
    late = (
        got["gelt"], got["slope"], got["fin"].reshape(width, hidden), got["fdn"].reshape(hidden, width),
        got["sq"].reshape(4, width, width), *(got[name] for name in LATE),
    )
    return layer, inner, late


def attention_backward(inner, late):
    rows, width = inner[5].shape
    pairs, _, _, feats = inner[0].shape
    heads, hidden = 2 * pairs, late[0].shape[0]
    scale = (width // heads) ** (-0.25) * unit_spread
    shape = jax.ShapeDtypeStruct
    dma = pltpu.SemaphoreType.DMA
    grid = (DEPTH, 2, 2)
    part = width // 16
    units = 12
    return pl.pallas_call(
        partial(backward_kernel, scale),
        out_shape=[shape((rows, width), f32)]
        + [shape((part, width), f32)] * 4
        + [shape((part, hidden), f32), shape((hidden // 16, width), f32), shape((16, width), f32)],
        in_specs=[vmem()] * 5 + [anywhere()] + [vmem()] * 2 + [anywhere()] * (5 + len(LATE)),
        out_specs=[vmem()] * 8,
        scratch_shapes=[pltpu.VMEM(one.shape, one.dtype) for one in late[5:]] + [
            pltpu.VMEM((pairs, 128 + TAIL, feats), bf16), pltpu.VMEM((pairs, 128 + TAIL, feats), bf16),
            pltpu.VMEM((pairs, rows, 128), bf16), pltpu.VMEM((pairs, rows, 128), bf16), pltpu.VMEM((pairs, rows, 128), bf16),
            pltpu.VMEM((pairs, rows, 128), bf16),
            pltpu.VMEM((rows, width), bf16),
            pltpu.VMEM((3, width, width), bf16),
            pltpu.VMEM((GELU_SLOTS, width // 2, rows), bf16), pltpu.VMEM((FEED_SLOTS, rows, width // 2), bf16),
            pltpu.VMEM((FEED_SLOTS, width, width // 2), bf16),
            pltpu.VMEM((*grid, hidden // 16, width), bf16),
            pltpu.VMEM((*grid, part, hidden), bf16),
            pltpu.VMEM((*grid, part, width), bf16),
            pltpu.VMEM((3, *grid, part, width), bf16),
            pltpu.VMEM((5, 16, width), f32),
            pltpu.VMEM((DEPTH + 2, 16, width), f32),
            pltpu.VMEM((units, DEPTH, 2, part, width), bf16),
            pltpu.VMEM((units, part, width // 2), bf16),
            pltpu.VMEM((units, part, width // 2), bf16),
            dma((pairs,)), dma((pairs,)), dma((4, GELU_SLOTS)), dma((3,)), dma((len(LATE),)),
            dma((units, SCATTER_COPIES)), dma((units, SCATTER_COPIES)),
            dma((DEPTH + 2,)), dma((DEPTH + 2,)),
        ] + [land for order in ORDERS for land in landing(order, part, width)],
        compiler_params=pltpu.CompilerParams(collective_id=1, has_side_effects=True, vmem_limit_bytes=65200 << 10),
        name="attention_backward",
    )(*inner, *late)


def finish_kernel(sums_ref, *refs):
    big = BIG
    ins, outs, vectors, mids, sem = refs[:big], refs[big : 2 * big], refs[2 * big : -1 - big], refs[-1 - big : -1], refs[-1]
    taken = [pltpu.make_async_copy(src, dst, sem.at[0, n]) for n, (src, dst) in enumerate(zip(ins, mids))]
    given = [pltpu.make_async_copy(src, dst, sem.at[1, n]) for n, (src, dst) in enumerate(zip(mids, outs))]
    for one in taken:
        one.start()
    me = lax.axis_index("fsdp")
    part, wide = vectors[0].shape[1], vectors[9].shape[1]
    width = sums_ref.shape[1]
    sums = sums_ref[...]
    turned = pltpu.roll(sums, lax.rem(width - part * me, width), 1)
    for n in range(9):
        vectors[n][...] = turned[n : n + 1, 0:part]
    inner = pltpu.roll(sums, lax.rem(width - wide * lax.rem(me, 4), width), 1)
    row = jnp.zeros((1, width), f32)
    for n in range(DEPTH):
        row = jnp.where(lax.div(me, 4) == n, inner[9 + n : 10 + n], row)
    vectors[9][...] = row[:, 0:wide]
    for one, two in zip(taken, given):
        one.wait()
        two.start()
    for two in given:
        two.wait()


BIG = 8


def finish(arrays, sums, part, wide):
    shape = jax.ShapeDtypeStruct
    return pl.pallas_call(
        finish_kernel,
        out_shape=[shape(a.shape, a.dtype) for a in arrays] + [shape((1, part), f32)] * 9 + [shape((1, wide), f32)],
        in_specs=[vmem()] + [anywhere()] * BIG,
        out_specs=[anywhere()] * BIG + [vmem()] * 10,
        scratch_shapes=[pltpu.VMEM(a.shape, a.dtype) for a in arrays] + [pltpu.SemaphoreType.DMA((2, BIG))],
        name="finish",
    )(sums, *arrays)


def to_pairs(rows):
    return rows.reshape(rows.shape[0], -1, 128).transpose(1, 0, 2)


def from_pairs(pairs):
    return pairs.transpose(1, 0, 2).reshape(pairs.shape[1], -1)


def per_device(
    tokens, doc_lengths, feature_ints, w_query, b_query, w_key, b_key, w_value, b_value, w_out, b_out,
    norm1_gain, norm1_bias, w_in, b_in, w_down, b_down, norm2_gain, norm2_bias, cotangent,
):
    layer_out, inner, late = attention_forward(
        tokens[0],
        (w_query, w_key, w_value, w_out, w_in, w_down),
        (b_query, b_key, b_value, b_out, norm1_gain, norm1_bias, b_down, norm2_gain, norm2_bias, b_in),
        feature_ints, cotangent[0], doc_lengths,
    )
    *grads, sums = attention_backward(inner, late)
    done = finish((layer_out, *grads), sums, b_query.shape[0], b_in.shape[0])
    layer_out, grad_input, gq, gk, gv, go, gin, gdn = done[:BIG]
    bq, bk, bv, bo, g1, o1, bd, g2, o2, bi = (one.reshape(-1) for one in done[BIG:])
    return (
        layer_out[None], grad_input[None],
        gq, bq, gk, bk, gv, bv, go, bo, g1, o1, gin, bi, gdn, bd, g2, o2,
    )


def forward_kernel_wide(
    scale, x_ref, wq_ref, wk_ref, wv_ref, bias_ref, ints_ref, len_ref,
    q_ref, k_ref, v_ref, pq_ref, pk_ref, att_ref, den_ref, peak_ref, state_ref,
    omx_ref, mask_ref, onehot_ref, strad_ref, stradrow_ref, send_ref, ssem, rsem,
):
    place = lax.axis_index("seq")
    peer = {"seq": 1 - place}
    peer_barrier([peer])
    pairs = q_ref.shape[0]
    doc_setup(len_ref, place, mask_ref, onehot_ref, strad_ref, stradrow_ref)
    features_setup(ints_ref, omx_ref)
    for n, (w_ref, o_ref) in enumerate(((wq_ref, q_ref), (wk_ref, k_ref), (wv_ref, v_ref))):
        for j in range(pairs // 2):
            cols = slice(256 * j, 256 * j + 256)
            got = (mul(x_ref[...], w_ref[:, cols]) + bias_ref[n : n + 1, cols].astype(f32)).astype(bf16)
            o_ref[2 * j] = got[:, 0:128]
            o_ref[2 * j + 1] = got[:, 128:256]

    def copy(p):
        return pltpu.make_async_remote_copy(
            src_ref=send_ref.at[p], dst_ref=state_ref.at[p], send_sem=ssem.at[p], recv_sem=rsem.at[p],
            device_id=peer, device_id_type=MESH,
        )

    @pl.loop(0, pairs)
    def _(p):
        forward_states(p, scale, q_ref, k_ref, v_ref, omx_ref, onehot_ref, strad_ref, stradrow_ref, pq_ref, pk_ref, peak_ref, send_ref)
        copy(p).start()

    @pl.loop(0, pairs)
    def _(p):
        copy(p).wait()
        forward_finish(p, scale, v_ref, pq_ref, pk_ref, mask_ref, strad_ref, peak_ref, state_ref, att_ref, den_ref)


def backward_kernel_wide(
    scale, q_ref, k_ref, v_ref, pq_ref, pk_ref, att_ref, den_ref, peak_ref, state_ref, gatt_ref, ints_ref, len_ref,
    gq_ref, gk_ref, gv_ref,
    gstate_ref, omx_ref, mask_ref, onehot_ref, strad_ref, stradrow_ref, send_ref, ssem, rsem,
):
    place = lax.axis_index("seq")
    peer = {"seq": 1 - place}
    peer_barrier([peer])
    pairs = q_ref.shape[0]
    doc_setup(len_ref, place, mask_ref, onehot_ref, strad_ref, stradrow_ref)
    features_setup(ints_ref, omx_ref)

    def copy(p):
        return pltpu.make_async_remote_copy(
            src_ref=send_ref.at[p], dst_ref=gstate_ref.at[p], send_sem=ssem.at[p], recv_sem=rsem.at[p],
            device_id=peer, device_id_type=MESH,
        )

    @pl.loop(0, pairs)
    def _(p):
        backward_states(p, scale, att_ref, den_ref, gatt_ref, pq_ref, strad_ref, peak_ref, state_ref, send_ref)
        copy(p).start()

    @pl.loop(0, pairs)
    def _(p):
        copy(p).wait()
        backward_finish(
            p, scale, q_ref, k_ref, v_ref, omx_ref, pq_ref, pk_ref, mask_ref, strad_ref, peak_ref, state_ref, gstate_ref,
            att_ref, den_ref, gatt_ref, gq_ref, gk_ref, gv_ref,
        )


def attention_forward_wide(x, wq, wk, wv, biases, ints, lengths):
    rows = x.shape[0]
    heads, size, feats = ints.shape
    pairs = heads // 2
    scale = size ** (-0.25) * unit_spread
    shape = jax.ShapeDtypeStruct
    return pl.pallas_call(
        partial(forward_kernel_wide, scale),
        out_shape=[
            shape((pairs, rows, 128), bf16), shape((pairs, rows, 128), bf16), shape((pairs, rows, 128), bf16),
            shape((pairs, 2, rows, feats), bf16), shape((pairs, 2, rows, feats), bf16),
            shape((pairs, rows, 128), bf16), shape((pairs, rows, 128), f32),
            shape((pairs, 2, 1, feats), f32), shape((pairs, 128 + TAIL, feats), bf16),
        ],
        in_specs=[vmem()] * 6 + [pl.BlockSpec(memory_space=pltpu.SMEM)],
        out_specs=[vmem()] * 9,
        scratch_shapes=scratch_masks(rows, heads, feats) + [
            pltpu.VMEM((pairs, 128 + TAIL, feats), bf16),
            pltpu.SemaphoreType.DMA((pairs,)),
            pltpu.SemaphoreType.DMA((pairs,)),
        ],
        compiler_params=pltpu.CompilerParams(collective_id=0, has_side_effects=True, vmem_limit_bytes=60 << 20),
        name="attention_forward",
    )(x, wq, wk, wv, biases, ints, lengths)


def attention_backward_wide(saved, gatt, ints, lengths):
    pairs, rows, _ = gatt.shape
    heads, size, feats = ints.shape
    scale = size ** (-0.25) * unit_spread
    shape = jax.ShapeDtypeStruct
    return pl.pallas_call(
        partial(backward_kernel_wide, scale),
        out_shape=[shape((pairs, rows, 128), bf16)] * 3,
        in_specs=[vmem()] * 11 + [pl.BlockSpec(memory_space=pltpu.SMEM)],
        out_specs=[vmem()] * 3,
        scratch_shapes=[pltpu.VMEM((pairs, 128 + TAIL, feats), bf16)] + scratch_masks(rows, heads, feats) + [
            pltpu.VMEM((pairs, 128 + TAIL, feats), bf16),
            pltpu.SemaphoreType.DMA((pairs,)),
            pltpu.SemaphoreType.DMA((pairs,)),
        ],
        compiler_params=pltpu.CompilerParams(collective_id=1, has_side_effects=True, vmem_limit_bytes=60 << 20),
        name="attention_backward",
    )(*saved, gatt, ints, lengths)


def gathered(piece):
    return lax.all_gather(piece, "fsdp", axis=0, tiled=True)


def per_device_wide(
    tokens, doc_lengths, feature_ints, w_query, b_query, w_key, b_key, w_value, b_value, w_out, b_out,
    norm1_gain, norm1_bias, w_in, b_in, w_down, b_down, norm2_gain, norm2_bias, cotangent,
):
    row_block = tokens[0]
    width = row_block.shape[1]
    fsdp = lax.axis_size("fsdp")
    me = lax.axis_index("fsdp")
    attn_stack = gathered(jnp.stack([w_query, w_key, w_value, w_out], axis=1))
    query_weight, key_weight, value_weight, out_weight = (attn_stack[:, i] for i in range(4))
    small = jnp.concatenate(
        [b_query, b_key, b_value, b_out, norm1_gain, norm1_bias, b_down, norm2_gain, norm2_bias, b_in]
    )
    small = lax.all_gather(small[None], "fsdp", axis=0, tiled=True)
    part = width // fsdp
    vectors = [small[:, part * i : part * (i + 1)].reshape(-1) for i in range(9)] + [small[:, 9 * part :].reshape(-1)]
    query_bias, key_bias, value_bias, out_bias, gain_one, offset_one, down_bias, gain_two, offset_two, in_bias = vectors
    saved = attention_forward_wide(
        row_block, query_weight, key_weight, value_weight, jnp.stack([query_bias, key_bias, value_bias]),
        feature_ints, doc_lengths,
    )
    att_rows = from_pairs(saved[5])
    residual_one = row_block.astype(f32) + affine(att_rows, out_weight, out_bias)
    hidden_wide, normed_one, inverse_one = layer_norm(residual_one, gain_one, offset_one)
    hidden_low = hidden_wide.astype(bf16)
    in_weight = gathered(w_in)
    down_weight = gathered(w_down)
    pre_act = affine(hidden_low, in_weight, in_bias)
    gelu_low = gelu_value(pre_act).astype(bf16)
    residual_two = hidden_low.astype(f32) + affine(gelu_low, down_weight, down_bias)
    layer_wide, normed_two, inverse_two = layer_norm(residual_two, gain_two, offset_two)
    grad_out = cotangent[0].astype(f32)
    grad_resid_two, grad_gain_two, grad_offset_two = norm_back(grad_out, normed_two, inverse_two, gain_two)
    grad_down_low = grad_resid_two.astype(bf16)
    grad_down_weight = mul_ta(gelu_low, grad_down_low)
    grad_down_bias = column_total(grad_down_low)
    grad_pre_low = (mul_tb(grad_down_low, down_weight) * gelu_slope(pre_act)).astype(bf16)
    grad_in_weight = mul_ta(hidden_low, grad_pre_low)
    grad_in_bias = column_total(grad_pre_low)
    grad_hidden = mul_tb(grad_pre_low, in_weight) + grad_resid_two
    grad_resid_one, grad_gain_one, grad_offset_one = norm_back(grad_hidden, normed_one, inverse_one, gain_one)
    grad_proj_low = grad_resid_one.astype(bf16)
    grad_out_weight = mul_ta(att_rows, grad_proj_low)
    grad_out_bias = column_total(grad_proj_low)
    grad_att_rows = mul_tb(grad_proj_low, out_weight).astype(bf16)
    grads = attention_backward_wide(saved, to_pairs(grad_att_rows), feature_ints, doc_lengths)
    grad_query_rows, grad_key_rows, grad_value_rows = (from_pairs(g) for g in grads)
    grad_query_weight = mul_ta(row_block, grad_query_rows)
    grad_key_weight = mul_ta(row_block, grad_key_rows)
    grad_value_weight = mul_ta(row_block, grad_value_rows)
    grad_input = (
        mul_tb(grad_query_rows, query_weight)
        + mul_tb(grad_key_rows, key_weight)
        + mul_tb(grad_value_rows, value_weight)
        + grad_resid_one
    )

    def owned(grad):
        shard = lax.psum_scatter(grad.astype(bf16), "fsdp", scatter_dimension=0, tiled=True)
        return lax.psum(shard, "seq").astype(f32)

    sums = jnp.stack(
        [
            column_total(grad_query_rows), column_total(grad_key_rows), column_total(grad_value_rows), grad_out_bias,
            grad_gain_one, grad_offset_one, grad_down_bias, grad_gain_two, grad_offset_two,
            *grad_in_bias.reshape(-1, width),
        ]
    )
    sums = lax.psum(sums, ("fsdp", "seq"))
    mine = [lax.dynamic_slice(sums[i], (me * part,), (part,)) for i in range(9)]
    wide = in_bias.shape[0] // fsdp
    mine_in = lax.dynamic_slice(sums[9:].reshape(-1), (me * wide,), (wide,))
    return (
        layer_wide.astype(bf16)[None],
        grad_input[None],
        owned(grad_query_weight), mine[0],
        owned(grad_key_weight), mine[1],
        owned(grad_value_weight), mine[2],
        owned(grad_out_weight), mine[3],
        mine[4], mine[5],
        owned(grad_in_weight), mine_in,
        owned(grad_down_weight), mine[6],
        mine[7], mine[8],
    )


def solution(mesh):
    rows, matrix, vector = P("fsdp", "seq", None), P("fsdp", None), P("fsdp")
    weights = (matrix, vector) * 4 + (vector, vector) + (matrix, vector) * 2 + (vector, vector)
    near = mesh.shape["fsdp"] == 4 * DEPTH and mesh.shape["seq"] == 2
    return jax.shard_map(
        per_device if near else per_device_wide,
        mesh=mesh,
        in_specs=(rows, matrix, P(), *weights, rows),
        out_specs=(rows, rows, *weights),
        check_vma=False,
    )
```
